32 devices in a mesh: dp: 16 (over z, x, core), tensor: 2 (over y).
Axes of the slice: x: 2, y: 2, z: 4, core: 2. Of those that a mesh axis runs over, the one named last changes fastest.
Arguments:
- tokens: bfloat16 [32768, 1024], P(('dp', 'tensor')), may hold values from -6 to 6
- w_qkv: bfloat16 [1024, 3, 1024], P('dp', None, 'tensor'), may hold values from -0.1875 to 0.1875
- w_out: bfloat16 [1024, 1024], P('tensor', 'dp'), may hold values from -0.75 to 0.75
- w_up: bfloat16 [1024, 4096], P('dp', 'tensor'), may hold values from -0.1875 to 0.1875
- w_down: bfloat16 [4096, 1024], P('tensor', 'dp'), may hold values from -0.09375 to 0.09375
- ln1_gain: float32 [1024], replicated, may hold values from 0.5 to 1.5
- ln1_bias: float32 [1024], replicated, may hold values from -1.5 to 1.5
- ln2_gain: float32 [1024], replicated, may hold values from 0.5 to 1.5
- ln2_bias: float32 [1024], replicated, may hold values from -1.5 to 1.5
- a_qkv: bfloat16 [8, 1024, 16], replicated, may hold values from -0.1875 to 0.1875
- b_qkv: bfloat16 [8, 16, 3, 1024], P(None, None, None, 'tensor'), may hold values from -0.75 to 0.75
- a_out: bfloat16 [8, 1024, 16], P(None, 'tensor'), may hold values from -0.75 to 0.75
- b_out: bfloat16 [8, 16, 1024], replicated, may hold values from -0.75 to 0.75
- a_up: bfloat16 [8, 1024, 16], replicated, may hold values from -0.1875 to 0.1875
- b_up: bfloat16 [8, 16, 4096], P(None, None, 'tensor'), may hold values from -0.75 to 0.75
- a_down: bfloat16 [8, 4096, 16], P(None, 'tensor'), may hold values from -0.09375 to 0.09375
- b_down: bfloat16 [8, 16, 1024], replicated, may hold values from -0.75 to 0.75
- adapter_idx: int32 [16, 4], P('dp'), may hold values from 0 to 7
- pic_start: int32 [16, 2], P('dp'), may hold values from 0 to 1792, as said below
- cotangent: bfloat16 [32768, 1024], P(('dp', 'tensor')), may hold values from -6 to 6
Outputs:
- layer_out: bfloat16 [32768, 1024], P(('dp', 'tensor'))
- grad_tokens: float32 [32768, 1024], P(('dp', 'tensor'))
- grad_a_qkv: float32 [8, 1024, 16], replicated
- grad_b_qkv: float32 [8, 16, 3, 1024], P(None, None, None, 'tensor')
- grad_a_out: float32 [8, 1024, 16], P(None, 'tensor')
- grad_b_out: float32 [8, 16, 1024], replicated
- grad_a_up: float32 [8, 1024, 16], replicated
- grad_b_up: float32 [8, 16, 4096], P(None, None, 'tensor')
- grad_a_down: float32 [8, 4096, 16], P(None, 'tensor')
- grad_b_down: float32 [8, 16, 1024], replicated
The draws below stay inside these ranges and needn't reach their ends.
Inputs may be any that keep to these rules, and one draw needn't show every extreme that they name: `pic_start`: each sequence has 2 picture spans of 256 tokens; span k starts between k * 1024 and (k + 1) * 1024 - 256, so spans never intersect.
All inputs are finite; a program needn't handle non-finite values.
Results may differ from the reference program's by a relative error of at most 0.014.
Values may be sent and summed in bfloat16 or wider, within the bound.
A program may use at most 320 MiB of HBM per device.

```python
import jax
import jax.numpy as jnp
from jax import lax

D = 1024
HEADS = 16
HD = 64
FF = 4096
RANK = 16
ADAPT = 8
LEN = 2048
SPAN = 256
NPIC = 2
BLOCK = 512
SEQS = 16
TOKENS = 32768


def draw_pic_start(key, part):
    region = LEN // NPIC
    offsets = jax.random.randint(key, (SEQS, NPIC), 0, region - SPAN + 1)
    return (offsets + region * jnp.arange(NPIC, dtype=jnp.int32)[None, :]).astype(jnp.int32)


def plant(array, key, least, top_value):
    longest = array.shape.index(max(array.shape))
    spots = []
    for shift in (0, 1):
        where = [jax.random.randint(jax.random.fold_in(key, axis), (), 0, length) for axis, length in enumerate(array.shape)]
        where[longest] = (where[longest] + shift) % array.shape[longest]
        spots.append(tuple(where))
    return array.at[spots[0]].set(least).at[spots[1]].set(top_value)


def block_levels(stream_key, shape, pieces, smallest, high):
    factor_of = 1.0
    for axis_at, shards_of in pieces:
        steps = jax.random.uniform(jax.random.fold_in(jax.random.fold_in(stream_key, 6), axis_at), (shards_of,), jnp.float32, smallest / len(pieces), high / len(pieces))
        factor_of = factor_of * jnp.repeat(jnp.exp(steps), shape[axis_at] // shards_of).reshape((-1,) + (1,) * (len(shape) - 1 - axis_at))
    return factor_of


def noise(rng, shape, scale, bound, cuts=(), kind=jnp.bfloat16):
    result = scale * jax.random.normal(rng, shape, jnp.float32)
    if cuts:
        result = result * block_levels(rng, shape, cuts, -0.22, 0.18)
    return jnp.clip(result, -bound, bound).astype(kind)


def setup_inputs(seed: int = 0) -> dict:
    seeds = jax.random.split(jax.random.key(seed), 21)
    return {
        "tokens": noise(seeds[0], (TOKENS, D), 1.0, 6.0, ((0, 32),)),
        "w_qkv": noise(seeds[1], (D, 3, D), D ** -0.5, 0.1875, ((0, 16), (2, 2))),
        "w_out": noise(seeds[2], (D, D), (D // 16) ** -0.5, 0.75, ((0, 2), (1, 16))),
        "w_up": noise(seeds[3], (D, FF), D ** -0.5, 0.1875, ((0, 16), (1, 2))),
        "w_down": noise(seeds[4], (FF, D), FF ** -0.5, 0.09375, ((0, 2), (1, 16))),
        "ln1_gain": jnp.clip(1.0 + 0.1 * jax.random.normal(seeds[5], (D,), jnp.float32), 0.5, 1.5),
        "ln1_bias": noise(seeds[6], (D,), 0.3, 1.5, (), jnp.float32),
        "ln2_gain": jnp.clip(1.0 + 0.1 * jax.random.normal(seeds[7], (D,), jnp.float32), 0.5, 1.5),
        "ln2_bias": noise(seeds[8], (D,), 0.3, 1.5, (), jnp.float32),
        "a_qkv": noise(seeds[9], (ADAPT, D, RANK), D ** -0.5, 0.1875),
        "b_qkv": noise(seeds[10], (ADAPT, RANK, 3, D), (4 * RANK) ** -0.5, 0.75, ((3, 2),)),
        "a_out": noise(seeds[11], (ADAPT, D, RANK), (D // 16) ** -0.5, 0.75, ((1, 2),)),
        "b_out": noise(seeds[12], (ADAPT, RANK, D), (4 * RANK) ** -0.5, 0.75),
        "a_up": noise(seeds[13], (ADAPT, D, RANK), D ** -0.5, 0.1875),
        "b_up": noise(seeds[14], (ADAPT, RANK, FF), (4 * RANK) ** -0.5, 0.75, ((2, 2),)),
        "a_down": noise(seeds[15], (ADAPT, FF, RANK), FF ** -0.5, 0.09375, ((1, 2),)),
        "b_down": noise(seeds[16], (ADAPT, RANK, D), (4 * RANK) ** -0.5, 0.75),
        "adapter_idx": plant(jax.random.randint(seeds[17], (SEQS, 4), 0, ADAPT), jax.random.fold_in(seeds[17], 1), 0, ADAPT - 1).astype(jnp.int32),
        "pic_start": draw_pic_start(jax.random.fold_in(seeds[20], 71), 0),
        "cotangent": noise(seeds[19], (TOKENS, D), 1.0, 6.0, ((0, 32),)),
    }


PRECISE = lax.Precision.HIGHEST

@jax.custom_vjp
def low(v):
    return lax.optimization_barrier(v.astype(jnp.bfloat16)).astype(jnp.float32)

@jax.custom_vjp
def low_back(v):
    return v

def low_keep(v):
    return (low(v), None)

def low_pass(kept, grad):
    return (grad,)

def back_keep(v):
    return (v, None)

def back_low(kept, grad):
    return (low(grad),)
low.defvjp(low_keep, low_pass)
low_back.defvjp(back_keep, back_low)

def product(left, right):
    return jnp.dot(left, right, precision=PRECISE)

def layer_norm(values, multiplier, addend):
    center = values - lax.optimization_barrier(jnp.mean(values, axis=-1, keepdims=True))
    spread = lax.optimization_barrier(jnp.mean(center * center, axis=-1, keepdims=True))
    return center * lax.rsqrt(spread + 1e-05) * multiplier + addend

def span_labels(positions, starts):
    inside = (positions[:, None] >= starts[None, :]) & (positions[:, None] < starts[None, :] + SPAN)
    labels = jnp.arange(1, starts.shape[0] + 1, dtype=jnp.int32)
    return lax.optimization_barrier(jnp.sum(jnp.where(inside, labels[None, :], 0), axis=1))

def allowed_mask(offset, row_count, length, starts):
    row_pos = offset + jnp.arange(row_count, dtype=jnp.int32)
    col_pos = jnp.arange(length, dtype=jnp.int32)
    row_span = span_labels(row_pos, starts)
    col_span = span_labels(col_pos, starts)
    causal = col_pos[None, :] <= row_pos[:, None]
    joined = (row_span[:, None] == col_span[None, :]) & (row_span[:, None] > 0)
    return causal | joined

def attention(queries, key_rows, value_rows, starts):
    length = queries.shape[0]
    factor = HD ** (-0.5)
    blocks = queries.reshape(length // BLOCK, BLOCK, HEADS, HD)
    offsets = jnp.arange(length // BLOCK, dtype=jnp.int32) * BLOCK

    def one_block(query_block, offset):
        scores = low_back(jnp.einsum('qhd,khd->hqk', query_block, key_rows, precision=PRECISE)) * factor
        allowed = allowed_mask(offset, BLOCK, length, starts)
        scores = jnp.where(allowed[None], scores, -1000000000.0)
        probabilities = low(jax.nn.softmax(scores, axis=-1))
        blended = jnp.einsum('hqk,khd->qhd', probabilities, value_rows, precision=PRECISE)
        return low(low_back(blended.reshape(BLOCK, HEADS * HD)))
    checked = jax.checkpoint(one_block)
    blended = lax.map(lambda couple: checked(couple[0], couple[1]), (blocks, offsets))
    return blended.reshape(length, HEADS * HD)

def sequence_layer(seq_tokens, adapters, frozen, selection, starts):
    a_qkv, b_qkv, a_out, b_out, a_up, b_up, a_down, b_down = adapters
    w_qkv, w_out, w_up, w_down, gain_one, shift_one, gain_two, shift_two = frozen

    def chosen(stacked, which_one):
        return lax.dynamic_index_in_dim(stacked, selection[which_one], 0, keepdims=False)
    normed = low(layer_norm(seq_tokens, gain_one, shift_one))
    low_attn = low(low_back(product(normed, chosen(a_qkv, 0))))
    project = product(normed, w_qkv.reshape(D, 3 * D)) + product(low_attn, chosen(b_qkv, 0).reshape(RANK, 3 * D))
    project = low(low_back(project)).reshape(LEN, 3, HEADS, HD)
    blended = attention(project[:, 0], project[:, 1], project[:, 2], starts)
    low_out = low(low_back(product(blended, chosen(a_out, 1))))
    residual = seq_tokens + low_back(product(blended, w_out) + product(low_out, chosen(b_out, 1)))
    normed_two = low(layer_norm(residual, gain_two, shift_two))
    low_up = low(low_back(product(normed_two, chosen(a_up, 2))))
    pre_act = low_back(product(normed_two, w_up) + product(low_up, chosen(b_up, 2)))
    hidden = low(jax.nn.gelu(pre_act, approximate=True))
    low_down = low(low_back(product(hidden, chosen(a_down, 3))))
    return residual + low_back(product(hidden, w_down) + product(low_down, chosen(b_down, 3)))

def reference(tokens, w_qkv, w_out, w_up, w_down, ln1_gain, ln1_bias, ln2_gain, ln2_bias, a_qkv, b_qkv, a_out, b_out, a_up, b_up, a_down, b_down, adapter_idx, pic_start, cotangent):
    frozen = tuple((member.astype(jnp.float32) for member in (w_qkv, w_out, w_up, w_down, ln1_gain, ln1_bias, ln2_gain, ln2_bias)))
    adapters = tuple((member.astype(jnp.float32) for member in (a_qkv, b_qkv, a_out, b_out, a_up, b_up, a_down, b_down)))
    inputs = tokens.astype(jnp.float32).reshape(SEQS, LEN, D)
    cotans = cotangent.astype(jnp.float32).reshape(SEQS, LEN, D)

    def one_sequence(running, member):
        seq_tokens, seq_grad, selection, starts = member
        output, pullback = jax.vjp(lambda sequence, adapted: sequence_layer(sequence, adapted, frozen, selection, starts), seq_tokens, adapters)
        grad_seq, grad_adapt = pullback(seq_grad)
        running = tuple((before + gradient for before, gradient in zip(running, grad_adapt)))
        return (running, (output, grad_seq))
    initial = tuple((jnp.zeros_like(member) for member in adapters))
    running, (outputs, input_grads) = lax.scan(one_sequence, initial, (inputs, cotans, adapter_idx, pic_start))
    return (outputs.reshape(SEQS * LEN, D).astype(jnp.bfloat16), input_grads.reshape(SEQS * LEN, D), running[0], running[1], running[2], running[3], running[4], running[5], running[6], running[7])
```

```python
import functools
import math

import jax
import jax.numpy as jnp
from jax import lax
from jax.experimental import pallas as pl
from jax.experimental.pallas import tpu as pltpu
from jax.sharding import PartitionSpec as P

HD = 64
SPAN = 256
BLOCK = 512


def matmul(left, right):
    return jnp.dot(left, right, preferred_element_type=jnp.float32)


def contract_rows(left, right):
    return lax.dot_general(
        left, right, (((0,), (0,)), ((), ())), preferred_element_type=jnp.float32
    )


def against(left, right):
    return lax.dot_general(
        left, right, (((1,), (1,)), ((), ())), preferred_element_type=jnp.float32
    )


def layer_norm(values, multiplier, addend):
    center = values - jnp.mean(values, axis=-1, keepdims=True)
    spread = jnp.mean(center * center, axis=-1, keepdims=True)
    return center * lax.rsqrt(spread + 1e-05) * multiplier + addend


def span_labels(positions, starts):
    inside = (positions[:, None] >= starts[None, :]) & (positions[:, None] < starts[None, :] + SPAN)
    labels = jnp.arange(1, starts.shape[0] + 1, dtype=jnp.int32)
    return jnp.sum(jnp.where(inside, labels[None, :], 0), axis=1)


def allowed_mask(offset, row_count, length, starts):
    row_pos = offset + jnp.arange(row_count, dtype=jnp.int32)
    col_pos = jnp.arange(length, dtype=jnp.int32)
    row_span = span_labels(row_pos, starts)
    col_span = span_labels(col_pos, starts)
    causal = col_pos[None, :] <= row_pos[:, None]
    joined = (row_span[:, None] == col_span[None, :]) & (row_span[:, None] > 0)
    return causal | joined


def masked_scores(query_block, key_rows, offset, length, starts, factor):
    scores = (
        jnp.einsum("qhd,khd->hqk", query_block, key_rows, preferred_element_type=jnp.float32)
        * factor
    )
    allowed = allowed_mask(offset, BLOCK, length, starts)
    return jnp.where(allowed[None], scores, -1000000000.0)


def attend(queries, key_rows, value_rows, starts):
    length, heads, width = queries.shape
    factor = width ** (-0.5)

    def one_block(block_number):
        offset = block_number * BLOCK
        query_block = lax.dynamic_slice_in_dim(queries, offset, BLOCK, 0)
        scores = masked_scores(query_block, key_rows, offset, length, starts, factor)
        peak = jnp.max(scores, axis=-1, keepdims=True)
        raised = jnp.exp(scores - peak)
        totals = jnp.sum(raised, axis=-1, keepdims=True)
        weights_low = (raised / totals).astype(jnp.bfloat16)
        blended = jnp.einsum(
            "hqk,khd->qhd", weights_low, value_rows, preferred_element_type=jnp.float32
        )
        return (
            blended.astype(jnp.bfloat16).reshape(BLOCK, heads * width),
            (peak + jnp.log(totals))[..., 0],
        )

    blended, log_sums = lax.map(one_block, jnp.arange(length // BLOCK, dtype=jnp.int32))
    return (blended.reshape(length, heads * width), log_sums)


def attend_back(queries, key_rows, value_rows, grad_mix, log_sums, starts):
    length, heads, width = queries.shape
    factor = width ** (-0.5)

    def one_block(carry, inputs_pair):
        key_grad, value_grad = carry
        block_number, block_sums = inputs_pair
        offset = block_number * BLOCK
        query_block = lax.dynamic_slice_in_dim(queries, offset, BLOCK, 0)
        grad_block = lax.dynamic_slice_in_dim(grad_mix, offset, BLOCK, 0)
        scores = masked_scores(query_block, key_rows, offset, length, starts, factor)
        weights = jnp.exp(scores - block_sums[:, :, None])
        dots = jnp.einsum(
            "qhd,khd->hqk", grad_block, value_rows, preferred_element_type=jnp.float32
        )
        inner = jnp.sum(weights * dots, axis=-1, keepdims=True)
        slopes = (weights * (dots - inner) * factor).astype(jnp.bfloat16)
        query_grad = jnp.einsum(
            "hqk,khd->qhd", slopes, key_rows, preferred_element_type=jnp.float32
        )
        key_grad = key_grad + jnp.einsum(
            "hqk,qhd->khd", slopes, query_block, preferred_element_type=jnp.float32
        )
        value_grad = value_grad + jnp.einsum(
            "hqk,qhd->khd",
            weights.astype(jnp.bfloat16),
            grad_block,
            preferred_element_type=jnp.float32,
        )
        return ((key_grad, value_grad), query_grad)

    initial = jnp.zeros(key_rows.shape, jnp.float32)
    numbers = jnp.arange(length // BLOCK, dtype=jnp.int32)
    (key_grad, value_grad), query_grad = lax.scan(
        one_block, (initial, initial), (numbers, log_sums)
    )
    return (query_grad.reshape(length, heads, width), key_grad, value_grad)


def fetch_frozen(first, second):
    return (
        lax.all_gather(first, "dp", axis=0, tiled=True),
        lax.all_gather(second, "dp", axis=1, tiled=True),
    )


def enter_rows(normed, reduced):
    return (
        lax.all_gather(normed, "tensor", axis=0, tiled=True),
        lax.all_gather(reduced, "tensor", axis=0, tiled=True),
    )


def leave_rows(partial_value, reduced):
    return (
        lax.psum_scatter(partial_value, "tensor", scatter_dimension=0, tiled=True),
        lax.psum_scatter(reduced, "tensor", scatter_dimension=0, tiled=True),
    )


def enter_grads(branch, reduced):
    return (
        lax.all_gather(branch, "tensor", axis=0, tiled=True),
        lax.all_gather(reduced, "tensor", axis=0, tiled=True),
    )


def leave_grads(partial_value, reduced):
    return (
        lax.psum_scatter(partial_value, "tensor", scatter_dimension=0, tiled=True),
        lax.psum_scatter(reduced, "tensor", scatter_dimension=0, tiled=True),
    )


def per_device(
    tokens,
    w_qkv,
    w_out,
    w_up,
    w_down,
    ln1_gain,
    ln1_bias,
    ln2_gain,
    ln2_bias,
    a_qkv,
    b_qkv,
    a_out,
    b_out,
    a_up,
    b_up,
    a_down,
    b_down,
    adapter_idx,
    pic_start,
    cotangent,
):
    selection = adapter_idx[0]
    starts = pic_start[0]

    def chosen(stacked, which_one):
        return lax.dynamic_index_in_dim(stacked, selection[which_one], 0, keepdims=False)

    low_qkv_in = chosen(a_qkv, 0)
    rank = low_qkv_in.shape[1]
    low_qkv_out = chosen(b_qkv, 0).reshape(rank, -1)
    low_out_in = chosen(a_out, 1)
    low_out_out = chosen(b_out, 1)
    low_up_in = chosen(a_up, 2)
    low_up_out = chosen(b_up, 2)
    low_down_in = chosen(a_down, 3)
    low_down_out = chosen(b_down, 3)
    heads_here = low_out_in.shape[0] // HD

    def run_forward(own_tokens, frozen):
        qkv_rows, out_rows, up_rows, down_rows = frozen
        qkv_full, out_full = fetch_frozen(qkv_rows, out_rows)
        qkv_flat = qkv_full.reshape(qkv_full.shape[0], -1)
        own_float = own_tokens.astype(jnp.float32)
        normed = layer_norm(own_float, ln1_gain, ln1_bias).astype(jnp.bfloat16)
        reduced = matmul(normed, low_qkv_in).astype(jnp.bfloat16)
        normed_all, reduced_all = enter_rows(normed, reduced)
        length = normed_all.shape[0]
        project = (matmul(normed_all, qkv_flat) + matmul(reduced_all, low_qkv_out)).astype(
            jnp.bfloat16
        )
        split = project.reshape(length, 3, heads_here, HD)
        blended, log_sums = attend(split[:, 0], split[:, 1], split[:, 2], starts)
        main_part, low_part = leave_rows(matmul(blended, out_full), matmul(blended, low_out_in))
        low_out_val = low_part.astype(jnp.bfloat16)
        residual = own_float + main_part + matmul(low_out_val, low_out_out)
        up_full, down_full = fetch_frozen(up_rows, down_rows)
        normed_two = layer_norm(residual, ln2_gain, ln2_bias).astype(jnp.bfloat16)
        reduced_two = matmul(normed_two, low_up_in).astype(jnp.bfloat16)
        normed_two_all, reduced_two_all = enter_rows(normed_two, reduced_two)
        pre_act = matmul(normed_two_all, up_full) + matmul(reduced_two_all, low_up_out)
        hidden = jax.nn.gelu(pre_act, approximate=True).astype(jnp.bfloat16)
        main_two, low_two = leave_rows(matmul(hidden, down_full), matmul(hidden, low_down_in))
        low_down_val = low_two.astype(jnp.bfloat16)
        output = residual + main_two + matmul(low_down_val, low_down_out)
        kept_state = (
            qkv_flat,
            out_full,
            up_full,
            down_full,
            normed,
            reduced_all,
            split,
            blended,
            log_sums,
            low_out_val,
            residual,
            normed_two,
            reduced_two_all,
            pre_act,
            hidden,
            low_down_val,
        )
        return (output, kept_state)

    frozen = (w_qkv, w_out, w_up, w_down)
    output, kept_state = run_forward(tokens, frozen)
    (
        qkv_flat,
        out_full,
        up_full,
        down_full,
        normed,
        reduced_all,
        split,
        blended,
        log_sums,
        low_out_val,
        residual,
        normed_two,
        reduced_two_all,
        pre_act,
        hidden,
        low_down_val,
    ) = kept_state
    cot_float = cotangent.astype(jnp.float32)
    grad_low_down = against(cotangent, low_down_out).astype(jnp.bfloat16)
    grad_b_down_here = contract_rows(low_down_val, cotangent)
    cot_all, grad_low_down_all = enter_grads(cotangent, grad_low_down)
    grad_hidden = against(cot_all, down_full) + against(grad_low_down_all, low_down_in)
    grad_a_down_here = contract_rows(hidden, grad_low_down_all)
    gelu_pull = jax.vjp(lambda inner_val: jax.nn.gelu(inner_val, approximate=True), pre_act)[1]
    grad_pre = gelu_pull(grad_hidden)[0].astype(jnp.bfloat16)
    grad_b_up_here = contract_rows(reduced_two_all, grad_pre)
    grad_normed_two, grad_reduced_two = leave_grads(
        against(grad_pre, up_full), against(grad_pre, low_up_out)
    )
    grad_low_up = grad_reduced_two.astype(jnp.bfloat16)
    grad_a_up_here = contract_rows(normed_two, grad_low_up)
    grad_normed_two = grad_normed_two + against(grad_low_up, low_up_in)
    norm_pull_two = jax.vjp(lambda inner_val: layer_norm(inner_val, ln2_gain, ln2_bias), residual)[
        1
    ]
    grad_resid = cot_float + norm_pull_two(grad_normed_two)[0]
    branch_low = grad_resid.astype(jnp.bfloat16)
    grad_low_out = against(branch_low, low_out_out).astype(jnp.bfloat16)
    grad_b_out_here = contract_rows(low_out_val, branch_low)
    branch_all, grad_low_out_all = enter_grads(branch_low, grad_low_out)
    grad_mix = (against(branch_all, out_full) + against(grad_low_out_all, low_out_in)).astype(
        jnp.bfloat16
    )
    grad_a_out_here = contract_rows(blended, grad_low_out_all)
    length = grad_mix.shape[0]
    query_grad, key_grad, value_grad = attend_back(
        split[:, 0],
        split[:, 1],
        split[:, 2],
        grad_mix.reshape(length, heads_here, HD),
        log_sums,
        starts,
    )
    grad_qkv = (
        jnp.stack([query_grad, key_grad, value_grad], axis=1)
        .reshape(length, -1)
        .astype(jnp.bfloat16)
    )
    grad_b_qkv_here = contract_rows(reduced_all, grad_qkv)
    grad_normed_one, grad_reduced_one = leave_grads(
        against(grad_qkv, qkv_flat), against(grad_qkv, low_qkv_out)
    )
    grad_low_qkv = grad_reduced_one.astype(jnp.bfloat16)
    grad_a_qkv_here = contract_rows(normed, grad_low_qkv)
    grad_normed_one = grad_normed_one + against(grad_low_qkv, low_qkv_in)
    norm_pull_one = jax.vjp(
        lambda inner_val: layer_norm(inner_val, ln1_gain, ln1_bias), tokens.astype(jnp.float32)
    )[1]
    grad_input = grad_resid + norm_pull_one(grad_normed_one)[0]
    slots = a_qkv.shape[0]

    def spread(gradient, which_one):
        onehot = (jnp.arange(slots, dtype=jnp.int32) == selection[which_one]).astype(jnp.float32)
        return onehot.reshape((slots,) + (1,) * gradient.ndim) * gradient[None]

    sharded = (
        lax.psum(spread(grad_b_qkv_here.reshape(rank, 3, -1), 0).astype(jnp.bfloat16), "dp").astype(
            jnp.float32
        ),
        lax.psum(spread(grad_a_out_here, 1).astype(jnp.bfloat16), "dp").astype(jnp.float32),
        lax.psum(spread(grad_b_up_here, 2).astype(jnp.bfloat16), "dp").astype(jnp.float32),
        lax.psum(spread(grad_a_down_here, 3).astype(jnp.bfloat16), "dp").astype(jnp.float32),
    )
    shared = lax.psum(
        (
            spread(grad_a_qkv_here, 0),
            spread(grad_b_out_here, 1),
            spread(grad_a_up_here, 2),
            spread(grad_b_down_here, 3),
        ),
        ("dp", "tensor"),
    )
    return (
        output.astype(jnp.bfloat16),
        grad_input,
        shared[0],
        sharded[0],
        sharded[1],
        shared[1],
        shared[2],
        sharded[2],
        sharded[3],
        shared[3],
    )


LOG2E = math.log2(math.e)
MASKED = -1e30
MIB = 1 << 20
BF = jnp.bfloat16
F32 = jnp.float32


def nt(a, b):
    return lax.dot_general(a, b, (((1,), (1,)), ((), ())), preferred_element_type=F32)


def nn(a, b):
    return lax.dot_general(a, b, (((1,), (0,)), ((), ())), preferred_element_type=F32)


def tn(a, b):
    return lax.dot_general(a, b, (((0,), (0,)), ((), ())), preferred_element_type=F32)


def last_key(starts_ref, pos):
    lim = pos
    for n in range(starts_ref.shape[0]):
        first = starts_ref[n]
        lim = jnp.where((pos >= first) & (pos < first + SPAN), first + SPAN - 1, lim)
    return lim


def head_parts(x):
    lane = lax.broadcasted_iota(jnp.int32, x.shape, 1)
    zero = jnp.zeros_like(x)
    return jnp.where(lane < HD, x, zero), jnp.where(lane >= HD, x, zero)


def attend_kernel(bq, starts_ref, q_ref, k_ref, v_ref, o_ref, lse_ref, vt_ref):
    qi = pl.program_id(1)
    bk = k_ref.shape[1]
    scale = LOG2E * HD ** -0.5

    @pl.when(qi == 0)
    def _():
        for n in range(k_ref.shape[0]):
            vt_ref[:, n * bk : (n + 1) * bk] = jnp.transpose(v_ref[n])

    qs = head_parts(q_ref[...])
    base = qi * bq
    lim = last_key(starts_ref, base + lax.broadcasted_iota(jnp.int32, (1, bq), 1))
    last = last_key(starts_ref, base + bq - 1)

    def step(masked, j, carry):
        off = pl.multiple_of(j * bk, bk)
        keys = k_ref[j]
        out = []
        for h in range(2):
            m, l, acc = carry[h]
            s = nt(keys, qs[h])
            if masked:
                kpos = off + lax.broadcasted_iota(jnp.int32, (bk, bq), 0)
                s = jnp.where(kpos <= lim, s, MASKED)
            mn = jnp.maximum(m, jnp.max(s, axis=0, keepdims=True))
            p = jnp.exp2((s - mn) * scale)
            al = jnp.exp2((m - mn) * scale)
            l = al * l + jnp.sum(p, axis=0, keepdims=True)
            acc = acc * al + nn(vt_ref[h * HD : (h + 1) * HD, pl.ds(off, bk)], p.astype(BF))
            out.append((mn, l, acc))
        return tuple(out)

    init = (jnp.full((1, bq), MASKED, F32), jnp.zeros((1, bq), F32), jnp.zeros((HD, bq), F32))
    carry = lax.fori_loop(0, base // bk, functools.partial(step, False), (init, init))
    carry = lax.fori_loop(base // bk, last // bk + 1, functools.partial(step, True), carry)
    mixed = jnp.concatenate([carry[h][2] / carry[h][1] for h in range(2)], axis=0)
    o_ref[...] = jnp.transpose(mixed).astype(BF)
    for h in range(2):
        lse_ref[0, h : h + 1, :] = carry[h][0] * scale + jnp.log2(carry[h][1])


def attend_rows(starts, qkv):
    parts, _, rows, width = qkv.shape
    pairs = width // (2 * HD)
    length = parts * rows
    bq = rows

    def all_parts(which):
        return pl.BlockSpec((parts, None, rows, 2 * HD), lambda p, i, s: (0, which, 0, p))

    return pl.pallas_call(
        functools.partial(attend_kernel, bq),
        out_shape=(
            jax.ShapeDtypeStruct((parts, rows, width), BF),
            jax.ShapeDtypeStruct((pairs, 2, length), F32),
        ),
        grid_spec=pltpu.PrefetchScalarGridSpec(
            num_scalar_prefetch=1,
            grid=(pairs, parts),
            in_specs=[
                pl.BlockSpec((None, None, rows, 2 * HD), lambda p, i, s: (i, 0, 0, p)),
                all_parts(1),
                all_parts(2),
            ],
            out_specs=[
                pl.BlockSpec((None, rows, 2 * HD), lambda p, i, s: (i, 0, p)),
                pl.BlockSpec((1, 2, rows), lambda p, i, s: (p, 0, i)),
            ],
            scratch_shapes=[pltpu.VMEM((2 * HD, length), BF)],
        ),
        compiler_params=pltpu.CompilerParams(
            dimension_semantics=("arbitrary", "arbitrary"), vmem_limit_bytes=48 * MIB
        ),
        name="attend",
    )(starts, qkv, qkv, qkv)


def attend_back_kernel(
    bq, bk, starts_ref, q_ref, k_ref, v_ref, o_ref, do_ref, lse_ref, g_ref,
    kt_ref, dqt_ref, delta_ref, qm_ref, dom_ref,
):
    parts, rows, _ = q_ref.shape
    length = parts * rows
    scale = LOG2E * HD ** -0.5
    nq = length // bq
    per = rows // bq
    dqt_ref[...] = jnp.zeros_like(dqt_ref)
    for i in range(nq):
        part, at = i // per, slice((i % per) * bq, (i % per + 1) * bq)
        flat = slice(i * bq, (i + 1) * bq)
        kt_ref[:, flat] = jnp.transpose(k_ref[part, at, :])
        do = do_ref[part, at, :]
        for h, (q_h, do_h) in enumerate(zip(head_parts(q_ref[part, at, :]), head_parts(do))):
            qm_ref[h, flat, :] = q_h
            dom_ref[h, flat, :] = do_h
        prod = jnp.transpose(do.astype(F32) * o_ref[part, at, :].astype(F32))
        for h in range(2):
            delta_ref[h : h + 1, flat] = jnp.sum(prod[h * HD : (h + 1) * HD], axis=0, keepdims=True)

    @pl.loop(0, length // bk)
    def _(j):
        koff = pl.multiple_of(j * bk, bk)
        part = j // (rows // bk)
        inside = pl.multiple_of((j % (rows // bk)) * bk, bk)
        keys = k_ref[part, pl.ds(inside, bk), :]
        vals = v_ref[part, pl.ds(inside, bk), :]

        def step(masked, i, carry):
            dk, dv = carry
            at = pl.ds(pl.multiple_of(i * bq, bq), bq)
            if masked:
                lim = last_key(starts_ref, i * bq + lax.broadcasted_iota(jnp.int32, (1, bq), 1))
                kpos = koff + lax.broadcasted_iota(jnp.int32, (bk, bq), 0)
                ok = kpos <= lim
            for h in range(2):
                q_h = qm_ref[h, at, :]
                do_h = dom_ref[h, at, :]
                p = jnp.exp2(nt(keys, q_h) * scale - lse_ref[0, h : h + 1, at])
                if masked:
                    p = jnp.where(ok, p, 0.0)
                dp = nt(vals, do_h)
                ds = (p * (dp - delta_ref[h : h + 1, at])).astype(BF)
                dv = dv + nn(p.astype(BF), do_h)
                dk = dk + nn(ds, q_h)
                dqt_ref[h * HD : (h + 1) * HD, at] += nn(
                    kt_ref[h * HD : (h + 1) * HD, pl.ds(koff, bk)], ds
                )
            return dk, dv

        first_q = koff
        for n in range(starts_ref.shape[0]):
            first = starts_ref[n]
            here = (koff >= first) & (koff < first + SPAN)
            first_q = jnp.where(here, jnp.minimum(first_q, first), first_q)
        full = (koff + bk + bq - 2) // bq
        zero = jnp.zeros((bk, 2 * HD), F32)
        carry = lax.fori_loop(first_q // bq, full, functools.partial(step, True), (zero, zero))
        dk, dv = lax.fori_loop(full, nq, functools.partial(step, False), carry)
        g_ref[part, 1, pl.ds(inside, bk), :] = (dk * HD ** -0.5).astype(BF)
        g_ref[part, 2, pl.ds(inside, bk), :] = dv.astype(BF)

    for i in range(nq):
        part, at = i // per, slice((i % per) * bq, (i % per + 1) * bq)
        dq = jnp.transpose(dqt_ref[:, i * bq : (i + 1) * bq])
        g_ref[part, 0, at, :] = (dq * HD ** -0.5).astype(BF)


def attend_rows_back(starts, qkv, mixed, grad_mix, lse):
    parts, _, rows, width = qkv.shape
    pairs = width // (2 * HD)
    length = parts * rows
    bq = bk = min(512, rows)

    def one(which):
        return pl.BlockSpec((parts, None, rows, 2 * HD), lambda p, s: (0, which, 0, p))

    flat = pl.BlockSpec((parts, rows, 2 * HD), lambda p, s: (0, 0, p))
    return pl.pallas_call(
        functools.partial(attend_back_kernel, bq, bk),
        out_shape=jax.ShapeDtypeStruct((parts, 3, rows, width), BF),
        grid_spec=pltpu.PrefetchScalarGridSpec(
            num_scalar_prefetch=1,
            grid=(pairs,),
            in_specs=[one(0), one(1), one(2), flat, flat,
                      pl.BlockSpec((1, 2, length), lambda p, s: (p, 0, 0))],
            out_specs=pl.BlockSpec((parts, 3, rows, 2 * HD), lambda p, s: (0, 0, 0, p)),
            scratch_shapes=[
                pltpu.VMEM((2 * HD, length), BF),
                pltpu.VMEM((2 * HD, length), F32),
                pltpu.VMEM((2, length), F32),
                pltpu.VMEM((2, length, 2 * HD), BF),
                pltpu.VMEM((2, length, 2 * HD), BF),
            ],
        ),
        compiler_params=pltpu.CompilerParams(
            dimension_semantics=("arbitrary",), vmem_limit_bytes=48 * MIB
        ),
        name="attend_back",
    )(starts, qkv, qkv, qkv, mixed, grad_mix, lse)


def stats(x):
    center = x - jnp.mean(x, axis=-1, keepdims=True)
    return center, lax.rsqrt(jnp.mean(center * center, axis=-1, keepdims=True) + 1e-05)


def norm_back(x, gain, grad):
    center, r = stats(x)
    n = center * r
    e = grad * gain
    return r * (e - jnp.mean(e, axis=-1, keepdims=True) - n * jnp.mean(e * n, axis=-1, keepdims=True))


def row_loop(rows, chunk, body):
    @pl.loop(0, rows // chunk)
    def _(i):
        body(pl.ds(pl.multiple_of(i * chunk, chunk), chunk))


def qkv_kernel(tok_ref, gain_ref, bias_ref, low_in_ref, w_ref, low_up_ref, out_ref, norm_ref, low_ref):
    rows = tok_ref.shape[0]
    first = (pl.program_id(0) == 0) & (pl.program_id(1) == 0)

    @pl.when(first)
    def _():
        def body(at):
            center, r = stats(tok_ref[at, :].astype(F32))
            normed = (center * r * gain_ref[...] + bias_ref[...]).astype(BF)
            norm_ref[at, :] = normed
            low_ref[at, :] = nt(normed, low_in_ref[...]).astype(BF)

        row_loop(rows, 256, body)

    w = w_ref[...].reshape(norm_ref.shape[1], -1)

    def body(at):
        y = nn(norm_ref[at, :], w) + nn(low_ref[at, :], low_up_ref[...])
        out_ref[at, :] = y.astype(BF)

    row_loop(rows, 512, body)


def whole(shape):
    return pl.BlockSpec(shape, lambda *_: (0,) * len(shape))


def project_qkv(tok, gain, bias, low_in, w, low_up):
    rows, features = tok.shape
    shards, groups, _, part, width = w.shape
    rank = low_in.shape[0]
    return pl.pallas_call(
        qkv_kernel,
        out_shape=(
            jax.ShapeDtypeStruct((groups, 3, rows, width), BF),
            jax.ShapeDtypeStruct((rows, features), BF),
            jax.ShapeDtypeStruct((rows, rank), BF),
        ),
        grid=(groups, 3),
        in_specs=[
            whole((rows, features)), whole((1, features)), whole((1, features)),
            whole((rank, features)),
            pl.BlockSpec((shards, None, None, part, width), lambda g, j: (0, g, j, 0, 0)),
            pl.BlockSpec((None, rank, width), lambda g, j: (g, 0, j)),
        ],
        out_specs=[
            pl.BlockSpec((None, None, rows, width), lambda g, j: (g, j, 0, 0)),
            whole((rows, features)),
            whole((rows, rank)),
        ],
        compiler_params=pltpu.CompilerParams(
            dimension_semantics=("arbitrary", "arbitrary"), vmem_limit_bytes=48 * MIB
        ),
        name="project_qkv",
    )(tok, gain, bias, low_in, w, low_up)


def qkv_back_kernel(
    g_ref, w_ref, low_up_ref, low_in_ref, norm_ref, low_ref, tok_ref, gain_ref, resid_ref,
    grad_ref, gb_ref, ga_ref, acc_ref, glow_ref,
):
    rows = tok_ref.shape[0]
    g, j = pl.program_id(0), pl.program_id(1)
    first = (g == 0) & (j == 0)
    final = (g == pl.num_programs(0) - 1) & (j == pl.num_programs(1) - 1)
    w = w_ref[...].reshape(tok_ref.shape[1], -1)

    @pl.when(first)
    def _():
        acc_ref[...] = jnp.zeros_like(acc_ref)
        glow_ref[...] = jnp.zeros_like(glow_ref)

    def body(at):
        part = g_ref[at, :]
        acc_ref[at, :] += nt(part, w)
        glow_ref[at, :] += nt(part, low_up_ref[...])

    row_loop(rows, 512, body)
    gb_ref[...] = tn(low_ref[...], g_ref[...]).astype(gb_ref.dtype)

    @pl.when(final)
    def _():
        def body(at):
            glow = glow_ref[at, :].astype(BF)
            total = acc_ref[at, :] + nn(glow, low_in_ref[...])
            grad_ref[at, :] = resid_ref[at, :] + norm_back(
                tok_ref[at, :].astype(F32), gain_ref[...], total
            )

        row_loop(rows, 256, body)
        ga_ref[...] = tn(glow_ref[...].astype(BF), norm_ref[...]).astype(ga_ref.dtype)


def project_qkv_back(grad, w, low_up, low_in, normed, low, tok, gain, resid):
    rows, features = tok.shape
    shards, groups, _, part, width = w.shape
    rank = low_in.shape[0]
    return pl.pallas_call(
        qkv_back_kernel,
        out_shape=(
            jax.ShapeDtypeStruct((rows, features), F32),
            jax.ShapeDtypeStruct((rank, groups * 3 * width), BF),
            jax.ShapeDtypeStruct((rank, features), BF),
        ),
        grid=(groups, 3),
        in_specs=[
            pl.BlockSpec((None, None, rows, width), lambda g, j: (g, j, 0, 0)),
            pl.BlockSpec((shards, None, None, part, width), lambda g, j: (0, g, j, 0, 0)),
            pl.BlockSpec((None, rank, width), lambda g, j: (g, 0, j)),
            whole((rank, features)), whole((rows, features)), whole((rows, rank)),
            whole((rows, features)), whole((1, features)), whole((rows, features)),
        ],
        out_specs=[
            whole((rows, features)),
            pl.BlockSpec((rank, width), lambda g, j: (0, g * 3 + j)),
            whole((rank, features)),
        ],
        scratch_shapes=[pltpu.VMEM((rows, features), F32), pltpu.VMEM((rows, rank), F32)],
        compiler_params=pltpu.CompilerParams(
            dimension_semantics=("arbitrary", "arbitrary"), vmem_limit_bytes=56 * MIB
        ),
        name="project_qkv_back",
    )(grad, w, low_up, low_in, normed, low, tok, gain, resid)


GELU = math.sqrt(2.0 / math.pi)


def gelu_and_slope(v):
    v2 = v * v
    t = jnp.tanh(GELU * v * (1.0 + 0.044715 * v2))
    half = 0.5 * (1.0 + t)
    return v * half, half + 0.5 * v * (1.0 - t * t) * (GELU * (1.0 + 3 * 0.044715 * v2))


def middle_kernel(
    nf, tt_ref, cc_ref, sc_ref, w_ref, sh_ref, tok_ref, mix_ref, cot_ref, gain_ref, bias_ref, rep_ref,
    out_ref, resid_ref, gmix_ref, gr_ref, lo_ref,
    acc_ref, norm_ref, hid_ref, slope_ref, lacc_ref, llow_ref,
):
    rows, features = tok_ref.shape
    s = pl.program_id(0)
    w = w_ref[...].reshape(features, -1)
    c = w.shape[1]
    sh = sh_ref[...]
    b_out, a_up, b_down = rep_ref[0], rep_ref[1], rep_ref[2]
    chunk = 512
    up0, down0, upb0, end0 = 2, 2 + nf, 2 + 2 * nf, 2 + 3 * nf

    @pl.when(s < up0)
    def _():
        def body(at):
            part = mix_ref[s, at, :]
            y = nt(part, w)
            low = nt(part, sh)

            @pl.when(s == 0)
            def _():
                resid_ref[at, :] = tok_ref[at, :].astype(F32) + y
                lacc_ref[at, :] = low

            @pl.when(s > 0)
            def _():
                resid_ref[at, :] += y
                lacc_ref[at, :] += low

        row_loop(rows, chunk, body)

    @pl.when(s == up0 - 1)
    def _():
        def body(at):
            low = lacc_ref[at, :].astype(BF)
            llow_ref[0, at, :] = low
            resid = resid_ref[at, :] + nn(low, b_out)
            resid_ref[at, :] = resid
            center, r = stats(resid)
            normed = (center * r * gain_ref[...] + bias_ref[...]).astype(BF)
            norm_ref[at, :] = normed
            llow_ref[1, at, :] = nt(normed, a_up).astype(BF)
            llow_ref[3, at, :] = nt(cot_ref[at, :], b_down).astype(BF)

        row_loop(rows, 256, body)

    @pl.when((s >= up0) & (s < down0))
    def _():
        f = s - up0

        def body(at):
            pre = nn(norm_ref[at, :], w) + nn(llow_ref[1, at, :], sh)
            hidden, slope = gelu_and_slope(pre)
            hid_ref[f, at, :] = hidden.astype(BF)
            slope_ref[f, at, :] = slope.astype(BF)

        row_loop(rows, 256, body)

    @pl.when((s >= down0) & (s < upb0))
    def _():
        f = s - down0

        def body(at):
            hidden = hid_ref[f, at, :]
            y = nt(hidden, w)
            low = nt(hidden, sh)

            @pl.when(f == 0)
            def _():
                acc_ref[at, :] = y
                lacc_ref[at, :] = low

            @pl.when(f > 0)
            def _():
                acc_ref[at, :] += y
                lacc_ref[at, :] += low

            g_hidden = nn(cot_ref[at, :], w) + nn(llow_ref[3, at, :], sh)
            slope_ref[f, at, :] = (g_hidden * slope_ref[f, at, :].astype(F32)).astype(BF)

        row_loop(rows, chunk, body)
        gr_ref[0:16, :] = tn(llow_ref[3], hid_ref[f]).astype(gr_ref.dtype)
        gr_ref[16:32, :] = tn(llow_ref[1], slope_ref[f]).astype(gr_ref.dtype)

    @pl.when(s == upb0 - 1)
    def _():
        def body(at):
            low = lacc_ref[at, :].astype(BF)
            llow_ref[2, at, :] = low
            out_ref[at, :] = (resid_ref[at, :] + acc_ref[at, :] + nn(low, b_down)).astype(BF)

        row_loop(rows, chunk, body)
        lo_ref[2] = tn(llow_ref[2], cot_ref[...]).astype(lo_ref.dtype)

    @pl.when((s >= upb0) & (s < end0))
    def _():
        f = s - upb0

        def body(at):
            part = slope_ref[f, at, :]
            y = nt(part, w)
            low = nt(part, sh)

            @pl.when(f == 0)
            def _():
                acc_ref[at, :] = y
                lacc_ref[at, :] = low

            @pl.when(f > 0)
            def _():
                acc_ref[at, :] += y
                lacc_ref[at, :] += low

        row_loop(rows, chunk, body)

    @pl.when(s == end0 - 1)
    def _():
        llow_ref[4] = lacc_ref[...].astype(BF)
        lo_ref[1] = tn(llow_ref[4], norm_ref[...]).astype(lo_ref.dtype)

        def body(at):
            total = acc_ref[at, :] + nn(llow_ref[4, at, :], a_up)
            g = cot_ref[at, :].astype(F32) + norm_back(resid_ref[at, :], gain_ref[...], total)
            resid_ref[at, :] = g
            branch = g.astype(BF)
            norm_ref[at, :] = branch
            llow_ref[5, at, :] = nt(branch, b_out).astype(BF)

        row_loop(rows, 256, body)
        lo_ref[0] = tn(llow_ref[0], norm_ref[...]).astype(lo_ref.dtype)

    @pl.when(s >= end0)
    def _():
        g = s - end0

        def body(at):
            y = nn(norm_ref[at, :], w) + nn(llow_ref[5, at, :], sh)
            gmix_ref[g, at, :] = y.astype(BF)

        row_loop(rows, chunk, body)
        gr_ref[0:16, :] = tn(llow_ref[5], mix_ref[g]).astype(gr_ref.dtype)


def middle(w, shared, tok, mix, cot, gain, bias, rep):
    rows, features = tok.shape
    shards, groups, part, total = w.shape
    rank = rep.shape[1]
    c = mix.shape[2]
    halves = (total // c - 1) // 2
    nf = groups * halves
    shift = (shared.shape[2] - total) // c
    blocks = [(f // halves, f % halves) for f in range(nf)]
    order = [(g, 0) for g in range(groups)]
    order += [(t, 1 + h) for t, h in blocks]
    order += [(t, 1 + halves + h) for t, h in blocks]
    order += [(t, 1 + h) for t, h in blocks]
    order += [(g, 0) for g in range(groups)]
    slot = [0] * (groups + nf) + list(range(nf)) + [nf - 1] * nf + [nf + g for g in range(groups)]
    tt = jnp.array([t for t, _ in order], jnp.int32)
    cc = jnp.array([x for _, x in order], jnp.int32)
    sc = jnp.array(slot, jnp.int32)
    once = pl.Buffered(1)

    def keep(shape):
        return pl.BlockSpec(shape, lambda s, *_: (0,) * len(shape), pipeline_mode=once)

    return pl.pallas_call(
        functools.partial(middle_kernel, nf),
        out_shape=(
            jax.ShapeDtypeStruct((rows, features), BF),
            jax.ShapeDtypeStruct((rows, features), F32),
            jax.ShapeDtypeStruct(mix.shape, BF),
            jax.ShapeDtypeStruct((nf + groups, 2 * rank, c), BF),
            jax.ShapeDtypeStruct((3, rank, features), BF),
        ),
        grid_spec=pltpu.PrefetchScalarGridSpec(
            num_scalar_prefetch=3,
            grid=(len(order),),
            in_specs=[
                pl.BlockSpec((shards, None, part, c), lambda s, tt, cc, sc: (0, tt[s], 0, cc[s])),
                pl.BlockSpec((None, rank, c), lambda s, tt, cc, sc: (tt[s], 0, cc[s] + shift)),
                keep((rows, features)), keep(mix.shape), keep((rows, features)),
                keep((1, features)), keep((1, features)), keep(rep.shape),
            ],
            out_specs=[
                keep((rows, features)), keep((rows, features)), keep(mix.shape),
                pl.BlockSpec((None, 2 * rank, c), lambda s, tt, cc, sc: (sc[s], 0, 0)),
                keep((3, rank, features)),
            ],
            scratch_shapes=[
                pltpu.VMEM((rows, features), F32),
                pltpu.VMEM((rows, features), BF),
                pltpu.VMEM((nf, rows, c), BF),
                pltpu.VMEM((nf, rows, c), BF),
                pltpu.VMEM((rows, rank), F32),
                pltpu.VMEM((6, rows, rank), BF),
            ],
        ),
        compiler_params=pltpu.CompilerParams(
            dimension_semantics=("arbitrary",), vmem_limit_bytes=60 * MIB
        ),
        name="middle",
    )(tt, cc, sc, w, shared, tok, mix, cot, gain, bias, rep)


def chip_device(
    tokens, w_qkv, w_out, w_up, w_down, ln1_gain, ln1_bias, ln2_gain, ln2_bias,
    a_qkv, b_qkv, a_out, b_out, a_up, b_up, a_down, b_down, adapter_idx, pic_start, cotangent,
):
    shards = lax.axis_size("dp")
    dp, t = lax.axis_index("dp"), lax.axis_index("tensor")
    b = dp % 2
    stays = b == t
    cores = [[2 * c, 2 * c + 1] for c in range(shards // 2)]
    sibling = [(i, i ^ 1) for i in range(shards)]
    swap = []
    for c in range(shards // 2):
        one, two = 2 * (2 * c + 1), 2 * (2 * c) + 1
        swap += [(one, two), (two, one)]

    def swapped(x):
        return lax.ppermute(x, ("dp", "tensor"), swap)

    def across(x):
        return lax.all_to_all(x, "dp", 0, 0, axis_index_groups=cores, tiled=True)

    rows, features = tokens.shape
    rank = a_qkv.shape[2]
    tok = jnp.where(stays, tokens, swapped(tokens))
    cot = jnp.where(stays, cotangent, swapped(cotangent))

    marks = jnp.concatenate([adapter_idx[0], pic_start[0]])
    other_marks = lax.ppermute(marks, "dp", sibling)
    mine = jnp.where(stays, marks, other_marks)
    theirs = jnp.where(stays, other_marks, marks)
    starts = mine[4:]

    def pick(stacked, which):
        return lax.dynamic_index_in_dim(stacked, which, 0, keepdims=False)

    def shared_pick(sel):
        return jnp.concatenate(
            [
                pick(b_qkv, sel[0]).reshape(rank, -1),
                pick(a_out, sel[1]).T,
                pick(b_up, sel[2]),
                pick(a_down, sel[3]).T,
            ],
            axis=1,
        )

    own_half = shared_pick(mine)
    far_half = lax.ppermute(shared_pick(theirs), "tensor", [(0, 1), (1, 0)])
    shared = jnp.stack([jnp.where(t == 0, own_half, far_half), jnp.where(t == 0, far_half, own_half)])
    a_qkv_low = pick(a_qkv, mine[0]).T
    rep = jnp.stack([pick(b_out, mine[1]), pick(a_up, mine[2]).T, pick(b_down, mine[3])])

    part = w_qkv.shape[0]
    qkv_shard = w_qkv.transpose(1, 0, 2)
    rest_shard = jnp.concatenate([w_out.T, w_up, w_down.T], axis=1)
    both = ("dp", "tensor")
    qkv_full = lax.all_gather(qkv_shard, both, axis=0)
    qkv_full = qkv_full.reshape(shards, 2, *qkv_shard.shape)
    rest_full = lax.all_gather(rest_shard, both, axis=0)
    rest_full = rest_full.reshape(shards, 2, *rest_shard.shape)
    all_marks = lax.all_gather(adapter_idx[0], "dp", axis=0)

    row = lambda v: v.reshape(1, -1)
    qkv, normed, low = project_qkv(tok, row(ln1_gain), row(ln1_bias), a_qkv_low, qkv_full, shared)
    qkv = across(qkv)
    mixed, lse = attend_rows(starts, qkv)
    mix = across(mixed)
    layer_out, g_resid, g_mix, g_blocks, g_rep = middle(
        rest_full, shared, tok, mix, cot, row(ln2_gain), row(ln2_bias), rep
    )
    g_qkv = across(attend_rows_back(starts, qkv, mixed, across(g_mix), lse))
    grad_tok, g_b_qkv, g_a_qkv = project_qkv_back(
        g_qkv, qkv_full, shared, a_qkv_low, normed, low, tok, row(ln1_gain), g_resid
    )

    out = jnp.where(stays, layer_out, swapped(layer_out))
    grad_input = jnp.where(stays, grad_tok, swapped(grad_tok.astype(BF)).astype(F32))

    slots = a_qkv.shape[0]
    width = w_qkv.shape[2]
    ffw = w_up.shape[1]
    nf = g_blocks.shape[0] - 2

    def total(mine_only, which):
        seqs = [2 * (d // 2) + u for d in range(shards) for u in range(2)]
        sel = all_marks[:, which][jnp.array(seqs)]
        onehot = (jnp.arange(slots, dtype=jnp.int32)[:, None] == sel[None, :]).astype(BF)
        return lax.dot_general(
            onehot, mine_only, (((1,), (0,)), ((), ())), preferred_element_type=F32
        )

    ff = g_blocks[:nf].reshape(nf, 2, rank, -1).transpose(1, 2, 0, 3)
    g_a_out = g_blocks[nf:, :rank].transpose(1, 0, 2)
    early_flat = jnp.concatenate(
        [ff.reshape(-1), g_a_out.reshape(-1), g_rep.reshape(-1)]
    ).reshape(-1, 1024)
    early_all = lax.all_gather(early_flat, both, axis=0).reshape(2 * shards, -1)
    sizes = [rank * 2 * ffw, rank * 2 * ffw, rank * 2 * width, rank * 3 * features]
    cuts = [0]
    for n in sizes:
        cuts.append(cuts[-1] + n)
    piece = [early_all[:, cuts[i] : cuts[i + 1]] for i in range(4)]

    def half(x, w):
        return lax.dynamic_index_in_dim(x.reshape(2 * shards, rank, 2, w), t, 2, keepdims=False)

    grad_a_down = total(half(piece[0], ffw), 3).transpose(0, 2, 1)
    grad_b_up = total(half(piece[1], ffw), 2)
    grad_a_out = total(half(piece[2], width), 1).transpose(0, 2, 1)
    rep_all = piece[3].reshape(2 * shards, 3, rank, features)
    grad_b_out = total(rep_all[:, 0], 1)
    grad_a_up = total(rep_all[:, 1], 2).transpose(0, 2, 1)
    grad_b_down = total(rep_all[:, 2], 3)

    late = jnp.concatenate([g_b_qkv, g_a_qkv], axis=1)
    late_all = lax.all_gather(late, both, axis=0)
    n = g_b_qkv.shape[1]
    grad_b_qkv = total(
        lax.dynamic_index_in_dim(
            late_all[:, :, :n].reshape(2 * shards, rank, 2, n // 2), t, 2, keepdims=False
        ),
        0,
    ).reshape(slots, rank, 3, width)
    grad_a_qkv = total(late_all[:, :, n:], 0).transpose(0, 2, 1)
    return (
        out, grad_input, grad_a_qkv, grad_b_qkv, grad_a_out, grad_b_out,
        grad_a_up, grad_b_up, grad_a_down, grad_b_down,
    )


def solution(mesh):
    placed = (
        P(("dp", "tensor"), None),
        P("dp", None, "tensor"),
        P("tensor", "dp"),
        P("dp", "tensor"),
        P("tensor", "dp"),
        P(),
        P(),
        P(),
        P(),
        P(),
        P(None, None, None, "tensor"),
        P(None, "tensor", None),
        P(),
        P(),
        P(None, None, "tensor"),
        P(None, "tensor", None),
        P(),
        P("dp", None),
        P("dp", None),
        P(("dp", "tensor"), None),
    )
    paired = mesh.shape["tensor"] == 2 and mesh.shape["dp"] % 2 == 0
    return jax.shard_map(
        chip_device if paired else per_device,
        mesh=mesh,
        in_specs=placed,
        out_specs=(
            P(("dp", "tensor"), None),
            P(("dp", "tensor"), None),
            P(),
            P(None, None, None, "tensor"),
            P(None, "tensor", None),
            P(),
            P(),
            P(None, None, "tensor"),
            P(None, "tensor", None),
            P(),
        ),
        check_vma=False,
    )
```

```python
import functools
import math

import jax
import jax.numpy as jnp
from jax import lax
from jax.experimental import pallas as pl
from jax.experimental.pallas import tpu as pltpu
from jax.sharding import PartitionSpec as P

HD = 64
SPAN = 256
BLOCK = 512


def matmul(left, right):
    return jnp.dot(left, right, preferred_element_type=jnp.float32)


def contract_rows(left, right):
    return lax.dot_general(
        left, right, (((0,), (0,)), ((), ())), preferred_element_type=jnp.float32
    )


def against(left, right):
    return lax.dot_general(
        left, right, (((1,), (1,)), ((), ())), preferred_element_type=jnp.float32
    )


def layer_norm(values, multiplier, addend):
    center = values - jnp.mean(values, axis=-1, keepdims=True)
    spread = jnp.mean(center * center, axis=-1, keepdims=True)
    return center * lax.rsqrt(spread + 1e-05) * multiplier + addend


def span_labels(positions, starts):
    inside = (positions[:, None] >= starts[None, :]) & (positions[:, None] < starts[None, :] + SPAN)
    labels = jnp.arange(1, starts.shape[0] + 1, dtype=jnp.int32)
    return jnp.sum(jnp.where(inside, labels[None, :], 0), axis=1)


def allowed_mask(offset, row_count, length, starts):
    row_pos = offset + jnp.arange(row_count, dtype=jnp.int32)
    col_pos = jnp.arange(length, dtype=jnp.int32)
    row_span = span_labels(row_pos, starts)
    col_span = span_labels(col_pos, starts)
    causal = col_pos[None, :] <= row_pos[:, None]
    joined = (row_span[:, None] == col_span[None, :]) & (row_span[:, None] > 0)
    return causal | joined


def masked_scores(query_block, key_rows, offset, length, starts, factor):
    scores = (
        jnp.einsum("qhd,khd->hqk", query_block, key_rows, preferred_element_type=jnp.float32)
        * factor
    )
    allowed = allowed_mask(offset, BLOCK, length, starts)
    return jnp.where(allowed[None], scores, -1000000000.0)


def attend(queries, key_rows, value_rows, starts):
    length, heads, width = queries.shape
    factor = width ** (-0.5)

    def one_block(block_number):
        offset = block_number * BLOCK
        query_block = lax.dynamic_slice_in_dim(queries, offset, BLOCK, 0)
        scores = masked_scores(query_block, key_rows, offset, length, starts, factor)
        peak = jnp.max(scores, axis=-1, keepdims=True)
        raised = jnp.exp(scores - peak)
        totals = jnp.sum(raised, axis=-1, keepdims=True)
        weights_low = (raised / totals).astype(jnp.bfloat16)
        blended = jnp.einsum(
            "hqk,khd->qhd", weights_low, value_rows, preferred_element_type=jnp.float32
        )
        return (
            blended.astype(jnp.bfloat16).reshape(BLOCK, heads * width),
            (peak + jnp.log(totals))[..., 0],
        )

    blended, log_sums = lax.map(one_block, jnp.arange(length // BLOCK, dtype=jnp.int32))
    return (blended.reshape(length, heads * width), log_sums)


def attend_back(queries, key_rows, value_rows, grad_mix, log_sums, starts):
    length, heads, width = queries.shape
    factor = width ** (-0.5)

    def one_block(carry, inputs_pair):
        key_grad, value_grad = carry
        block_number, block_sums = inputs_pair
        offset = block_number * BLOCK
        query_block = lax.dynamic_slice_in_dim(queries, offset, BLOCK, 0)
        grad_block = lax.dynamic_slice_in_dim(grad_mix, offset, BLOCK, 0)
        scores = masked_scores(query_block, key_rows, offset, length, starts, factor)
        weights = jnp.exp(scores - block_sums[:, :, None])
        dots = jnp.einsum(
            "qhd,khd->hqk", grad_block, value_rows, preferred_element_type=jnp.float32
        )
        inner = jnp.sum(weights * dots, axis=-1, keepdims=True)
        slopes = (weights * (dots - inner) * factor).astype(jnp.bfloat16)
        query_grad = jnp.einsum(
            "hqk,khd->qhd", slopes, key_rows, preferred_element_type=jnp.float32
        )
        key_grad = key_grad + jnp.einsum(
            "hqk,qhd->khd", slopes, query_block, preferred_element_type=jnp.float32
        )
        value_grad = value_grad + jnp.einsum(
            "hqk,qhd->khd",
            weights.astype(jnp.bfloat16),
            grad_block,
            preferred_element_type=jnp.float32,
        )
        return ((key_grad, value_grad), query_grad)

    initial = jnp.zeros(key_rows.shape, jnp.float32)
    numbers = jnp.arange(length // BLOCK, dtype=jnp.int32)
    (key_grad, value_grad), query_grad = lax.scan(
        one_block, (initial, initial), (numbers, log_sums)
    )
    return (query_grad.reshape(length, heads, width), key_grad, value_grad)


def fetch_frozen(first, second):
    return (
        lax.all_gather(first, "dp", axis=0, tiled=True),
        lax.all_gather(second, "dp", axis=1, tiled=True),
    )


def enter_rows(normed, reduced):
    return (
        lax.all_gather(normed, "tensor", axis=0, tiled=True),
        lax.all_gather(reduced, "tensor", axis=0, tiled=True),
    )


def leave_rows(partial_value, reduced):
    return (
        lax.psum_scatter(partial_value, "tensor", scatter_dimension=0, tiled=True),
        lax.psum_scatter(reduced, "tensor", scatter_dimension=0, tiled=True),
    )


def enter_grads(branch, reduced):
    return (
        lax.all_gather(branch, "tensor", axis=0, tiled=True),
        lax.all_gather(reduced, "tensor", axis=0, tiled=True),
    )


def leave_grads(partial_value, reduced):
    return (
        lax.psum_scatter(partial_value, "tensor", scatter_dimension=0, tiled=True),
        lax.psum_scatter(reduced, "tensor", scatter_dimension=0, tiled=True),
    )


def per_device(
    tokens,
    w_qkv,
    w_out,
    w_up,
    w_down,
    ln1_gain,
    ln1_bias,
    ln2_gain,
    ln2_bias,
    a_qkv,
    b_qkv,
    a_out,
    b_out,
    a_up,
    b_up,
    a_down,
    b_down,
    adapter_idx,
    pic_start,
    cotangent,
):
    selection = adapter_idx[0]
    starts = pic_start[0]

    def chosen(stacked, which_one):
        return lax.dynamic_index_in_dim(stacked, selection[which_one], 0, keepdims=False)

    low_qkv_in = chosen(a_qkv, 0)
    rank = low_qkv_in.shape[1]
    low_qkv_out = chosen(b_qkv, 0).reshape(rank, -1)
    low_out_in = chosen(a_out, 1)
    low_out_out = chosen(b_out, 1)
    low_up_in = chosen(a_up, 2)
    low_up_out = chosen(b_up, 2)
    low_down_in = chosen(a_down, 3)
    low_down_out = chosen(b_down, 3)
    heads_here = low_out_in.shape[0] // HD

    def run_forward(own_tokens, frozen):
        qkv_rows, out_rows, up_rows, down_rows = frozen
        qkv_full, out_full = fetch_frozen(qkv_rows, out_rows)
        qkv_flat = qkv_full.reshape(qkv_full.shape[0], -1)
        own_float = own_tokens.astype(jnp.float32)
        normed = layer_norm(own_float, ln1_gain, ln1_bias).astype(jnp.bfloat16)
        reduced = matmul(normed, low_qkv_in).astype(jnp.bfloat16)
        normed_all, reduced_all = enter_rows(normed, reduced)
        length = normed_all.shape[0]
        project = (matmul(normed_all, qkv_flat) + matmul(reduced_all, low_qkv_out)).astype(
            jnp.bfloat16
        )
        split = project.reshape(length, 3, heads_here, HD)
        blended, log_sums = attend(split[:, 0], split[:, 1], split[:, 2], starts)
        main_part, low_part = leave_rows(matmul(blended, out_full), matmul(blended, low_out_in))
        low_out_val = low_part.astype(jnp.bfloat16)
        residual = own_float + main_part + matmul(low_out_val, low_out_out)
        up_full, down_full = fetch_frozen(up_rows, down_rows)
        normed_two = layer_norm(residual, ln2_gain, ln2_bias).astype(jnp.bfloat16)
        reduced_two = matmul(normed_two, low_up_in).astype(jnp.bfloat16)
        normed_two_all, reduced_two_all = enter_rows(normed_two, reduced_two)
        pre_act = matmul(normed_two_all, up_full) + matmul(reduced_two_all, low_up_out)
        hidden = jax.nn.gelu(pre_act, approximate=True).astype(jnp.bfloat16)
        main_two, low_two = leave_rows(matmul(hidden, down_full), matmul(hidden, low_down_in))
        low_down_val = low_two.astype(jnp.bfloat16)
        output = residual + main_two + matmul(low_down_val, low_down_out)
        kept_state = (
            qkv_flat,
            out_full,
            up_full,
            down_full,
            normed,
            reduced_all,
            split,
            blended,
            log_sums,
            low_out_val,
            residual,
            normed_two,
            reduced_two_all,
            pre_act,
            hidden,
            low_down_val,
        )
        return (output, kept_state)

    frozen = (w_qkv, w_out, w_up, w_down)
    output, kept_state = run_forward(tokens, frozen)
    (
        qkv_flat,
        out_full,
        up_full,
        down_full,
        normed,
        reduced_all,
        split,
        blended,
        log_sums,
        low_out_val,
        residual,
        normed_two,
        reduced_two_all,
        pre_act,
        hidden,
        low_down_val,
    ) = kept_state
    cot_float = cotangent.astype(jnp.float32)
    grad_low_down = against(cotangent, low_down_out).astype(jnp.bfloat16)
    grad_b_down_here = contract_rows(low_down_val, cotangent)
    cot_all, grad_low_down_all = enter_grads(cotangent, grad_low_down)
    grad_hidden = against(cot_all, down_full) + against(grad_low_down_all, low_down_in)
    grad_a_down_here = contract_rows(hidden, grad_low_down_all)
    gelu_pull = jax.vjp(lambda inner_val: jax.nn.gelu(inner_val, approximate=True), pre_act)[1]
    grad_pre = gelu_pull(grad_hidden)[0].astype(jnp.bfloat16)
    grad_b_up_here = contract_rows(reduced_two_all, grad_pre)
    grad_normed_two, grad_reduced_two = leave_grads(
        against(grad_pre, up_full), against(grad_pre, low_up_out)
    )
    grad_low_up = grad_reduced_two.astype(jnp.bfloat16)
    grad_a_up_here = contract_rows(normed_two, grad_low_up)
    grad_normed_two = grad_normed_two + against(grad_low_up, low_up_in)
    norm_pull_two = jax.vjp(lambda inner_val: layer_norm(inner_val, ln2_gain, ln2_bias), residual)[
        1
    ]
    grad_resid = cot_float + norm_pull_two(grad_normed_two)[0]
    branch_low = grad_resid.astype(jnp.bfloat16)
    grad_low_out = against(branch_low, low_out_out).astype(jnp.bfloat16)
    grad_b_out_here = contract_rows(low_out_val, branch_low)
    branch_all, grad_low_out_all = enter_grads(branch_low, grad_low_out)
    grad_mix = (against(branch_all, out_full) + against(grad_low_out_all, low_out_in)).astype(
        jnp.bfloat16
    )
    grad_a_out_here = contract_rows(blended, grad_low_out_all)
    length = grad_mix.shape[0]
    query_grad, key_grad, value_grad = attend_back(
        split[:, 0],
        split[:, 1],
        split[:, 2],
        grad_mix.reshape(length, heads_here, HD),
        log_sums,
        starts,
    )
    grad_qkv = (
        jnp.stack([query_grad, key_grad, value_grad], axis=1)
        .reshape(length, -1)
        .astype(jnp.bfloat16)
    )
    grad_b_qkv_here = contract_rows(reduced_all, grad_qkv)
    grad_normed_one, grad_reduced_one = leave_grads(
        against(grad_qkv, qkv_flat), against(grad_qkv, low_qkv_out)
    )
    grad_low_qkv = grad_reduced_one.astype(jnp.bfloat16)
    grad_a_qkv_here = contract_rows(normed, grad_low_qkv)
    grad_normed_one = grad_normed_one + against(grad_low_qkv, low_qkv_in)
    norm_pull_one = jax.vjp(
        lambda inner_val: layer_norm(inner_val, ln1_gain, ln1_bias), tokens.astype(jnp.float32)
    )[1]
    grad_input = grad_resid + norm_pull_one(grad_normed_one)[0]
    slots = a_qkv.shape[0]

    def spread(gradient, which_one):
        onehot = (jnp.arange(slots, dtype=jnp.int32) == selection[which_one]).astype(jnp.float32)
        return onehot.reshape((slots,) + (1,) * gradient.ndim) * gradient[None]

    sharded = (
        lax.psum(spread(grad_b_qkv_here.reshape(rank, 3, -1), 0).astype(jnp.bfloat16), "dp").astype(
            jnp.float32
        ),
        lax.psum(spread(grad_a_out_here, 1).astype(jnp.bfloat16), "dp").astype(jnp.float32),
        lax.psum(spread(grad_b_up_here, 2).astype(jnp.bfloat16), "dp").astype(jnp.float32),
        lax.psum(spread(grad_a_down_here, 3).astype(jnp.bfloat16), "dp").astype(jnp.float32),
    )
    shared = lax.psum(
        (
            spread(grad_a_qkv_here, 0),
            spread(grad_b_out_here, 1),
            spread(grad_a_up_here, 2),
            spread(grad_b_down_here, 3),
        ),
        ("dp", "tensor"),
    )
    return (
        output.astype(jnp.bfloat16),
        grad_input,
        shared[0],
        sharded[0],
        sharded[1],
        shared[1],
        shared[2],
        sharded[2],
        sharded[3],
        shared[3],
    )


LOG2E = math.log2(math.e)
MASKED = -1e30
MIB = 1 << 20
BF = jnp.bfloat16
F32 = jnp.float32


def nt(a, b):
    return lax.dot_general(a, b, (((1,), (1,)), ((), ())), preferred_element_type=F32)


def nn(a, b):
    return lax.dot_general(a, b, (((1,), (0,)), ((), ())), preferred_element_type=F32)


def tn(a, b):
    return lax.dot_general(a, b, (((0,), (0,)), ((), ())), preferred_element_type=F32)


def last_key(starts_ref, pos):
    lim = pos
    for n in range(starts_ref.shape[0]):
        first = starts_ref[n]
        lim = jnp.where((pos >= first) & (pos < first + SPAN), first + SPAN - 1, lim)
    return lim


def head_parts(x):
    lane = lax.broadcasted_iota(jnp.int32, x.shape, 1)
    zero = jnp.zeros_like(x)
    return jnp.where(lane < HD, x, zero), jnp.where(lane >= HD, x, zero)


def cost(flops, moved):
    return pl.CostEstimate(flops=int(flops), bytes_accessed=int(moved), transcendentals=0)


def attend_kernel(bq, starts_ref, q_ref, k_ref, v_ref, o_ref, lse_ref, vt_ref):
    qi = pl.program_id(1)
    bk = k_ref.shape[1]
    scale = LOG2E * HD ** -0.5

    @pl.when(qi == 0)
    def _():
        for n in range(k_ref.shape[0]):
            vt_ref[:, n * bk : (n + 1) * bk] = jnp.transpose(v_ref[n])

    qs = head_parts(q_ref[...])
    base = qi * bq
    lim = last_key(starts_ref, base + lax.broadcasted_iota(jnp.int32, (1, bq), 1))
    last = last_key(starts_ref, base + bq - 1)

    def step(masked, j, carry):
        off = pl.multiple_of(j * bk, bk)
        keys = k_ref[j]
        out = []
        for h in range(2):
            m, l, acc = carry[h]
            s = nt(keys, qs[h])
            if masked:
                kpos = off + lax.broadcasted_iota(jnp.int32, (bk, bq), 0)
                s = jnp.where(kpos <= lim, s, MASKED)
            mn = jnp.maximum(m, jnp.max(s, axis=0, keepdims=True))
            p = jnp.exp2((s - mn) * scale)
            al = jnp.exp2((m - mn) * scale)
            l = al * l + jnp.sum(p, axis=0, keepdims=True)
            acc = acc * al + nn(vt_ref[h * HD : (h + 1) * HD, pl.ds(off, bk)], p.astype(BF))
            out.append((mn, l, acc))
        return tuple(out)

    init = (jnp.full((1, bq), MASKED, F32), jnp.zeros((1, bq), F32), jnp.zeros((HD, bq), F32))
    carry = lax.fori_loop(0, base // bk, functools.partial(step, False), (init, init))
    carry = lax.fori_loop(base // bk, last // bk + 1, functools.partial(step, True), carry)
    mixed = jnp.concatenate([carry[h][2] / carry[h][1] for h in range(2)], axis=0)
    o_ref[...] = jnp.transpose(mixed).astype(BF)
    for h in range(2):
        lse_ref[0, h : h + 1, :] = carry[h][0] * scale + jnp.log2(carry[h][1])


def attend_rows(starts, qkv):
    parts, _, rows, width = qkv.shape
    pairs = width // (2 * HD)
    length = parts * rows
    bq = rows

    def all_parts(which):
        return pl.BlockSpec((parts, None, rows, 2 * HD), lambda p, i, s: (0, which, 0, p))

    return pl.pallas_call(
        functools.partial(attend_kernel, bq),
        out_shape=(
            jax.ShapeDtypeStruct((parts, rows, width), BF),
            jax.ShapeDtypeStruct((pairs, 2, length), F32),
        ),
        grid_spec=pltpu.PrefetchScalarGridSpec(
            num_scalar_prefetch=1,
            grid=(pairs, parts),
            in_specs=[
                pl.BlockSpec((None, None, rows, 2 * HD), lambda p, i, s: (i, 0, 0, p)),
                all_parts(1),
                all_parts(2),
            ],
            out_specs=[
                pl.BlockSpec((None, rows, 2 * HD), lambda p, i, s: (i, 0, p)),
                pl.BlockSpec((1, 2, rows), lambda p, i, s: (p, 0, i)),
            ],
            scratch_shapes=[pltpu.VMEM((2 * HD, length), BF)],
        ),
        compiler_params=pltpu.CompilerParams(
            dimension_semantics=("arbitrary", "arbitrary"), vmem_limit_bytes=48 * MIB
        ),
        cost_estimate=cost(24 * length * length * width, 16 * length * width),
        name="attend",
    )(starts, qkv, qkv, qkv)


def attend_back_kernel(
    bq, bk, starts_ref, q_ref, k_ref, v_ref, o_ref, do_ref, lse_ref, g_ref,
    kt_ref, dqt_ref, delta_ref, qm_ref, dom_ref,
):
    parts, rows, _ = q_ref.shape
    length = parts * rows
    scale = LOG2E * HD ** -0.5
    nq = length // bq
    per = rows // bq
    dqt_ref[...] = jnp.zeros_like(dqt_ref)
    for i in range(nq):
        part, at = i // per, slice((i % per) * bq, (i % per + 1) * bq)
        flat = slice(i * bq, (i + 1) * bq)
        kt_ref[:, flat] = jnp.transpose(k_ref[part, at, :])
        do = do_ref[part, at, :]
        for h, (q_h, do_h) in enumerate(zip(head_parts(q_ref[part, at, :]), head_parts(do))):
            qm_ref[h, flat, :] = q_h
            dom_ref[h, flat, :] = do_h
        prod = jnp.transpose(do.astype(F32) * o_ref[part, at, :].astype(F32))
        for h in range(2):
            delta_ref[h : h + 1, flat] = jnp.sum(prod[h * HD : (h + 1) * HD], axis=0, keepdims=True)

    @pl.loop(0, length // bk)
    def _(j):
        koff = pl.multiple_of(j * bk, bk)
        part = j // (rows // bk)
        inside = pl.multiple_of((j % (rows // bk)) * bk, bk)
        keys = k_ref[part, pl.ds(inside, bk), :]
        vals = v_ref[part, pl.ds(inside, bk), :]

        def step(masked, i, carry):
            dk, dv = carry
            at = pl.ds(pl.multiple_of(i * bq, bq), bq)
            if masked:
                lim = last_key(starts_ref, i * bq + lax.broadcasted_iota(jnp.int32, (1, bq), 1))
                kpos = koff + lax.broadcasted_iota(jnp.int32, (bk, bq), 0)
                ok = kpos <= lim
            for h in range(2):
                q_h = qm_ref[h, at, :]
                do_h = dom_ref[h, at, :]
                p = jnp.exp2(nt(keys, q_h) * scale - lse_ref[0, h : h + 1, at])
                if masked:
                    p = jnp.where(ok, p, 0.0)
                dp = nt(vals, do_h)
                ds = (p * (dp - delta_ref[h : h + 1, at])).astype(BF)
                dv = dv + nn(p.astype(BF), do_h)
                dk = dk + nn(ds, q_h)
                dqt_ref[h * HD : (h + 1) * HD, at] += nn(
                    kt_ref[h * HD : (h + 1) * HD, pl.ds(koff, bk)], ds
                )
            return dk, dv

        first_q = koff
        for n in range(starts_ref.shape[0]):
            first = starts_ref[n]
            here = (koff >= first) & (koff < first + SPAN)
            first_q = jnp.where(here, jnp.minimum(first_q, first), first_q)
        full = (koff + bk + bq - 2) // bq
        zero = jnp.zeros((bk, 2 * HD), F32)
        carry = lax.fori_loop(first_q // bq, full, functools.partial(step, True), (zero, zero))
        dk, dv = lax.fori_loop(full, nq, functools.partial(step, False), carry)
        g_ref[part, 1, pl.ds(inside, bk), :] = (dk * HD ** -0.5).astype(BF)
        g_ref[part, 2, pl.ds(inside, bk), :] = dv.astype(BF)

    for i in range(nq):
        part, at = i // per, slice((i % per) * bq, (i % per + 1) * bq)
        dq = jnp.transpose(dqt_ref[:, i * bq : (i + 1) * bq])
        g_ref[part, 0, at, :] = (dq * HD ** -0.5).astype(BF)


def attend_rows_back(starts, qkv, mixed, grad_mix, lse):
    parts, _, rows, width = qkv.shape
    pairs = width // (2 * HD)
    length = parts * rows
    bq = bk = min(512, rows)

    def one(which):
        return pl.BlockSpec((parts, None, rows, 2 * HD), lambda p, s: (0, which, 0, p))

    flat = pl.BlockSpec((parts, rows, 2 * HD), lambda p, s: (0, 0, p))
    return pl.pallas_call(
        functools.partial(attend_back_kernel, bq, bk),
        out_shape=jax.ShapeDtypeStruct((parts, 3, rows, width), BF),
        grid_spec=pltpu.PrefetchScalarGridSpec(
            num_scalar_prefetch=1,
            grid=(pairs,),
            in_specs=[one(0), one(1), one(2), flat, flat,
                      pl.BlockSpec((1, 2, length), lambda p, s: (p, 0, 0))],
            out_specs=pl.BlockSpec((parts, 3, rows, 2 * HD), lambda p, s: (0, 0, 0, p)),
            scratch_shapes=[
                pltpu.VMEM((2 * HD, length), BF),
                pltpu.VMEM((2 * HD, length), F32),
                pltpu.VMEM((2, length), F32),
                pltpu.VMEM((2, length, 2 * HD), BF),
                pltpu.VMEM((2, length, 2 * HD), BF),
            ],
        ),
        compiler_params=pltpu.CompilerParams(
            dimension_semantics=("arbitrary",), vmem_limit_bytes=48 * MIB
        ),
        cost_estimate=cost(40 * length * length * width, 24 * length * width),
        name="attend_back",
    )(starts, qkv, qkv, qkv, mixed, grad_mix, lse)


def stats(x):
    center = x - jnp.mean(x, axis=-1, keepdims=True)
    return center, lax.rsqrt(jnp.mean(center * center, axis=-1, keepdims=True) + 1e-05)


def norm_back(x, gain, grad):
    center, r = stats(x)
    n = center * r
    e = grad * gain
    return r * (e - jnp.mean(e, axis=-1, keepdims=True) - n * jnp.mean(e * n, axis=-1, keepdims=True))


def row_loop(rows, chunk, body):
    if chunk == rows:
        body(slice(None))
        return

    @pl.loop(0, rows // chunk)
    def _(i):
        body(pl.ds(pl.multiple_of(i * chunk, chunk), chunk))


def qkv_kernel(tok_ref, gain_ref, bias_ref, low_in_ref, w_ref, low_up_ref, out_ref, norm_ref, low_ref):
    rows = tok_ref.shape[0]
    first = (pl.program_id(0) == 0) & (pl.program_id(1) == 0)

    @pl.when(first)
    def _():
        def body(at):
            center, r = stats(tok_ref[at, :].astype(F32))
            normed = (center * r * gain_ref[...] + bias_ref[...]).astype(BF)
            norm_ref[at, :] = normed
            low_ref[at, :] = nt(normed, low_in_ref[...]).astype(BF)

        row_loop(rows, 256, body)

    w = w_ref[...].reshape(norm_ref.shape[1], -1)

    def body(at):
        y = nn(norm_ref[at, :], w) + nn(low_ref[at, :], low_up_ref[...])
        out_ref[at, :] = y.astype(BF)

    row_loop(rows, rows, body)


def whole(shape):
    return pl.BlockSpec(shape, lambda *_: (0,) * len(shape))


def project_qkv(tok, gain, bias, low_in, w, low_up):
    rows, features = tok.shape
    shards, groups, _, part, width = w.shape
    rank = low_in.shape[0]
    return pl.pallas_call(
        qkv_kernel,
        out_shape=(
            jax.ShapeDtypeStruct((groups, 3, rows, width), BF),
            jax.ShapeDtypeStruct((rows, features), BF),
            jax.ShapeDtypeStruct((rows, rank), BF),
        ),
        grid=(groups, 3),
        in_specs=[
            whole((rows, features)), whole((1, features)), whole((1, features)),
            whole((rank, features)),
            pl.BlockSpec((shards, None, None, part, width), lambda g, j: (0, g, j, 0, 0)),
            pl.BlockSpec((None, rank, width), lambda g, j: (g, 0, j)),
        ],
        out_specs=[
            pl.BlockSpec((None, None, rows, width), lambda g, j: (g, j, 0, 0)),
            whole((rows, features)),
            whole((rows, rank)),
        ],
        compiler_params=pltpu.CompilerParams(
            dimension_semantics=("arbitrary", "arbitrary"), vmem_limit_bytes=48 * MIB
        ),
        cost_estimate=cost(4 * rows * features * groups * 3 * width, 4 * rows * groups * 3 * width),
        name="project_qkv",
    )(tok, gain, bias, low_in, w, low_up)


def qkv_back_kernel(
    g_ref, w_ref, low_up_ref, low_in_ref, norm_ref, low_ref, tok_ref, gain_ref, resid_ref, tag_ref,
    grad_ref, send_ref, gr_ref, acc_ref, glow_ref,
):
    rows = tok_ref.shape[0]
    g, j = pl.program_id(0), pl.program_id(1)
    first = (g == 0) & (j == 0)
    final = (g == pl.num_programs(0) - 1) & (j == pl.num_programs(1) - 1)
    g_steps = gr_ref.shape[0] - 1 - tok_ref.shape[1] // g_ref.shape[1]
    w = w_ref[...].reshape(tok_ref.shape[1], -1)

    @pl.when(first)
    def _():
        acc_ref[...] = jnp.zeros_like(acc_ref)
        glow_ref[...] = jnp.zeros_like(glow_ref)

    def body(at):
        part = g_ref[at, :]
        acc_ref[at, :] += nt(part, w)
        glow_ref[at, :] += nt(part, low_up_ref[...])

    row_loop(rows, rows, body)
    gr_ref[g * 3 + j] = tn(low_ref[...], g_ref[...]).astype(BF)

    @pl.when(final)
    def _():
        def body(at):
            glow = glow_ref[at, :].astype(BF)
            total = acc_ref[at, :] + nn(glow, low_in_ref[...])
            grad = resid_ref[at, :] + norm_back(tok_ref[at, :].astype(F32), gain_ref[...], total)
            grad_ref[at, :] = grad
            send_ref[at, :] = grad.astype(BF)

        row_loop(rows, 256, body)
        y = tn(glow_ref[...].astype(BF), norm_ref[...]).astype(BF)
        c = g_ref.shape[1]
        for n in range(y.shape[1] // c):
            gr_ref[g_steps + n] = y[:, n * c : (n + 1) * c]
        gr_ref[gr_ref.shape[0] - 1] = tag_ref[...]


def project_qkv_back(grad, w, low_up, low_in, normed, low, tok, gain, resid, tag):
    rows, features = tok.shape
    shards, groups, _, part, width = w.shape
    rank = low_in.shape[0]
    return pl.pallas_call(
        qkv_back_kernel,
        out_shape=(
            jax.ShapeDtypeStruct((rows, features), F32),
            jax.ShapeDtypeStruct((rows, features), BF),
            jax.ShapeDtypeStruct((groups * 3 + features // width + 1, rank, width), BF),
        ),
        grid=(groups, 3),
        in_specs=[
            pl.BlockSpec((None, None, rows, width), lambda g, j: (g, j, 0, 0)),
            pl.BlockSpec((shards, None, None, part, width), lambda g, j: (0, g, j, 0, 0)),
            pl.BlockSpec((None, rank, width), lambda g, j: (g, 0, j)),
            whole((rank, features)), whole((rows, features)), whole((rows, rank)),
            whole((rows, features)), whole((1, features)), whole((rows, features)),
            whole((rank, width)),
        ],
        out_specs=[
            whole((rows, features)),
            whole((rows, features)),
            whole((groups * 3 + features // width + 1, rank, width)),
        ],
        scratch_shapes=[pltpu.VMEM((rows, features), F32), pltpu.VMEM((rows, rank), F32)],
        compiler_params=pltpu.CompilerParams(
            dimension_semantics=("arbitrary", "arbitrary"), vmem_limit_bytes=60 * MIB
        ),
        cost_estimate=cost(5 * rows * features * groups * 3 * width, 4 * rows * groups * 3 * width),
        name="project_qkv_back",
    )(grad, w, low_up, low_in, normed, low, tok, gain, resid, tag)


GELU = math.sqrt(2.0 / math.pi)


def gelu_and_slope(v):
    v2 = v * v
    half = 0.5 + 0.5 * jnp.tanh(v * (GELU + (GELU * 0.044715) * v2))
    hidden = v * half
    return hidden, half + hidden * (1.0 - half) * (2.0 * GELU + (6.0 * 0.044715 * GELU) * v2)


def middle_kernel(
    groups, nf, wt_ref, wc_ref, gi_ref,
    w_ref, sh_ref, wo_ref, sho_ref, tok_ref, mix_ref, cot_ref, gain_ref, bias_ref, rep_ref,
    out_ref, resid_ref, gmix_ref, gr_ref,
    acc_ref, norm_ref, hid_ref, slope_ref, lacc_ref, llow_ref,
):
    rows, features = tok_ref.shape
    rank = sh_ref.shape[0]
    s = pl.program_id(0)
    b_out, a_up, b_down = rep_ref[0], rep_ref[1], rep_ref[2]
    co = wo_ref.shape[-1]
    up0, down0 = groups, groups + nf
    upb0, end0 = groups + 2 * nf, groups + 3 * nf

    for g in range(groups):

        @pl.when(s == g)
        def _():
            part = mix_ref[g]
            y = nt(part, wo_ref[...].reshape(features, co))
            low = nt(part, sho_ref[...])
            if g == 0:
                resid_ref[...] = tok_ref[...].astype(F32) + y
                lacc_ref[...] = low
            else:
                resid_ref[...] += y
                lacc_ref[...] += low

    @pl.when(s == up0 - 1)
    def _():
        def body(at):
            low = lacc_ref[at, :].astype(BF)
            llow_ref[0, at, :] = low
            resid = resid_ref[at, :] + nn(low, b_out)
            resid_ref[at, :] = resid
            center, r = stats(resid)
            normed = (center * r * gain_ref[...] + bias_ref[...]).astype(BF)
            norm_ref[at, :] = normed
            llow_ref[1, at, :] = nt(normed, a_up).astype(BF)

        row_loop(rows, 256, body)
        llow_ref[3] = nt(cot_ref[...], b_down).astype(BF)
        acc_ref[...] = jnp.zeros_like(acc_ref)
        lacc_ref[...] = jnp.zeros_like(lacc_ref)

    @pl.when((s >= up0) & (s < down0))
    def _():
        f = s - up0
        w = w_ref[...].reshape(features, -1)

        def body(at):
            pre = nn(norm_ref[at, :], w) + nn(llow_ref[1, at, :], sh_ref[...])
            hidden, slope = gelu_and_slope(pre)
            hid_ref[f, at, :] = hidden.astype(BF)
            slope_ref[f, at, :] = slope.astype(BF)

        row_loop(rows, 512, body)

    @pl.when((s >= down0) & (s < upb0))
    def _():
        f = s - down0
        w = w_ref[...].reshape(features, -1)
        sh = sh_ref[...]
        hidden = hid_ref[f]
        acc_ref[...] += nt(hidden, w)
        lacc_ref[...] += nt(hidden, sh)
        g_hidden = nn(cot_ref[...], w) + nn(llow_ref[3], sh)
        g_pre = (g_hidden * slope_ref[f].astype(F32)).astype(BF)
        slope_ref[f] = g_pre
        gr_ref[:rank, :] = tn(llow_ref[3], hidden).astype(BF)
        gr_ref[rank:, :] = tn(llow_ref[1], g_pre).astype(BF)

    @pl.when(s == upb0 - 1)
    def _():
        def body(at):
            low = lacc_ref[at, :].astype(BF)
            llow_ref[2, at, :] = low
            out_ref[at, :] = (resid_ref[at, :] + acc_ref[at, :] + nn(low, b_down)).astype(BF)

        row_loop(rows, 512, body)
        acc_ref[...] = jnp.zeros_like(acc_ref)
        lacc_ref[...] = jnp.zeros_like(lacc_ref)

    @pl.when((s >= upb0) & (s < end0))
    def _():
        f = s - upb0
        w = w_ref[...].reshape(features, -1)
        part = slope_ref[f]
        acc_ref[...] += nt(part, w)
        lacc_ref[...] += nt(part, sh_ref[...])

    @pl.when(s == end0 - 1)
    def _():
        gr_ref[:rank, :] = tn(llow_ref[2], cot_ref[...]).astype(BF)
        llow_ref[4] = lacc_ref[...].astype(BF)
        gr_ref[rank:, :] = tn(llow_ref[4], norm_ref[...]).astype(BF)

        def body(at):
            total = acc_ref[at, :] + nn(llow_ref[4, at, :], a_up)
            g = cot_ref[at, :].astype(F32) + norm_back(resid_ref[at, :], gain_ref[...], total)
            resid_ref[at, :] = g
            branch = g.astype(BF)
            norm_ref[at, :] = branch
            llow_ref[5, at, :] = nt(branch, b_out).astype(BF)

        row_loop(rows, 256, body)

    for g in range(groups):

        @pl.when(s == end0 + g)
        def _():
            wo = wo_ref[...].reshape(features, co)
            y = nn(norm_ref[...], wo) + nn(llow_ref[5], sho_ref[...])
            gmix_ref[g] = y.astype(BF)
            gr_ref[:rank, g * co : (g + 1) * co] = tn(llow_ref[5], mix_ref[g]).astype(BF)
            if g == 0:
                gr_ref[rank:, :] = tn(llow_ref[0], norm_ref[...]).astype(BF)


def middle(w, shared, tok, mix, cot, gain, bias, rep):
    rows, features = tok.shape
    shards, groups, part, total = w.shape
    rank = rep.shape[1]
    co = mix.shape[2]
    ffw = (total - co) // 2
    c = features
    halves = ffw // c
    nf = groups * halves
    first = (shared.shape[2] - 2 * ffw) // c
    out_at, out_shared = total // co - 1, (shared.shape[2] - 2 * ffw) // co - 1
    blocks = [(f // halves, f % halves) for f in range(nf)]
    up = [(t, h) for t, h in blocks]
    down = [(t, halves + h) for t, h in blocks]
    order = [up[0]] * groups + up + down + up + [up[-1]] * groups
    of_grad = [0] * (groups + nf) + list(range(nf)) + [nf + 1] * nf + [nf] * groups
    table = lambda v: jnp.array(v, jnp.int32)
    last = len(order) - groups

    def group(s):
        return jnp.where(s < groups, s, jnp.maximum(s - last, 0))

    once = pl.Buffered(1)

    def keep(shape):
        return pl.BlockSpec(shape, lambda s, *_: (0,) * len(shape), pipeline_mode=once)

    return pl.pallas_call(
        functools.partial(middle_kernel, groups, nf),
        out_shape=(
            jax.ShapeDtypeStruct((rows, features), BF),
            jax.ShapeDtypeStruct((rows, features), F32),
            jax.ShapeDtypeStruct(mix.shape, BF),
            jax.ShapeDtypeStruct((nf + 2, 2 * rank, c), BF),
        ),
        grid_spec=pltpu.PrefetchScalarGridSpec(
            num_scalar_prefetch=3,
            grid=(len(order),),
            in_specs=[
                pl.BlockSpec((shards, None, part, c), lambda s, wt, wc, gi: (0, wt[s], 0, wc[s])),
                pl.BlockSpec((None, rank, c), lambda s, wt, wc, gi: (wt[s], 0, wc[s] + first)),
                pl.BlockSpec((shards, None, part, co), lambda s, *_: (0, group(s), 0, out_at)),
                pl.BlockSpec((None, rank, co), lambda s, *_: (group(s), 0, out_shared)),
                keep((rows, features)), keep(mix.shape), keep((rows, features)),
                keep((1, features)), keep((1, features)), keep(rep.shape),
            ],
            out_specs=[
                keep((rows, features)), keep((rows, features)), keep(mix.shape),
                pl.BlockSpec((None, 2 * rank, c), lambda s, wt, wc, gi: (gi[s], 0, 0)),
            ],
            scratch_shapes=[
                pltpu.VMEM((rows, features), F32),
                pltpu.VMEM((rows, features), BF),
                pltpu.VMEM((nf, rows, c), BF),
                pltpu.VMEM((nf, rows, c), BF),
                pltpu.VMEM((rows, rank), F32),
                pltpu.VMEM((6, rows, rank), BF),
            ],
        ),
        compiler_params=pltpu.CompilerParams(
            dimension_semantics=("arbitrary",), vmem_limit_bytes=62 * MIB
        ),
        cost_estimate=cost(6 * rows * features * groups * total, 4 * features * groups * total),
        name="middle",
    )(
        table([t for t, _ in order]), table([x for _, x in order]), table(of_grad),
        w, shared, w, shared, tok, mix, cot, gain, bias, rep,
    )


def spread_kernel(n_all, kinds, planes, *refs):
    n_swap = len(kinds)
    shard = refs[:n_all]
    swap_in = refs[n_all : n_all + n_swap]
    full = refs[n_all + n_swap : 2 * n_all + n_swap]
    swap_out = refs[2 * n_all + n_swap : 2 * n_all + 2 * n_swap]
    out_sem, in_sem, own_sem, swap_sem = refs[2 * n_all + 2 * n_swap :]
    dp, t = lax.axis_index("dp"), lax.axis_index("tensor")
    z, x, c = dp // 4, (dp // 2) % 2, dp % 2
    moves = c != t
    low, high = z > 0, z < planes - 1

    def place(z_, x_, c_):
        return z_ * 4 + x_ * 2 + c_

    x1, t1 = x, 1 - t
    x2, t2 = 1 - x, t
    x3, t3 = 1 - x, 1 - t
    below, above = (jnp.maximum(dp - 4, 0), t), (jnp.minimum(dp + 4, 4 * planes - 1), t)
    one, two = (place(z, x1, c), t1), (place(z, x2, c), t2)
    sib = (place(z, x, 1 - c), t)
    partner = (place(z, x, t), c)

    barrier = pltpu.get_barrier_semaphore()

    def greet(who):
        pl.semaphore_signal(barrier, inc=1, device_id=who, device_id_type=pl.DeviceIdType.MESH)

    for who in (one, two, sib):
        greet(who)
    pl.when(low)(lambda: greet(below))
    pl.when(high)(lambda: greet(above))
    pl.when(moves)(lambda: greet(partner))
    count = 3 + low.astype(jnp.int32) + high.astype(jnp.int32) + moves.astype(jnp.int32)
    pl.semaphore_wait(barrier, count)

    pending = []

    keeps = jnp.logical_not(moves)
    rules = {"partner": (moves, partner, moves), "near": (moves, one, keeps), "sibling": (keeps, sib, moves)}

    def swap_copy(n):
        return pltpu.make_async_remote_copy(
            src_ref=swap_in[n], dst_ref=swap_out[n], send_sem=swap_sem.at[n, 0],
            recv_sem=swap_sem.at[n, 1], device_id=rules[kinds[n]][1],
            device_id_type=pl.DeviceIdType.MESH,
        )

    for n in range(n_swap):
        pl.when(rules[kinds[n]][0])(lambda n=n: swap_copy(n).start())

    def copy(n, at, who, sem, own=False):
        slot = full[n].at[at[0], at[1]]
        return pltpu.make_async_remote_copy(
            src_ref=shard[n] if own else slot, dst_ref=slot, send_sem=out_sem.at[n, sem],
            recv_sem=in_sem.at[n, at[0] * 2 + at[1]], device_id=who,
            device_id_type=pl.DeviceIdType.MESH,
        )

    def send(cond, *args, **kw):
        if cond is None:
            copy(*args, **kw).start()
        else:
            pl.when(cond)(lambda: copy(*args, **kw).start())
        pending.append((cond, args, kw))

    def arrive(n, at):
        copy(n, at, sib, 0).wait_recv()

    def own_copy(n):
        return pltpu.make_async_copy(shard[n], full[n].at[dp, t], own_sem.at[n])

    def sem(kind, zz):
        return kind * planes + zz

    def at_z(n, zz, forward, cond):
        own = forward is None
        at = (place(zz, x, c), t)

        def run():
            if not own:
                arrive(n, at)
                towards, ok, kind = forward
                pl.when(ok)(lambda: copy(n, at, towards, sem(kind, zz)).start())
            for who, kind in ((one, 2), (two, 3), (sib, 5)):
                copy(n, at, who, sem(kind, zz), own=own).start()

        if own:
            run()
        else:
            pl.when(cond)(run)
            pending.append((cond & forward[1], (n, at, forward[0], sem(forward[2], zz)), {}))
        for who, kind in ((one, 2), (two, 3), (sib, 5)):
            pending.append((cond, (n, at, who, sem(kind, zz)), {"own": own}))

    def at_side(n, zz, xs, ts, targets, cond):
        at = (place(zz, xs, c), ts)

        def run():
            arrive(n, at)
            for who, kind in targets:
                copy(n, at, who, sem(kind, zz)).start()

        if cond is None:
            run()
        else:
            pl.when(cond)(run)
        for who, kind in targets:
            pending.append((cond, (n, at, who, sem(kind, zz)), {}))

    for n in range(n_all):
        at = (dp, t)
        send(low, n, at, below, sem(0, z), own=True)
        send(high, n, at, above, sem(1, z), own=True)
        at_z(n, z, None, None)
        own_copy(n).start()

    def both_ways(k, act):
        if k == 0:
            act(z, None, None)
        else:
            act(z - k, (above, high, 1), z >= k)
            act(z + k, (below, low, 0), z + k < planes)

    for time in range(1, planes + 2):
        for n in range(n_all):
            if time < planes:
                both_ways(time, lambda zz, forward, cond: at_z(n, zz, forward, cond))
            if time - 1 < planes:
                both_ways(time - 1, lambda zz, _, cond: at_side(n, zz, x1, t1, ((two, 4), (sib, 6)), cond))
                both_ways(time - 1, lambda zz, _, cond: at_side(n, zz, x2, t2, ((sib, 7),), cond))
            if time >= 2:
                both_ways(time - 2, lambda zz, _, cond: at_side(n, zz, x3, t3, ((sib, 8),), cond))

    for n in range(n_all):
        for zz in range(planes):
            for x_, t_ in ((x, t), (x1, t1), (x2, t2), (x3, t3)):
                arrive(n, (place(zz, x_, 1 - c), t_))
        own_copy(n).wait()
    for n in range(n_swap):
        pl.when(rules[kinds[n]][0])(lambda n=n: swap_copy(n).wait_send())
        pl.when(rules[kinds[n]][2])(lambda n=n: swap_copy(n).wait_recv())
    for cond, args, kw in pending:
        if cond is None:
            copy(*args, **kw).wait_send()
        else:
            pl.when(cond)(lambda args=args, kw=kw: copy(*args, **kw).wait_send())


def spread(gathered, handed, shards, ident):
    planes = shards // 4
    swapped = [a for a, _ in handed]
    n_all, n_swap = len(gathered), len(swapped)
    anywhere = pl.BlockSpec(memory_space=pl.ANY)
    return pl.pallas_call(
        functools.partial(spread_kernel, n_all, [k for _, k in handed], planes),
        out_shape=[jax.ShapeDtypeStruct((shards, 2) + a.shape, a.dtype) for a in gathered]
        + [jax.ShapeDtypeStruct(a.shape, a.dtype) for a in swapped],
        in_specs=[anywhere] * (n_all + n_swap),
        out_specs=[anywhere] * (n_all + n_swap),
        scratch_shapes=[
            pltpu.SemaphoreType.DMA((n_all, 9 * planes)),
            pltpu.SemaphoreType.DMA((n_all, 2 * shards)),
            pltpu.SemaphoreType.DMA((n_all,)),
            pltpu.SemaphoreType.DMA((max(n_swap, 1), 2)),
        ],
        compiler_params=pltpu.CompilerParams(collective_id=ident, has_side_effects=True),
        cost_estimate=cost(0, 60 * MIB),
        name="spread%d" % ident,
    )(*gathered, *swapped)


def sum_kernel(pieces, sel_ref, t_ref, *refs):
    ins, outs = refs[: len(refs) - len(pieces)], refs[len(refs) - len(pieces) :]
    slot = pl.program_id(0)
    for out in outs:
        out[...] = jnp.zeros_like(out)

    @pl.loop(0, ins[0].shape[0])
    def _(d):
        for which in sorted({p[1] for p in pieces}):

            @pl.when(sel_ref[d, which] == slot)
            def _():
                for (at, mine, blocks), out in zip(pieces, outs):
                    if mine != which:
                        continue
                    rank = out.shape[-2]
                    c = ins[at].shape[-1]
                    for k, (block, row) in enumerate(blocks):
                        new = ins[at][d, block, row : row + rank, :].astype(F32)
                        if len(out.shape) == 3:
                            out[k] += new
                        else:
                            out[:, k * c : (k + 1) * c] += new


def sum_picks(sel, t, arrays, pieces, slots, rank, name):
    in_specs = []
    for a, shape, where in arrays:
        in_specs.append(
            pl.BlockSpec(
                (a.shape[0],) + shape, lambda s, sel, t, where=where: (0,) + where(t[0]),
                pipeline_mode=pl.Buffered(1),
            )
        )
    shapes = []
    for at, _, blocks, flat in pieces:
        n, c = len(blocks), arrays[at][1][-1]
        shapes.append((rank, n * c) if flat else (n, rank, c))
    return pl.pallas_call(
        functools.partial(sum_kernel, [p[:3] for p in pieces]),
        out_shape=[jax.ShapeDtypeStruct((slots,) + shape, F32) for shape in shapes],
        grid_spec=pltpu.PrefetchScalarGridSpec(
            num_scalar_prefetch=2, grid=(slots,), in_specs=in_specs,
            out_specs=[
                pl.BlockSpec((None,) + shape, lambda s, sel, t, n=len(shape): (s,) + (0,) * n)
                for shape in shapes
            ],
        ),
        compiler_params=pltpu.CompilerParams(
            dimension_semantics=("arbitrary",), vmem_limit_bytes=48 * MIB
        ),
        cost_estimate=cost(0, 30 * MIB),
        name=name,
    )(sel, t, *[a for a, _, _ in arrays])


def chip_device(
    tokens, w_qkv, w_out, w_up, w_down, ln1_gain, ln1_bias, ln2_gain, ln2_bias,
    a_qkv, b_qkv, a_out, b_out, a_up, b_up, a_down, b_down, adapter_idx, pic_start, cotangent,
):
    shards = lax.axis_size("dp")
    dp, t = lax.axis_index("dp"), lax.axis_index("tensor")
    keeps = dp % 2 == t
    both = ("dp", "tensor")
    cores = [[2 * c, 2 * c + 1] for c in range(shards // 2)]
    swap = []
    for c in range(shards // 2):
        one, two = 2 * (2 * c + 1), 2 * (2 * c) + 1
        swap += [(one, two), (two, one)]

    def swapped(x):
        return lax.ppermute(x, both, swap)

    def across(x):
        return lax.all_to_all(x, "dp", 0, 0, axis_index_groups=cores, tiled=True)

    def row(v):
        return v.reshape(1, -1)

    rank, slots = a_qkv.shape[2], a_qkv.shape[0]
    features, width = tokens.shape[1], w_out.shape[0]
    chosen = adapter_idx[0]

    def pick(stacked, which):
        return lax.dynamic_index_in_dim(stacked, chosen[which], 0, keepdims=False)

    half = jnp.concatenate(
        [pick(b_qkv, 0).reshape(rank, -1), pick(a_out, 1).T, pick(b_up, 2), pick(a_down, 3).T], axis=1
    )
    rest = jnp.concatenate(
        [pick(a_qkv, 0).T, pick(b_out, 1), pick(a_up, 2).T, pick(b_down, 3)], axis=1
    )
    marks = jnp.concatenate([chosen, pic_start[0]])
    marks = jnp.pad(marks, (0, 128 - marks.shape[0]))[None] * jnp.ones((8, 1), jnp.int32)

    qkv_shard = w_qkv.transpose(1, 0, 2)
    rest_shard = jnp.concatenate([w_up, w_down.T, w_out.T], axis=1)
    qkv_full, far_tokens, near_half, partner_half, core_half, core_rest, core_marks = spread(
        [qkv_shard],
        [
            (tokens, "partner"), (half, "near"), (half, "partner"),
            (half, "sibling"), (rest, "sibling"), (marks, "sibling"),
        ],
        shards,
        0,
    )
    rest_full = lax.all_gather(rest_shard, both, axis=0)
    rest_full = rest_full.reshape(shards, 2, *rest_shard.shape)
    cot = jnp.where(keeps, cotangent, swapped(cotangent))
    tok = jnp.where(keeps, tokens, far_tokens)
    own_half = jnp.where(keeps, half, core_half)
    far_half = jnp.where(keeps, near_half, partner_half)
    shared = jnp.where(t == 0, jnp.stack([own_half, far_half]), jnp.stack([far_half, own_half]))
    rep = jnp.where(keeps, rest, core_rest).reshape(rank, 4, features).transpose(1, 0, 2)
    marks = jnp.where(keeps, marks, core_marks)[0]
    starts = marks[4 : 4 + pic_start.shape[1]]
    tag = jnp.pad(marks[:4].astype(BF)[None], ((0, rank - 1), (0, width - 4)))

    qkv, normed, low = project_qkv(tok, row(ln1_gain), row(ln1_bias), rep[0], qkv_full, shared)
    qkv = across(qkv)
    mixed, lse = attend_rows(starts, qkv)
    layer_out, g_resid, g_mix, g_early = middle(
        rest_full, shared, tok, across(mixed), cot, row(ln2_gain), row(ln2_bias), rep[1:]
    )
    early = lax.all_gather(g_early, both, axis=0)
    out = jnp.where(keeps, layer_out, swapped(layer_out))
    g_qkv = across(attend_rows_back(starts, qkv, mixed, across(g_mix), lse))
    grad_tok, grad_send, g_late = project_qkv_back(
        g_qkv, qkv_full, shared, rep[0], normed, low, tok, row(ln1_gain), g_resid, tag
    )
    late, far_grad = spread([g_late], [(grad_send, "partner")], shards, 1)
    grad_input = jnp.where(keeps, grad_tok, far_grad.astype(F32))

    late = late.reshape(2 * shards, *g_late.shape)
    sel = late[:, -1, 0, :4].astype(jnp.int32)
    side = t.reshape(1).astype(jnp.int32)
    nf, c = g_early.shape[0] - 2, g_early.shape[2]
    near = range(nf // 2)
    rows2 = 2 * rank
    early = early.reshape(2 * shards, *g_early.shape)
    grad_a_out, grad_b_out, grad_a_up, grad_b_up, grad_a_down, grad_b_down = sum_picks(
        sel, side,
        [
            (early, (nf // 2, rows2, c), lambda u: (u, 0, 0)),
            (early, (1, rows2, width), lambda u: (nf, 0, u)),
            (early, (2, rows2, c), lambda u: (nf // 2, 0, 0)),
        ],
        [
            (1, 1, [(0, 0)], True),
            (2, 1, [(0, rank)], True),
            (2, 2, [(1, rank)], True),
            (0, 2, [(i, rank) for i in near], True),
            (0, 3, [(i, 0) for i in near], True),
            (2, 3, [(1, 0)], True),
        ],
        slots, rank, "sum_early",
    )
    grad_b_qkv, grad_a_qkv = sum_picks(
        sel, side,
        [
            (late, (3, rank, width), lambda u: (u, 0, 0)),
            (late, (2, rank, width), lambda u: (3, 0, 0)),
        ],
        [(0, 0, [(0, 0), (1, 0), (2, 0)], False), (1, 0, [(0, 0), (1, 0)], True)],
        slots, rank, "sum_late",
    )
    turned = lambda v: v.transpose(0, 2, 1)
    return (
        out, grad_input, turned(grad_a_qkv), grad_b_qkv.transpose(0, 2, 1, 3),
        turned(grad_a_out), grad_b_out, turned(grad_a_up), grad_b_up, turned(grad_a_down), grad_b_down,
    )


def solution(mesh):
    placed = (
        P(("dp", "tensor"), None),
        P("dp", None, "tensor"),
        P("tensor", "dp"),
        P("dp", "tensor"),
        P("tensor", "dp"),
        P(),
        P(),
        P(),
        P(),
        P(),
        P(None, None, None, "tensor"),
        P(None, "tensor", None),
        P(),
        P(),
        P(None, None, "tensor"),
        P(None, "tensor", None),
        P(),
        P("dp", None),
        P("dp", None),
        P(("dp", "tensor"), None),
    )
    paired = mesh.shape["tensor"] == 2 and mesh.shape["dp"] % 2 == 0
    return jax.shard_map(
        chip_device if paired else per_device,
        mesh=mesh,
        in_specs=placed,
        out_specs=(
            P(("dp", "tensor"), None),
            P(("dp", "tensor"), None),
            P(),
            P(None, None, None, "tensor"),
            P(None, "tensor", None),
            P(),
            P(),
            P(None, None, "tensor"),
            P(None, "tensor", None),
            P(),
        ),
        check_vma=False,
    )
```

```python
import functools
import math

import jax
import jax.numpy as jnp
from jax import lax
from jax.experimental import pallas as pl
from jax.experimental.pallas import tpu as pltpu
from jax.sharding import PartitionSpec as P

HD = 64
SPAN = 256
BLOCK = 512


def matmul(left, right):
    return jnp.dot(left, right, preferred_element_type=jnp.float32)


def contract_rows(left, right):
    return lax.dot_general(
        left, right, (((0,), (0,)), ((), ())), preferred_element_type=jnp.float32
    )


def against(left, right):
    return lax.dot_general(
        left, right, (((1,), (1,)), ((), ())), preferred_element_type=jnp.float32
    )


def layer_norm(values, multiplier, addend):
    center = values - jnp.mean(values, axis=-1, keepdims=True)
    spread = jnp.mean(center * center, axis=-1, keepdims=True)
    return center * lax.rsqrt(spread + 1e-05) * multiplier + addend


def span_labels(positions, starts):
    inside = (positions[:, None] >= starts[None, :]) & (positions[:, None] < starts[None, :] + SPAN)
    labels = jnp.arange(1, starts.shape[0] + 1, dtype=jnp.int32)
    return jnp.sum(jnp.where(inside, labels[None, :], 0), axis=1)


def allowed_mask(offset, row_count, length, starts):
    row_pos = offset + jnp.arange(row_count, dtype=jnp.int32)
    col_pos = jnp.arange(length, dtype=jnp.int32)
    row_span = span_labels(row_pos, starts)
    col_span = span_labels(col_pos, starts)
    causal = col_pos[None, :] <= row_pos[:, None]
    joined = (row_span[:, None] == col_span[None, :]) & (row_span[:, None] > 0)
    return causal | joined


def masked_scores(query_block, key_rows, offset, length, starts, factor):
    scores = (
        jnp.einsum("qhd,khd->hqk", query_block, key_rows, preferred_element_type=jnp.float32)
        * factor
    )
    allowed = allowed_mask(offset, BLOCK, length, starts)
    return jnp.where(allowed[None], scores, -1000000000.0)


def attend(queries, key_rows, value_rows, starts):
    length, heads, width = queries.shape
    factor = width ** (-0.5)

    def one_block(block_number):
        offset = block_number * BLOCK
        query_block = lax.dynamic_slice_in_dim(queries, offset, BLOCK, 0)
        scores = masked_scores(query_block, key_rows, offset, length, starts, factor)
        peak = jnp.max(scores, axis=-1, keepdims=True)
        raised = jnp.exp(scores - peak)
        totals = jnp.sum(raised, axis=-1, keepdims=True)
        weights_low = (raised / totals).astype(jnp.bfloat16)
        blended = jnp.einsum(
            "hqk,khd->qhd", weights_low, value_rows, preferred_element_type=jnp.float32
        )
        return (
            blended.astype(jnp.bfloat16).reshape(BLOCK, heads * width),
            (peak + jnp.log(totals))[..., 0],
        )

    blended, log_sums = lax.map(one_block, jnp.arange(length // BLOCK, dtype=jnp.int32))
    return (blended.reshape(length, heads * width), log_sums)


def attend_back(queries, key_rows, value_rows, grad_mix, log_sums, starts):
    length, heads, width = queries.shape
    factor = width ** (-0.5)

    def one_block(carry, inputs_pair):
        key_grad, value_grad = carry
        block_number, block_sums = inputs_pair
        offset = block_number * BLOCK
        query_block = lax.dynamic_slice_in_dim(queries, offset, BLOCK, 0)
        grad_block = lax.dynamic_slice_in_dim(grad_mix, offset, BLOCK, 0)
        scores = masked_scores(query_block, key_rows, offset, length, starts, factor)
        weights = jnp.exp(scores - block_sums[:, :, None])
        dots = jnp.einsum(
            "qhd,khd->hqk", grad_block, value_rows, preferred_element_type=jnp.float32
        )
        inner = jnp.sum(weights * dots, axis=-1, keepdims=True)
        slopes = (weights * (dots - inner) * factor).astype(jnp.bfloat16)
        query_grad = jnp.einsum(
            "hqk,khd->qhd", slopes, key_rows, preferred_element_type=jnp.float32
        )
        key_grad = key_grad + jnp.einsum(
            "hqk,qhd->khd", slopes, query_block, preferred_element_type=jnp.float32
        )
        value_grad = value_grad + jnp.einsum(
            "hqk,qhd->khd",
            weights.astype(jnp.bfloat16),
            grad_block,
            preferred_element_type=jnp.float32,
        )
        return ((key_grad, value_grad), query_grad)

    initial = jnp.zeros(key_rows.shape, jnp.float32)
    numbers = jnp.arange(length // BLOCK, dtype=jnp.int32)
    (key_grad, value_grad), query_grad = lax.scan(
        one_block, (initial, initial), (numbers, log_sums)
    )
    return (query_grad.reshape(length, heads, width), key_grad, value_grad)


def fetch_frozen(first, second):
    return (
        lax.all_gather(first, "dp", axis=0, tiled=True),
        lax.all_gather(second, "dp", axis=1, tiled=True),
    )


def enter_rows(normed, reduced):
    return (
        lax.all_gather(normed, "tensor", axis=0, tiled=True),
        lax.all_gather(reduced, "tensor", axis=0, tiled=True),
    )


def leave_rows(partial_value, reduced):
    return (
        lax.psum_scatter(partial_value, "tensor", scatter_dimension=0, tiled=True),
        lax.psum_scatter(reduced, "tensor", scatter_dimension=0, tiled=True),
    )


def enter_grads(branch, reduced):
    return (
        lax.all_gather(branch, "tensor", axis=0, tiled=True),
        lax.all_gather(reduced, "tensor", axis=0, tiled=True),
    )


def leave_grads(partial_value, reduced):
    return (
        lax.psum_scatter(partial_value, "tensor", scatter_dimension=0, tiled=True),
        lax.psum_scatter(reduced, "tensor", scatter_dimension=0, tiled=True),
    )


def per_device(
    tokens,
    w_qkv,
    w_out,
    w_up,
    w_down,
    ln1_gain,
    ln1_bias,
    ln2_gain,
    ln2_bias,
    a_qkv,
    b_qkv,
    a_out,
    b_out,
    a_up,
    b_up,
    a_down,
    b_down,
    adapter_idx,
    pic_start,
    cotangent,
):
    selection = adapter_idx[0]
    starts = pic_start[0]

    def chosen(stacked, which_one):
        return lax.dynamic_index_in_dim(stacked, selection[which_one], 0, keepdims=False)

    low_qkv_in = chosen(a_qkv, 0)
    rank = low_qkv_in.shape[1]
    low_qkv_out = chosen(b_qkv, 0).reshape(rank, -1)
    low_out_in = chosen(a_out, 1)
    low_out_out = chosen(b_out, 1)
    low_up_in = chosen(a_up, 2)
    low_up_out = chosen(b_up, 2)
    low_down_in = chosen(a_down, 3)
    low_down_out = chosen(b_down, 3)
    heads_here = low_out_in.shape[0] // HD

    def run_forward(own_tokens, frozen):
        qkv_rows, out_rows, up_rows, down_rows = frozen
        qkv_full, out_full = fetch_frozen(qkv_rows, out_rows)
        qkv_flat = qkv_full.reshape(qkv_full.shape[0], -1)
        own_float = own_tokens.astype(jnp.float32)
        normed = layer_norm(own_float, ln1_gain, ln1_bias).astype(jnp.bfloat16)
        reduced = matmul(normed, low_qkv_in).astype(jnp.bfloat16)
        normed_all, reduced_all = enter_rows(normed, reduced)
        length = normed_all.shape[0]
        project = (matmul(normed_all, qkv_flat) + matmul(reduced_all, low_qkv_out)).astype(
            jnp.bfloat16
        )
        split = project.reshape(length, 3, heads_here, HD)
        blended, log_sums = attend(split[:, 0], split[:, 1], split[:, 2], starts)
        main_part, low_part = leave_rows(matmul(blended, out_full), matmul(blended, low_out_in))
        low_out_val = low_part.astype(jnp.bfloat16)
        residual = own_float + main_part + matmul(low_out_val, low_out_out)
        up_full, down_full = fetch_frozen(up_rows, down_rows)
        normed_two = layer_norm(residual, ln2_gain, ln2_bias).astype(jnp.bfloat16)
        reduced_two = matmul(normed_two, low_up_in).astype(jnp.bfloat16)
        normed_two_all, reduced_two_all = enter_rows(normed_two, reduced_two)
        pre_act = matmul(normed_two_all, up_full) + matmul(reduced_two_all, low_up_out)
        hidden = jax.nn.gelu(pre_act, approximate=True).astype(jnp.bfloat16)
        main_two, low_two = leave_rows(matmul(hidden, down_full), matmul(hidden, low_down_in))
        low_down_val = low_two.astype(jnp.bfloat16)
        output = residual + main_two + matmul(low_down_val, low_down_out)
        kept_state = (
            qkv_flat,
            out_full,
            up_full,
            down_full,
            normed,
            reduced_all,
            split,
            blended,
            log_sums,
            low_out_val,
            residual,
            normed_two,
            reduced_two_all,
            pre_act,
            hidden,
            low_down_val,
        )
        return (output, kept_state)

    frozen = (w_qkv, w_out, w_up, w_down)
    output, kept_state = run_forward(tokens, frozen)
    (
        qkv_flat,
        out_full,
        up_full,
        down_full,
        normed,
        reduced_all,
        split,
        blended,
        log_sums,
        low_out_val,
        residual,
        normed_two,
        reduced_two_all,
        pre_act,
        hidden,
        low_down_val,
    ) = kept_state
    cot_float = cotangent.astype(jnp.float32)
    grad_low_down = against(cotangent, low_down_out).astype(jnp.bfloat16)
    grad_b_down_here = contract_rows(low_down_val, cotangent)
    cot_all, grad_low_down_all = enter_grads(cotangent, grad_low_down)
    grad_hidden = against(cot_all, down_full) + against(grad_low_down_all, low_down_in)
    grad_a_down_here = contract_rows(hidden, grad_low_down_all)
    gelu_pull = jax.vjp(lambda inner_val: jax.nn.gelu(inner_val, approximate=True), pre_act)[1]
    grad_pre = gelu_pull(grad_hidden)[0].astype(jnp.bfloat16)
    grad_b_up_here = contract_rows(reduced_two_all, grad_pre)
    grad_normed_two, grad_reduced_two = leave_grads(
        against(grad_pre, up_full), against(grad_pre, low_up_out)
    )
    grad_low_up = grad_reduced_two.astype(jnp.bfloat16)
    grad_a_up_here = contract_rows(normed_two, grad_low_up)
    grad_normed_two = grad_normed_two + against(grad_low_up, low_up_in)
    norm_pull_two = jax.vjp(lambda inner_val: layer_norm(inner_val, ln2_gain, ln2_bias), residual)[
        1
    ]
    grad_resid = cot_float + norm_pull_two(grad_normed_two)[0]
    branch_low = grad_resid.astype(jnp.bfloat16)
    grad_low_out = against(branch_low, low_out_out).astype(jnp.bfloat16)
    grad_b_out_here = contract_rows(low_out_val, branch_low)
    branch_all, grad_low_out_all = enter_grads(branch_low, grad_low_out)
    grad_mix = (against(branch_all, out_full) + against(grad_low_out_all, low_out_in)).astype(
        jnp.bfloat16
    )
    grad_a_out_here = contract_rows(blended, grad_low_out_all)
    length = grad_mix.shape[0]
    query_grad, key_grad, value_grad = attend_back(
        split[:, 0],
        split[:, 1],
        split[:, 2],
        grad_mix.reshape(length, heads_here, HD),
        log_sums,
        starts,
    )
    grad_qkv = (
        jnp.stack([query_grad, key_grad, value_grad], axis=1)
        .reshape(length, -1)
        .astype(jnp.bfloat16)
    )
    grad_b_qkv_here = contract_rows(reduced_all, grad_qkv)
    grad_normed_one, grad_reduced_one = leave_grads(
        against(grad_qkv, qkv_flat), against(grad_qkv, low_qkv_out)
    )
    grad_low_qkv = grad_reduced_one.astype(jnp.bfloat16)
    grad_a_qkv_here = contract_rows(normed, grad_low_qkv)
    grad_normed_one = grad_normed_one + against(grad_low_qkv, low_qkv_in)
    norm_pull_one = jax.vjp(
        lambda inner_val: layer_norm(inner_val, ln1_gain, ln1_bias), tokens.astype(jnp.float32)
    )[1]
    grad_input = grad_resid + norm_pull_one(grad_normed_one)[0]
    slots = a_qkv.shape[0]

    def spread(gradient, which_one):
        onehot = (jnp.arange(slots, dtype=jnp.int32) == selection[which_one]).astype(jnp.float32)
        return onehot.reshape((slots,) + (1,) * gradient.ndim) * gradient[None]

    sharded = (
        lax.psum(spread(grad_b_qkv_here.reshape(rank, 3, -1), 0).astype(jnp.bfloat16), "dp").astype(
            jnp.float32
        ),
        lax.psum(spread(grad_a_out_here, 1).astype(jnp.bfloat16), "dp").astype(jnp.float32),
        lax.psum(spread(grad_b_up_here, 2).astype(jnp.bfloat16), "dp").astype(jnp.float32),
        lax.psum(spread(grad_a_down_here, 3).astype(jnp.bfloat16), "dp").astype(jnp.float32),
    )
    shared = lax.psum(
        (
            spread(grad_a_qkv_here, 0),
            spread(grad_b_out_here, 1),
            spread(grad_a_up_here, 2),
            spread(grad_b_down_here, 3),
        ),
        ("dp", "tensor"),
    )
    return (
        output.astype(jnp.bfloat16),
        grad_input,
        shared[0],
        sharded[0],
        sharded[1],
        shared[1],
        shared[2],
        sharded[2],
        sharded[3],
        shared[3],
    )


LOG2E = math.log2(math.e)
MASKED = -1e30
MIB = 1 << 20
BF = jnp.bfloat16
F32 = jnp.float32
MESH = pl.DeviceIdType.MESH


def nt(a, b):
    return lax.dot_general(a, b, (((1,), (1,)), ((), ())), preferred_element_type=F32)


def nn(a, b):
    return lax.dot_general(a, b, (((1,), (0,)), ((), ())), preferred_element_type=F32)


def tn(a, b):
    return lax.dot_general(a, b, (((0,), (0,)), ((), ())), preferred_element_type=F32)


def last_key(starts_ref, pos):
    lim = pos
    for n in range(starts_ref.shape[0]):
        first = starts_ref[n]
        lim = jnp.where((pos >= first) & (pos < first + SPAN), first + SPAN - 1, lim)
    return lim


def head_parts(x):
    lane = lax.broadcasted_iota(jnp.int32, x.shape, 1)
    zero = jnp.zeros_like(x)
    return jnp.where(lane < HD, x, zero), jnp.where(lane >= HD, x, zero)


def cost(flops, moved):
    return pl.CostEstimate(flops=int(flops), bytes_accessed=int(moved), transcendentals=0)


def pair_core():
    dp, t = lax.axis_index("dp"), lax.axis_index("tensor")
    b = dp % 2
    return b, (dp + 1 - 2 * b, t)


def greet_core(sib):
    barrier = pltpu.get_barrier_semaphore()
    pl.semaphore_signal(barrier, inc=1, device_id=sib, device_id_type=MESH)
    pl.semaphore_wait(barrier, 1)


def to_core(src, dst, sems, n, sib):
    return pltpu.make_async_remote_copy(
        src_ref=src, dst_ref=dst, send_sem=sems.at[0, n], recv_sem=sems.at[1, n],
        device_id=sib, device_id_type=MESH,
    )


def attend_kernel(
    starts_ref, q_ref, k_ref, v_ref, o_ref, lse_ref, mix_ref, vt_ref, send_ref, sems, own_sems
):
    p, qi = pl.program_id(0), pl.program_id(1)
    pairs = pl.num_programs(0)
    bq = bk = k_ref.shape[1]
    scale = LOG2E * HD ** -0.5
    b, sib = pair_core()
    pl.when((p == 0) & (qi == 0))(lambda: greet_core(sib))

    @pl.when(qi == 0)
    def _():
        for n in range(k_ref.shape[0]):
            vt_ref[:, n * bk : (n + 1) * bk] = jnp.transpose(v_ref[n])

    qs = head_parts(q_ref[...])
    base = qi * bq
    lim = last_key(starts_ref, base + lax.broadcasted_iota(jnp.int32, (1, bq), 1))

    def step(masked, j, carry):
        off = pl.multiple_of(j * bk, bk)
        keys = k_ref[j]
        out = []
        for h in range(2):
            m, l, acc = carry[h]
            s = nt(keys, qs[h])
            if masked:
                kpos = off + lax.broadcasted_iota(jnp.int32, (bk, bq), 0)
                s = jnp.where(kpos <= lim, s, MASKED)
            mn = jnp.maximum(m, jnp.max(s, axis=0, keepdims=True))
            w = jnp.exp2((s - mn) * scale)
            al = jnp.exp2((m - mn) * scale)
            l = al * l + jnp.sum(w, axis=0, keepdims=True)
            acc = acc * al + nn(vt_ref[h * HD : (h + 1) * HD, pl.ds(off, bk)], w.astype(BF))
            out.append((mn, l, acc))
        return tuple(out)

    init = (jnp.full((1, bq), MASKED, F32), jnp.zeros((1, bq), F32), jnp.zeros((HD, bq), F32))
    carry = lax.fori_loop(0, qi, functools.partial(step, False), (init, init))
    carry = step(True, qi, carry)
    mixed = jnp.transpose(jnp.concatenate([carry[h][2] / carry[h][1] for h in range(2)], axis=0)).astype(BF)
    o_ref[...] = mixed
    for h in range(2):
        lse_ref[0, h : h + 1, :] = carry[h][0] * scale + jnp.log2(carry[h][1])

    def place(n, core):
        return mix_ref.at[core, :, pl.ds(pl.multiple_of(n * 2 * HD, 2 * HD), 2 * HD)]

    def far(n):
        return to_core(send_ref.at[n, 1], place(n, b), sems, n, sib)

    def own(n):
        return pltpu.make_async_copy(send_ref.at[n, 0], place(n, b), own_sems.at[n])

    @pl.when(qi == b)
    def _():
        send_ref[p, 0] = mixed
        own(p).start()

    @pl.when(qi != b)
    def _():
        send_ref[p, 1] = mixed
        far(p).start()

    @pl.when((p == pairs - 1) & (qi == pl.num_programs(1) - 1))
    def _():
        for n in range(send_ref.shape[0]):
            own(n).wait()
            far(n).wait()


def attend_rows(starts, qkv, ident):
    parts, _, rows, width = qkv.shape
    pairs = width // (2 * HD)
    length = parts * rows

    def all_parts(which):
        return pl.BlockSpec((parts, None, rows, 2 * HD), lambda p, i, s: (0, which, 0, p))

    return pl.pallas_call(
        attend_kernel,
        out_shape=(
            jax.ShapeDtypeStruct((parts, rows, width), BF),
            jax.ShapeDtypeStruct((pairs, 2, length), F32),
            jax.ShapeDtypeStruct((parts, rows, width), BF),
        ),
        grid_spec=pltpu.PrefetchScalarGridSpec(
            num_scalar_prefetch=1,
            grid=(pairs, parts),
            in_specs=[
                pl.BlockSpec((None, None, rows, 2 * HD), lambda p, i, s: (i, 0, 0, p)),
                all_parts(1),
                all_parts(2),
            ],
            out_specs=[
                pl.BlockSpec((None, rows, 2 * HD), lambda p, i, s: (i, 0, p)),
                pl.BlockSpec((1, 2, rows), lambda p, i, s: (p, 0, i)),
                pl.BlockSpec(memory_space=pl.ANY),
            ],
            scratch_shapes=[
                pltpu.VMEM((2 * HD, length), BF),
                pltpu.VMEM((pairs, 2, rows, 2 * HD), BF),
                pltpu.SemaphoreType.DMA((2, pairs)),
                pltpu.SemaphoreType.DMA((pairs,)),
            ],
        ),
        compiler_params=pltpu.CompilerParams(
            dimension_semantics=("arbitrary", "arbitrary"), vmem_limit_bytes=48 * MIB,
            collective_id=ident, has_side_effects=True,
        ),
        cost_estimate=cost(24 * length * length * width, 16 * length * width),
        name="attend",
    )(starts, qkv, qkv, qkv)


def attend_back_kernel(
    bq, bk, starts_ref, q_ref, k_ref, v_ref, o_ref, do_ref, lse_ref, all_ref,
    kt_ref, dqt_ref, delta_ref, qm_ref, dom_ref, dk_ref, dv_ref, send_ref, sems, own_sems,
):
    p_now = pl.program_id(0)
    b, sib = pair_core()
    pl.when(p_now == 0)(lambda: greet_core(sib))
    g_ref = send_ref.at[p_now]
    parts, rows, _ = q_ref.shape
    length = parts * rows
    scale = LOG2E * HD ** -0.5
    nq = length // bq
    per = rows // bq
    dqt_ref[...] = jnp.zeros_like(dqt_ref)
    for i in range(nq):
        part, at = i // per, slice((i % per) * bq, (i % per + 1) * bq)
        flat = slice(i * bq, (i + 1) * bq)
        kt_ref[:, flat] = jnp.transpose(k_ref[part, at, :])
        do = do_ref[part, at, :]
        for h, (q_h, do_h) in enumerate(zip(head_parts(q_ref[part, at, :]), head_parts(do))):
            qm_ref[h, flat, :] = q_h
            dom_ref[h, flat, :] = do_h
        prod = jnp.transpose(do.astype(F32) * o_ref[part, at, :].astype(F32))
        for h in range(2):
            delta_ref[h : h + 1, flat] = jnp.sum(prod[h * HD : (h + 1) * HD], axis=0, keepdims=True)

    half = bk // 2

    def tile(masked, keys, vals, koff, nk, qoff, nq_):
        at = pl.ds(qoff, nq_)
        dk = dv = None
        if masked:
            lim = last_key(starts_ref, qoff + lax.broadcasted_iota(jnp.int32, (1, nq_), 1))
            ok = koff + lax.broadcasted_iota(jnp.int32, (nk, nq_), 0) <= lim
        for h in range(2):
            q_h = qm_ref[h, at, :]
            do_h = dom_ref[h, at, :]
            p = jnp.exp2(nt(keys, q_h) * scale - lse_ref[0, h : h + 1, at])
            if masked:
                p = jnp.where(ok, p, 0.0)
            ds = (p * (nt(vals, do_h) - delta_ref[h : h + 1, at])).astype(BF)
            v_part, k_part = nn(p.astype(BF), do_h), nn(ds, q_h)
            dv = v_part if dv is None else dv + v_part
            dk = k_part if dk is None else dk + k_part
            head = slice(h * HD, (h + 1) * HD)
            dqt_ref[head, at] += nn(kt_ref[head, pl.ds(koff, nk)], ds)
        return dk, dv

    @pl.loop(0, length // bk)
    def _(j):
        koff = pl.multiple_of(j * bk, bk)
        part = j // (rows // bk)
        inside = pl.multiple_of((j % (rows // bk)) * bk, bk)
        keys = k_ref[part, pl.ds(inside, bk), :]
        vals = v_ref[part, pl.ds(inside, bk), :]

        def step(i, carry):
            dk, dv = tile(False, keys, vals, koff, bk, pl.multiple_of(i * bq, bq), bq)
            return carry[0] + dk, carry[1] + dv

        zero = jnp.zeros((bk, 2 * HD), F32)
        dk, dv = lax.fori_loop(j + 1, nq, step, (zero, zero))
        own = tile(True, keys, vals, koff, bk, koff, bk)
        dk_ref[...] = dk + own[0]
        dv_ref[...] = dv + own[1]

        @pl.when(j % (rows // bk) > 0)
        def _():
            before = pl.multiple_of(jnp.maximum(koff - half, 0), half)
            got = tile(True, keys[:half], vals[:half], koff, half, before, half)
            dk_ref[:half, :] += got[0]
            dv_ref[:half, :] += got[1]

        g_ref[part, 1, pl.ds(inside, bk), :] = (dk_ref[...] * HD ** -0.5).astype(BF)
        g_ref[part, 2, pl.ds(inside, bk), :] = dv_ref[...].astype(BF)

    for i in range(nq):
        part, at = i // per, slice((i % per) * bq, (i % per + 1) * bq)
        dq = jnp.transpose(dqt_ref[:, i * bq : (i + 1) * bq])
        g_ref[part, 0, at, :] = (dq * HD ** -0.5).astype(BF)

    def place(n):
        return all_ref.at[b, :, :, pl.ds(pl.multiple_of(n * 2 * HD, 2 * HD), 2 * HD)]

    def far(n):
        return to_core(send_ref.at[n, 1 - b], place(n), sems, n, sib)

    def own(n):
        return pltpu.make_async_copy(send_ref.at[n, b], place(n), own_sems.at[n])

    far(p_now).start()
    own(p_now).start()

    @pl.when(p_now == pl.num_programs(0) - 1)
    def _():
        for n in range(send_ref.shape[0]):
            own(n).wait()
            far(n).wait()


def attend_rows_back(starts, qkv, mixed, grad_mix, lse, ident):
    parts, _, rows, width = qkv.shape
    pairs = width // (2 * HD)
    length = parts * rows
    bq = bk = max(min(512, rows), 2 * SPAN)

    def one(which):
        return pl.BlockSpec((parts, None, rows, 2 * HD), lambda p, s: (0, which, 0, p))

    flat = pl.BlockSpec((parts, rows, 2 * HD), lambda p, s: (0, 0, p))
    return pl.pallas_call(
        functools.partial(attend_back_kernel, bq, bk),
        out_shape=jax.ShapeDtypeStruct((parts, 3, rows, width), BF),
        grid_spec=pltpu.PrefetchScalarGridSpec(
            num_scalar_prefetch=1,
            grid=(pairs,),
            in_specs=[one(0), one(1), one(2), flat, flat,
                      pl.BlockSpec((1, 2, length), lambda p, s: (p, 0, 0))],
            out_specs=pl.BlockSpec(memory_space=pl.ANY),
            scratch_shapes=[
                pltpu.VMEM((2 * HD, length), BF),
                pltpu.VMEM((2 * HD, length), F32),
                pltpu.VMEM((2, length), F32),
                pltpu.VMEM((2, length, 2 * HD), BF),
                pltpu.VMEM((2, length, 2 * HD), BF),
                pltpu.VMEM((bk, 2 * HD), F32),
                pltpu.VMEM((bk, 2 * HD), F32),
                pltpu.VMEM((pairs, parts, 3, rows, 2 * HD), BF),
                pltpu.SemaphoreType.DMA((2, pairs)),
                pltpu.SemaphoreType.DMA((pairs,)),
            ],
        ),
        compiler_params=pltpu.CompilerParams(
            dimension_semantics=("arbitrary",), vmem_limit_bytes=48 * MIB,
            collective_id=ident, has_side_effects=True,
        ),
        cost_estimate=cost(40 * length * length * width, 24 * length * width),
        name="attend_back",
    )(starts, qkv, qkv, qkv, mixed, grad_mix, lse)


def stats(x):
    center = x - jnp.mean(x, axis=-1, keepdims=True)
    return center, lax.rsqrt(jnp.mean(center * center, axis=-1, keepdims=True) + 1e-05)


def norm_back(x, gain, grad):
    center, r = stats(x)
    n = center * r
    e = grad * gain
    return r * (e - jnp.mean(e, axis=-1, keepdims=True) - n * jnp.mean(e * n, axis=-1, keepdims=True))


def row_loop(rows, chunk, body):
    if chunk == rows:
        body(slice(None))
        return

    @pl.loop(0, rows // chunk)
    def _(i):
        body(pl.ds(pl.multiple_of(i * chunk, chunk), chunk))


def qkv_kernel(
    tok_ref, gain_ref, bias_ref, low_in_ref, w_ref, low_up_ref, norm_ref, low_ref, all_ref,
    send_ref, sems, own_sems,
):
    rows = tok_ref.shape[0]
    side, j = pl.program_id(0), pl.program_id(1)
    b, sib = pair_core()

    @pl.when((side == 0) & (j == 0))
    def _():
        def body(at):
            center, r = stats(tok_ref[at, :].astype(F32))
            normed = (center * r * gain_ref[...] + bias_ref[...]).astype(BF)
            norm_ref[at, :] = normed
            low_ref[at, :] = nt(normed, low_in_ref[...]).astype(BF)

        row_loop(rows, 256, body)
        greet_core(sib)

    w = w_ref[...].reshape(norm_ref.shape[1], -1)
    y = nn(norm_ref[...], w) + nn(low_ref[...], low_up_ref[...])
    send_ref[side, j] = y.astype(BF)

    def far(n):
        return to_core(send_ref.at[0, n], all_ref.at[b, n], sems, n, sib)

    def own(n):
        return pltpu.make_async_copy(send_ref.at[1, n], all_ref.at[b, n], own_sems.at[n])

    pl.when(side == 0)(lambda: far(j).start())
    pl.when(side == 1)(lambda: own(j).start())

    @pl.when((side == 1) & (j == 2))
    def _():
        for n in range(3):
            own(n).wait()
            far(n).wait()


def whole(shape):
    return pl.BlockSpec(shape, lambda *_: (0,) * len(shape))


def project_qkv(tok, gain, bias, low_in, w, low_up, ident):
    rows, features = tok.shape
    shards, groups, _, part, width = w.shape
    rank = low_in.shape[0]

    def heads(side):
        b = lax.axis_index("dp") % 2
        return jnp.where(side == 0, 1 - b, b)

    return pl.pallas_call(
        qkv_kernel,
        out_shape=(
            jax.ShapeDtypeStruct((rows, features), BF),
            jax.ShapeDtypeStruct((rows, rank), BF),
            jax.ShapeDtypeStruct((groups, 3, rows, width), BF),
        ),
        grid=(groups, 3),
        in_specs=[
            whole((rows, features)), whole((1, features)), whole((1, features)),
            whole((rank, features)),
            pl.BlockSpec((shards, None, None, part, width), lambda g, j: (0, heads(g), j, 0, 0)),
            pl.BlockSpec((None, rank, width), lambda g, j: (heads(g), 0, j)),
        ],
        out_specs=[
            whole((rows, features)), whole((rows, rank)), pl.BlockSpec(memory_space=pl.ANY),
        ],
        scratch_shapes=[
            pltpu.VMEM((groups, 3, rows, width), BF),
            pltpu.SemaphoreType.DMA((2, 3)),
            pltpu.SemaphoreType.DMA((3,)),
        ],
        compiler_params=pltpu.CompilerParams(
            dimension_semantics=("arbitrary", "arbitrary"), vmem_limit_bytes=48 * MIB,
            collective_id=ident, has_side_effects=True,
        ),
        cost_estimate=cost(4 * rows * features * groups * 3 * width, 4 * rows * groups * 3 * width),
        name="project_qkv",
    )(tok, gain, bias, low_in, w, low_up)


def qkv_back_kernel(
    g_ref, w_ref, low_up_ref, low_in_ref, norm_ref, low_ref, tok_ref, gain_ref, resid_ref, tag_ref,
    grad_ref, send_ref, gr_ref, acc_ref, glow_ref,
):
    rows = tok_ref.shape[0]
    g, j = pl.program_id(0), pl.program_id(1)
    first = (g == 0) & (j == 0)
    final = (g == pl.num_programs(0) - 1) & (j == pl.num_programs(1) - 1)
    g_steps = gr_ref.shape[0] - 1 - tok_ref.shape[1] // g_ref.shape[1]
    w = w_ref[...].reshape(tok_ref.shape[1], -1)

    @pl.when(first)
    def _():
        acc_ref[...] = jnp.zeros_like(acc_ref)
        glow_ref[...] = jnp.zeros_like(glow_ref)

    def body(at):
        part = g_ref[at, :]
        acc_ref[at, :] += nt(part, w)
        glow_ref[at, :] += nt(part, low_up_ref[...])

    row_loop(rows, rows, body)
    gr_ref[g * 3 + j] = tn(low_ref[...], g_ref[...]).astype(BF)

    @pl.when(final)
    def _():
        def body(at):
            glow = glow_ref[at, :].astype(BF)
            total = acc_ref[at, :] + nn(glow, low_in_ref[...])
            grad = resid_ref[at, :] + norm_back(tok_ref[at, :].astype(F32), gain_ref[...], total)
            grad_ref[at, :] = grad
            send_ref[at, :] = grad.astype(BF)

        row_loop(rows, 256, body)
        y = tn(glow_ref[...].astype(BF), norm_ref[...]).astype(BF)
        c = g_ref.shape[1]
        for n in range(y.shape[1] // c):
            gr_ref[g_steps + n] = y[:, n * c : (n + 1) * c]
        gr_ref[gr_ref.shape[0] - 1] = tag_ref[...]


def project_qkv_back(grad, w, low_up, low_in, normed, low, tok, gain, resid, tag):
    rows, features = tok.shape
    shards, groups, _, part, width = w.shape
    rank = low_in.shape[0]
    return pl.pallas_call(
        qkv_back_kernel,
        out_shape=(
            jax.ShapeDtypeStruct((rows, features), F32),
            jax.ShapeDtypeStruct((rows, features), BF),
            jax.ShapeDtypeStruct((groups * 3 + features // width + 1, rank, width), BF),
        ),
        grid=(groups, 3),
        in_specs=[
            pl.BlockSpec((None, None, rows, width), lambda g, j: (g, j, 0, 0)),
            pl.BlockSpec((shards, None, None, part, width), lambda g, j: (0, g, j, 0, 0)),
            pl.BlockSpec((None, rank, width), lambda g, j: (g, 0, j)),
            whole((rank, features)), whole((rows, features)), whole((rows, rank)),
            whole((rows, features)), whole((1, features)), whole((rows, features)),
            whole((rank, width)),
        ],
        out_specs=[
            whole((rows, features)),
            whole((rows, features)),
            whole((groups * 3 + features // width + 1, rank, width)),
        ],
        scratch_shapes=[pltpu.VMEM((rows, features), F32), pltpu.VMEM((rows, rank), F32)],
        compiler_params=pltpu.CompilerParams(
            dimension_semantics=("arbitrary", "arbitrary"), vmem_limit_bytes=60 * MIB
        ),
        cost_estimate=cost(5 * rows * features * groups * 3 * width, 4 * rows * groups * 3 * width),
        name="project_qkv_back",
    )(grad, w, low_up, low_in, normed, low, tok, gain, resid, tag)


GELU = math.sqrt(2.0 / math.pi)


def gelu_and_slope(v):
    v2 = v * v
    half = 0.5 + 0.5 * jnp.tanh(v * (GELU + (GELU * 0.044715) * v2))
    hidden = v * half
    return hidden, half + hidden * (1.0 - half) * (2.0 * GELU + (6.0 * 0.044715 * GELU) * v2)


def middle_kernel(
    groups, nf,
    w_ref, sh_ref, wo_ref, sho_ref, tok_ref, mix_ref, cot_ref, gain_ref, bias_ref, rep_ref,
    out_ref, resid_ref, gr_ref, do_ref,
    acc_ref, norm_ref, hid_ref, slope_ref, lacc_ref, llow_ref, send_ref, sems, own_sem,
):
    rows, features = tok_ref.shape
    rank = sh_ref.shape[0]
    s = pl.program_id(0)
    b_out, a_up, b_down = rep_ref[0], rep_ref[1], rep_ref[2]
    co = wo_ref.shape[-1]
    up0, down0 = groups, groups + nf
    upb0, end0 = groups + 2 * nf, groups + 3 * nf
    b, sib = pair_core()
    pl.when(s == 0)(lambda: greet_core(sib))

    for g in range(groups):

        @pl.when(s == g)
        def _():
            part = mix_ref[g]
            y = nt(part, wo_ref[...].reshape(features, co))
            low = nt(part, sho_ref[...])
            if g == 0:
                resid_ref[...] = tok_ref[...].astype(F32) + y
                lacc_ref[...] = low
            else:
                resid_ref[...] += y
                lacc_ref[...] += low

    @pl.when(s == up0 - 1)
    def _():
        def body(at):
            low = lacc_ref[at, :].astype(BF)
            llow_ref[0, at, :] = low
            resid = resid_ref[at, :] + nn(low, b_out)
            resid_ref[at, :] = resid
            center, r = stats(resid)
            normed = (center * r * gain_ref[...] + bias_ref[...]).astype(BF)
            norm_ref[at, :] = normed
            llow_ref[1, at, :] = nt(normed, a_up).astype(BF)

        row_loop(rows, 256, body)
        llow_ref[3] = nt(cot_ref[...], b_down).astype(BF)
        acc_ref[...] = jnp.zeros_like(acc_ref)
        lacc_ref[...] = jnp.zeros_like(lacc_ref)

    @pl.when((s >= up0) & (s < down0))
    def _():
        f = s - up0
        w = w_ref[...].reshape(features, -1)

        def body(at):
            pre = nn(norm_ref[at, :], w) + nn(llow_ref[1, at, :], sh_ref[...])
            hidden, slope = gelu_and_slope(pre)
            hid_ref[f, at, :] = hidden.astype(BF)
            slope_ref[f, at, :] = slope.astype(BF)

        row_loop(rows, 512, body)

    @pl.when((s >= down0) & (s < upb0))
    def _():
        f = s - down0
        w = w_ref[...].reshape(features, -1)
        sh = sh_ref[...]
        hidden = hid_ref[f]
        acc_ref[...] += nt(hidden, w)
        lacc_ref[...] += nt(hidden, sh)
        g_hidden = nn(cot_ref[...], w) + nn(llow_ref[3], sh)
        g_pre = (g_hidden * slope_ref[f].astype(F32)).astype(BF)
        slope_ref[f] = g_pre
        gr_ref[:rank, :] = tn(llow_ref[3], hidden).astype(BF)
        gr_ref[rank:, :] = tn(llow_ref[1], g_pre).astype(BF)

    @pl.when(s == upb0 - 1)
    def _():
        def body(at):
            low = lacc_ref[at, :].astype(BF)
            llow_ref[2, at, :] = low
            out_ref[at, :] = (resid_ref[at, :] + acc_ref[at, :] + nn(low, b_down)).astype(BF)

        row_loop(rows, 512, body)
        acc_ref[...] = jnp.zeros_like(acc_ref)
        lacc_ref[...] = jnp.zeros_like(lacc_ref)

    @pl.when((s >= upb0) & (s < end0))
    def _():
        f = s - upb0
        w = w_ref[...].reshape(features, -1)
        part = slope_ref[f]
        acc_ref[...] += nt(part, w)
        lacc_ref[...] += nt(part, sh_ref[...])

    @pl.when(s == end0 - 1)
    def _():
        gr_ref[:rank, :] = tn(llow_ref[2], cot_ref[...]).astype(BF)
        llow_ref[4] = lacc_ref[...].astype(BF)
        gr_ref[rank:, :] = tn(llow_ref[4], norm_ref[...]).astype(BF)

        def body(at):
            total = acc_ref[at, :] + nn(llow_ref[4, at, :], a_up)
            g = cot_ref[at, :].astype(F32) + norm_back(resid_ref[at, :], gain_ref[...], total)
            resid_ref[at, :] = g
            branch = g.astype(BF)
            norm_ref[at, :] = branch
            llow_ref[5, at, :] = nt(branch, b_out).astype(BF)

        row_loop(rows, 256, body)

    def far():
        return to_core(send_ref.at[0], do_ref.at[b], sems, 0, sib)

    def own():
        return pltpu.make_async_copy(send_ref.at[1], do_ref.at[b], own_sem)

    @pl.when(s >= end0)
    def _():
        turn = s - end0
        g = jnp.where(turn == 0, 1 - b, b)
        wo = wo_ref[...].reshape(features, co)
        y = nn(norm_ref[...], wo) + nn(llow_ref[5], sho_ref[...])
        send_ref[turn] = y.astype(BF)
        at = pl.ds(pl.multiple_of(g * co, co), co)
        gr_ref[:rank, at] = tn(llow_ref[5], mix_ref[g]).astype(BF)

    @pl.when(s == end0)
    def _():
        far().start()
        gr_ref[rank:, :] = tn(llow_ref[0], norm_ref[...]).astype(BF)

    @pl.when(s == end0 + 1)
    def _():
        own().start()
        own().wait()
        far().wait()


def middle(w, shared, tok, mix, cot, gain, bias, rep, ident):
    rows, features = tok.shape
    shards, groups, part, total = w.shape
    rank = rep.shape[1]
    co = mix.shape[2]
    ffw = (total - co) // 2
    c = features
    halves = ffw // c
    nf = groups * halves
    first = (shared.shape[2] - 2 * ffw) // c
    out_at, out_shared = 2 * ffw // co, (shared.shape[2] - 2 * ffw) // co - 1
    blocks = [(f // halves, f % halves) for f in range(nf)]
    up = [(t, h, h) for t, h in blocks]
    down_step = [(t, halves + h, halves + h) for t, h in blocks]
    shared_group = [t for t, _ in blocks]
    order = [up[0]] * groups + up + down_step + up + [up[-1]] * groups
    shared_of = [0] * groups + shared_group * 3 + [shared_group[-1]] * groups
    of_grad = [0] * (groups + nf) + list(range(nf)) + [nf + 1] * nf + [nf] * groups
    last = len(order) - groups
    anywhere = pl.BlockSpec(memory_space=pl.ANY)

    def group(s):
        b = lax.axis_index("dp") % 2
        return jnp.where(s < last, jnp.minimum(s, groups - 1), jnp.where(s == last, 1 - b, b))

    once = pl.Buffered(1)

    def keep(shape):
        return pl.BlockSpec(shape, lambda s, *_: (0,) * len(shape), pipeline_mode=once)

    def at(table_row):
        def index(s):
            got = table_row[0]
            for n in range(1, len(table_row)):
                if table_row[n] != table_row[n - 1]:
                    got = got + jnp.where(s >= n, table_row[n] - table_row[n - 1], 0)
            return got
        return index

    w_t, w_c = at([x[0] for x in order]), at([x[1] for x in order])
    s_t, s_c, gi = at(shared_of), at([x[2] for x in order]), at(of_grad)
    return pl.pallas_call(
        functools.partial(middle_kernel, groups, nf),
        out_shape=(
            jax.ShapeDtypeStruct((rows, features), BF),
            jax.ShapeDtypeStruct((rows, features), F32),
            jax.ShapeDtypeStruct((nf + 2, 2 * rank, c), BF),
            jax.ShapeDtypeStruct(mix.shape, BF),
        ),
        grid=(len(order),),
        in_specs=[
            pl.BlockSpec((shards, None, part, c), lambda s: (0, w_t(s), 0, w_c(s))),
            pl.BlockSpec((None, rank, c), lambda s: (s_t(s), 0, s_c(s) + first)),
            pl.BlockSpec((shards, None, part, co), lambda s: (0, group(s), 0, out_at)),
            pl.BlockSpec((None, rank, co), lambda s: (group(s), 0, out_shared)),
            keep((rows, features)), keep(mix.shape), keep((rows, features)),
            keep((1, features)), keep((1, features)), keep(rep.shape),
        ],
        out_specs=[
            keep((rows, features)), keep((rows, features)),
            pl.BlockSpec((None, 2 * rank, c), lambda s: (gi(s), 0, 0)), anywhere,
        ],
        scratch_shapes=[
            pltpu.VMEM((rows, features), F32),
            pltpu.VMEM((rows, features), BF),
            pltpu.VMEM((nf, rows, c), BF),
            pltpu.VMEM((nf, rows, c), BF),
            pltpu.VMEM((rows, rank), F32),
            pltpu.VMEM((6, rows, rank), BF),
            pltpu.VMEM(mix.shape, BF),
            pltpu.SemaphoreType.DMA((2, 1)),
            pltpu.SemaphoreType.DMA,
        ],
        compiler_params=pltpu.CompilerParams(
            dimension_semantics=("arbitrary",), vmem_limit_bytes=62 * MIB,
            collective_id=ident, has_side_effects=True,
        ),
        cost_estimate=cost(6 * rows * features * groups * total, 4 * features * groups * total),
        name="middle",
    )(w, shared, w, shared, tok, mix, cot, gain, bias, rep)


class Gather:
    def __init__(self, shard, full, out_sem, in_sem, own_sem, planes, y_first):
        self.shard, self.full, self.planes = shard, full, planes
        self.chunks = out_sem.shape[0]
        self.out_sem, self.in_sem, self.own_sem = out_sem, in_sem, own_sem
        self.rounds = planes + 2
        dp, t = lax.axis_index("dp"), lax.axis_index("tensor")
        z, x, c = dp // 4, (dp // 2) % 2, dp % 2
        self.dp, self.z, self.x, self.c, self.t = dp, z, x, c, t
        self.low, self.high = z > 0, z < planes - 1
        fx = 0 if y_first else 1 - c
        self.side1 = (x + fx) % 2, (t + 1 - fx) % 2
        self.side2 = (x + 1 - fx) % 2, (t + fx) % 2
        self.side3 = 1 - x, 1 - t
        self.below = jnp.maximum(dp - 4, 0), t
        self.above = jnp.minimum(dp + 4, 4 * planes - 1), t
        self.one = self.place(z, self.side1[0], c), self.side1[1]
        self.two = self.place(z, self.side2[0], c), self.side2[1]
        self.sib = self.place(z, x, 1 - c), t
        self.near = dp, 1 - t
        self.sides = (x, t), self.side1, self.side2, self.side3
        self.plan = [self.lay_out(k) for k in range(self.rounds)]

    def place(self, z, x, c):
        return z * 4 + x * 2 + c

    def greet(self, extra=()):
        barrier = pltpu.get_barrier_semaphore()

        def hello(who):
            pl.semaphore_signal(barrier, inc=1, device_id=who, device_id_type=MESH)

        for who in (self.one, self.two, self.sib):
            hello(who)
        count = 3
        for cond, who in ((self.low, self.below), (self.high, self.above)) + tuple(extra):
            pl.when(cond)(lambda who=who: hello(who))
            count = count + cond.astype(jnp.int32)
        pl.semaphore_wait(barrier, count)

    def piece(self, ref, n):
        if self.chunks == 1:
            return ref
        size = ref.shape[-2] // self.chunks
        every = (slice(None),) * (len(ref.shape) - 2)
        return ref.at[every + (pl.ds(n * size, size), slice(None))]

    def copy(self, n, at, who, sem, own=False):
        slot = self.piece(self.full.at[at[0], at[1]], n)
        return pltpu.make_async_remote_copy(
            src_ref=self.piece(self.shard, n) if own else slot, dst_ref=slot,
            send_sem=self.out_sem.at[n, sem],
            recv_sem=self.in_sem.at[n, at[0] * 2 + at[1]], device_id=who, device_id_type=MESH,
        )

    def arrive(self, n, at):
        self.copy(n, at, self.sib, 0).wait_recv()

    def own_copy(self, n):
        here = self.piece(self.full.at[self.dp, self.t], n)
        return pltpu.make_async_copy(self.piece(self.shard, n), here, self.own_sem.at[n])

    def sem(self, kind, zz):
        return kind * self.planes + zz

    def lay_out(self, k):
        z, planes = self.z, self.planes
        events = []

        def at(zz, side):
            return self.place(zz, side[0], self.c), side[1]

        def ways(hops):
            if hops == 0:
                return [(z, None, None)]
            return [
                (z - hops, z >= hops, (self.above, self.high, 1)),
                (z + hops, z + hops < planes, (self.below, self.low, 0)),
            ]

        def both(first, second):
            return second if first is None else first if second is None else first & second

        own_side = self.x, self.t
        for n in range(self.chunks):
            if k < planes:
                for zz, cond, forward in ways(k):
                    sends = [(cond, self.one, 2), (cond, self.two, 3), (cond, self.sib, 5)]
                    if k == 0:
                        sends = [(self.low, self.below, 0), (self.high, self.above, 1)] + sends
                    else:
                        sends = [(both(cond, forward[1]), forward[0], forward[2])] + sends
                    events.append((n, cond, at(zz, own_side), k == 0, zz, sends))
            if 1 <= k <= planes:
                for zz, cond, _ in ways(k - 1):
                    sends = [(cond, self.two, 4), (cond, self.sib, 6)]
                    events.append((n, cond, at(zz, self.side1), False, zz, sends))
                    events.append((n, cond, at(zz, self.side2), False, zz, [(cond, self.sib, 7)]))
            if k >= 2:
                for zz, cond, _ in ways(k - 2):
                    events.append((n, cond, at(zz, self.side3), False, zz, [(cond, self.sib, 8)]))
        return [
            (n, cond, where, own, [(c, who, self.sem(kind, zz)) for c, who, kind in sends])
            for n, cond, where, own, zz, sends in events
        ]

    def when(self, cond, act):
        if cond is None:
            act()
        else:
            pl.when(cond)(act)

    def slot(self, i):
        self.round(i // 2, i % 2)

    def round(self, k, chunk=None):
        for n, cond, where, own, sends in self.plan[k]:
            if chunk is not None and n != chunk:
                continue
            if not own:
                self.when(cond, lambda n=n, where=where: self.arrive(n, where))
            for c, who, sem in sends:
                self.when(
                    c,
                    lambda n=n, where=where, who=who, sem=sem, own=own: self.copy(
                        n, where, who, sem, own
                    ).start(),
                )
            if own:
                self.own_copy(n).start()

    def finish(self):
        for n in range(self.chunks):
            for zz in range(self.planes):
                for x, t in self.sides:
                    self.arrive(n, (self.place(zz, x, 1 - self.c), t))
            self.own_copy(n).wait()
        for events in self.plan:
            for n, _, where, own, sends in events:
                for c, who, sem in sends:
                    self.when(
                        c,
                        lambda n=n, where=where, who=who, sem=sem, own=own: self.copy(
                            n, where, who, sem, own
                        ).wait_send(),
                    )


def gather_sems(n, planes):
    return [
        pltpu.SemaphoreType.DMA((n, 9 * planes)),
        pltpu.SemaphoreType.DMA((n, 8 * planes)),
        pltpu.SemaphoreType.DMA((n,)),
    ]


def spread_kernel(n_all, kinds, planes, *refs):
    n_swap = len(kinds)
    shard = refs[:n_all]
    swap_in = refs[n_all : n_all + n_swap]
    full = refs[n_all + n_swap : 2 * n_all + n_swap]
    swap_out = refs[2 * n_all + n_swap : 2 * n_all + 2 * n_swap]
    *sems, swap_sem = refs[2 * n_all + 2 * n_swap :]
    g = Gather(shard[0], full[0], *sems, planes, True)
    moves = g.c != g.t
    keeps = jnp.logical_not(moves)
    partner = (g.place(g.z, g.x, g.t), g.c)
    g.greet([(moves, partner)])
    rules = {"partner": (moves, partner, moves), "near": (moves, g.near, keeps), "sibling": (keeps, g.sib, moves)}

    def swap_copy(n):
        return pltpu.make_async_remote_copy(
            src_ref=swap_in[n], dst_ref=swap_out[n], send_sem=swap_sem.at[n, 0],
            recv_sem=swap_sem.at[n, 1], device_id=rules[kinds[n]][1], device_id_type=MESH,
        )

    for n in range(n_swap):
        pl.when(rules[kinds[n]][0])(lambda n=n: swap_copy(n).start())
    for k in range(g.rounds):
        g.round(k)
    g.finish()
    for n in range(n_swap):
        pl.when(rules[kinds[n]][0])(lambda n=n: swap_copy(n).wait_send())
        pl.when(rules[kinds[n]][2])(lambda n=n: swap_copy(n).wait_recv())


def spread(gathered, handed, shards, ident):
    planes = shards // 4
    swapped = [a for a, _ in handed]
    n_all, n_swap = len(gathered), len(swapped)
    anywhere = pl.BlockSpec(memory_space=pl.ANY)
    return pl.pallas_call(
        functools.partial(spread_kernel, n_all, [k for _, k in handed], planes),
        out_shape=[jax.ShapeDtypeStruct((shards, 2) + a.shape, a.dtype) for a in gathered]
        + [jax.ShapeDtypeStruct(a.shape, a.dtype) for a in swapped],
        in_specs=[anywhere] * (n_all + n_swap),
        out_specs=[anywhere] * (n_all + n_swap),
        scratch_shapes=[
            *gather_sems(n_all, planes),
            pltpu.SemaphoreType.DMA((max(n_swap, 1), 2)),
        ],
        compiler_params=pltpu.CompilerParams(collective_id=ident, has_side_effects=True),
        cost_estimate=cost(0, 60 * MIB),
        name="spread%d" % ident,
    )(*gathered, *swapped)


def sum_kernel(pieces, sel_ref, t_ref, *refs):
    ins, outs = refs[: len(refs) - len(pieces)], refs[len(refs) - len(pieces) :]
    step = pl.program_id(0)
    devices = ins[0].shape[0]

    @pl.when(step == 0)
    def _():
        for out in outs:
            out[...] = jnp.zeros_like(out)

    @pl.loop(0, devices)
    def _(d):
        for (at, which, blocks), out in zip(pieces, outs):
            slot = sel_ref[step * devices + d, which]
            rank = out.shape[-2]
            c = ins[at].shape[-1]
            for k, (block, row) in enumerate(blocks):
                new = ins[at][d, block, row : row + rank, :].astype(F32)
                if len(out.shape) == 4:
                    out[slot, k] += new
                else:
                    out[slot, :, k * c : (k + 1) * c] += new


def sum_picks(sel, t, arrays, pieces, slots, rank, name):
    steps = 4
    in_specs = []
    for a, shape, where in arrays:
        in_specs.append(
            pl.BlockSpec(
                (a.shape[0] // steps,) + shape, lambda s, sel, t, where=where: (s,) + where(t[0])
            )
        )
    shapes = []
    for at, _, blocks, flat in pieces:
        n, c = len(blocks), arrays[at][1][-1]
        shapes.append((slots, rank, n * c) if flat else (slots, n, rank, c))
    return pl.pallas_call(
        functools.partial(sum_kernel, [p[:3] for p in pieces]),
        out_shape=[jax.ShapeDtypeStruct(shape, F32) for shape in shapes],
        grid_spec=pltpu.PrefetchScalarGridSpec(
            num_scalar_prefetch=2, grid=(steps,), in_specs=in_specs,
            out_specs=[whole(shape) for shape in shapes],
        ),
        compiler_params=pltpu.CompilerParams(
            dimension_semantics=("arbitrary",), vmem_limit_bytes=48 * MIB
        ),
        cost_estimate=cost(0, 30 * MIB),
        name=name,
    )(sel, t, *[a for a, _, _ in arrays])


def pick_kernel(idx_ref, bq_ref, ao_ref, bu_ref, ad_ref, aq_ref, bo_ref, au_ref, bd_ref, marks_ref, half_ref, rest_ref, m_ref):
    at = 0
    for j in range(bq_ref.shape[0]):
        half_ref[:, at : at + bq_ref.shape[2]] = bq_ref[j]
        at += bq_ref.shape[2]
    for ref in (ao_ref, bu_ref, ad_ref):
        half_ref[:, at : at + ref.shape[1]] = ref[...]
        at += ref.shape[1]
    for n, ref in enumerate((aq_ref, bo_ref, au_ref, bd_ref)):
        rest_ref[n] = ref[...]
    m_ref[...] = jnp.broadcast_to(marks_ref[...], m_ref.shape)


def pick_adapters(idx, split, full, marks):
    rank = full[0].shape[1]
    width = split[0].shape[1] * split[0].shape[3] + sum(a.shape[2] for a in split[1:])

    def one(a, which):
        rest = a.shape[1:]
        return pl.BlockSpec((None,) + rest, lambda i, idx: (idx[which],) + (0,) * len(rest))

    in_specs = [one(a, n) for n, a in enumerate(split)] + [one(a, n) for n, a in enumerate(full)]
    return pl.pallas_call(
        pick_kernel,
        out_shape=(
            jax.ShapeDtypeStruct((rank, width), BF),
            jax.ShapeDtypeStruct((len(full),) + full[0].shape[1:], BF),
            jax.ShapeDtypeStruct((8, 128), jnp.int32),
        ),
        grid_spec=pltpu.PrefetchScalarGridSpec(
            num_scalar_prefetch=1, grid=(1,), in_specs=in_specs + [whole(marks.shape)],
            out_specs=[whole((rank, width)), whole((len(full),) + full[0].shape[1:]), whole((8, 128))],
        ),
        compiler_params=pltpu.CompilerParams(dimension_semantics=("arbitrary",)),
        cost_estimate=cost(0, MIB),
        name="pick_adapters",
    )(idx, *split, *full, marks)


def chip_device(
    tokens, w_qkv, w_out, w_up, w_down, ln1_gain, ln1_bias, ln2_gain, ln2_bias,
    a_qkv, b_qkv, a_out, b_out, a_up, b_up, a_down, b_down, adapter_idx, pic_start, cotangent,
):
    shards = lax.axis_size("dp")
    dp, t = lax.axis_index("dp"), lax.axis_index("tensor")
    keeps = dp % 2 == t
    both = ("dp", "tensor")
    swap = []
    for c in range(shards // 2):
        one, two = 2 * (2 * c + 1), 2 * (2 * c) + 1
        swap += [(one, two), (two, one)]

    def swapped(x):
        return lax.ppermute(x, both, swap)

    def row(v):
        return v.reshape(1, -1)

    rank, slots = a_qkv.shape[2], a_qkv.shape[0]
    features, width = tokens.shape[1], w_out.shape[0]
    chosen = adapter_idx[0]

    turned = lambda v: v.transpose(0, 2, 1)
    marks = jnp.concatenate([chosen, pic_start[0]])
    half, rest, marks = pick_adapters(
        chosen,
        [b_qkv.transpose(0, 2, 1, 3), turned(a_out), b_up, turned(a_down)],
        [turned(a_qkv), b_out, turned(a_up), b_down],
        jnp.pad(marks, (0, 128 - marks.shape[0]))[None],
    )

    qkv_shard = w_qkv.transpose(1, 0, 2)
    rest_shard = jnp.concatenate([w_up, w_down.T, w_out.T], axis=1)
    rest_full = lax.all_gather(rest_shard, both, axis=0)
    rest_full = rest_full.reshape(shards, 2, *rest_shard.shape)
    qkv_full, far_tokens, near_half, partner_half, core_half, core_rest, core_marks = spread(
        [qkv_shard],
        [
            (tokens, "partner"), (half, "near"), (half, "partner"),
            (half, "sibling"), (rest, "sibling"), (marks, "sibling"),
        ],
        shards,
        0,
    )
    later, far_tokens = lax.optimization_barrier((cotangent, far_tokens))
    cot = jnp.where(keeps, cotangent, swapped(later))
    tok = jnp.where(keeps, tokens, far_tokens)
    own_half = jnp.where(keeps, half, core_half)
    far_half = jnp.where(keeps, near_half, partner_half)
    shared = jnp.where(t == 0, jnp.stack([own_half, far_half]), jnp.stack([far_half, own_half]))
    rep = jnp.where(keeps, rest, core_rest)
    marks = jnp.where(keeps, marks, core_marks)[0]
    starts = marks[4 : 4 + pic_start.shape[1]]
    tag = jnp.pad(marks[:4].astype(BF)[None], ((0, rank - 1), (0, width - 4)))

    normed, low, qkv = project_qkv(tok, row(ln1_gain), row(ln1_bias), rep[0], qkv_full, shared, 2)
    mixed, lse, mix = attend_rows(starts, qkv, 3)
    layer_out, g_resid, g_early, g_mix = middle(
        rest_full, shared, tok, mix, cot, row(ln2_gain), row(ln2_bias), rep[1:], 4
    )
    early = lax.all_gather(g_early, both, axis=0)
    out = jnp.where(keeps, layer_out, swapped(layer_out))
    g_qkv = attend_rows_back(starts, qkv, mixed, g_mix, lse, 5)
    grad_tok, grad_send, g_late = project_qkv_back(
        g_qkv, qkv_full, shared, rep[0], normed, low, tok, row(ln1_gain), g_resid, tag
    )
    late, far_grad = spread([g_late], [(grad_send, "partner")], shards, 1)
    grad_input = jnp.where(keeps, grad_tok, far_grad.astype(F32))

    late = late.reshape(2 * shards, *g_late.shape)
    sel = late[:, -1, 0, :4].astype(jnp.int32)
    side = t.reshape(1).astype(jnp.int32)
    nf, c = g_early.shape[0] - 2, g_early.shape[2]
    near = range(nf // 2)
    rows2 = 2 * rank
    early = early.reshape(2 * shards, *g_early.shape)
    grad_a_out, grad_b_out, grad_a_up, grad_b_up, grad_a_down, grad_b_down = sum_picks(
        sel, side,
        [
            (early, (nf // 2, rows2, c), lambda u: (u, 0, 0)),
            (early, (1, rows2, width), lambda u: (nf, 0, u)),
            (early, (2, rows2, c), lambda u: (nf // 2, 0, 0)),
        ],
        [
            (1, 1, [(0, 0)], True),
            (2, 1, [(0, rank)], True),
            (2, 2, [(1, rank)], True),
            (0, 2, [(i, rank) for i in near], True),
            (0, 3, [(i, 0) for i in near], True),
            (2, 3, [(1, 0)], True),
        ],
        slots, rank, "sum_early",
    )
    grad_b_qkv, grad_a_qkv = sum_picks(
        sel, side,
        [
            (late, (3, rank, width), lambda u: (u, 0, 0)),
            (late, (2, rank, width), lambda u: (3, 0, 0)),
        ],
        [(0, 0, [(0, 0), (1, 0), (2, 0)], False), (1, 0, [(0, 0), (1, 0)], True)],
        slots, rank, "sum_late",
    )
    return (
        out, grad_input, turned(grad_a_qkv), grad_b_qkv.transpose(0, 2, 1, 3),
        turned(grad_a_out), grad_b_out, turned(grad_a_up), grad_b_up, turned(grad_a_down), grad_b_down,
    )


def solution(mesh):
    placed = (
        P(("dp", "tensor"), None),
        P("dp", None, "tensor"),
        P("tensor", "dp"),
        P("dp", "tensor"),
        P("tensor", "dp"),
        P(),
        P(),
        P(),
        P(),
        P(),
        P(None, None, None, "tensor"),
        P(None, "tensor", None),
        P(),
        P(),
        P(None, None, "tensor"),
        P(None, "tensor", None),
        P(),
        P("dp", None),
        P("dp", None),
        P(("dp", "tensor"), None),
    )
    paired = mesh.shape["tensor"] == 2 and mesh.shape["dp"] % 2 == 0
    return jax.shard_map(
        chip_device if paired else per_device,
        mesh=mesh,
        in_specs=placed,
        out_specs=(
            P(("dp", "tensor"), None),
            P(("dp", "tensor"), None),
            P(),
            P(None, None, None, "tensor"),
            P(None, "tensor", None),
            P(),
            P(),
            P(None, None, "tensor"),
            P(None, "tensor", None),
            P(),
        ),
        check_vma=False,
    )
```

```python
import functools
import math

import jax
import jax.numpy as jnp
from jax import lax
from jax.experimental import pallas as pl
from jax.experimental.pallas import tpu as pltpu
from jax.sharding import PartitionSpec as P

HD = 64
SPAN = 256
BLOCK = 512


def matmul(left, right):
    return jnp.dot(left, right, preferred_element_type=jnp.float32)


def contract_rows(left, right):
    return lax.dot_general(
        left, right, (((0,), (0,)), ((), ())), preferred_element_type=jnp.float32
    )


def against(left, right):
    return lax.dot_general(
        left, right, (((1,), (1,)), ((), ())), preferred_element_type=jnp.float32
    )


def layer_norm(values, multiplier, addend):
    center = values - jnp.mean(values, axis=-1, keepdims=True)
    spread = jnp.mean(center * center, axis=-1, keepdims=True)
    return center * lax.rsqrt(spread + 1e-05) * multiplier + addend


def span_labels(positions, starts):
    inside = (positions[:, None] >= starts[None, :]) & (positions[:, None] < starts[None, :] + SPAN)
    labels = jnp.arange(1, starts.shape[0] + 1, dtype=jnp.int32)
    return jnp.sum(jnp.where(inside, labels[None, :], 0), axis=1)


def allowed_mask(offset, row_count, length, starts):
    row_pos = offset + jnp.arange(row_count, dtype=jnp.int32)
    col_pos = jnp.arange(length, dtype=jnp.int32)
    row_span = span_labels(row_pos, starts)
    col_span = span_labels(col_pos, starts)
    causal = col_pos[None, :] <= row_pos[:, None]
    joined = (row_span[:, None] == col_span[None, :]) & (row_span[:, None] > 0)
    return causal | joined


def masked_scores(query_block, key_rows, offset, length, starts, factor):
    scores = (
        jnp.einsum("qhd,khd->hqk", query_block, key_rows, preferred_element_type=jnp.float32)
        * factor
    )
    allowed = allowed_mask(offset, BLOCK, length, starts)
    return jnp.where(allowed[None], scores, -1000000000.0)


def attend(queries, key_rows, value_rows, starts):
    length, heads, width = queries.shape
    factor = width ** (-0.5)

    def one_block(block_number):
        offset = block_number * BLOCK
        query_block = lax.dynamic_slice_in_dim(queries, offset, BLOCK, 0)
        scores = masked_scores(query_block, key_rows, offset, length, starts, factor)
        peak = jnp.max(scores, axis=-1, keepdims=True)
        raised = jnp.exp(scores - peak)
        totals = jnp.sum(raised, axis=-1, keepdims=True)
        weights_low = (raised / totals).astype(jnp.bfloat16)
        blended = jnp.einsum(
            "hqk,khd->qhd", weights_low, value_rows, preferred_element_type=jnp.float32
        )
        return (
            blended.astype(jnp.bfloat16).reshape(BLOCK, heads * width),
            (peak + jnp.log(totals))[..., 0],
        )

    blended, log_sums = lax.map(one_block, jnp.arange(length // BLOCK, dtype=jnp.int32))
    return (blended.reshape(length, heads * width), log_sums)


def attend_back(queries, key_rows, value_rows, grad_mix, log_sums, starts):
    length, heads, width = queries.shape
    factor = width ** (-0.5)

    def one_block(carry, inputs_pair):
        key_grad, value_grad = carry
        block_number, block_sums = inputs_pair
        offset = block_number * BLOCK
        query_block = lax.dynamic_slice_in_dim(queries, offset, BLOCK, 0)
        grad_block = lax.dynamic_slice_in_dim(grad_mix, offset, BLOCK, 0)
        scores = masked_scores(query_block, key_rows, offset, length, starts, factor)
        weights = jnp.exp(scores - block_sums[:, :, None])
        dots = jnp.einsum(
            "qhd,khd->hqk", grad_block, value_rows, preferred_element_type=jnp.float32
        )
        inner = jnp.sum(weights * dots, axis=-1, keepdims=True)
        slopes = (weights * (dots - inner) * factor).astype(jnp.bfloat16)
        query_grad = jnp.einsum(
            "hqk,khd->qhd", slopes, key_rows, preferred_element_type=jnp.float32
        )
        key_grad = key_grad + jnp.einsum(
            "hqk,qhd->khd", slopes, query_block, preferred_element_type=jnp.float32
        )
        value_grad = value_grad + jnp.einsum(
            "hqk,qhd->khd",
            weights.astype(jnp.bfloat16),
            grad_block,
            preferred_element_type=jnp.float32,
        )
        return ((key_grad, value_grad), query_grad)

    initial = jnp.zeros(key_rows.shape, jnp.float32)
    numbers = jnp.arange(length // BLOCK, dtype=jnp.int32)
    (key_grad, value_grad), query_grad = lax.scan(
        one_block, (initial, initial), (numbers, log_sums)
    )
    return (query_grad.reshape(length, heads, width), key_grad, value_grad)


def fetch_frozen(first, second):
    return (
        lax.all_gather(first, "dp", axis=0, tiled=True),
        lax.all_gather(second, "dp", axis=1, tiled=True),
    )


def enter_rows(normed, reduced):
    return (
        lax.all_gather(normed, "tensor", axis=0, tiled=True),
        lax.all_gather(reduced, "tensor", axis=0, tiled=True),
    )


def leave_rows(partial_value, reduced):
    return (
        lax.psum_scatter(partial_value, "tensor", scatter_dimension=0, tiled=True),
        lax.psum_scatter(reduced, "tensor", scatter_dimension=0, tiled=True),
    )


def enter_grads(branch, reduced):
    return (
        lax.all_gather(branch, "tensor", axis=0, tiled=True),
        lax.all_gather(reduced, "tensor", axis=0, tiled=True),
    )


def leave_grads(partial_value, reduced):
    return (
        lax.psum_scatter(partial_value, "tensor", scatter_dimension=0, tiled=True),
        lax.psum_scatter(reduced, "tensor", scatter_dimension=0, tiled=True),
    )


def per_device(
    tokens,
    w_qkv,
    w_out,
    w_up,
    w_down,
    ln1_gain,
    ln1_bias,
    ln2_gain,
    ln2_bias,
    a_qkv,
    b_qkv,
    a_out,
    b_out,
    a_up,
    b_up,
    a_down,
    b_down,
    adapter_idx,
    pic_start,
    cotangent,
):
    selection = adapter_idx[0]
    starts = pic_start[0]

    def chosen(stacked, which_one):
        return lax.dynamic_index_in_dim(stacked, selection[which_one], 0, keepdims=False)

    low_qkv_in = chosen(a_qkv, 0)
    rank = low_qkv_in.shape[1]
    low_qkv_out = chosen(b_qkv, 0).reshape(rank, -1)
    low_out_in = chosen(a_out, 1)
    low_out_out = chosen(b_out, 1)
    low_up_in = chosen(a_up, 2)
    low_up_out = chosen(b_up, 2)
    low_down_in = chosen(a_down, 3)
    low_down_out = chosen(b_down, 3)
    heads_here = low_out_in.shape[0] // HD

    def run_forward(own_tokens, frozen):
        qkv_rows, out_rows, up_rows, down_rows = frozen
        qkv_full, out_full = fetch_frozen(qkv_rows, out_rows)
        qkv_flat = qkv_full.reshape(qkv_full.shape[0], -1)
        own_float = own_tokens.astype(jnp.float32)
        normed = layer_norm(own_float, ln1_gain, ln1_bias).astype(jnp.bfloat16)
        reduced = matmul(normed, low_qkv_in).astype(jnp.bfloat16)
        normed_all, reduced_all = enter_rows(normed, reduced)
        length = normed_all.shape[0]
        project = (matmul(normed_all, qkv_flat) + matmul(reduced_all, low_qkv_out)).astype(
            jnp.bfloat16
        )
        split = project.reshape(length, 3, heads_here, HD)
        blended, log_sums = attend(split[:, 0], split[:, 1], split[:, 2], starts)
        main_part, low_part = leave_rows(matmul(blended, out_full), matmul(blended, low_out_in))
        low_out_val = low_part.astype(jnp.bfloat16)
        residual = own_float + main_part + matmul(low_out_val, low_out_out)
        up_full, down_full = fetch_frozen(up_rows, down_rows)
        normed_two = layer_norm(residual, ln2_gain, ln2_bias).astype(jnp.bfloat16)
        reduced_two = matmul(normed_two, low_up_in).astype(jnp.bfloat16)
        normed_two_all, reduced_two_all = enter_rows(normed_two, reduced_two)
        pre_act = matmul(normed_two_all, up_full) + matmul(reduced_two_all, low_up_out)
        hidden = jax.nn.gelu(pre_act, approximate=True).astype(jnp.bfloat16)
        main_two, low_two = leave_rows(matmul(hidden, down_full), matmul(hidden, low_down_in))
        low_down_val = low_two.astype(jnp.bfloat16)
        output = residual + main_two + matmul(low_down_val, low_down_out)
        kept_state = (
            qkv_flat,
            out_full,
            up_full,
            down_full,
            normed,
            reduced_all,
            split,
            blended,
            log_sums,
            low_out_val,
            residual,
            normed_two,
            reduced_two_all,
            pre_act,
            hidden,
            low_down_val,
        )
        return (output, kept_state)

    frozen = (w_qkv, w_out, w_up, w_down)
    output, kept_state = run_forward(tokens, frozen)
    (
        qkv_flat,
        out_full,
        up_full,
        down_full,
        normed,
        reduced_all,
        split,
        blended,
        log_sums,
        low_out_val,
        residual,
        normed_two,
        reduced_two_all,
        pre_act,
        hidden,
        low_down_val,
    ) = kept_state
    cot_float = cotangent.astype(jnp.float32)
    grad_low_down = against(cotangent, low_down_out).astype(jnp.bfloat16)
    grad_b_down_here = contract_rows(low_down_val, cotangent)
    cot_all, grad_low_down_all = enter_grads(cotangent, grad_low_down)
    grad_hidden = against(cot_all, down_full) + against(grad_low_down_all, low_down_in)
    grad_a_down_here = contract_rows(hidden, grad_low_down_all)
    gelu_pull = jax.vjp(lambda inner_val: jax.nn.gelu(inner_val, approximate=True), pre_act)[1]
    grad_pre = gelu_pull(grad_hidden)[0].astype(jnp.bfloat16)
    grad_b_up_here = contract_rows(reduced_two_all, grad_pre)
    grad_normed_two, grad_reduced_two = leave_grads(
        against(grad_pre, up_full), against(grad_pre, low_up_out)
    )
    grad_low_up = grad_reduced_two.astype(jnp.bfloat16)
    grad_a_up_here = contract_rows(normed_two, grad_low_up)
    grad_normed_two = grad_normed_two + against(grad_low_up, low_up_in)
    norm_pull_two = jax.vjp(lambda inner_val: layer_norm(inner_val, ln2_gain, ln2_bias), residual)[
        1
    ]
    grad_resid = cot_float + norm_pull_two(grad_normed_two)[0]
    branch_low = grad_resid.astype(jnp.bfloat16)
    grad_low_out = against(branch_low, low_out_out).astype(jnp.bfloat16)
    grad_b_out_here = contract_rows(low_out_val, branch_low)
    branch_all, grad_low_out_all = enter_grads(branch_low, grad_low_out)
    grad_mix = (against(branch_all, out_full) + against(grad_low_out_all, low_out_in)).astype(
        jnp.bfloat16
    )
    grad_a_out_here = contract_rows(blended, grad_low_out_all)
    length = grad_mix.shape[0]
    query_grad, key_grad, value_grad = attend_back(
        split[:, 0],
        split[:, 1],
        split[:, 2],
        grad_mix.reshape(length, heads_here, HD),
        log_sums,
        starts,
    )
    grad_qkv = (
        jnp.stack([query_grad, key_grad, value_grad], axis=1)
        .reshape(length, -1)
        .astype(jnp.bfloat16)
    )
    grad_b_qkv_here = contract_rows(reduced_all, grad_qkv)
    grad_normed_one, grad_reduced_one = leave_grads(
        against(grad_qkv, qkv_flat), against(grad_qkv, low_qkv_out)
    )
    grad_low_qkv = grad_reduced_one.astype(jnp.bfloat16)
    grad_a_qkv_here = contract_rows(normed, grad_low_qkv)
    grad_normed_one = grad_normed_one + against(grad_low_qkv, low_qkv_in)
    norm_pull_one = jax.vjp(
        lambda inner_val: layer_norm(inner_val, ln1_gain, ln1_bias), tokens.astype(jnp.float32)
    )[1]
    grad_input = grad_resid + norm_pull_one(grad_normed_one)[0]
    slots = a_qkv.shape[0]

    def spread(gradient, which_one):
        onehot = (jnp.arange(slots, dtype=jnp.int32) == selection[which_one]).astype(jnp.float32)
        return onehot.reshape((slots,) + (1,) * gradient.ndim) * gradient[None]

    sharded = (
        lax.psum(spread(grad_b_qkv_here.reshape(rank, 3, -1), 0).astype(jnp.bfloat16), "dp").astype(
            jnp.float32
        ),
        lax.psum(spread(grad_a_out_here, 1).astype(jnp.bfloat16), "dp").astype(jnp.float32),
        lax.psum(spread(grad_b_up_here, 2).astype(jnp.bfloat16), "dp").astype(jnp.float32),
        lax.psum(spread(grad_a_down_here, 3).astype(jnp.bfloat16), "dp").astype(jnp.float32),
    )
    shared = lax.psum(
        (
            spread(grad_a_qkv_here, 0),
            spread(grad_b_out_here, 1),
            spread(grad_a_up_here, 2),
            spread(grad_b_down_here, 3),
        ),
        ("dp", "tensor"),
    )
    return (
        output.astype(jnp.bfloat16),
        grad_input,
        shared[0],
        sharded[0],
        sharded[1],
        shared[1],
        shared[2],
        sharded[2],
        sharded[3],
        shared[3],
    )


SPREAD_CHUNKS = 1
LOG2E = math.log2(math.e)
MASKED = -1e30
MIB = 1 << 20
BF = jnp.bfloat16
F32 = jnp.float32
MESH = pl.DeviceIdType.MESH


def nt(a, b):
    return lax.dot_general(a, b, (((1,), (1,)), ((), ())), preferred_element_type=F32)


def nn(a, b):
    return lax.dot_general(a, b, (((1,), (0,)), ((), ())), preferred_element_type=F32)


def tn(a, b):
    return lax.dot_general(a, b, (((0,), (0,)), ((), ())), preferred_element_type=F32)


def last_key(starts_ref, pos):
    lim = pos
    for n in range(starts_ref.shape[0]):
        first = starts_ref[n]
        lim = jnp.where((pos >= first) & (pos < first + SPAN), first + SPAN - 1, lim)
    return lim


def head_parts(x):
    lane = lax.broadcasted_iota(jnp.int32, x.shape, 1)
    zero = jnp.zeros_like(x)
    return jnp.where(lane < HD, x, zero), jnp.where(lane >= HD, x, zero)


def cost(flops, moved):
    return pl.CostEstimate(flops=int(flops), bytes_accessed=int(moved), transcendentals=0)


def pair_core():
    dp, t = lax.axis_index("dp"), lax.axis_index("tensor")
    b = dp % 2
    return b, (dp + 1 - 2 * b, t)


def greet_core(sib):
    barrier = pltpu.get_barrier_semaphore()
    pl.semaphore_signal(barrier, inc=1, device_id=sib, device_id_type=MESH)
    pl.semaphore_wait(barrier, 1)


def to_core(src, dst, sems, n, sib):
    return pltpu.make_async_remote_copy(
        src_ref=src, dst_ref=dst, send_sem=sems.at[0, n], recv_sem=sems.at[1, n],
        device_id=sib, device_id_type=MESH,
    )


def attend_kernel(
    starts_ref, q_ref, k_ref, v_ref, o_ref, lse_ref, mix_ref, vt_ref, send_ref, sems, own_sems
):
    p, qi = pl.program_id(0), pl.program_id(1)
    pairs = pl.num_programs(0)
    bq = bk = k_ref.shape[1]
    scale = LOG2E * HD ** -0.5
    b, sib = pair_core()
    pl.when((p == 0) & (qi == 0))(lambda: greet_core(sib))

    @pl.when(qi == 0)
    def _():
        for n in range(k_ref.shape[0]):
            vt_ref[:, n * bk : (n + 1) * bk] = jnp.transpose(v_ref[n])

    qs = head_parts(q_ref[...])
    base = qi * bq
    lim = last_key(starts_ref, base + lax.broadcasted_iota(jnp.int32, (1, bq), 1))

    def step(masked, j, carry):
        off = pl.multiple_of(j * bk, bk)
        keys = k_ref[j]
        out = []
        for h in range(2):
            m, l, acc = carry[h]
            s = nt(keys, qs[h])
            if masked:
                kpos = off + lax.broadcasted_iota(jnp.int32, (bk, bq), 0)
                s = jnp.where(kpos <= lim, s, MASKED)
            mn = jnp.maximum(m, jnp.max(s, axis=0, keepdims=True))
            w = jnp.exp2((s - mn) * scale)
            al = jnp.exp2((m - mn) * scale)
            l = al * l + jnp.sum(w, axis=0, keepdims=True)
            acc = acc * al + nn(vt_ref[h * HD : (h + 1) * HD, pl.ds(off, bk)], w.astype(BF))
            out.append((mn, l, acc))
        return tuple(out)

    init = (jnp.full((1, bq), MASKED, F32), jnp.zeros((1, bq), F32), jnp.zeros((HD, bq), F32))
    carry = lax.fori_loop(0, qi, functools.partial(step, False), (init, init))
    carry = step(True, qi, carry)
    mixed = jnp.transpose(jnp.concatenate([carry[h][2] / carry[h][1] for h in range(2)], axis=0)).astype(BF)
    o_ref[...] = mixed
    for h in range(2):
        lse_ref[0, h : h + 1, :] = carry[h][0] * scale + jnp.log2(carry[h][1])

    def place(n, core):
        return mix_ref.at[core, :, pl.ds(pl.multiple_of(n * 2 * HD, 2 * HD), 2 * HD)]

    def far(n):
        return to_core(send_ref.at[n, 1], place(n, b), sems, n, sib)

    def own(n):
        return pltpu.make_async_copy(send_ref.at[n, 0], place(n, b), own_sems.at[n])

    @pl.when(qi == b)
    def _():
        send_ref[p, 0] = mixed
        own(p).start()

    @pl.when(qi != b)
    def _():
        send_ref[p, 1] = mixed
        far(p).start()

    @pl.when((p == pairs - 1) & (qi == pl.num_programs(1) - 1))
    def _():
        for n in range(send_ref.shape[0]):
            own(n).wait()
            far(n).wait()


def attend_rows(starts, qkv, ident):
    parts, _, rows, width = qkv.shape
    pairs = width // (2 * HD)
    length = parts * rows

    def all_parts(which):
        return pl.BlockSpec((parts, None, rows, 2 * HD), lambda p, i, s: (0, which, 0, p))

    return pl.pallas_call(
        attend_kernel,
        out_shape=(
            jax.ShapeDtypeStruct((parts, rows, width), BF),
            jax.ShapeDtypeStruct((pairs, 2, length), F32),
            jax.ShapeDtypeStruct((parts, rows, width), BF),
        ),
        grid_spec=pltpu.PrefetchScalarGridSpec(
            num_scalar_prefetch=1,
            grid=(pairs, parts),
            in_specs=[
                pl.BlockSpec((None, None, rows, 2 * HD), lambda p, i, s: (i, 0, 0, p)),
                all_parts(1),
                all_parts(2),
            ],
            out_specs=[
                pl.BlockSpec((None, rows, 2 * HD), lambda p, i, s: (i, 0, p)),
                pl.BlockSpec((1, 2, rows), lambda p, i, s: (p, 0, i)),
                pl.BlockSpec(memory_space=pl.ANY),
            ],
            scratch_shapes=[
                pltpu.VMEM((2 * HD, length), BF),
                pltpu.VMEM((pairs, 2, rows, 2 * HD), BF),
                pltpu.SemaphoreType.DMA((2, pairs)),
                pltpu.SemaphoreType.DMA((pairs,)),
            ],
        ),
        compiler_params=pltpu.CompilerParams(
            dimension_semantics=("arbitrary", "arbitrary"), vmem_limit_bytes=48 * MIB,
            collective_id=ident, has_side_effects=True,
        ),
        cost_estimate=cost(24 * length * length * width, 16 * length * width),
        name="attend",
    )(starts, qkv, qkv, qkv)


def attend_back_kernel(
    bq, bk, starts_ref, q_ref, k_ref, v_ref, o_ref, do_ref, lse_ref, all_ref,
    kt_ref, dqt_ref, delta_ref, qm_ref, dom_ref, dk_ref, dv_ref, send_ref, sems, own_sems,
):
    p_now = pl.program_id(0)
    b, sib = pair_core()
    pl.when(p_now == 0)(lambda: greet_core(sib))
    g_ref = send_ref.at[p_now]
    parts, rows, _ = q_ref.shape
    length = parts * rows
    scale = LOG2E * HD ** -0.5
    nq = length // bq
    per = rows // bq
    dqt_ref[...] = jnp.zeros_like(dqt_ref)
    for i in range(nq):
        part, at = i // per, slice((i % per) * bq, (i % per + 1) * bq)
        flat = slice(i * bq, (i + 1) * bq)
        kt_ref[:, flat] = jnp.transpose(k_ref[part, at, :])
        do = do_ref[part, at, :]
        for h, (q_h, do_h) in enumerate(zip(head_parts(q_ref[part, at, :]), head_parts(do))):
            qm_ref[h, flat, :] = q_h
            dom_ref[h, flat, :] = do_h
        prod = jnp.transpose(do.astype(F32) * o_ref[part, at, :].astype(F32))
        for h in range(2):
            delta_ref[h : h + 1, flat] = jnp.sum(prod[h * HD : (h + 1) * HD], axis=0, keepdims=True)

    half = bk // 2

    def tile(masked, keys, vals, koff, nk, qoff, nq_):
        at = pl.ds(qoff, nq_)
        dk = dv = None
        if masked:
            lim = last_key(starts_ref, qoff + lax.broadcasted_iota(jnp.int32, (1, nq_), 1))
            ok = koff + lax.broadcasted_iota(jnp.int32, (nk, nq_), 0) <= lim
        for h in range(2):
            q_h = qm_ref[h, at, :]
            do_h = dom_ref[h, at, :]
            p = jnp.exp2(nt(keys, q_h) * scale - lse_ref[0, h : h + 1, at])
            if masked:
                p = jnp.where(ok, p, 0.0)
            ds = (p * (nt(vals, do_h) - delta_ref[h : h + 1, at])).astype(BF)
            v_part, k_part = nn(p.astype(BF), do_h), nn(ds, q_h)
            dv = v_part if dv is None else dv + v_part
            dk = k_part if dk is None else dk + k_part
            head = slice(h * HD, (h + 1) * HD)
            dqt_ref[head, at] += nn(kt_ref[head, pl.ds(koff, nk)], ds)
        return dk, dv

    @pl.loop(0, length // bk)
    def _(j):
        koff = pl.multiple_of(j * bk, bk)
        part = j // (rows // bk)
        inside = pl.multiple_of((j % (rows // bk)) * bk, bk)
        keys = k_ref[part, pl.ds(inside, bk), :]
        vals = v_ref[part, pl.ds(inside, bk), :]

        def step(i, carry):
            dk, dv = tile(False, keys, vals, koff, bk, pl.multiple_of(i * bq, bq), bq)
            return carry[0] + dk, carry[1] + dv

        zero = jnp.zeros((bk, 2 * HD), F32)
        dk, dv = lax.fori_loop(j + 1, nq, step, (zero, zero))
        own = tile(True, keys, vals, koff, bk, koff, bk)
        dk_ref[...] = dk + own[0]
        dv_ref[...] = dv + own[1]

        @pl.when(j % (rows // bk) > 0)
        def _():
            before = pl.multiple_of(jnp.maximum(koff - half, 0), half)
            got = tile(True, keys[:half], vals[:half], koff, half, before, half)
            dk_ref[:half, :] += got[0]
            dv_ref[:half, :] += got[1]

        g_ref[part, 1, pl.ds(inside, bk), :] = (dk_ref[...] * HD ** -0.5).astype(BF)
        g_ref[part, 2, pl.ds(inside, bk), :] = dv_ref[...].astype(BF)

    for i in range(nq):
        part, at = i // per, slice((i % per) * bq, (i % per + 1) * bq)
        dq = jnp.transpose(dqt_ref[:, i * bq : (i + 1) * bq])
        g_ref[part, 0, at, :] = (dq * HD ** -0.5).astype(BF)

    def place(n):
        return all_ref.at[b, :, :, pl.ds(pl.multiple_of(n * 2 * HD, 2 * HD), 2 * HD)]

    def far(n):
        return to_core(send_ref.at[n, 1 - b], place(n), sems, n, sib)

    def own(n):
        return pltpu.make_async_copy(send_ref.at[n, b], place(n), own_sems.at[n])

    far(p_now).start()
    own(p_now).start()

    @pl.when(p_now == pl.num_programs(0) - 1)
    def _():
        for n in range(send_ref.shape[0]):
            own(n).wait()
            far(n).wait()


def attend_rows_back(starts, qkv, mixed, grad_mix, lse, ident):
    parts, _, rows, width = qkv.shape
    pairs = width // (2 * HD)
    length = parts * rows
    bq = bk = max(min(512, rows), 2 * SPAN)

    def one(which):
        return pl.BlockSpec((parts, None, rows, 2 * HD), lambda p, s: (0, which, 0, p))

    flat = pl.BlockSpec((parts, rows, 2 * HD), lambda p, s: (0, 0, p))
    return pl.pallas_call(
        functools.partial(attend_back_kernel, bq, bk),
        out_shape=jax.ShapeDtypeStruct((parts, 3, rows, width), BF),
        grid_spec=pltpu.PrefetchScalarGridSpec(
            num_scalar_prefetch=1,
            grid=(pairs,),
            in_specs=[one(0), one(1), one(2), flat, flat,
                      pl.BlockSpec((1, 2, length), lambda p, s: (p, 0, 0))],
            out_specs=pl.BlockSpec(memory_space=pl.ANY),
            scratch_shapes=[
                pltpu.VMEM((2 * HD, length), BF),
                pltpu.VMEM((2 * HD, length), F32),
                pltpu.VMEM((2, length), F32),
                pltpu.VMEM((2, length, 2 * HD), BF),
                pltpu.VMEM((2, length, 2 * HD), BF),
                pltpu.VMEM((bk, 2 * HD), F32),
                pltpu.VMEM((bk, 2 * HD), F32),
                pltpu.VMEM((pairs, parts, 3, rows, 2 * HD), BF),
                pltpu.SemaphoreType.DMA((2, pairs)),
                pltpu.SemaphoreType.DMA((pairs,)),
            ],
        ),
        compiler_params=pltpu.CompilerParams(
            dimension_semantics=("arbitrary",), vmem_limit_bytes=48 * MIB,
            collective_id=ident, has_side_effects=True,
        ),
        cost_estimate=cost(40 * length * length * width, 24 * length * width),
        name="attend_back",
    )(starts, qkv, qkv, qkv, mixed, grad_mix, lse)


def stats(x):
    center = x - jnp.mean(x, axis=-1, keepdims=True)
    return center, lax.rsqrt(jnp.mean(center * center, axis=-1, keepdims=True) + 1e-05)


def norm_back(x, gain, grad):
    center, r = stats(x)
    n = center * r
    e = grad * gain
    return r * (e - jnp.mean(e, axis=-1, keepdims=True) - n * jnp.mean(e * n, axis=-1, keepdims=True))


def row_loop(rows, chunk, body):
    if chunk == rows:
        body(slice(None))
        return

    @pl.loop(0, rows // chunk)
    def _(i):
        body(pl.ds(pl.multiple_of(i * chunk, chunk), chunk))


def qkv_kernel(
    tok_ref, gain_ref, bias_ref, low_in_ref, w_ref, low_up_ref, norm_ref, low_ref, all_ref,
    send_ref, sems, own_sems,
):
    rows = tok_ref.shape[0]
    side, j = pl.program_id(0), pl.program_id(1)
    b, sib = pair_core()

    @pl.when((side == 0) & (j == 0))
    def _():
        def body(at):
            center, r = stats(tok_ref[at, :].astype(F32))
            normed = (center * r * gain_ref[...] + bias_ref[...]).astype(BF)
            norm_ref[at, :] = normed
            low_ref[at, :] = nt(normed, low_in_ref[...]).astype(BF)

        row_loop(rows, 256, body)
        greet_core(sib)

    w = w_ref[...].reshape(norm_ref.shape[1], -1)
    y = nn(norm_ref[...], w) + nn(low_ref[...], low_up_ref[...])
    send_ref[side, j] = y.astype(BF)

    def far(n):
        return to_core(send_ref.at[0, n], all_ref.at[b, n], sems, n, sib)

    def own(n):
        return pltpu.make_async_copy(send_ref.at[1, n], all_ref.at[b, n], own_sems.at[n])

    pl.when(side == 0)(lambda: far(j).start())
    pl.when(side == 1)(lambda: own(j).start())

    @pl.when((side == 1) & (j == 2))
    def _():
        for n in range(3):
            own(n).wait()
            far(n).wait()


def whole(shape):
    return pl.BlockSpec(shape, lambda *_: (0,) * len(shape))


def project_qkv(tok, gain, bias, low_in, w, low_up, ident):
    rows, features = tok.shape
    shards, groups, _, part, width = w.shape
    rank = low_in.shape[0]

    def heads(side):
        b = lax.axis_index("dp") % 2
        return jnp.where(side == 0, 1 - b, b)

    return pl.pallas_call(
        qkv_kernel,
        out_shape=(
            jax.ShapeDtypeStruct((rows, features), BF),
            jax.ShapeDtypeStruct((rows, rank), BF),
            jax.ShapeDtypeStruct((groups, 3, rows, width), BF),
        ),
        grid=(groups, 3),
        in_specs=[
            whole((rows, features)), whole((1, features)), whole((1, features)),
            whole((rank, features)),
            pl.BlockSpec((shards, None, None, part, width), lambda g, j: (0, heads(g), j, 0, 0)),
            pl.BlockSpec((None, rank, width), lambda g, j: (heads(g), 0, j)),
        ],
        out_specs=[
            whole((rows, features)), whole((rows, rank)), pl.BlockSpec(memory_space=pl.ANY),
        ],
        scratch_shapes=[
            pltpu.VMEM((groups, 3, rows, width), BF),
            pltpu.SemaphoreType.DMA((2, 3)),
            pltpu.SemaphoreType.DMA((3,)),
        ],
        compiler_params=pltpu.CompilerParams(
            dimension_semantics=("arbitrary", "arbitrary"), vmem_limit_bytes=48 * MIB,
            collective_id=ident, has_side_effects=True,
        ),
        cost_estimate=cost(4 * rows * features * groups * 3 * width, 4 * rows * groups * 3 * width),
        name="project_qkv",
    )(tok, gain, bias, low_in, w, low_up)


def qkv_back_kernel(
    planes, g_ref, w_any, low_up_ref, low_in_ref, norm_ref, low_ref, tok_ref, gain_ref, resid_ref, tag_ref,
    grad_ref, late_ref, far_ref,
    w_ref, own_ref, glow_ref, send_ref, w_sem, swap_sem, *sems,
):
    s = pl.program_id(0)
    groups, _, rows, width = g_ref.shape
    chunk, features = tok_ref.shape
    parts = rows // chunk
    gather = Gather(own_ref, late_ref, *sems, planes)
    moves = gather.c != gather.t
    partner = (gather.place(gather.z, gather.x, gather.t), gather.c)
    blocks = [(g, j) for g in range(groups) for j in range(3)]

    def load_w():
        return pltpu.make_async_copy(w_any, w_ref, w_sem)

    def swap(n):
        return to_core(
            send_ref.at[n], far_ref.at[pl.ds(n * chunk, chunk)], swap_sem, n, partner
        )

    @pl.when(s == 0)
    def _():
        load_w().start()
        gather.greet([(moves, partner)])
        low = low_ref[...]
        glow = None
        for n, (g, j) in enumerate(blocks):
            part = g_ref[g, j]
            more = nt(part, low_up_ref[g, :, j * width : (j + 1) * width])
            glow = more if glow is None else glow + more
            own_ref[n] = tn(low, part).astype(BF)
        glow = glow.astype(BF)
        glow_ref[...] = glow
        y = tn(glow, norm_ref[...]).astype(BF)
        for n in range(features // width):
            own_ref[len(blocks) + n] = y[:, n * width : (n + 1) * width]
        own_ref[own_ref.shape[0] - 1] = tag_ref[...]
        gather.round(0)

    pl.when(s == 1)(lambda: load_w().wait())

    @pl.when(s > 0)
    def _():
        at = pl.ds(pl.multiple_of((s - 1) * chunk, chunk), chunk)
        total = nn(glow_ref[at, :], low_in_ref[...])
        for g, j in blocks:
            total = total + nt(g_ref[g, j, at, :], w_ref[:, g, j].reshape(features, width))
        grad = resid_ref[...] + norm_back(tok_ref[...].astype(F32), gain_ref[...], total)
        grad_ref[...] = grad
        send_ref[s - 1] = grad.astype(BF)

        @pl.when(moves)
        def _():
            swap(s - 1).start()

    for k in range(1, gather.rounds):
        pl.when(s == min(k, parts))(lambda k=k: gather.round(k))

    @pl.when(s == parts)
    def _():
        gather.finish()

        @pl.when(moves)
        def _():
            for n in range(parts):
                swap(n).wait()


def project_qkv_back(grad, w, low_up, low_in, normed, low, tok, gain, resid, tag, ident):
    rows, features = tok.shape
    shards, groups, _, part, width = w.shape
    rank = low_in.shape[0]
    planes = shards // 4
    parts = 4
    chunk = rows // parts
    late = (groups * 3 + features // width + 1, rank, width)
    anywhere = pl.BlockSpec(memory_space=pl.ANY)

    def keep(shape):
        return pl.BlockSpec(shape, lambda s: (0,) * len(shape), pipeline_mode=pl.Buffered(1))

    some = pl.BlockSpec((chunk, features), lambda s: (jnp.maximum(s - 1, 0), 0))
    return pl.pallas_call(
        functools.partial(qkv_back_kernel, planes),
        out_shape=(
            jax.ShapeDtypeStruct((rows, features), F32),
            jax.ShapeDtypeStruct((shards, 2) + late, BF),
            jax.ShapeDtypeStruct((rows, features), BF),
        ),
        grid=(1 + parts,),
        in_specs=[
            keep(grad.shape), anywhere, keep((groups, rank, 3 * width)), keep((rank, features)),
            keep((rows, features)), keep((rows, rank)), some, keep((1, features)), some,
            keep((rank, width)),
        ],
        out_specs=[some, anywhere, anywhere],
        scratch_shapes=[
            pltpu.VMEM(w.shape, BF),
            pltpu.VMEM(late, BF),
            pltpu.VMEM((rows, rank), BF),
            pltpu.VMEM((parts, chunk, features), BF),
            pltpu.SemaphoreType.DMA,
            pltpu.SemaphoreType.DMA((2, parts)),
            *gather_sems(1, planes),
        ],
        compiler_params=pltpu.CompilerParams(
            dimension_semantics=("arbitrary",), vmem_limit_bytes=56 * MIB,
            collective_id=ident, has_side_effects=True,
        ),
        cost_estimate=cost(5 * rows * features * groups * 3 * width, 4 * rows * groups * 3 * width),
        name="project_qkv_back",
    )(grad, w, low_up, low_in, normed, low, tok, gain, resid, tag)


GELU = math.sqrt(2.0 / math.pi)


def gelu_and_slope(v):
    v2 = v * v
    half = 0.5 + 0.5 * jnp.tanh(v * (GELU + (GELU * 0.044715) * v2))
    hidden = v * half
    return hidden, half + hidden * (1.0 - half) * (2.0 * GELU + (6.0 * 0.044715 * GELU) * v2)


def middle_kernel(
    groups, nf,
    w_ref, sh_ref, wo_ref, sho_ref, tok_ref, mix_ref, cot_ref, gain_ref, bias_ref, rep_ref,
    out_ref, resid_ref, gr_ref, do_ref,
    acc_ref, norm_ref, hid_ref, slope_ref, lacc_ref, llow_ref, send_ref, sems, own_sem,
):
    rows, features = tok_ref.shape
    rank = sh_ref.shape[0]
    s = pl.program_id(0)
    b_out, a_up, b_down = rep_ref[0], rep_ref[1], rep_ref[2]
    co = wo_ref.shape[-1]
    up0, down0 = groups, groups + nf
    upb0, end0 = groups + 2 * nf, groups + 3 * nf
    b, sib = pair_core()
    pl.when(s == 0)(lambda: greet_core(sib))

    for g in range(groups):

        @pl.when(s == g)
        def _():
            part = mix_ref[g]
            y = nt(part, wo_ref[...].reshape(features, co))
            low = nt(part, sho_ref[...])
            if g == 0:
                resid_ref[...] = tok_ref[...].astype(F32) + y
                lacc_ref[...] = low
            else:
                resid_ref[...] += y
                lacc_ref[...] += low

    @pl.when(s == up0 - 1)
    def _():
        def body(at):
            low = lacc_ref[at, :].astype(BF)
            llow_ref[0, at, :] = low
            resid = resid_ref[at, :] + nn(low, b_out)
            resid_ref[at, :] = resid
            center, r = stats(resid)
            normed = (center * r * gain_ref[...] + bias_ref[...]).astype(BF)
            norm_ref[at, :] = normed
            llow_ref[1, at, :] = nt(normed, a_up).astype(BF)

        row_loop(rows, 256, body)
        llow_ref[3] = nt(cot_ref[...], b_down).astype(BF)
        acc_ref[...] = jnp.zeros_like(acc_ref)
        lacc_ref[...] = jnp.zeros_like(lacc_ref)

    @pl.when((s >= up0) & (s < down0))
    def _():
        f = s - up0
        w = w_ref[...].reshape(features, -1)

        def body(at):
            pre = nn(norm_ref[at, :], w) + nn(llow_ref[1, at, :], sh_ref[...])
            hidden, slope = gelu_and_slope(pre)
            hid_ref[f, at, :] = hidden.astype(BF)
            slope_ref[f, at, :] = slope.astype(BF)

        row_loop(rows, 512, body)

    @pl.when((s >= down0) & (s < upb0))
    def _():
        f = s - down0
        w = w_ref[...].reshape(features, -1)
        sh = sh_ref[...]
        hidden = hid_ref[f]
        acc_ref[...] += nt(hidden, w)
        lacc_ref[...] += nt(hidden, sh)
        g_hidden = nn(cot_ref[...], w) + nn(llow_ref[3], sh)
        g_pre = (g_hidden * slope_ref[f].astype(F32)).astype(BF)
        slope_ref[f] = g_pre
        gr_ref[:rank, :] = tn(llow_ref[3], hidden).astype(BF)
        gr_ref[rank:, :] = tn(llow_ref[1], g_pre).astype(BF)

    @pl.when(s == upb0 - 1)
    def _():
        def body(at):
            low = lacc_ref[at, :].astype(BF)
            llow_ref[2, at, :] = low
            out_ref[at, :] = (resid_ref[at, :] + acc_ref[at, :] + nn(low, b_down)).astype(BF)

        row_loop(rows, 512, body)
        acc_ref[...] = jnp.zeros_like(acc_ref)
        lacc_ref[...] = jnp.zeros_like(lacc_ref)

    @pl.when((s >= upb0) & (s < end0))
    def _():
        f = s - upb0
        w = w_ref[...].reshape(features, -1)
        part = slope_ref[f]
        acc_ref[...] += nt(part, w)
        lacc_ref[...] += nt(part, sh_ref[...])

    @pl.when(s == end0 - 1)
    def _():
        gr_ref[:rank, :] = tn(llow_ref[2], cot_ref[...]).astype(BF)
        llow_ref[4] = lacc_ref[...].astype(BF)
        gr_ref[rank:, :] = tn(llow_ref[4], norm_ref[...]).astype(BF)

        def body(at):
            total = acc_ref[at, :] + nn(llow_ref[4, at, :], a_up)
            g = cot_ref[at, :].astype(F32) + norm_back(resid_ref[at, :], gain_ref[...], total)
            resid_ref[at, :] = g
            branch = g.astype(BF)
            norm_ref[at, :] = branch
            llow_ref[5, at, :] = nt(branch, b_out).astype(BF)

        row_loop(rows, 256, body)

    def far():
        return to_core(send_ref.at[0], do_ref.at[b], sems, 0, sib)

    def own():
        return pltpu.make_async_copy(send_ref.at[1], do_ref.at[b], own_sem)

    @pl.when(s >= end0)
    def _():
        turn = s - end0
        g = jnp.where(turn == 0, 1 - b, b)
        wo = wo_ref[...].reshape(features, co)
        y = nn(norm_ref[...], wo) + nn(llow_ref[5], sho_ref[...])
        send_ref[turn] = y.astype(BF)
        at = pl.ds(pl.multiple_of(g * co, co), co)
        gr_ref[:rank, at] = tn(llow_ref[5], mix_ref[g]).astype(BF)

    @pl.when(s == end0)
    def _():
        far().start()
        gr_ref[rank:, :] = tn(llow_ref[0], norm_ref[...]).astype(BF)

    @pl.when(s == end0 + 1)
    def _():
        own().start()
        own().wait()
        far().wait()


def middle(w, shared, tok, mix, cot, gain, bias, rep, ident):
    rows, features = tok.shape
    shards, groups, part, total = w.shape
    rank = rep.shape[1]
    co = mix.shape[2]
    ffw = (total - co) // 2
    c = features
    halves = ffw // c
    nf = groups * halves
    first = (shared.shape[2] - 2 * ffw) // c
    out_at, out_shared = 2 * ffw // co, (shared.shape[2] - 2 * ffw) // co - 1
    blocks = [(f // halves, f % halves) for f in range(nf)]
    up = [(t, h, h) for t, h in blocks]
    down_step = [(t, halves + h, halves + h) for t, h in blocks]
    shared_group = [t for t, _ in blocks]
    order = [up[0]] * groups + up + down_step + up + [up[-1]] * groups
    shared_of = [0] * groups + shared_group * 3 + [shared_group[-1]] * groups
    of_grad = [0] * (groups + nf) + list(range(nf)) + [nf + 1] * nf + [nf] * groups
    last = len(order) - groups
    anywhere = pl.BlockSpec(memory_space=pl.ANY)

    def group(s):
        b = lax.axis_index("dp") % 2
        return jnp.where(s < last, jnp.minimum(s, groups - 1), jnp.where(s == last, 1 - b, b))

    once = pl.Buffered(1)

    def keep(shape):
        return pl.BlockSpec(shape, lambda s, *_: (0,) * len(shape), pipeline_mode=once)

    def at(table_row):
        def index(s):
            got = table_row[0]
            for n in range(1, len(table_row)):
                if table_row[n] != table_row[n - 1]:
                    got = got + jnp.where(s >= n, table_row[n] - table_row[n - 1], 0)
            return got
        return index

    w_t, w_c = at([x[0] for x in order]), at([x[1] for x in order])
    s_t, s_c, gi = at(shared_of), at([x[2] for x in order]), at(of_grad)
    return pl.pallas_call(
        functools.partial(middle_kernel, groups, nf),
        out_shape=(
            jax.ShapeDtypeStruct((rows, features), BF),
            jax.ShapeDtypeStruct((rows, features), F32),
            jax.ShapeDtypeStruct((nf + 2, 2 * rank, c), BF),
            jax.ShapeDtypeStruct(mix.shape, BF),
        ),
        grid=(len(order),),
        in_specs=[
            pl.BlockSpec((shards, None, part, c), lambda s: (0, w_t(s), 0, w_c(s))),
            pl.BlockSpec((None, rank, c), lambda s: (s_t(s), 0, s_c(s) + first)),
            pl.BlockSpec((shards, None, part, co), lambda s: (0, group(s), 0, out_at)),
            pl.BlockSpec((None, rank, co), lambda s: (group(s), 0, out_shared)),
            keep((rows, features)), keep(mix.shape), keep((rows, features)),
            keep((1, features)), keep((1, features)), keep(rep.shape),
        ],
        out_specs=[
            keep((rows, features)), keep((rows, features)),
            pl.BlockSpec((None, 2 * rank, c), lambda s: (gi(s), 0, 0)), anywhere,
        ],
        scratch_shapes=[
            pltpu.VMEM((rows, features), F32),
            pltpu.VMEM((rows, features), BF),
            pltpu.VMEM((nf, rows, c), BF),
            pltpu.VMEM((nf, rows, c), BF),
            pltpu.VMEM((rows, rank), F32),
            pltpu.VMEM((6, rows, rank), BF),
            pltpu.VMEM(mix.shape, BF),
            pltpu.SemaphoreType.DMA((2, 1)),
            pltpu.SemaphoreType.DMA,
        ],
        compiler_params=pltpu.CompilerParams(
            dimension_semantics=("arbitrary",), vmem_limit_bytes=62 * MIB,
            collective_id=ident, has_side_effects=True,
        ),
        cost_estimate=cost(6 * rows * features * groups * total, 4 * features * groups * total),
        name="middle",
    )(w, shared, w, shared, tok, mix, cot, gain, bias, rep)


class Gather:
    def __init__(self, shard, full, out_sem, in_sem, own_sem, planes):
        self.shard, self.full, self.planes = shard, full, planes
        self.chunks = out_sem.shape[0]
        self.out_sem, self.in_sem, self.own_sem = out_sem, in_sem, own_sem
        self.rounds = planes + 2
        dp, t = lax.axis_index("dp"), lax.axis_index("tensor")
        z, x, c = dp // 4, (dp // 2) % 2, dp % 2
        self.dp, self.z, self.x, self.c, self.t = dp, z, x, c, t
        self.low, self.high = z > 0, z < planes - 1
        self.below = jnp.maximum(dp - 4, 0), t
        self.above = jnp.minimum(dp + 4, 4 * planes - 1), t
        self.near = dp, 1 - t
        self.across = self.place(z, 1 - x, c), t
        self.sib = self.place(z, x, 1 - c), t
        self.plan = [self.lay_out(k) for k in range(self.rounds)]

    def place(self, z, x, c):
        return z * 4 + x * 2 + c

    def greet(self, extra=()):
        barrier = pltpu.get_barrier_semaphore()

        def hello(who):
            pl.semaphore_signal(barrier, inc=1, device_id=who, device_id_type=MESH)

        for who in (self.near, self.across, self.sib):
            hello(who)
        count = 3
        for cond, who in ((self.low, self.below), (self.high, self.above)) + tuple(extra):
            pl.when(cond)(lambda who=who: hello(who))
            count = count + cond.astype(jnp.int32)
        pl.semaphore_wait(barrier, count)

    def piece(self, ref, n):
        if self.chunks == 1:
            return ref
        size = ref.shape[-2] // self.chunks
        every = (slice(None),) * (len(ref.shape) - 2)
        return ref.at[every + (pl.ds(n * size, size), slice(None))]

    def copy(self, n, at, who, sem, own=False):
        slot = self.piece(self.full.at[at[0], at[1]], n)
        return pltpu.make_async_remote_copy(
            src_ref=self.piece(self.shard, n) if own else slot, dst_ref=slot,
            send_sem=self.out_sem.at[n, sem],
            recv_sem=self.in_sem.at[n, at[0] * 2 + at[1]], device_id=who, device_id_type=MESH,
        )

    def arrive(self, n, at):
        self.copy(n, at, self.sib, 0).wait_recv()

    def own_copy(self, n):
        here = self.piece(self.full.at[self.dp, self.t], n)
        return pltpu.make_async_copy(self.piece(self.shard, n), here, self.own_sem.at[n])

    def lay_out(self, k):
        z, planes, t = self.z, self.planes, self.t
        events = []

        def ways(hops):
            if not 0 <= hops < planes:
                return []
            if hops == 0:
                return [(z, None, [(self.low, self.below, 0), (self.high, self.above, 1)])]
            up, down = z >= hops, z + hops < planes
            return [
                (z - hops, up, [(up & self.high, self.above, 1)]),
                (z + hops, down, [(down & self.low, self.below, 0)]),
            ]

        for n in range(self.chunks):
            for zz, cond, on in ways(k):
                sends = on + [(cond, self.across, 2), (cond, self.sib, 4)]
                if k == 0:
                    sends = [(None, self.near, 3)] + sends
                events.append((n, cond, (self.place(zz, self.x, self.c), t), k == 0, zz, sends))
            for zz, cond, on in ways(k - 1):
                sends = [(c, who, kind + 5) for c, who, kind in on]
                sends += [(cond, self.across, 7), (cond, self.sib, 8)]
                events.append((n, cond, (self.place(zz, self.x, self.c), 1 - t), False, zz, sends))
                far = self.place(zz, 1 - self.x, self.c), t
                events.append((n, cond, far, False, zz, [(cond, self.sib, 9)]))
            for zz, cond, _ in ways(k - 2):
                far = self.place(zz, 1 - self.x, self.c), 1 - t
                events.append((n, cond, far, False, zz, [(cond, self.sib, 10)]))
        return [
            (n, cond, where, own, [(c, who, kind * planes + zz) for c, who, kind in sends])
            for n, cond, where, own, zz, sends in events
        ]

    def when(self, cond, act):
        if cond is None:
            act()
        else:
            pl.when(cond)(act)

    def round(self, k):
        for n, cond, where, own, sends in self.plan[k]:
            if not own:
                self.when(cond, lambda n=n, where=where: self.arrive(n, where))
            for c, who, sem in sends:
                self.when(
                    c,
                    lambda n=n, where=where, who=who, sem=sem, own=own: self.copy(
                        n, where, who, sem, own
                    ).start(),
                )
            if own:
                self.own_copy(n).start()

    def finish(self):
        for n in range(self.chunks):
            for zz in range(self.planes):
                for x in (self.x, 1 - self.x):
                    for t in (self.t, 1 - self.t):
                        self.arrive(n, (self.place(zz, x, 1 - self.c), t))
            self.own_copy(n).wait()
        for events in self.plan:
            for n, _, where, own, sends in events:
                for c, who, sem in sends:
                    self.when(
                        c,
                        lambda n=n, where=where, who=who, sem=sem, own=own: self.copy(
                            n, where, who, sem, own
                        ).wait_send(),
                    )


def gather_sems(n, planes):
    return [
        pltpu.SemaphoreType.DMA((n, 11 * planes)),
        pltpu.SemaphoreType.DMA((n, 8 * planes)),
        pltpu.SemaphoreType.DMA((n,)),
    ]


def spread_kernel(n_all, kinds, planes, *refs):
    n_swap = len(kinds)
    shard = refs[:n_all]
    swap_in = refs[n_all : n_all + n_swap]
    full = refs[n_all + n_swap : 2 * n_all + n_swap]
    swap_out = refs[2 * n_all + n_swap : 2 * n_all + 2 * n_swap]
    *sems, swap_sem = refs[2 * n_all + 2 * n_swap :]
    g = Gather(shard[0], full[0], *sems, planes)
    moves = g.c != g.t
    keeps = jnp.logical_not(moves)
    partner = (g.place(g.z, g.x, g.t), g.c)
    g.greet([(moves, partner)])
    rules = {"partner": (moves, partner, moves), "near": (moves, g.near, keeps), "sibling": (keeps, g.sib, moves)}

    def swap_copy(n):
        return pltpu.make_async_remote_copy(
            src_ref=swap_in[n], dst_ref=swap_out[n], send_sem=swap_sem.at[n, 0],
            recv_sem=swap_sem.at[n, 1], device_id=rules[kinds[n]][1], device_id_type=MESH,
        )

    for n in range(n_swap):
        pl.when(rules[kinds[n]][0])(lambda n=n: swap_copy(n).start())
    for k in range(g.rounds):
        g.round(k)
    g.finish()
    for n in range(n_swap):
        pl.when(rules[kinds[n]][0])(lambda n=n: swap_copy(n).wait_send())
        pl.when(rules[kinds[n]][2])(lambda n=n: swap_copy(n).wait_recv())


def spread(gathered, handed, shards, ident):
    planes = shards // 4
    swapped = [a for a, _ in handed]
    n_all, n_swap = len(gathered), len(swapped)
    anywhere = pl.BlockSpec(memory_space=pl.ANY)
    return pl.pallas_call(
        functools.partial(spread_kernel, n_all, [k for _, k in handed], planes),
        out_shape=[jax.ShapeDtypeStruct((shards, 2) + a.shape, a.dtype) for a in gathered]
        + [jax.ShapeDtypeStruct(a.shape, a.dtype) for a in swapped],
        in_specs=[anywhere] * (n_all + n_swap),
        out_specs=[anywhere] * (n_all + n_swap),
        scratch_shapes=[
            *gather_sems(SPREAD_CHUNKS, planes),
            pltpu.SemaphoreType.DMA((max(n_swap, 1), 2)),
        ],
        compiler_params=pltpu.CompilerParams(collective_id=ident, has_side_effects=True),
        cost_estimate=cost(0, 60 * MIB),
        name="spread%d" % ident,
    )(*gathered, *swapped)


def sum_kernel(pieces, sel_ref, t_ref, *refs):
    ins, outs = refs[: len(refs) - len(pieces)], refs[len(refs) - len(pieces) :]
    step = pl.program_id(0)
    devices = ins[0].shape[0]

    @pl.when(step == 0)
    def _():
        for out in outs:
            out[...] = jnp.zeros_like(out)

    @pl.loop(0, devices)
    def _(d):
        for (at, which, blocks), out in zip(pieces, outs):
            slot = sel_ref[step * devices + d, which]
            rank = out.shape[-2]
            c = ins[at].shape[-1]
            for k, (block, row) in enumerate(blocks):
                new = ins[at][d, block, row : row + rank, :].astype(F32)
                if len(out.shape) == 4:
                    out[slot, k] += new
                else:
                    out[slot, :, k * c : (k + 1) * c] += new


def sum_picks(sel, t, arrays, pieces, slots, rank, name):
    steps = 4
    in_specs = []
    for a, shape, where in arrays:
        in_specs.append(
            pl.BlockSpec(
                (a.shape[0] // steps,) + shape, lambda s, sel, t, where=where: (s,) + where(t[0])
            )
        )
    shapes = []
    for at, _, blocks, flat in pieces:
        n, c = len(blocks), arrays[at][1][-1]
        shapes.append((slots, rank, n * c) if flat else (slots, n, rank, c))
    return pl.pallas_call(
        functools.partial(sum_kernel, [p[:3] for p in pieces]),
        out_shape=[jax.ShapeDtypeStruct(shape, F32) for shape in shapes],
        grid_spec=pltpu.PrefetchScalarGridSpec(
            num_scalar_prefetch=2, grid=(steps,), in_specs=in_specs,
            out_specs=[whole(shape) for shape in shapes],
        ),
        compiler_params=pltpu.CompilerParams(
            dimension_semantics=("arbitrary",), vmem_limit_bytes=48 * MIB
        ),
        cost_estimate=cost(0, 30 * MIB),
        name=name,
    )(sel, t, *[a for a, _, _ in arrays])


def pick_kernel(idx_ref, bq_ref, ao_ref, bu_ref, ad_ref, aq_ref, bo_ref, au_ref, bd_ref, marks_ref, half_ref, rest_ref, m_ref):
    at = 0
    for j in range(bq_ref.shape[0]):
        half_ref[:, at : at + bq_ref.shape[2]] = bq_ref[j]
        at += bq_ref.shape[2]
    for ref in (ao_ref, bu_ref, ad_ref):
        half_ref[:, at : at + ref.shape[1]] = ref[...]
        at += ref.shape[1]
    for n, ref in enumerate((aq_ref, bo_ref, au_ref, bd_ref)):
        rest_ref[n] = ref[...]
    m_ref[...] = jnp.broadcast_to(marks_ref[...], m_ref.shape)


def pick_adapters(idx, split, full, marks):
    rank = full[0].shape[1]
    width = split[0].shape[1] * split[0].shape[3] + sum(a.shape[2] for a in split[1:])

    def one(a, which):
        rest = a.shape[1:]
        return pl.BlockSpec((None,) + rest, lambda i, idx: (idx[which],) + (0,) * len(rest))

    in_specs = [one(a, n) for n, a in enumerate(split)] + [one(a, n) for n, a in enumerate(full)]
    return pl.pallas_call(
        pick_kernel,
        out_shape=(
            jax.ShapeDtypeStruct((rank, width), BF),
            jax.ShapeDtypeStruct((len(full),) + full[0].shape[1:], BF),
            jax.ShapeDtypeStruct((8, 128), jnp.int32),
        ),
        grid_spec=pltpu.PrefetchScalarGridSpec(
            num_scalar_prefetch=1, grid=(1,), in_specs=in_specs + [whole(marks.shape)],
            out_specs=[whole((rank, width)), whole((len(full),) + full[0].shape[1:]), whole((8, 128))],
        ),
        compiler_params=pltpu.CompilerParams(dimension_semantics=("arbitrary",)),
        cost_estimate=cost(0, MIB),
        name="pick_adapters",
    )(idx, *split, *full, marks)


def chip_device(
    tokens, w_qkv, w_out, w_up, w_down, ln1_gain, ln1_bias, ln2_gain, ln2_bias,
    a_qkv, b_qkv, a_out, b_out, a_up, b_up, a_down, b_down, adapter_idx, pic_start, cotangent,
):
    shards = lax.axis_size("dp")
    dp, t = lax.axis_index("dp"), lax.axis_index("tensor")
    keeps = dp % 2 == t
    both = ("dp", "tensor")
    swap = []
    for c in range(shards // 2):
        one, two = 2 * (2 * c + 1), 2 * (2 * c) + 1
        swap += [(one, two), (two, one)]

    def swapped(x):
        return lax.ppermute(x, both, swap)

    def row(v):
        return v.reshape(1, -1)

    rank, slots = a_qkv.shape[2], a_qkv.shape[0]
    features, width = tokens.shape[1], w_out.shape[0]
    chosen = adapter_idx[0]

    turned = lambda v: v.transpose(0, 2, 1)
    marks = jnp.concatenate([chosen, pic_start[0]])
    half, rest, marks = pick_adapters(
        chosen,
        [b_qkv.transpose(0, 2, 1, 3), turned(a_out), b_up, turned(a_down)],
        [turned(a_qkv), b_out, turned(a_up), b_down],
        jnp.pad(marks, (0, 128 - marks.shape[0]))[None],
    )

    qkv_shard = w_qkv.transpose(1, 0, 2)
    rest_shard = jnp.concatenate([w_up, w_down.T, w_out.T], axis=1)
    rest_full = lax.all_gather(rest_shard, both, axis=0)
    rest_full = rest_full.reshape(shards, 2, *rest_shard.shape)
    qkv_full, far_tokens, near_half, partner_half, core_half, core_rest, core_marks = spread(
        [qkv_shard],
        [
            (tokens, "partner"), (half, "near"), (half, "partner"),
            (half, "sibling"), (rest, "sibling"), (marks, "sibling"),
        ],
        shards,
        0,
    )
    later, far_tokens = lax.optimization_barrier((cotangent, far_tokens))
    cot = jnp.where(keeps, cotangent, swapped(later))
    tok = jnp.where(keeps, tokens, far_tokens)
    own_half = jnp.where(keeps, half, core_half)
    far_half = jnp.where(keeps, near_half, partner_half)
    shared = jnp.where(t == 0, jnp.stack([own_half, far_half]), jnp.stack([far_half, own_half]))
    rep = jnp.where(keeps, rest, core_rest)
    marks = jnp.where(keeps, marks, core_marks)[0]
    starts = marks[4 : 4 + pic_start.shape[1]]
    tag = jnp.pad(marks[:4].astype(BF)[None], ((0, rank - 1), (0, width - 4)))

    normed, low, qkv = project_qkv(tok, row(ln1_gain), row(ln1_bias), rep[0], qkv_full, shared, 2)
    mixed, lse, mix = attend_rows(starts, qkv, 3)
    layer_out, g_resid, g_early, g_mix = middle(
        rest_full, shared, tok, mix, cot, row(ln2_gain), row(ln2_bias), rep[1:], 4
    )
    early = lax.all_gather(g_early, both, axis=0)
    out = jnp.where(keeps, layer_out, swapped(layer_out))
    g_qkv = attend_rows_back(starts, qkv, mixed, g_mix, lse, 5)
    grad_tok, late, far_grad = project_qkv_back(
        g_qkv, qkv_full, shared, rep[0], normed, low, tok, row(ln1_gain), g_resid, tag, 1
    )
    grad_input = jnp.where(keeps, grad_tok, far_grad.astype(F32))

    late = late.reshape(2 * shards, *late.shape[2:])
    sel = late[:, -1, 0, :4].astype(jnp.int32)
    side = t.reshape(1).astype(jnp.int32)
    nf, c = g_early.shape[0] - 2, g_early.shape[2]
    near = range(nf // 2)
    rows2 = 2 * rank
    early = early.reshape(2 * shards, *g_early.shape)
    (
        grad_a_out, grad_b_out, grad_a_up, grad_b_up, grad_a_down, grad_b_down, grad_b_qkv, grad_a_qkv,
    ) = sum_picks(
        sel, side,
        [
            (early, (nf // 2, rows2, c), lambda u: (u, 0, 0)),
            (early, (1, rows2, width), lambda u: (nf, 0, u)),
            (early, (2, rows2, c), lambda u: (nf // 2, 0, 0)),
            (late, (3, rank, width), lambda u: (u, 0, 0)),
            (late, (2, rank, width), lambda u: (3, 0, 0)),
        ],
        [
            (1, 1, [(0, 0)], True),
            (2, 1, [(0, rank)], True),
            (2, 2, [(1, rank)], True),
            (0, 2, [(i, rank) for i in near], True),
            (0, 3, [(i, 0) for i in near], True),
            (2, 3, [(1, 0)], True),
            (3, 0, [(0, 0), (1, 0), (2, 0)], False),
            (4, 0, [(0, 0), (1, 0)], True),
        ],
        slots, rank, "sum_picks",
    )
    return (
        out, grad_input, turned(grad_a_qkv), grad_b_qkv.transpose(0, 2, 1, 3),
        turned(grad_a_out), grad_b_out, turned(grad_a_up), grad_b_up, turned(grad_a_down), grad_b_down,
    )


def solution(mesh):
    placed = (
        P(("dp", "tensor"), None),
        P("dp", None, "tensor"),
        P("tensor", "dp"),
        P("dp", "tensor"),
        P("tensor", "dp"),
        P(),
        P(),
        P(),
        P(),
        P(),
        P(None, None, None, "tensor"),
        P(None, "tensor", None),
        P(),
        P(),
        P(None, None, "tensor"),
        P(None, "tensor", None),
        P(),
        P("dp", None),
        P("dp", None),
        P(("dp", "tensor"), None),
    )
    paired = mesh.shape["tensor"] == 2 and mesh.shape["dp"] % 2 == 0
    return jax.shard_map(
        chip_device if paired else per_device,
        mesh=mesh,
        in_specs=placed,
        out_specs=(
            P(("dp", "tensor"), None),
            P(("dp", "tensor"), None),
            P(),
            P(None, None, None, "tensor"),
            P(None, "tensor", None),
            P(),
            P(),
            P(None, None, "tensor"),
            P(None, "tensor", None),
            P(),
        ),
        check_vma=False,
    )
```

```python
import functools
import math

import jax
import jax.numpy as jnp
from jax import lax
from jax.experimental import pallas as pl
from jax.experimental.pallas import tpu as pltpu
from jax.sharding import PartitionSpec as P

HD = 64
SPAN = 256
BLOCK = 512


def matmul(left, right):
    return jnp.dot(left, right, preferred_element_type=jnp.float32)


def contract_rows(left, right):
    return lax.dot_general(
        left, right, (((0,), (0,)), ((), ())), preferred_element_type=jnp.float32
    )


def against(left, right):
    return lax.dot_general(
        left, right, (((1,), (1,)), ((), ())), preferred_element_type=jnp.float32
    )


def layer_norm(values, multiplier, addend):
    center = values - jnp.mean(values, axis=-1, keepdims=True)
    spread = jnp.mean(center * center, axis=-1, keepdims=True)
    return center * lax.rsqrt(spread + 1e-05) * multiplier + addend


def span_labels(positions, starts):
    inside = (positions[:, None] >= starts[None, :]) & (positions[:, None] < starts[None, :] + SPAN)
    labels = jnp.arange(1, starts.shape[0] + 1, dtype=jnp.int32)
    return jnp.sum(jnp.where(inside, labels[None, :], 0), axis=1)


def allowed_mask(offset, row_count, length, starts):
    row_pos = offset + jnp.arange(row_count, dtype=jnp.int32)
    col_pos = jnp.arange(length, dtype=jnp.int32)
    row_span = span_labels(row_pos, starts)
    col_span = span_labels(col_pos, starts)
    causal = col_pos[None, :] <= row_pos[:, None]
    joined = (row_span[:, None] == col_span[None, :]) & (row_span[:, None] > 0)
    return causal | joined


def masked_scores(query_block, key_rows, offset, length, starts, factor):
    scores = (
        jnp.einsum("qhd,khd->hqk", query_block, key_rows, preferred_element_type=jnp.float32)
        * factor
    )
    allowed = allowed_mask(offset, BLOCK, length, starts)
    return jnp.where(allowed[None], scores, -1000000000.0)


def attend(queries, key_rows, value_rows, starts):
    length, heads, width = queries.shape
    factor = width ** (-0.5)

    def one_block(block_number):
        offset = block_number * BLOCK
        query_block = lax.dynamic_slice_in_dim(queries, offset, BLOCK, 0)
        scores = masked_scores(query_block, key_rows, offset, length, starts, factor)
        peak = jnp.max(scores, axis=-1, keepdims=True)
        raised = jnp.exp(scores - peak)
        totals = jnp.sum(raised, axis=-1, keepdims=True)
        weights_low = (raised / totals).astype(jnp.bfloat16)
        blended = jnp.einsum(
            "hqk,khd->qhd", weights_low, value_rows, preferred_element_type=jnp.float32
        )
        return (
            blended.astype(jnp.bfloat16).reshape(BLOCK, heads * width),
            (peak + jnp.log(totals))[..., 0],
        )

    blended, log_sums = lax.map(one_block, jnp.arange(length // BLOCK, dtype=jnp.int32))
    return (blended.reshape(length, heads * width), log_sums)


def attend_back(queries, key_rows, value_rows, grad_mix, log_sums, starts):
    length, heads, width = queries.shape
    factor = width ** (-0.5)

    def one_block(carry, inputs_pair):
        key_grad, value_grad = carry
        block_number, block_sums = inputs_pair
        offset = block_number * BLOCK
        query_block = lax.dynamic_slice_in_dim(queries, offset, BLOCK, 0)
        grad_block = lax.dynamic_slice_in_dim(grad_mix, offset, BLOCK, 0)
        scores = masked_scores(query_block, key_rows, offset, length, starts, factor)
        weights = jnp.exp(scores - block_sums[:, :, None])
        dots = jnp.einsum(
            "qhd,khd->hqk", grad_block, value_rows, preferred_element_type=jnp.float32
        )
        inner = jnp.sum(weights * dots, axis=-1, keepdims=True)
        slopes = (weights * (dots - inner) * factor).astype(jnp.bfloat16)
        query_grad = jnp.einsum(
            "hqk,khd->qhd", slopes, key_rows, preferred_element_type=jnp.float32
        )
        key_grad = key_grad + jnp.einsum(
            "hqk,qhd->khd", slopes, query_block, preferred_element_type=jnp.float32
        )
        value_grad = value_grad + jnp.einsum(
            "hqk,qhd->khd",
            weights.astype(jnp.bfloat16),
            grad_block,
            preferred_element_type=jnp.float32,
        )
        return ((key_grad, value_grad), query_grad)

    initial = jnp.zeros(key_rows.shape, jnp.float32)
    numbers = jnp.arange(length // BLOCK, dtype=jnp.int32)
    (key_grad, value_grad), query_grad = lax.scan(
        one_block, (initial, initial), (numbers, log_sums)
    )
    return (query_grad.reshape(length, heads, width), key_grad, value_grad)


def fetch_frozen(first, second):
    return (
        lax.all_gather(first, "dp", axis=0, tiled=True),
        lax.all_gather(second, "dp", axis=1, tiled=True),
    )


def enter_rows(normed, reduced):
    return (
        lax.all_gather(normed, "tensor", axis=0, tiled=True),
        lax.all_gather(reduced, "tensor", axis=0, tiled=True),
    )


def leave_rows(partial_value, reduced):
    return (
        lax.psum_scatter(partial_value, "tensor", scatter_dimension=0, tiled=True),
        lax.psum_scatter(reduced, "tensor", scatter_dimension=0, tiled=True),
    )


def enter_grads(branch, reduced):
    return (
        lax.all_gather(branch, "tensor", axis=0, tiled=True),
        lax.all_gather(reduced, "tensor", axis=0, tiled=True),
    )


def leave_grads(partial_value, reduced):
    return (
        lax.psum_scatter(partial_value, "tensor", scatter_dimension=0, tiled=True),
        lax.psum_scatter(reduced, "tensor", scatter_dimension=0, tiled=True),
    )


def per_device(
    tokens,
    w_qkv,
    w_out,
    w_up,
    w_down,
    ln1_gain,
    ln1_bias,
    ln2_gain,
    ln2_bias,
    a_qkv,
    b_qkv,
    a_out,
    b_out,
    a_up,
    b_up,
    a_down,
    b_down,
    adapter_idx,
    pic_start,
    cotangent,
):
    selection = adapter_idx[0]
    starts = pic_start[0]

    def chosen(stacked, which_one):
        return lax.dynamic_index_in_dim(stacked, selection[which_one], 0, keepdims=False)

    low_qkv_in = chosen(a_qkv, 0)
    rank = low_qkv_in.shape[1]
    low_qkv_out = chosen(b_qkv, 0).reshape(rank, -1)
    low_out_in = chosen(a_out, 1)
    low_out_out = chosen(b_out, 1)
    low_up_in = chosen(a_up, 2)
    low_up_out = chosen(b_up, 2)
    low_down_in = chosen(a_down, 3)
    low_down_out = chosen(b_down, 3)
    heads_here = low_out_in.shape[0] // HD

    def run_forward(own_tokens, frozen):
        qkv_rows, out_rows, up_rows, down_rows = frozen
        qkv_full, out_full = fetch_frozen(qkv_rows, out_rows)
        qkv_flat = qkv_full.reshape(qkv_full.shape[0], -1)
        own_float = own_tokens.astype(jnp.float32)
        normed = layer_norm(own_float, ln1_gain, ln1_bias).astype(jnp.bfloat16)
        reduced = matmul(normed, low_qkv_in).astype(jnp.bfloat16)
        normed_all, reduced_all = enter_rows(normed, reduced)
        length = normed_all.shape[0]
        project = (matmul(normed_all, qkv_flat) + matmul(reduced_all, low_qkv_out)).astype(
            jnp.bfloat16
        )
        split = project.reshape(length, 3, heads_here, HD)
        blended, log_sums = attend(split[:, 0], split[:, 1], split[:, 2], starts)
        main_part, low_part = leave_rows(matmul(blended, out_full), matmul(blended, low_out_in))
        low_out_val = low_part.astype(jnp.bfloat16)
        residual = own_float + main_part + matmul(low_out_val, low_out_out)
        up_full, down_full = fetch_frozen(up_rows, down_rows)
        normed_two = layer_norm(residual, ln2_gain, ln2_bias).astype(jnp.bfloat16)
        reduced_two = matmul(normed_two, low_up_in).astype(jnp.bfloat16)
        normed_two_all, reduced_two_all = enter_rows(normed_two, reduced_two)
        pre_act = matmul(normed_two_all, up_full) + matmul(reduced_two_all, low_up_out)
        hidden = jax.nn.gelu(pre_act, approximate=True).astype(jnp.bfloat16)
        main_two, low_two = leave_rows(matmul(hidden, down_full), matmul(hidden, low_down_in))
        low_down_val = low_two.astype(jnp.bfloat16)
        output = residual + main_two + matmul(low_down_val, low_down_out)
        kept_state = (
            qkv_flat,
            out_full,
            up_full,
            down_full,
            normed,
            reduced_all,
            split,
            blended,
            log_sums,
            low_out_val,
            residual,
            normed_two,
            reduced_two_all,
            pre_act,
            hidden,
            low_down_val,
        )
        return (output, kept_state)

    frozen = (w_qkv, w_out, w_up, w_down)
    output, kept_state = run_forward(tokens, frozen)
    (
        qkv_flat,
        out_full,
        up_full,
        down_full,
        normed,
        reduced_all,
        split,
        blended,
        log_sums,
        low_out_val,
        residual,
        normed_two,
        reduced_two_all,
        pre_act,
        hidden,
        low_down_val,
    ) = kept_state
    cot_float = cotangent.astype(jnp.float32)
    grad_low_down = against(cotangent, low_down_out).astype(jnp.bfloat16)
    grad_b_down_here = contract_rows(low_down_val, cotangent)
    cot_all, grad_low_down_all = enter_grads(cotangent, grad_low_down)
    grad_hidden = against(cot_all, down_full) + against(grad_low_down_all, low_down_in)
    grad_a_down_here = contract_rows(hidden, grad_low_down_all)
    gelu_pull = jax.vjp(lambda inner_val: jax.nn.gelu(inner_val, approximate=True), pre_act)[1]
    grad_pre = gelu_pull(grad_hidden)[0].astype(jnp.bfloat16)
    grad_b_up_here = contract_rows(reduced_two_all, grad_pre)
    grad_normed_two, grad_reduced_two = leave_grads(
        against(grad_pre, up_full), against(grad_pre, low_up_out)
    )
    grad_low_up = grad_reduced_two.astype(jnp.bfloat16)
    grad_a_up_here = contract_rows(normed_two, grad_low_up)
    grad_normed_two = grad_normed_two + against(grad_low_up, low_up_in)
    norm_pull_two = jax.vjp(lambda inner_val: layer_norm(inner_val, ln2_gain, ln2_bias), residual)[
        1
    ]
    grad_resid = cot_float + norm_pull_two(grad_normed_two)[0]
    branch_low = grad_resid.astype(jnp.bfloat16)
    grad_low_out = against(branch_low, low_out_out).astype(jnp.bfloat16)
    grad_b_out_here = contract_rows(low_out_val, branch_low)
    branch_all, grad_low_out_all = enter_grads(branch_low, grad_low_out)
    grad_mix = (against(branch_all, out_full) + against(grad_low_out_all, low_out_in)).astype(
        jnp.bfloat16
    )
    grad_a_out_here = contract_rows(blended, grad_low_out_all)
    length = grad_mix.shape[0]
    query_grad, key_grad, value_grad = attend_back(
        split[:, 0],
        split[:, 1],
        split[:, 2],
        grad_mix.reshape(length, heads_here, HD),
        log_sums,
        starts,
    )
    grad_qkv = (
        jnp.stack([query_grad, key_grad, value_grad], axis=1)
        .reshape(length, -1)
        .astype(jnp.bfloat16)
    )
    grad_b_qkv_here = contract_rows(reduced_all, grad_qkv)
    grad_normed_one, grad_reduced_one = leave_grads(
        against(grad_qkv, qkv_flat), against(grad_qkv, low_qkv_out)
    )
    grad_low_qkv = grad_reduced_one.astype(jnp.bfloat16)
    grad_a_qkv_here = contract_rows(normed, grad_low_qkv)
    grad_normed_one = grad_normed_one + against(grad_low_qkv, low_qkv_in)
    norm_pull_one = jax.vjp(
        lambda inner_val: layer_norm(inner_val, ln1_gain, ln1_bias), tokens.astype(jnp.float32)
    )[1]
    grad_input = grad_resid + norm_pull_one(grad_normed_one)[0]
    slots = a_qkv.shape[0]

    def spread(gradient, which_one):
        onehot = (jnp.arange(slots, dtype=jnp.int32) == selection[which_one]).astype(jnp.float32)
        return onehot.reshape((slots,) + (1,) * gradient.ndim) * gradient[None]

    sharded = (
        lax.psum(spread(grad_b_qkv_here.reshape(rank, 3, -1), 0).astype(jnp.bfloat16), "dp").astype(
            jnp.float32
        ),
        lax.psum(spread(grad_a_out_here, 1).astype(jnp.bfloat16), "dp").astype(jnp.float32),
        lax.psum(spread(grad_b_up_here, 2).astype(jnp.bfloat16), "dp").astype(jnp.float32),
        lax.psum(spread(grad_a_down_here, 3).astype(jnp.bfloat16), "dp").astype(jnp.float32),
    )
    shared = lax.psum(
        (
            spread(grad_a_qkv_here, 0),
            spread(grad_b_out_here, 1),
            spread(grad_a_up_here, 2),
            spread(grad_b_down_here, 3),
        ),
        ("dp", "tensor"),
    )
    return (
        output.astype(jnp.bfloat16),
        grad_input,
        shared[0],
        sharded[0],
        sharded[1],
        shared[1],
        shared[2],
        sharded[2],
        sharded[3],
        shared[3],
    )


SPREAD_CHUNKS = 1
LOG2E = math.log2(math.e)
MASKED = -1e30
MIB = 1 << 20
VMEM = 62 * MIB
BF = jnp.bfloat16
F32 = jnp.float32
MESH = pl.DeviceIdType.MESH


def nt(a, b):
    return lax.dot_general(a, b, (((1,), (1,)), ((), ())), preferred_element_type=F32)


def nn(a, b):
    return lax.dot_general(a, b, (((1,), (0,)), ((), ())), preferred_element_type=F32)


def tn(a, b):
    return lax.dot_general(a, b, (((0,), (0,)), ((), ())), preferred_element_type=F32)


def last_key(starts_ref, pos):
    lim = pos
    for n in range(starts_ref.shape[0]):
        first = starts_ref[n]
        lim = jnp.where((pos >= first) & (pos < first + SPAN), first + SPAN - 1, lim)
    return lim


def head_parts(x):
    lane = lax.broadcasted_iota(jnp.int32, x.shape, 1)
    zero = jnp.zeros_like(x)
    return jnp.where(lane < HD, x, zero), jnp.where(lane >= HD, x, zero)


def cost(flops, moved):
    return pl.CostEstimate(flops=int(flops), bytes_accessed=int(moved), transcendentals=0)


def pair_core():
    dp, t = lax.axis_index("dp"), lax.axis_index("tensor")
    b = dp % 2
    return b, (dp + 1 - 2 * b, t)


def greet_core(sib):
    barrier = pltpu.get_barrier_semaphore()
    pl.semaphore_signal(barrier, inc=1, device_id=sib, device_id_type=MESH)
    pl.semaphore_wait(barrier, 1)


def to_core(src, dst, sems, n, sib):
    return pltpu.make_async_remote_copy(
        src_ref=src, dst_ref=dst, send_sem=sems.at[0, n], recv_sem=sems.at[1, n],
        device_id=sib, device_id_type=MESH,
    )


def attend_kernel(
    starts_ref, q_ref, k_ref, v_ref, o_ref, lse_ref, mix_ref, vt_ref, send_ref, sems, own_sems
):
    p, qi = pl.program_id(0), pl.program_id(1)
    pairs = pl.num_programs(0)
    bq = bk = k_ref.shape[1]
    scale = LOG2E * HD ** -0.5
    b, sib = pair_core()
    pl.when((p == 0) & (qi == 0))(lambda: greet_core(sib))

    @pl.when(qi == 0)
    def _():
        for n in range(k_ref.shape[0]):
            vt_ref[:, n * bk : (n + 1) * bk] = jnp.transpose(v_ref[n])

    qs = head_parts(q_ref[...])
    base = qi * bq
    lim = last_key(starts_ref, base + lax.broadcasted_iota(jnp.int32, (1, bq), 1))

    sub = 256
    qt = [jnp.transpose(x) for x in qs]

    def step(masked, j, carry):
        off = pl.multiple_of(j * bk, bk)
        state = list(carry)
        turns = [(h, n) for n in range(bk // sub) for h in range(2)]

        def first(n):
            return max(0, n * sub - SPAN) // SPAN * SPAN if masked else 0

        def scores(h, n):
            at = first(n)
            s = nn(k_ref[j, n * sub : (n + 1) * sub, :], qt[h][:, at:])
            if masked:
                ok = off + n * sub + lax.broadcasted_iota(jnp.int32, s.shape, 0) <= lim[:, at:]
                s = jnp.where(ok, s, MASKED)
            return s

        def take(h, n, s):
            at = first(n)
            m, l, acc = (x[:, at:] for x in state[h])
            top = jnp.maximum(m, jnp.max(s, axis=0, keepdims=True))
            w = jnp.exp2((s - top) * scale)
            al = jnp.exp2((m - top) * scale)
            l = al * l + jnp.sum(w, axis=0, keepdims=True)
            keys = pl.ds(pl.multiple_of(off + n * sub, sub), sub)
            acc = acc * al + nn(vt_ref[h * HD : (h + 1) * HD, keys], w.astype(BF))
            new = top, l, acc
            if at:
                new = [jnp.concatenate([x[:, :at], y], axis=1) for x, y in zip(state[h], new)]
            state[h] = tuple(new)

        ahead = [scores(*turn) for turn in turns[:4]]
        for i, turn in enumerate(turns):
            if i + 4 < len(turns):
                ahead.append(scores(*turns[i + 4]))
            take(*turn, ahead[i])
        return tuple(state)

    init = (jnp.full((1, bq), MASKED, F32), jnp.zeros((1, bq), F32), jnp.zeros((HD, bq), F32))
    carry = lax.fori_loop(0, qi, functools.partial(step, False), (init, init))
    carry = step(True, qi, carry)
    mixed = jnp.transpose(jnp.concatenate([carry[h][2] / carry[h][1] for h in range(2)], axis=0)).astype(BF)
    o_ref[...] = mixed
    for h in range(2):
        lse_ref[0, h : h + 1, :] = carry[h][0] * scale + jnp.log2(carry[h][1])

    def place(n, core):
        return mix_ref.at[core, :, pl.ds(pl.multiple_of(n * 2 * HD, 2 * HD), 2 * HD)]

    def far(n):
        return to_core(send_ref.at[n, 1], place(n, b), sems, n, sib)

    def own(n):
        return pltpu.make_async_copy(send_ref.at[n, 0], place(n, b), own_sems.at[n])

    @pl.when(qi == b)
    def _():
        send_ref[p, 0] = mixed
        own(p).start()

    @pl.when(qi != b)
    def _():
        send_ref[p, 1] = mixed
        far(p).start()

    @pl.when((p == pairs - 1) & (qi == pl.num_programs(1) - 1))
    def _():
        for n in range(send_ref.shape[0]):
            own(n).wait()
            far(n).wait()


def attend_rows(starts, qkv, ident):
    parts, _, rows, width = qkv.shape
    pairs = width // (2 * HD)
    length = parts * rows

    def all_parts(which):
        return pl.BlockSpec((parts, None, rows, 2 * HD), lambda p, i, s: (0, which, 0, p))

    return pl.pallas_call(
        attend_kernel,
        out_shape=(
            jax.ShapeDtypeStruct((parts, rows, width), BF),
            jax.ShapeDtypeStruct((pairs, 2, length), F32),
            jax.ShapeDtypeStruct((parts, rows, width), BF),
        ),
        grid_spec=pltpu.PrefetchScalarGridSpec(
            num_scalar_prefetch=1,
            grid=(pairs, parts),
            in_specs=[
                pl.BlockSpec((None, None, rows, 2 * HD), lambda p, i, s: (i, 0, 0, p)),
                all_parts(1),
                all_parts(2),
            ],
            out_specs=[
                pl.BlockSpec((None, rows, 2 * HD), lambda p, i, s: (i, 0, p)),
                pl.BlockSpec((1, 2, rows), lambda p, i, s: (p, 0, i)),
                pl.BlockSpec(memory_space=pl.ANY),
            ],
            scratch_shapes=[
                pltpu.VMEM((2 * HD, length), BF),
                pltpu.VMEM((pairs, 2, rows, 2 * HD), BF),
                pltpu.SemaphoreType.DMA((2, pairs)),
                pltpu.SemaphoreType.DMA((pairs,)),
            ],
        ),
        compiler_params=pltpu.CompilerParams(
            dimension_semantics=("arbitrary", "arbitrary"), vmem_limit_bytes=VMEM,
            collective_id=ident, has_side_effects=True,
        ),
        cost_estimate=cost(24 * length * length * width, 16 * length * width),
        name="attend",
    )(starts, qkv, qkv, qkv)


def attend_back_kernel(
    bq, bk, starts_ref, q_ref, k_ref, v_ref, o_ref, do_ref, lse_ref, all_ref,
    kt_ref, dqt_ref, delta_ref, qm_ref, dom_ref, dk_ref, dv_ref, send_ref, sems, own_sems, qt_ref, dot_ref,
):
    p_now = pl.program_id(0)
    b, sib = pair_core()
    pl.when(p_now == 0)(lambda: greet_core(sib))
    g_ref = send_ref.at[p_now]
    parts, rows, _ = q_ref.shape
    length = parts * rows
    scale = LOG2E * HD ** -0.5
    nq = length // bq
    per = rows // bq
    dqt_ref[...] = jnp.zeros_like(dqt_ref)
    for i in range(nq):
        part, at = i // per, slice((i % per) * bq, (i % per + 1) * bq)
        flat = slice(i * bq, (i + 1) * bq)
        kt_ref[:, flat] = jnp.transpose(k_ref[part, at, :])
        do = do_ref[part, at, :]
        for h, (q_h, do_h) in enumerate(zip(head_parts(q_ref[part, at, :]), head_parts(do))):
            qm_ref[h, flat, :] = q_h
            dom_ref[h, flat, :] = do_h
            qt_ref[h, :, flat] = jnp.transpose(q_h)
            dot_ref[h, :, flat] = jnp.transpose(do_h)
        prod = jnp.transpose(do.astype(F32) * o_ref[part, at, :].astype(F32))
        for h in range(2):
            delta_ref[h : h + 1, flat] = jnp.sum(prod[h * HD : (h + 1) * HD], axis=0, keepdims=True)

    half = bk // 2

    def tile(masked, keys, vals, koff, nk, qoff, nq_):
        at = pl.ds(qoff, nq_)
        dk = dv = None
        if masked:
            lim = last_key(starts_ref, qoff + lax.broadcasted_iota(jnp.int32, (1, nq_), 1))
            ok = koff + lax.broadcasted_iota(jnp.int32, (nk, nq_), 0) <= lim
        heads = range(2)
        ss = [nn(keys, qt_ref[h, :, at]) for h in heads]
        dps = [nn(vals, dot_ref[h, :, at]) for h in heads]
        ps = [jnp.exp2(ss[h] * scale - lse_ref[0, h : h + 1, at]) for h in heads]
        if masked:
            ps = [jnp.where(ok, p, 0.0) for p in ps]
        dss = [(ps[h] * (dps[h] - delta_ref[h : h + 1, at])).astype(BF) for h in heads]
        pbs = [p.astype(BF) for p in ps]
        dv = nn(pbs[0], dom_ref[0, at, :]) + nn(pbs[1], dom_ref[1, at, :])
        dk = nn(dss[0], qm_ref[0, at, :]) + nn(dss[1], qm_ref[1, at, :])
        for h in heads:
            head = slice(h * HD, (h + 1) * HD)
            dqt_ref[head, at] += nn(kt_ref[head, pl.ds(koff, nk)], dss[h])
        return dk, dv

    @pl.loop(0, length // bk)
    def _(j):
        koff = pl.multiple_of(j * bk, bk)
        part = j // (rows // bk)
        inside = pl.multiple_of((j % (rows // bk)) * bk, bk)
        keys = k_ref[part, pl.ds(inside, bk), :]
        vals = v_ref[part, pl.ds(inside, bk), :]

        def step(i, carry):
            dk, dv = tile(False, keys, vals, koff, bk, pl.multiple_of(i * bq, bq), bq)
            return carry[0] + dk, carry[1] + dv

        zero = jnp.zeros((bk, 2 * HD), F32)
        dk, dv = lax.fori_loop(j + 1, nq, step, (zero, zero))
        own = tile(True, keys, vals, koff, bk, koff, bk)
        dk_ref[...] = dk + own[0]
        dv_ref[...] = dv + own[1]

        @pl.when(j % (rows // bk) > 0)
        def _():
            before = pl.multiple_of(jnp.maximum(koff - half, 0), half)
            got = tile(True, keys[:half], vals[:half], koff, half, before, half)
            dk_ref[:half, :] += got[0]
            dv_ref[:half, :] += got[1]

        g_ref[part, 1, pl.ds(inside, bk), :] = (dk_ref[...] * HD ** -0.5).astype(BF)
        g_ref[part, 2, pl.ds(inside, bk), :] = dv_ref[...].astype(BF)

    for i in range(nq):
        part, at = i // per, slice((i % per) * bq, (i % per + 1) * bq)
        dq = jnp.transpose(dqt_ref[:, i * bq : (i + 1) * bq])
        g_ref[part, 0, at, :] = (dq * HD ** -0.5).astype(BF)

    def place(n):
        return all_ref.at[b, :, :, pl.ds(pl.multiple_of(n * 2 * HD, 2 * HD), 2 * HD)]

    def far(n):
        return to_core(send_ref.at[n, 1 - b], place(n), sems, n, sib)

    def own(n):
        return pltpu.make_async_copy(send_ref.at[n, b], place(n), own_sems.at[n])

    far(p_now).start()
    own(p_now).start()

    @pl.when(p_now == pl.num_programs(0) - 1)
    def _():
        for n in range(send_ref.shape[0]):
            own(n).wait()
            far(n).wait()


def attend_rows_back(starts, qkv, mixed, grad_mix, lse, ident):
    parts, _, rows, width = qkv.shape
    pairs = width // (2 * HD)
    length = parts * rows
    bq = bk = max(min(512, rows), 2 * SPAN)

    def one(which):
        return pl.BlockSpec((parts, None, rows, 2 * HD), lambda p, s: (0, which, 0, p))

    flat = pl.BlockSpec((parts, rows, 2 * HD), lambda p, s: (0, 0, p))
    return pl.pallas_call(
        functools.partial(attend_back_kernel, bq, bk),
        out_shape=jax.ShapeDtypeStruct((parts, 3, rows, width), BF),
        grid_spec=pltpu.PrefetchScalarGridSpec(
            num_scalar_prefetch=1,
            grid=(pairs,),
            in_specs=[one(0), one(1), one(2), flat, flat,
                      pl.BlockSpec((1, 2, length), lambda p, s: (p, 0, 0))],
            out_specs=pl.BlockSpec(memory_space=pl.ANY),
            scratch_shapes=[
                pltpu.VMEM((2 * HD, length), BF),
                pltpu.VMEM((2 * HD, length), F32),
                pltpu.VMEM((2, length), F32),
                pltpu.VMEM((2, length, 2 * HD), BF),
                pltpu.VMEM((2, length, 2 * HD), BF),
                pltpu.VMEM((bk, 2 * HD), F32),
                pltpu.VMEM((bk, 2 * HD), F32),
                pltpu.VMEM((pairs, parts, 3, rows, 2 * HD), BF),
                pltpu.SemaphoreType.DMA((2, pairs)),
                pltpu.SemaphoreType.DMA((pairs,)),
                pltpu.VMEM((2, 2 * HD, length), BF),
                pltpu.VMEM((2, 2 * HD, length), BF),
            ],
        ),
        compiler_params=pltpu.CompilerParams(
            dimension_semantics=("arbitrary",), vmem_limit_bytes=VMEM,
            collective_id=ident, has_side_effects=True,
        ),
        cost_estimate=cost(40 * length * length * width, 24 * length * width),
        name="attend_back",
    )(starts, qkv, qkv, qkv, mixed, grad_mix, lse)


def stats(x):
    center = x - jnp.mean(x, axis=-1, keepdims=True)
    return center, lax.rsqrt(jnp.mean(center * center, axis=-1, keepdims=True) + 1e-05)


def norm_back(x, gain, grad):
    center, r = stats(x)
    n = center * r
    e = grad * gain
    return r * (e - jnp.mean(e, axis=-1, keepdims=True) - n * jnp.mean(e * n, axis=-1, keepdims=True))


def row_loop(rows, chunk, body):
    if chunk == rows:
        body(slice(None))
        return

    @pl.loop(0, rows // chunk)
    def _(i):
        body(pl.ds(pl.multiple_of(i * chunk, chunk), chunk))


def qkv_kernel(
    tok_ref, gain_ref, bias_ref, low_in_ref, w_ref, low_up_ref, norm_ref, low_ref, all_ref,
    send_ref, sems, own_sems,
):
    rows = tok_ref.shape[0]
    side, j = pl.program_id(0), pl.program_id(1)
    b, sib = pair_core()

    @pl.when((side == 0) & (j == 0))
    def _():
        def body(at):
            center, r = stats(tok_ref[at, :].astype(F32))
            normed = (center * r * gain_ref[...] + bias_ref[...]).astype(BF)
            norm_ref[at, :] = normed
            low_ref[at, :] = nt(normed, low_in_ref[...]).astype(BF)

        row_loop(rows, 256, body)
        greet_core(sib)

    w = w_ref[...].reshape(norm_ref.shape[1], -1)
    y = nn(norm_ref[...], w) + nn(low_ref[...], low_up_ref[...])
    send_ref[side, j] = y.astype(BF)

    def far(n):
        return to_core(send_ref.at[0, n], all_ref.at[b, n], sems, n, sib)

    def own(n):
        return pltpu.make_async_copy(send_ref.at[1, n], all_ref.at[b, n], own_sems.at[n])

    pl.when(side == 0)(lambda: far(j).start())
    pl.when(side == 1)(lambda: own(j).start())

    @pl.when((side == 1) & (j == 2))
    def _():
        for n in range(3):
            own(n).wait()
            far(n).wait()


def whole(shape):
    return pl.BlockSpec(shape, lambda *_: (0,) * len(shape))


def project_qkv(tok, gain, bias, low_in, w, low_up, ident):
    rows, features = tok.shape
    shards, groups, _, part, width = w.shape
    rank = low_in.shape[0]

    def heads(side):
        b = lax.axis_index("dp") % 2
        return jnp.where(side == 0, 1 - b, b)

    return pl.pallas_call(
        qkv_kernel,
        out_shape=(
            jax.ShapeDtypeStruct((rows, features), BF),
            jax.ShapeDtypeStruct((rows, rank), BF),
            jax.ShapeDtypeStruct((groups, 3, rows, width), BF),
        ),
        grid=(groups, 3),
        in_specs=[
            whole((rows, features)), whole((1, features)), whole((1, features)),
            whole((rank, features)),
            pl.BlockSpec((shards, None, None, part, width), lambda g, j: (0, heads(g), j, 0, 0)),
            pl.BlockSpec((None, rank, width), lambda g, j: (heads(g), 0, j)),
        ],
        out_specs=[
            whole((rows, features)), whole((rows, rank)), pl.BlockSpec(memory_space=pl.ANY),
        ],
        scratch_shapes=[
            pltpu.VMEM((groups, 3, rows, width), BF),
            pltpu.SemaphoreType.DMA((2, 3)),
            pltpu.SemaphoreType.DMA((3,)),
        ],
        compiler_params=pltpu.CompilerParams(
            dimension_semantics=("arbitrary", "arbitrary"), vmem_limit_bytes=VMEM,
            collective_id=ident, has_side_effects=True,
        ),
        cost_estimate=cost(4 * rows * features * groups * 3 * width, 4 * rows * groups * 3 * width),
        name="project_qkv",
    )(tok, gain, bias, low_in, w, low_up)


def qkv_back_kernel(
    planes, g_ref, w_any, low_up_ref, low_in_ref, norm_ref, low_ref, tok_ref, gain_ref, resid_ref, tag_ref,
    grad_ref, late_ref, far_ref,
    w_ref, own_ref, glow_ref, send_ref, w_sem, swap_sem, *sems,
):
    s = pl.program_id(0)
    groups, _, rows, width = g_ref.shape
    chunk, features = tok_ref.shape
    parts = rows // chunk
    gather = Gather(own_ref, late_ref, *sems, planes)
    moves = gather.c != gather.t
    partner = (gather.place(gather.z, gather.x, gather.t), gather.c)
    blocks = [(g, j) for g in range(groups) for j in range(3)]

    def load_w():
        return pltpu.make_async_copy(w_any, w_ref, w_sem)

    def swap(n):
        return to_core(
            send_ref.at[n], far_ref.at[pl.ds(n * chunk, chunk)], swap_sem, n, partner
        )

    @pl.when(s == 0)
    def _():
        load_w().start()
        gather.greet([(moves, partner)])
        low = low_ref[...]
        glow = None
        for n, (g, j) in enumerate(blocks):
            part = g_ref[g, j]
            more = nt(part, low_up_ref[g, :, j * width : (j + 1) * width])
            glow = more if glow is None else glow + more
            own_ref[n] = tn(low, part).astype(BF)
        glow = glow.astype(BF)
        glow_ref[...] = glow
        y = tn(glow, norm_ref[...]).astype(BF)
        for n in range(features // width):
            own_ref[len(blocks) + n] = y[:, n * width : (n + 1) * width]
        own_ref[own_ref.shape[0] - 1] = tag_ref[...]
        gather.round(0)

    pl.when(s == 1)(lambda: load_w().wait())

    @pl.when(s > 0)
    def _():
        at = pl.ds(pl.multiple_of((s - 1) * chunk, chunk), chunk)
        total = nn(glow_ref[at, :], low_in_ref[...])
        for g, j in blocks:
            total = total + nt(g_ref[g, j, at, :], w_ref[:, g, j].reshape(features, width))
        grad = resid_ref[...] + norm_back(tok_ref[...].astype(F32), gain_ref[...], total)
        grad_ref[...] = grad
        send_ref[s - 1] = grad.astype(BF)

        @pl.when(moves)
        def _():
            swap(s - 1).start()

    for k in range(1, gather.rounds):
        pl.when(s == min(k, parts))(lambda k=k: gather.round(k))

    @pl.when(s == parts)
    def _():
        gather.finish()

        @pl.when(moves)
        def _():
            for n in range(parts):
                swap(n).wait()


def project_qkv_back(grad, w, low_up, low_in, normed, low, tok, gain, resid, tag, ident):
    rows, features = tok.shape
    shards, groups, _, part, width = w.shape
    rank = low_in.shape[0]
    planes = shards // 4
    parts = 4
    chunk = rows // parts
    late = (groups * 3 + features // width + 1, rank, width)
    anywhere = pl.BlockSpec(memory_space=pl.ANY)

    def keep(shape):
        return pl.BlockSpec(shape, lambda s: (0,) * len(shape), pipeline_mode=pl.Buffered(1))

    some = pl.BlockSpec((chunk, features), lambda s: (jnp.maximum(s - 1, 0), 0))
    return pl.pallas_call(
        functools.partial(qkv_back_kernel, planes),
        out_shape=(
            jax.ShapeDtypeStruct((rows, features), F32),
            jax.ShapeDtypeStruct((shards, 2) + late, BF),
            jax.ShapeDtypeStruct((rows, features), BF),
        ),
        grid=(1 + parts,),
        in_specs=[
            keep(grad.shape), anywhere, keep((groups, rank, 3 * width)), keep((rank, features)),
            keep((rows, features)), keep((rows, rank)), some, keep((1, features)), some,
            keep((rank, width)),
        ],
        out_specs=[some, anywhere, anywhere],
        scratch_shapes=[
            pltpu.VMEM(w.shape, BF),
            pltpu.VMEM(late, BF),
            pltpu.VMEM((rows, rank), BF),
            pltpu.VMEM((parts, chunk, features), BF),
            pltpu.SemaphoreType.DMA,
            pltpu.SemaphoreType.DMA((2, parts)),
            *gather_sems(1, planes),
        ],
        compiler_params=pltpu.CompilerParams(
            dimension_semantics=("arbitrary",), vmem_limit_bytes=VMEM,
            collective_id=ident, has_side_effects=True,
        ),
        cost_estimate=cost(5 * rows * features * groups * 3 * width, 4 * rows * groups * 3 * width),
        name="project_qkv_back",
    )(grad, w, low_up, low_in, normed, low, tok, gain, resid, tag)


GELU = math.sqrt(2.0 / math.pi)


def gelu_and_slope(v):
    v2 = v * v
    half = 0.5 + 0.5 * jnp.tanh(v * (GELU + (GELU * 0.044715) * v2))
    hidden = v * half
    return hidden, half + hidden * (1.0 - half) * (2.0 * GELU + (6.0 * 0.044715 * GELU) * v2)


def middle_kernel(
    groups, nf,
    w_ref, sh_ref, wo_ref, sho_ref, tok_ref, mix_ref, cot_ref, gain_ref, bias_ref, rep_ref,
    out_ref, resid_ref, gr_ref, do_ref,
    acc_ref, norm_ref, hid_ref, slope_ref, lacc_ref, llow_ref, send_ref, sems, own_sem,
):
    rows, features = tok_ref.shape
    rank = sh_ref.shape[0]
    s = pl.program_id(0)
    b_out, a_up, b_down = rep_ref[0], rep_ref[1], rep_ref[2]
    co = wo_ref.shape[-1]
    up0, down0 = groups, groups + nf
    upb0, end0 = groups + 2 * nf, groups + 3 * nf
    b, sib = pair_core()
    pl.when(s == 0)(lambda: greet_core(sib))

    for g in range(groups):

        @pl.when(s == g)
        def _():
            part = mix_ref[g]
            y = nt(part, wo_ref[...].reshape(features, co))
            low = nt(part, sho_ref[...])
            if g == 0:
                resid_ref[...] = tok_ref[...].astype(F32) + y
                lacc_ref[...] = low
            else:
                resid_ref[...] += y
                lacc_ref[...] += low

    @pl.when(s == up0 - 1)
    def _():
        def body(at):
            low = lacc_ref[at, :].astype(BF)
            llow_ref[0, at, :] = low
            resid = resid_ref[at, :] + nn(low, b_out)
            resid_ref[at, :] = resid
            center, r = stats(resid)
            normed = (center * r * gain_ref[...] + bias_ref[...]).astype(BF)
            norm_ref[at, :] = normed
            llow_ref[1, at, :] = nt(normed, a_up).astype(BF)

        row_loop(rows, 256, body)
        llow_ref[3] = nt(cot_ref[...], b_down).astype(BF)
        acc_ref[...] = jnp.zeros_like(acc_ref)
        lacc_ref[...] = jnp.zeros_like(lacc_ref)

    @pl.when((s >= up0) & (s < down0))
    def _():
        f = s - up0
        w = w_ref[...].reshape(features, -1)

        chunks = [slice(n * 256, (n + 1) * 256) for n in range(rows // 256)]

        def scores(at):
            return nn(norm_ref[at, :], w) + nn(llow_ref[1, at, :], sh_ref[...])

        ahead = [scores(at) for at in chunks[:2]]
        for n, at in enumerate(chunks):
            if n + 2 < len(chunks):
                ahead.append(scores(chunks[n + 2]))
            hidden, slope = gelu_and_slope(ahead[n])
            hid_ref[f, at, :] = hidden.astype(BF)
            slope_ref[f, at, :] = slope.astype(BF)

    @pl.when((s >= down0) & (s < upb0))
    def _():
        f = s - down0
        w = w_ref[...].reshape(features, -1)
        sh = sh_ref[...]
        hidden = hid_ref[f]
        acc_ref[...] += nt(hidden, w)
        lacc_ref[...] += nt(hidden, sh)
        g_hidden = nn(cot_ref[...], w) + nn(llow_ref[3], sh)
        g_pre = (g_hidden * slope_ref[f].astype(F32)).astype(BF)
        slope_ref[f] = g_pre
        gr_ref[:rank, :] = tn(llow_ref[3], hidden).astype(BF)
        gr_ref[rank:, :] = tn(llow_ref[1], g_pre).astype(BF)

    @pl.when(s == upb0 - 1)
    def _():
        def body(at):
            low = lacc_ref[at, :].astype(BF)
            llow_ref[2, at, :] = low
            out_ref[at, :] = (resid_ref[at, :] + acc_ref[at, :] + nn(low, b_down)).astype(BF)

        row_loop(rows, 512, body)
        acc_ref[...] = jnp.zeros_like(acc_ref)
        lacc_ref[...] = jnp.zeros_like(lacc_ref)

    @pl.when((s >= upb0) & (s < end0))
    def _():
        f = s - upb0
        w = w_ref[...].reshape(features, -1)
        part = slope_ref[f]
        acc_ref[...] += nt(part, w)
        lacc_ref[...] += nt(part, sh_ref[...])

    @pl.when(s == end0 - 1)
    def _():
        gr_ref[:rank, :] = tn(llow_ref[2], cot_ref[...]).astype(BF)
        llow_ref[4] = lacc_ref[...].astype(BF)
        gr_ref[rank:, :] = tn(llow_ref[4], norm_ref[...]).astype(BF)

        def body(at):
            total = acc_ref[at, :] + nn(llow_ref[4, at, :], a_up)
            g = cot_ref[at, :].astype(F32) + norm_back(resid_ref[at, :], gain_ref[...], total)
            resid_ref[at, :] = g
            branch = g.astype(BF)
            norm_ref[at, :] = branch
            llow_ref[5, at, :] = nt(branch, b_out).astype(BF)

        row_loop(rows, 256, body)

    def far():
        return to_core(send_ref.at[0], do_ref.at[b], sems, 0, sib)

    def own():
        return pltpu.make_async_copy(send_ref.at[1], do_ref.at[b], own_sem)

    @pl.when(s >= end0)
    def _():
        turn = s - end0
        g = jnp.where(turn == 0, 1 - b, b)
        wo = wo_ref[...].reshape(features, co)
        y = nn(norm_ref[...], wo) + nn(llow_ref[5], sho_ref[...])
        send_ref[turn] = y.astype(BF)
        at = pl.ds(pl.multiple_of(g * co, co), co)
        gr_ref[:rank, at] = tn(llow_ref[5], mix_ref[g]).astype(BF)

    @pl.when(s == end0)
    def _():
        far().start()
        gr_ref[rank:, :] = tn(llow_ref[0], norm_ref[...]).astype(BF)

    @pl.when(s == end0 + 1)
    def _():
        own().start()
        own().wait()
        far().wait()


def middle(w, shared, tok, mix, cot, gain, bias, rep, ident):
    rows, features = tok.shape
    shards, groups, part, total = w.shape
    rank = rep.shape[1]
    co = mix.shape[2]
    ffw = (total - co) // 2
    c = features
    halves = ffw // c
    nf = groups * halves
    first = (shared.shape[2] - 2 * ffw) // c
    out_at, out_shared = 2 * ffw // co, (shared.shape[2] - 2 * ffw) // co - 1
    blocks = [(f // halves, f % halves) for f in range(nf)]
    up = [(t, h, h) for t, h in blocks]
    down_step = [(t, halves + h, halves + h) for t, h in blocks]
    shared_group = [t for t, _ in blocks]
    order = [up[0]] * groups + up + down_step + up + [up[-1]] * groups
    shared_of = [0] * groups + shared_group * 3 + [shared_group[-1]] * groups
    of_grad = [0] * (groups + nf) + list(range(nf)) + [nf + 1] * nf + [nf] * groups
    last = len(order) - groups
    anywhere = pl.BlockSpec(memory_space=pl.ANY)

    def group(s):
        b = lax.axis_index("dp") % 2
        return jnp.where(s < last, jnp.minimum(s, groups - 1), jnp.where(s == last, 1 - b, b))

    once = pl.Buffered(1)

    def keep(shape):
        return pl.BlockSpec(shape, lambda s, *_: (0,) * len(shape), pipeline_mode=once)

    def at(table_row):
        def index(s):
            got = table_row[0]
            for n in range(1, len(table_row)):
                if table_row[n] != table_row[n - 1]:
                    got = got + jnp.where(s >= n, table_row[n] - table_row[n - 1], 0)
            return got
        return index

    w_t, w_c = at([x[0] for x in order]), at([x[1] for x in order])
    s_t, s_c, gi = at(shared_of), at([x[2] for x in order]), at(of_grad)
    return pl.pallas_call(
        functools.partial(middle_kernel, groups, nf),
        out_shape=(
            jax.ShapeDtypeStruct((rows, features), BF),
            jax.ShapeDtypeStruct((rows, features), F32),
            jax.ShapeDtypeStruct((nf + 2, 2 * rank, c), BF),
            jax.ShapeDtypeStruct(mix.shape, BF),
        ),
        grid=(len(order),),
        in_specs=[
            pl.BlockSpec((shards, None, part, c), lambda s: (0, w_t(s), 0, w_c(s))),
            pl.BlockSpec((None, rank, c), lambda s: (s_t(s), 0, s_c(s) + first)),
            pl.BlockSpec((shards, None, part, co), lambda s: (0, group(s), 0, out_at)),
            pl.BlockSpec((None, rank, co), lambda s: (group(s), 0, out_shared)),
            keep((rows, features)), keep(mix.shape), keep((rows, features)),
            keep((1, features)), keep((1, features)), keep(rep.shape),
        ],
        out_specs=[
            keep((rows, features)), keep((rows, features)),
            pl.BlockSpec((None, 2 * rank, c), lambda s: (gi(s), 0, 0)), anywhere,
        ],
        scratch_shapes=[
            pltpu.VMEM((rows, features), F32),
            pltpu.VMEM((rows, features), BF),
            pltpu.VMEM((nf, rows, c), BF),
            pltpu.VMEM((nf, rows, c), BF),
            pltpu.VMEM((rows, rank), F32),
            pltpu.VMEM((6, rows, rank), BF),
            pltpu.VMEM(mix.shape, BF),
            pltpu.SemaphoreType.DMA((2, 1)),
            pltpu.SemaphoreType.DMA,
        ],
        compiler_params=pltpu.CompilerParams(
            dimension_semantics=("arbitrary",), vmem_limit_bytes=VMEM,
            collective_id=ident, has_side_effects=True,
        ),
        cost_estimate=cost(6 * rows * features * groups * total, 4 * features * groups * total),
        name="middle",
    )(w, shared, w, shared, tok, mix, cot, gain, bias, rep)


class Gather:
    def __init__(self, shard, full, out_sem, in_sem, own_sem, planes):
        self.shard, self.full, self.planes = shard, full, planes
        self.chunks = out_sem.shape[0]
        self.out_sem, self.in_sem, self.own_sem = out_sem, in_sem, own_sem
        self.rounds = planes + 2
        dp, t = lax.axis_index("dp"), lax.axis_index("tensor")
        z, x, c = dp // 4, (dp // 2) % 2, dp % 2
        self.dp, self.z, self.x, self.c, self.t = dp, z, x, c, t
        self.low, self.high = z > 0, z < planes - 1
        self.below = jnp.maximum(dp - 4, 0), t
        self.above = jnp.minimum(dp + 4, 4 * planes - 1), t
        self.near = dp, 1 - t
        self.across = self.place(z, 1 - x, c), t
        self.sib = self.place(z, x, 1 - c), t
        self.plan = [self.lay_out(k) for k in range(self.rounds)]

    def place(self, z, x, c):
        return z * 4 + x * 2 + c

    def greet(self, extra=()):
        barrier = pltpu.get_barrier_semaphore()

        def hello(who):
            pl.semaphore_signal(barrier, inc=1, device_id=who, device_id_type=MESH)

        for who in (self.near, self.across, self.sib):
            hello(who)
        count = 3
        for cond, who in ((self.low, self.below), (self.high, self.above)) + tuple(extra):
            pl.when(cond)(lambda who=who: hello(who))
            count = count + cond.astype(jnp.int32)
        pl.semaphore_wait(barrier, count)

    def piece(self, ref, n):
        if self.chunks == 1:
            return ref
        size = ref.shape[-2] // self.chunks
        every = (slice(None),) * (len(ref.shape) - 2)
        return ref.at[every + (pl.ds(n * size, size), slice(None))]

    def copy(self, n, at, who, sem, own=False):
        slot = self.piece(self.full.at[at[0], at[1]], n)
        return pltpu.make_async_remote_copy(
            src_ref=self.piece(self.shard, n) if own else slot, dst_ref=slot,
            send_sem=self.out_sem.at[n, sem],
            recv_sem=self.in_sem.at[n, at[0] * 2 + at[1]], device_id=who, device_id_type=MESH,
        )

    def arrive(self, n, at):
        self.copy(n, at, self.sib, 0).wait_recv()

    def own_copy(self, n):
        here = self.piece(self.full.at[self.dp, self.t], n)
        return pltpu.make_async_copy(self.piece(self.shard, n), here, self.own_sem.at[n])

    def lay_out(self, k):
        z, planes, t = self.z, self.planes, self.t
        events = []

        def ways(hops):
            if not 0 <= hops < planes:
                return []
            if hops == 0:
                return [(z, None, [(self.low, self.below, 0), (self.high, self.above, 1)])]
            up, down = z >= hops, z + hops < planes
            return [
                (z - hops, up, [(up & self.high, self.above, 1)]),
                (z + hops, down, [(down & self.low, self.below, 0)]),
            ]

        for n in range(self.chunks):
            for zz, cond, on in ways(k):
                sends = on + [(cond, self.across, 2), (cond, self.sib, 4)]
                if k == 0:
                    sends = [(None, self.near, 3)] + sends
                events.append((n, cond, (self.place(zz, self.x, self.c), t), k == 0, zz, sends))
            for zz, cond, on in ways(k - 1):
                sends = [(c, who, kind + 5) for c, who, kind in on]
                sends += [(cond, self.across, 7), (cond, self.sib, 8)]
                events.append((n, cond, (self.place(zz, self.x, self.c), 1 - t), False, zz, sends))
                far = self.place(zz, 1 - self.x, self.c), t
                events.append((n, cond, far, False, zz, [(cond, self.sib, 9)]))
            for zz, cond, _ in ways(k - 2):
                far = self.place(zz, 1 - self.x, self.c), 1 - t
                events.append((n, cond, far, False, zz, [(cond, self.sib, 10)]))
        return [
            (n, cond, where, own, [(c, who, kind * planes + zz) for c, who, kind in sends])
            for n, cond, where, own, zz, sends in events
        ]

    def when(self, cond, act):
        if cond is None:
            act()
        else:
            pl.when(cond)(act)

    def round(self, k):
        for n, cond, where, own, sends in self.plan[k]:
            if not own:
                self.when(cond, lambda n=n, where=where: self.arrive(n, where))
            for c, who, sem in sends:
                self.when(
                    c,
                    lambda n=n, where=where, who=who, sem=sem, own=own: self.copy(
                        n, where, who, sem, own
                    ).start(),
                )
            if own:
                self.own_copy(n).start()

    def finish(self):
        for n in range(self.chunks):
            for zz in range(self.planes):
                for x in (self.x, 1 - self.x):
                    for t in (self.t, 1 - self.t):
                        self.arrive(n, (self.place(zz, x, 1 - self.c), t))
            self.own_copy(n).wait()
        for events in self.plan:
            for n, _, where, own, sends in events:
                for c, who, sem in sends:
                    self.when(
                        c,
                        lambda n=n, where=where, who=who, sem=sem, own=own: self.copy(
                            n, where, who, sem, own
                        ).wait_send(),
                    )


def gather_sems(n, planes):
    return [
        pltpu.SemaphoreType.DMA((n, 11 * planes)),
        pltpu.SemaphoreType.DMA((n, 8 * planes)),
        pltpu.SemaphoreType.DMA((n,)),
    ]


def spread_kernel(n_all, kinds, planes, *refs):
    n_swap = len(kinds)
    shard = refs[:n_all]
    swap_in = refs[n_all : n_all + n_swap]
    full = refs[n_all + n_swap : 2 * n_all + n_swap]
    swap_out = refs[2 * n_all + n_swap : 2 * n_all + 2 * n_swap]
    *sems, swap_sem = refs[2 * n_all + 2 * n_swap :]
    g = Gather(shard[0], full[0], *sems, planes)
    moves = g.c != g.t
    keeps = jnp.logical_not(moves)
    partner = (g.place(g.z, g.x, g.t), g.c)
    g.greet([(moves, partner)])
    rules = {"partner": (moves, partner, moves), "near": (moves, g.near, keeps), "sibling": (keeps, g.sib, moves)}

    def swap_copy(n):
        return pltpu.make_async_remote_copy(
            src_ref=swap_in[n], dst_ref=swap_out[n], send_sem=swap_sem.at[n, 0],
            recv_sem=swap_sem.at[n, 1], device_id=rules[kinds[n]][1], device_id_type=MESH,
        )

    for n in range(n_swap):
        pl.when(rules[kinds[n]][0])(lambda n=n: swap_copy(n).start())
    for k in range(g.rounds):
        g.round(k)
    g.finish()
    for n in range(n_swap):
        pl.when(rules[kinds[n]][0])(lambda n=n: swap_copy(n).wait_send())
        pl.when(rules[kinds[n]][2])(lambda n=n: swap_copy(n).wait_recv())


def spread(gathered, handed, shards, ident):
    planes = shards // 4
    swapped = [a for a, _ in handed]
    n_all, n_swap = len(gathered), len(swapped)
    anywhere = pl.BlockSpec(memory_space=pl.ANY)
    return pl.pallas_call(
        functools.partial(spread_kernel, n_all, [k for _, k in handed], planes),
        out_shape=[jax.ShapeDtypeStruct((shards, 2) + a.shape, a.dtype) for a in gathered]
        + [jax.ShapeDtypeStruct(a.shape, a.dtype) for a in swapped],
        in_specs=[anywhere] * (n_all + n_swap),
        out_specs=[anywhere] * (n_all + n_swap),
        scratch_shapes=[
            *gather_sems(SPREAD_CHUNKS, planes),
            pltpu.SemaphoreType.DMA((max(n_swap, 1), 2)),
        ],
        compiler_params=pltpu.CompilerParams(collective_id=ident, has_side_effects=True),
        cost_estimate=cost(0, 60 * MIB),
        name="spread%d" % ident,
    )(*gathered, *swapped)


def sum_kernel(pieces, sel_ref, t_ref, *refs):
    ins, outs = refs[: len(refs) - len(pieces)], refs[len(refs) - len(pieces) :]
    step = pl.program_id(0)
    devices = ins[0].shape[0]

    @pl.when(step == 0)
    def _():
        for out in outs:
            out[...] = jnp.zeros_like(out)

    @pl.loop(0, devices)
    def _(d):
        for (at, which, blocks), out in zip(pieces, outs):
            slot = sel_ref[step * devices + d, which]
            rank = out.shape[-2]
            c = ins[at].shape[-1]
            for k, (block, row) in enumerate(blocks):
                new = ins[at][d, block, row : row + rank, :].astype(F32)
                if len(out.shape) == 4:
                    out[slot, k] += new
                else:
                    out[slot, :, k * c : (k + 1) * c] += new


def sum_picks(sel, t, arrays, pieces, slots, rank, name):
    steps = 4
    in_specs = []
    for a, shape, where in arrays:
        in_specs.append(
            pl.BlockSpec(
                (a.shape[0] // steps,) + shape, lambda s, sel, t, where=where: (s,) + where(t[0])
            )
        )
    shapes = []
    for at, _, blocks, flat in pieces:
        n, c = len(blocks), arrays[at][1][-1]
        shapes.append((slots, rank, n * c) if flat else (slots, n, rank, c))
    return pl.pallas_call(
        functools.partial(sum_kernel, [p[:3] for p in pieces]),
        out_shape=[jax.ShapeDtypeStruct(shape, F32) for shape in shapes],
        grid_spec=pltpu.PrefetchScalarGridSpec(
            num_scalar_prefetch=2, grid=(steps,), in_specs=in_specs,
            out_specs=[whole(shape) for shape in shapes],
        ),
        compiler_params=pltpu.CompilerParams(
            dimension_semantics=("arbitrary",), vmem_limit_bytes=VMEM
        ),
        cost_estimate=cost(0, 30 * MIB),
        name=name,
    )(sel, t, *[a for a, _, _ in arrays])


def pick_kernel(idx_ref, bq_ref, ao_ref, bu_ref, ad_ref, aq_ref, bo_ref, au_ref, bd_ref, marks_ref, half_ref, rest_ref, m_ref):
    at = 0
    for j in range(bq_ref.shape[0]):
        half_ref[:, at : at + bq_ref.shape[2]] = bq_ref[j]
        at += bq_ref.shape[2]
    for ref in (ao_ref, bu_ref, ad_ref):
        half_ref[:, at : at + ref.shape[1]] = ref[...]
        at += ref.shape[1]
    for n, ref in enumerate((aq_ref, bo_ref, au_ref, bd_ref)):
        rest_ref[n] = ref[...]
    m_ref[...] = jnp.broadcast_to(marks_ref[...], m_ref.shape)


def pick_adapters(idx, split, full, marks):
    rank = full[0].shape[1]
    width = split[0].shape[1] * split[0].shape[3] + sum(a.shape[2] for a in split[1:])

    def one(a, which):
        rest = a.shape[1:]
        return pl.BlockSpec((None,) + rest, lambda i, idx: (idx[which],) + (0,) * len(rest))

    in_specs = [one(a, n) for n, a in enumerate(split)] + [one(a, n) for n, a in enumerate(full)]
    return pl.pallas_call(
        pick_kernel,
        out_shape=(
            jax.ShapeDtypeStruct((rank, width), BF),
            jax.ShapeDtypeStruct((len(full),) + full[0].shape[1:], BF),
            jax.ShapeDtypeStruct((8, 128), jnp.int32),
        ),
        grid_spec=pltpu.PrefetchScalarGridSpec(
            num_scalar_prefetch=1, grid=(1,), in_specs=in_specs + [whole(marks.shape)],
            out_specs=[whole((rank, width)), whole((len(full),) + full[0].shape[1:]), whole((8, 128))],
        ),
        compiler_params=pltpu.CompilerParams(dimension_semantics=("arbitrary",)),
        cost_estimate=cost(0, MIB),
        name="pick_adapters",
    )(idx, *split, *full, marks)


def chip_device(
    tokens, w_qkv, w_out, w_up, w_down, ln1_gain, ln1_bias, ln2_gain, ln2_bias,
    a_qkv, b_qkv, a_out, b_out, a_up, b_up, a_down, b_down, adapter_idx, pic_start, cotangent,
):
    shards = lax.axis_size("dp")
    dp, t = lax.axis_index("dp"), lax.axis_index("tensor")
    keeps = dp % 2 == t
    both = ("dp", "tensor")
    swap = []
    for c in range(shards // 2):
        one, two = 2 * (2 * c + 1), 2 * (2 * c) + 1
        swap += [(one, two), (two, one)]

    def swapped(x):
        return lax.ppermute(x, both, swap)

    def row(v):
        return v.reshape(1, -1)

    rank, slots = a_qkv.shape[2], a_qkv.shape[0]
    features, width = tokens.shape[1], w_out.shape[0]
    chosen = adapter_idx[0]

    turned = lambda v: v.transpose(0, 2, 1)
    marks = jnp.concatenate([chosen, pic_start[0]])
    half, rest, marks = pick_adapters(
        chosen,
        [b_qkv.transpose(0, 2, 1, 3), turned(a_out), b_up, turned(a_down)],
        [turned(a_qkv), b_out, turned(a_up), b_down],
        jnp.pad(marks, (0, 128 - marks.shape[0]))[None],
    )

    qkv_shard = w_qkv.transpose(1, 0, 2)
    rest_shard = jnp.concatenate([w_up, w_down.T, w_out.T], axis=1)
    rest_full = lax.all_gather(rest_shard, both, axis=0)
    rest_full = rest_full.reshape(shards, 2, *rest_shard.shape)
    qkv_full, far_tokens, near_half, partner_half, core_half, core_rest, core_marks = spread(
        [qkv_shard],
        [
            (tokens, "partner"), (half, "near"), (half, "partner"),
            (half, "sibling"), (rest, "sibling"), (marks, "sibling"),
        ],
        shards,
        0,
    )
    later, far_tokens = lax.optimization_barrier((cotangent, far_tokens))
    cot = jnp.where(keeps, cotangent, swapped(later))
    tok = jnp.where(keeps, tokens, far_tokens)
    own_half = jnp.where(keeps, half, core_half)
    far_half = jnp.where(keeps, near_half, partner_half)
    shared = jnp.where(t == 0, jnp.stack([own_half, far_half]), jnp.stack([far_half, own_half]))
    rep = jnp.where(keeps, rest, core_rest)
    marks = jnp.where(keeps, marks, core_marks)[0]
    starts = marks[4 : 4 + pic_start.shape[1]]
    tag = jnp.pad(marks[:4].astype(BF)[None], ((0, rank - 1), (0, width - 4)))

    normed, low, qkv = project_qkv(tok, row(ln1_gain), row(ln1_bias), rep[0], qkv_full, shared, 2)
    mixed, lse, mix = attend_rows(starts, qkv, 3)
    layer_out, g_resid, g_early, g_mix = middle(
        rest_full, shared, tok, mix, cot, row(ln2_gain), row(ln2_bias), rep[1:], 4
    )
    early = lax.all_gather(g_early, both, axis=0)
    out = jnp.where(keeps, layer_out, swapped(layer_out))
    g_qkv = attend_rows_back(starts, qkv, mixed, g_mix, lse, 5)
    grad_tok, late, far_grad = project_qkv_back(
        g_qkv, qkv_full, shared, rep[0], normed, low, tok, row(ln1_gain), g_resid, tag, 1
    )
    grad_input = jnp.where(keeps, grad_tok, far_grad.astype(F32))

    late = late.reshape(2 * shards, *late.shape[2:])
    sel = late[:, -1, 0, :4].astype(jnp.int32)
    side = t.reshape(1).astype(jnp.int32)
    nf, c = g_early.shape[0] - 2, g_early.shape[2]
    near = range(nf // 2)
    rows2 = 2 * rank
    early = early.reshape(2 * shards, *g_early.shape)
    (
        grad_a_out, grad_b_out, grad_a_up, grad_b_up, grad_a_down, grad_b_down, grad_b_qkv, grad_a_qkv,
    ) = sum_picks(
        sel, side,
        [
            (early, (nf // 2, rows2, c), lambda u: (u, 0, 0)),
            (early, (1, rows2, width), lambda u: (nf, 0, u)),
            (early, (2, rows2, c), lambda u: (nf // 2, 0, 0)),
            (late, (3, rank, width), lambda u: (u, 0, 0)),
            (late, (2, rank, width), lambda u: (3, 0, 0)),
        ],
        [
            (1, 1, [(0, 0)], True),
            (2, 1, [(0, rank)], True),
            (2, 2, [(1, rank)], True),
            (0, 2, [(i, rank) for i in near], True),
            (0, 3, [(i, 0) for i in near], True),
            (2, 3, [(1, 0)], True),
            (3, 0, [(0, 0), (1, 0), (2, 0)], False),
            (4, 0, [(0, 0), (1, 0)], True),
        ],
        slots, rank, "sum_picks",
    )
    return (
        out, grad_input, turned(grad_a_qkv), grad_b_qkv.transpose(0, 2, 1, 3),
        turned(grad_a_out), grad_b_out, turned(grad_a_up), grad_b_up, turned(grad_a_down), grad_b_down,
    )


def solution(mesh):
    placed = (
        P(("dp", "tensor"), None),
        P("dp", None, "tensor"),
        P("tensor", "dp"),
        P("dp", "tensor"),
        P("tensor", "dp"),
        P(),
        P(),
        P(),
        P(),
        P(),
        P(None, None, None, "tensor"),
        P(None, "tensor", None),
        P(),
        P(),
        P(None, None, "tensor"),
        P(None, "tensor", None),
        P(),
        P("dp", None),
        P("dp", None),
        P(("dp", "tensor"), None),
    )
    paired = mesh.shape["tensor"] == 2 and mesh.shape["dp"] % 2 == 0
    return jax.shard_map(
        chip_device if paired else per_device,
        mesh=mesh,
        in_specs=placed,
        out_specs=(
            P(("dp", "tensor"), None),
            P(("dp", "tensor"), None),
            P(),
            P(None, None, None, "tensor"),
            P(None, "tensor", None),
            P(),
            P(),
            P(None, None, "tensor"),
            P(None, "tensor", None),
            P(),
        ),
        check_vma=False,
    )
```

```python
import functools
import math

import jax
import jax.numpy as jnp
from jax import lax
from jax.experimental import pallas as pl
from jax.experimental.pallas import tpu as pltpu
from jax.sharding import PartitionSpec as P

HD = 64
SPAN = 256
BLOCK = 512


def matmul(left, right):
    return jnp.dot(left, right, preferred_element_type=jnp.float32)


def contract_rows(left, right):
    return lax.dot_general(
        left, right, (((0,), (0,)), ((), ())), preferred_element_type=jnp.float32
    )


def against(left, right):
    return lax.dot_general(
        left, right, (((1,), (1,)), ((), ())), preferred_element_type=jnp.float32
    )


def layer_norm(values, multiplier, addend):
    center = values - jnp.mean(values, axis=-1, keepdims=True)
    spread = jnp.mean(center * center, axis=-1, keepdims=True)
    return center * lax.rsqrt(spread + 1e-05) * multiplier + addend


def span_labels(positions, starts):
    inside = (positions[:, None] >= starts[None, :]) & (positions[:, None] < starts[None, :] + SPAN)
    labels = jnp.arange(1, starts.shape[0] + 1, dtype=jnp.int32)
    return jnp.sum(jnp.where(inside, labels[None, :], 0), axis=1)


def allowed_mask(offset, row_count, length, starts):
    row_pos = offset + jnp.arange(row_count, dtype=jnp.int32)
    col_pos = jnp.arange(length, dtype=jnp.int32)
    row_span = span_labels(row_pos, starts)
    col_span = span_labels(col_pos, starts)
    causal = col_pos[None, :] <= row_pos[:, None]
    joined = (row_span[:, None] == col_span[None, :]) & (row_span[:, None] > 0)
    return causal | joined


def masked_scores(query_block, key_rows, offset, length, starts, factor):
    scores = (
        jnp.einsum("qhd,khd->hqk", query_block, key_rows, preferred_element_type=jnp.float32)
        * factor
    )
    allowed = allowed_mask(offset, BLOCK, length, starts)
    return jnp.where(allowed[None], scores, -1000000000.0)


def attend(queries, key_rows, value_rows, starts):
    length, heads, width = queries.shape
    factor = width ** (-0.5)

    def one_block(block_number):
        offset = block_number * BLOCK
        query_block = lax.dynamic_slice_in_dim(queries, offset, BLOCK, 0)
        scores = masked_scores(query_block, key_rows, offset, length, starts, factor)
        peak = jnp.max(scores, axis=-1, keepdims=True)
        raised = jnp.exp(scores - peak)
        totals = jnp.sum(raised, axis=-1, keepdims=True)
        weights_low = (raised / totals).astype(jnp.bfloat16)
        blended = jnp.einsum(
            "hqk,khd->qhd", weights_low, value_rows, preferred_element_type=jnp.float32
        )
        return (
            blended.astype(jnp.bfloat16).reshape(BLOCK, heads * width),
            (peak + jnp.log(totals))[..., 0],
        )

    blended, log_sums = lax.map(one_block, jnp.arange(length // BLOCK, dtype=jnp.int32))
    return (blended.reshape(length, heads * width), log_sums)


def attend_back(queries, key_rows, value_rows, grad_mix, log_sums, starts):
    length, heads, width = queries.shape
    factor = width ** (-0.5)

    def one_block(carry, inputs_pair):
        key_grad, value_grad = carry
        block_number, block_sums = inputs_pair
        offset = block_number * BLOCK
        query_block = lax.dynamic_slice_in_dim(queries, offset, BLOCK, 0)
        grad_block = lax.dynamic_slice_in_dim(grad_mix, offset, BLOCK, 0)
        scores = masked_scores(query_block, key_rows, offset, length, starts, factor)
        weights = jnp.exp(scores - block_sums[:, :, None])
        dots = jnp.einsum(
            "qhd,khd->hqk", grad_block, value_rows, preferred_element_type=jnp.float32
        )
        inner = jnp.sum(weights * dots, axis=-1, keepdims=True)
        slopes = (weights * (dots - inner) * factor).astype(jnp.bfloat16)
        query_grad = jnp.einsum(
            "hqk,khd->qhd", slopes, key_rows, preferred_element_type=jnp.float32
        )
        key_grad = key_grad + jnp.einsum(
            "hqk,qhd->khd", slopes, query_block, preferred_element_type=jnp.float32
        )
        value_grad = value_grad + jnp.einsum(
            "hqk,qhd->khd",
            weights.astype(jnp.bfloat16),
            grad_block,
            preferred_element_type=jnp.float32,
        )
        return ((key_grad, value_grad), query_grad)

    initial = jnp.zeros(key_rows.shape, jnp.float32)
    numbers = jnp.arange(length // BLOCK, dtype=jnp.int32)
    (key_grad, value_grad), query_grad = lax.scan(
        one_block, (initial, initial), (numbers, log_sums)
    )
    return (query_grad.reshape(length, heads, width), key_grad, value_grad)


def fetch_frozen(first, second):
    return (
        lax.all_gather(first, "dp", axis=0, tiled=True),
        lax.all_gather(second, "dp", axis=1, tiled=True),
    )


def enter_rows(normed, reduced):
    return (
        lax.all_gather(normed, "tensor", axis=0, tiled=True),
        lax.all_gather(reduced, "tensor", axis=0, tiled=True),
    )


def leave_rows(partial_value, reduced):
    return (
        lax.psum_scatter(partial_value, "tensor", scatter_dimension=0, tiled=True),
        lax.psum_scatter(reduced, "tensor", scatter_dimension=0, tiled=True),
    )


def enter_grads(branch, reduced):
    return (
        lax.all_gather(branch, "tensor", axis=0, tiled=True),
        lax.all_gather(reduced, "tensor", axis=0, tiled=True),
    )


def leave_grads(partial_value, reduced):
    return (
        lax.psum_scatter(partial_value, "tensor", scatter_dimension=0, tiled=True),
        lax.psum_scatter(reduced, "tensor", scatter_dimension=0, tiled=True),
    )


def per_device(
    tokens,
    w_qkv,
    w_out,
    w_up,
    w_down,
    ln1_gain,
    ln1_bias,
    ln2_gain,
    ln2_bias,
    a_qkv,
    b_qkv,
    a_out,
    b_out,
    a_up,
    b_up,
    a_down,
    b_down,
    adapter_idx,
    pic_start,
    cotangent,
):
    selection = adapter_idx[0]
    starts = pic_start[0]

    def chosen(stacked, which_one):
        return lax.dynamic_index_in_dim(stacked, selection[which_one], 0, keepdims=False)

    low_qkv_in = chosen(a_qkv, 0)
    rank = low_qkv_in.shape[1]
    low_qkv_out = chosen(b_qkv, 0).reshape(rank, -1)
    low_out_in = chosen(a_out, 1)
    low_out_out = chosen(b_out, 1)
    low_up_in = chosen(a_up, 2)
    low_up_out = chosen(b_up, 2)
    low_down_in = chosen(a_down, 3)
    low_down_out = chosen(b_down, 3)
    heads_here = low_out_in.shape[0] // HD

    def run_forward(own_tokens, frozen):
        qkv_rows, out_rows, up_rows, down_rows = frozen
        qkv_full, out_full = fetch_frozen(qkv_rows, out_rows)
        qkv_flat = qkv_full.reshape(qkv_full.shape[0], -1)
        own_float = own_tokens.astype(jnp.float32)
        normed = layer_norm(own_float, ln1_gain, ln1_bias).astype(jnp.bfloat16)
        reduced = matmul(normed, low_qkv_in).astype(jnp.bfloat16)
        normed_all, reduced_all = enter_rows(normed, reduced)
        length = normed_all.shape[0]
        project = (matmul(normed_all, qkv_flat) + matmul(reduced_all, low_qkv_out)).astype(
            jnp.bfloat16
        )
        split = project.reshape(length, 3, heads_here, HD)
        blended, log_sums = attend(split[:, 0], split[:, 1], split[:, 2], starts)
        main_part, low_part = leave_rows(matmul(blended, out_full), matmul(blended, low_out_in))
        low_out_val = low_part.astype(jnp.bfloat16)
        residual = own_float + main_part + matmul(low_out_val, low_out_out)
        up_full, down_full = fetch_frozen(up_rows, down_rows)
        normed_two = layer_norm(residual, ln2_gain, ln2_bias).astype(jnp.bfloat16)
        reduced_two = matmul(normed_two, low_up_in).astype(jnp.bfloat16)
        normed_two_all, reduced_two_all = enter_rows(normed_two, reduced_two)
        pre_act = matmul(normed_two_all, up_full) + matmul(reduced_two_all, low_up_out)
        hidden = jax.nn.gelu(pre_act, approximate=True).astype(jnp.bfloat16)
        main_two, low_two = leave_rows(matmul(hidden, down_full), matmul(hidden, low_down_in))
        low_down_val = low_two.astype(jnp.bfloat16)
        output = residual + main_two + matmul(low_down_val, low_down_out)
        kept_state = (
            qkv_flat,
            out_full,
            up_full,
            down_full,
            normed,
            reduced_all,
            split,
            blended,
            log_sums,
            low_out_val,
            residual,
            normed_two,
            reduced_two_all,
            pre_act,
            hidden,
            low_down_val,
        )
        return (output, kept_state)

    frozen = (w_qkv, w_out, w_up, w_down)
    output, kept_state = run_forward(tokens, frozen)
    (
        qkv_flat,
        out_full,
        up_full,
        down_full,
        normed,
        reduced_all,
        split,
        blended,
        log_sums,
        low_out_val,
        residual,
        normed_two,
        reduced_two_all,
        pre_act,
        hidden,
        low_down_val,
    ) = kept_state
    cot_float = cotangent.astype(jnp.float32)
    grad_low_down = against(cotangent, low_down_out).astype(jnp.bfloat16)
    grad_b_down_here = contract_rows(low_down_val, cotangent)
    cot_all, grad_low_down_all = enter_grads(cotangent, grad_low_down)
    grad_hidden = against(cot_all, down_full) + against(grad_low_down_all, low_down_in)
    grad_a_down_here = contract_rows(hidden, grad_low_down_all)
    gelu_pull = jax.vjp(lambda inner_val: jax.nn.gelu(inner_val, approximate=True), pre_act)[1]
    grad_pre = gelu_pull(grad_hidden)[0].astype(jnp.bfloat16)
    grad_b_up_here = contract_rows(reduced_two_all, grad_pre)
    grad_normed_two, grad_reduced_two = leave_grads(
        against(grad_pre, up_full), against(grad_pre, low_up_out)
    )
    grad_low_up = grad_reduced_two.astype(jnp.bfloat16)
    grad_a_up_here = contract_rows(normed_two, grad_low_up)
    grad_normed_two = grad_normed_two + against(grad_low_up, low_up_in)
    norm_pull_two = jax.vjp(lambda inner_val: layer_norm(inner_val, ln2_gain, ln2_bias), residual)[
        1
    ]
    grad_resid = cot_float + norm_pull_two(grad_normed_two)[0]
    branch_low = grad_resid.astype(jnp.bfloat16)
    grad_low_out = against(branch_low, low_out_out).astype(jnp.bfloat16)
    grad_b_out_here = contract_rows(low_out_val, branch_low)
    branch_all, grad_low_out_all = enter_grads(branch_low, grad_low_out)
    grad_mix = (against(branch_all, out_full) + against(grad_low_out_all, low_out_in)).astype(
        jnp.bfloat16
    )
    grad_a_out_here = contract_rows(blended, grad_low_out_all)
    length = grad_mix.shape[0]
    query_grad, key_grad, value_grad = attend_back(
        split[:, 0],
        split[:, 1],
        split[:, 2],
        grad_mix.reshape(length, heads_here, HD),
        log_sums,
        starts,
    )
    grad_qkv = (
        jnp.stack([query_grad, key_grad, value_grad], axis=1)
        .reshape(length, -1)
        .astype(jnp.bfloat16)
    )
    grad_b_qkv_here = contract_rows(reduced_all, grad_qkv)
    grad_normed_one, grad_reduced_one = leave_grads(
        against(grad_qkv, qkv_flat), against(grad_qkv, low_qkv_out)
    )
    grad_low_qkv = grad_reduced_one.astype(jnp.bfloat16)
    grad_a_qkv_here = contract_rows(normed, grad_low_qkv)
    grad_normed_one = grad_normed_one + against(grad_low_qkv, low_qkv_in)
    norm_pull_one = jax.vjp(
        lambda inner_val: layer_norm(inner_val, ln1_gain, ln1_bias), tokens.astype(jnp.float32)
    )[1]
    grad_input = grad_resid + norm_pull_one(grad_normed_one)[0]
    slots = a_qkv.shape[0]

    def spread(gradient, which_one):
        onehot = (jnp.arange(slots, dtype=jnp.int32) == selection[which_one]).astype(jnp.float32)
        return onehot.reshape((slots,) + (1,) * gradient.ndim) * gradient[None]

    sharded = (
        lax.psum(spread(grad_b_qkv_here.reshape(rank, 3, -1), 0).astype(jnp.bfloat16), "dp").astype(
            jnp.float32
        ),
        lax.psum(spread(grad_a_out_here, 1).astype(jnp.bfloat16), "dp").astype(jnp.float32),
        lax.psum(spread(grad_b_up_here, 2).astype(jnp.bfloat16), "dp").astype(jnp.float32),
        lax.psum(spread(grad_a_down_here, 3).astype(jnp.bfloat16), "dp").astype(jnp.float32),
    )
    shared = lax.psum(
        (
            spread(grad_a_qkv_here, 0),
            spread(grad_b_out_here, 1),
            spread(grad_a_up_here, 2),
            spread(grad_b_down_here, 3),
        ),
        ("dp", "tensor"),
    )
    return (
        output.astype(jnp.bfloat16),
        grad_input,
        shared[0],
        sharded[0],
        sharded[1],
        shared[1],
        shared[2],
        sharded[2],
        sharded[3],
        shared[3],
    )


SPREAD_CHUNKS = 1
LOG2E = math.log2(math.e)
MASKED = -1e30
MIB = 1 << 20
VMEM = 62 * MIB
BF = jnp.bfloat16
F32 = jnp.float32
MESH = pl.DeviceIdType.MESH


def nt(a, b):
    return lax.dot_general(a, b, (((1,), (1,)), ((), ())), preferred_element_type=F32)


def nn(a, b):
    return lax.dot_general(a, b, (((1,), (0,)), ((), ())), preferred_element_type=F32)


def tn(a, b):
    return lax.dot_general(a, b, (((0,), (0,)), ((), ())), preferred_element_type=F32)


def last_key(starts_ref, pos):
    lim = pos
    for n in range(starts_ref.shape[0]):
        first = starts_ref[n]
        lim = jnp.where((pos >= first) & (pos < first + SPAN), first + SPAN - 1, lim)
    return lim


def head_parts(x):
    lane = lax.broadcasted_iota(jnp.int32, x.shape, 1)
    zero = jnp.zeros_like(x)
    return jnp.where(lane < HD, x, zero), jnp.where(lane >= HD, x, zero)


def cost(flops, moved):
    return pl.CostEstimate(flops=int(flops), bytes_accessed=int(moved), transcendentals=0)


def pair_core():
    dp, t = lax.axis_index("dp"), lax.axis_index("tensor")
    b = dp % 2
    return b, (dp + 1 - 2 * b, t)


def greet_core(sib):
    barrier = pltpu.get_barrier_semaphore()
    pl.semaphore_signal(barrier, inc=1, device_id=sib, device_id_type=MESH)
    pl.semaphore_wait(barrier, 1)


def to_core(src, dst, sems, n, sib):
    return pltpu.make_async_remote_copy(
        src_ref=src, dst_ref=dst, send_sem=sems.at[0, n], recv_sem=sems.at[1, n],
        device_id=sib, device_id_type=MESH,
    )


def attend_kernel(
    starts_ref, q_ref, k_ref, v_ref, o_ref, lse_ref, mix_ref, vt_ref, send_ref, sems, own_sems
):
    p, qi = pl.program_id(0), pl.program_id(1)
    pairs = pl.num_programs(0)
    bq = bk = k_ref.shape[1]
    scale = LOG2E * HD ** -0.5
    b, sib = pair_core()
    pl.when((p == 0) & (qi == 0))(lambda: greet_core(sib))

    @pl.when(qi == 0)
    def _():
        for n in range(k_ref.shape[0]):
            vt_ref[:, n * bk : (n + 1) * bk] = jnp.transpose(v_ref[n])

    qs = head_parts(q_ref[...])
    base = qi * bq
    lim = last_key(starts_ref, base + lax.broadcasted_iota(jnp.int32, (1, bq), 1))

    sub = 256
    qt = [jnp.transpose(x) for x in qs]

    def step(masked, j, carry):
        off = pl.multiple_of(j * bk, bk)
        state = list(carry)
        turns = [(h, n) for n in range(bk // sub) for h in range(2)]

        def first(n):
            return max(0, n * sub - SPAN) // SPAN * SPAN if masked else 0

        def scores(h, n):
            at = first(n)
            s = nn(k_ref[j, n * sub : (n + 1) * sub, :], qt[h][:, at:])
            if masked:
                ok = off + n * sub + lax.broadcasted_iota(jnp.int32, s.shape, 0) <= lim[:, at:]
                s = jnp.where(ok, s, MASKED)
            return s

        def take(h, n, s):
            at = first(n)
            m, l, acc = (x[:, at:] for x in state[h])
            top = jnp.maximum(m, jnp.max(s, axis=0, keepdims=True))
            w = jnp.exp2((s - top) * scale)
            al = jnp.exp2((m - top) * scale)
            l = al * l + jnp.sum(w, axis=0, keepdims=True)
            keys = pl.ds(pl.multiple_of(off + n * sub, sub), sub)
            acc = acc * al + nn(vt_ref[h * HD : (h + 1) * HD, keys], w.astype(BF))
            new = top, l, acc
            if at:
                new = [jnp.concatenate([x[:, :at], y], axis=1) for x, y in zip(state[h], new)]
            state[h] = tuple(new)

        ahead = [scores(*turn) for turn in turns[:4]]
        for i, turn in enumerate(turns):
            if i + 4 < len(turns):
                ahead.append(scores(*turns[i + 4]))
            take(*turn, ahead[i])
        return tuple(state)

    init = (jnp.full((1, bq), MASKED, F32), jnp.zeros((1, bq), F32), jnp.zeros((HD, bq), F32))
    carry = lax.fori_loop(0, qi, functools.partial(step, False), (init, init))
    carry = step(True, qi, carry)
    mixed = jnp.transpose(jnp.concatenate([carry[h][2] / carry[h][1] for h in range(2)], axis=0)).astype(BF)
    o_ref[...] = mixed
    for h in range(2):
        lse_ref[0, h : h + 1, :] = carry[h][0] * scale + jnp.log2(carry[h][1])

    def place(n, core):
        return mix_ref.at[core, :, pl.ds(pl.multiple_of(n * 2 * HD, 2 * HD), 2 * HD)]

    def far(n):
        return to_core(send_ref.at[n, 1], place(n, b), sems, n, sib)

    def own(n):
        return pltpu.make_async_copy(send_ref.at[n, 0], place(n, b), own_sems.at[n])

    @pl.when(qi == b)
    def _():
        send_ref[p, 0] = mixed
        own(p).start()

    @pl.when(qi != b)
    def _():
        send_ref[p, 1] = mixed
        far(p).start()

    @pl.when((p == pairs - 1) & (qi == pl.num_programs(1) - 1))
    def _():
        for n in range(send_ref.shape[0]):
            own(n).wait()
            far(n).wait()


def attend_rows(starts, qkv, ident):
    parts, _, rows, width = qkv.shape
    pairs = width // (2 * HD)
    length = parts * rows

    def all_parts(which):
        return pl.BlockSpec((parts, None, rows, 2 * HD), lambda p, i, s: (0, which, 0, p))

    return pl.pallas_call(
        attend_kernel,
        out_shape=(
            jax.ShapeDtypeStruct((parts, rows, width), BF),
            jax.ShapeDtypeStruct((pairs, 2, length), F32),
            jax.ShapeDtypeStruct((parts, rows, width), BF),
        ),
        grid_spec=pltpu.PrefetchScalarGridSpec(
            num_scalar_prefetch=1,
            grid=(pairs, parts),
            in_specs=[
                pl.BlockSpec((None, None, rows, 2 * HD), lambda p, i, s: (i, 0, 0, p)),
                all_parts(1),
                all_parts(2),
            ],
            out_specs=[
                pl.BlockSpec((None, rows, 2 * HD), lambda p, i, s: (i, 0, p)),
                pl.BlockSpec((1, 2, rows), lambda p, i, s: (p, 0, i)),
                pl.BlockSpec(memory_space=pl.ANY),
            ],
            scratch_shapes=[
                pltpu.VMEM((2 * HD, length), BF),
                pltpu.VMEM((pairs, 2, rows, 2 * HD), BF),
                pltpu.SemaphoreType.DMA((2, pairs)),
                pltpu.SemaphoreType.DMA((pairs,)),
            ],
        ),
        compiler_params=pltpu.CompilerParams(
            dimension_semantics=("arbitrary", "arbitrary"), vmem_limit_bytes=VMEM,
            collective_id=ident, has_side_effects=True,
        ),
        cost_estimate=cost(24 * length * length * width, 16 * length * width),
        name="attend",
    )(starts, qkv, qkv, qkv)


def attend_back_kernel(
    bq, bk, starts_ref, q_ref, k_ref, v_ref, o_ref, do_ref, lse_ref, all_ref,
    kt_ref, dqt_ref, delta_ref, qm_ref, dom_ref, dk_ref, dv_ref, send_ref, sems, own_sems, qt_ref, dot_ref,
):
    p_now = pl.program_id(0)
    b, sib = pair_core()
    pl.when(p_now == 0)(lambda: greet_core(sib))
    g_ref = send_ref.at[p_now]
    parts, rows, _ = q_ref.shape
    length = parts * rows
    scale = LOG2E * HD ** -0.5
    nq = length // bq
    per = rows // bq
    dqt_ref[...] = jnp.zeros_like(dqt_ref)
    for i in range(nq):
        part, at = i // per, slice((i % per) * bq, (i % per + 1) * bq)
        flat = slice(i * bq, (i + 1) * bq)
        kt_ref[:, flat] = jnp.transpose(k_ref[part, at, :])
        do = do_ref[part, at, :]
        for h, (q_h, do_h) in enumerate(zip(head_parts(q_ref[part, at, :]), head_parts(do))):
            qm_ref[h, flat, :] = q_h
            dom_ref[h, flat, :] = do_h
            qt_ref[h, :, flat] = jnp.transpose(q_h)
            dot_ref[h, :, flat] = jnp.transpose(do_h)
        prod = jnp.transpose(do.astype(F32) * o_ref[part, at, :].astype(F32))
        for h in range(2):
            delta_ref[h : h + 1, flat] = jnp.sum(prod[h * HD : (h + 1) * HD], axis=0, keepdims=True)

    half = bk // 2

    def tile(masked, keys, vals, koff, nk, qoff, nq_):
        at = pl.ds(qoff, nq_)
        dk = dv = None
        if masked:
            lim = last_key(starts_ref, qoff + lax.broadcasted_iota(jnp.int32, (1, nq_), 1))
            ok = koff + lax.broadcasted_iota(jnp.int32, (nk, nq_), 0) <= lim
        heads = range(2)
        ss = [nn(keys, qt_ref[h, :, at]) for h in heads]
        dps = [nn(vals, dot_ref[h, :, at]) for h in heads]
        ps = [jnp.exp2(ss[h] * scale - lse_ref[0, h : h + 1, at]) for h in heads]
        if masked:
            ps = [jnp.where(ok, p, 0.0) for p in ps]
        dss = [(ps[h] * (dps[h] - delta_ref[h : h + 1, at])).astype(BF) for h in heads]
        pbs = [p.astype(BF) for p in ps]
        dv = nn(pbs[0], dom_ref[0, at, :]) + nn(pbs[1], dom_ref[1, at, :])
        dk = nn(dss[0], qm_ref[0, at, :]) + nn(dss[1], qm_ref[1, at, :])
        for h in heads:
            head = slice(h * HD, (h + 1) * HD)
            dqt_ref[head, at] += nn(kt_ref[head, pl.ds(koff, nk)], dss[h])
        return dk, dv

    @pl.loop(0, length // bk)
    def _(j):
        koff = pl.multiple_of(j * bk, bk)
        part = j // (rows // bk)
        inside = pl.multiple_of((j % (rows // bk)) * bk, bk)
        keys = k_ref[part, pl.ds(inside, bk), :]
        vals = v_ref[part, pl.ds(inside, bk), :]

        def step(i, carry):
            dk, dv = tile(False, keys, vals, koff, bk, pl.multiple_of(i * bq, bq), bq)
            return carry[0] + dk, carry[1] + dv

        zero = jnp.zeros((bk, 2 * HD), F32)
        dk, dv = lax.fori_loop(j + 1, nq, step, (zero, zero))
        own = tile(True, keys, vals, koff, bk, koff, bk)
        dk_ref[...] = dk + own[0]
        dv_ref[...] = dv + own[1]

        @pl.when(j % (rows // bk) > 0)
        def _():
            before = pl.multiple_of(jnp.maximum(koff - half, 0), half)
            got = tile(True, keys[:half], vals[:half], koff, half, before, half)
            dk_ref[:half, :] += got[0]
            dv_ref[:half, :] += got[1]

        g_ref[part, 1, pl.ds(inside, bk), :] = (dk_ref[...] * HD ** -0.5).astype(BF)
        g_ref[part, 2, pl.ds(inside, bk), :] = dv_ref[...].astype(BF)

    for i in range(nq):
        part, at = i // per, slice((i % per) * bq, (i % per + 1) * bq)
        dq = jnp.transpose(dqt_ref[:, i * bq : (i + 1) * bq])
        g_ref[part, 0, at, :] = (dq * HD ** -0.5).astype(BF)

    def place(n):
        return all_ref.at[b, :, :, pl.ds(pl.multiple_of(n * 2 * HD, 2 * HD), 2 * HD)]

    def far(n):
        return to_core(send_ref.at[n, 1 - b], place(n), sems, n, sib)

    def own(n):
        return pltpu.make_async_copy(send_ref.at[n, b], place(n), own_sems.at[n])

    far(p_now).start()
    own(p_now).start()

    @pl.when(p_now == pl.num_programs(0) - 1)
    def _():
        for n in range(send_ref.shape[0]):
            own(n).wait()
            far(n).wait()


def attend_rows_back(starts, qkv, mixed, grad_mix, lse, ident):
    parts, _, rows, width = qkv.shape
    pairs = width // (2 * HD)
    length = parts * rows
    bq = bk = max(min(512, rows), 2 * SPAN)

    def one(which):
        return pl.BlockSpec((parts, None, rows, 2 * HD), lambda p, s: (0, which, 0, p))

    flat = pl.BlockSpec((parts, rows, 2 * HD), lambda p, s: (0, 0, p))
    return pl.pallas_call(
        functools.partial(attend_back_kernel, bq, bk),
        out_shape=jax.ShapeDtypeStruct((parts, 3, rows, width), BF),
        grid_spec=pltpu.PrefetchScalarGridSpec(
            num_scalar_prefetch=1,
            grid=(pairs,),
            in_specs=[one(0), one(1), one(2), flat, flat,
                      pl.BlockSpec((1, 2, length), lambda p, s: (p, 0, 0))],
            out_specs=pl.BlockSpec(memory_space=pl.ANY),
            scratch_shapes=[
                pltpu.VMEM((2 * HD, length), BF),
                pltpu.VMEM((2 * HD, length), F32),
                pltpu.VMEM((2, length), F32),
                pltpu.VMEM((2, length, 2 * HD), BF),
                pltpu.VMEM((2, length, 2 * HD), BF),
                pltpu.VMEM((bk, 2 * HD), F32),
                pltpu.VMEM((bk, 2 * HD), F32),
                pltpu.VMEM((pairs, parts, 3, rows, 2 * HD), BF),
                pltpu.SemaphoreType.DMA((2, pairs)),
                pltpu.SemaphoreType.DMA((pairs,)),
                pltpu.VMEM((2, 2 * HD, length), BF),
                pltpu.VMEM((2, 2 * HD, length), BF),
            ],
        ),
        compiler_params=pltpu.CompilerParams(
            dimension_semantics=("arbitrary",), vmem_limit_bytes=VMEM,
            collective_id=ident, has_side_effects=True,
        ),
        cost_estimate=cost(40 * length * length * width, 24 * length * width),
        name="attend_back",
    )(starts, qkv, qkv, qkv, mixed, grad_mix, lse)


def stats(x):
    center = x - jnp.mean(x, axis=-1, keepdims=True)
    return center, lax.rsqrt(jnp.mean(center * center, axis=-1, keepdims=True) + 1e-05)


def norm_back(x, gain, grad):
    center, r = stats(x)
    n = center * r
    e = grad * gain
    return r * (e - jnp.mean(e, axis=-1, keepdims=True) - n * jnp.mean(e * n, axis=-1, keepdims=True))


def row_loop(rows, chunk, body):
    if chunk == rows:
        body(slice(None))
        return

    @pl.loop(0, rows // chunk)
    def _(i):
        body(pl.ds(pl.multiple_of(i * chunk, chunk), chunk))


def qkv_kernel(
    tok_ref, gain_ref, bias_ref, low_in_ref, w_ref, low_up_ref, norm_ref, low_ref, all_ref,
    send_ref, sems, own_sems,
):
    rows = tok_ref.shape[0]
    side, j = pl.program_id(0), pl.program_id(1)
    b, sib = pair_core()

    @pl.when((side == 0) & (j == 0))
    def _():
        def body(at):
            center, r = stats(tok_ref[at, :].astype(F32))
            normed = (center * r * gain_ref[...] + bias_ref[...]).astype(BF)
            norm_ref[at, :] = normed
            low_ref[at, :] = nt(normed, low_in_ref[...]).astype(BF)

        row_loop(rows, 256, body)
        greet_core(sib)

    w = w_ref[...].reshape(norm_ref.shape[1], -1)
    y = nn(norm_ref[...], w) + nn(low_ref[...], low_up_ref[...])
    send_ref[side, j] = y.astype(BF)

    def far(n):
        return to_core(send_ref.at[0, n], all_ref.at[b, n], sems, n, sib)

    def own(n):
        return pltpu.make_async_copy(send_ref.at[1, n], all_ref.at[b, n], own_sems.at[n])

    pl.when(side == 0)(lambda: far(j).start())
    pl.when(side == 1)(lambda: own(j).start())

    @pl.when((side == 1) & (j == 2))
    def _():
        for n in range(3):
            own(n).wait()
            far(n).wait()


def whole(shape):
    return pl.BlockSpec(shape, lambda *_: (0,) * len(shape))


def project_qkv(tok, gain, bias, low_in, w, low_up, ident):
    rows, features = tok.shape
    shards, groups, _, part, width = w.shape
    rank = low_in.shape[0]

    def heads(side):
        b = lax.axis_index("dp") % 2
        return jnp.where(side == 0, 1 - b, b)

    return pl.pallas_call(
        qkv_kernel,
        out_shape=(
            jax.ShapeDtypeStruct((rows, features), BF),
            jax.ShapeDtypeStruct((rows, rank), BF),
            jax.ShapeDtypeStruct((groups, 3, rows, width), BF),
        ),
        grid=(groups, 3),
        in_specs=[
            whole((rows, features)), whole((1, features)), whole((1, features)),
            whole((rank, features)),
            pl.BlockSpec((shards, None, None, part, width), lambda g, j: (0, heads(g), j, 0, 0)),
            pl.BlockSpec((None, rank, width), lambda g, j: (heads(g), 0, j)),
        ],
        out_specs=[
            whole((rows, features)), whole((rows, rank)), pl.BlockSpec(memory_space=pl.ANY),
        ],
        scratch_shapes=[
            pltpu.VMEM((groups, 3, rows, width), BF),
            pltpu.SemaphoreType.DMA((2, 3)),
            pltpu.SemaphoreType.DMA((3,)),
        ],
        compiler_params=pltpu.CompilerParams(
            dimension_semantics=("arbitrary", "arbitrary"), vmem_limit_bytes=VMEM,
            collective_id=ident, has_side_effects=True,
        ),
        cost_estimate=cost(4 * rows * features * groups * 3 * width, 4 * rows * groups * 3 * width),
        name="project_qkv",
    )(tok, gain, bias, low_in, w, low_up)


def qkv_back_kernel(
    planes, g_ref, w_any, low_up_ref, low_in_ref, norm_ref, low_ref, tok_ref, gain_ref, resid_ref, tag_ref,
    grad_ref, late_ref, far_ref,
    w_ref, own_ref, glow_ref, send_ref, w_sem, swap_sem, *sems,
):
    s = pl.program_id(0)
    groups, _, rows, width = g_ref.shape
    chunk, features = tok_ref.shape
    parts = rows // chunk
    gather = Gather(own_ref.at[0], late_ref, *sems, planes, own_ref.at[1])
    moves = gather.c != gather.t
    partner = (gather.place(gather.z, gather.x, gather.t), gather.c)
    blocks = [(g, j) for g in range(groups) for j in range(3)]

    def load_w():
        return pltpu.make_async_copy(w_any, w_ref, w_sem)

    def swap(n):
        return to_core(
            send_ref.at[n], far_ref.at[pl.ds(n * chunk, chunk)], swap_sem, n, partner
        )

    @pl.when(s == 0)
    def _():
        load_w().start()
        gather.greet([(moves, partner)])
        low = low_ref[...]
        glow = None
        for n, (g, j) in enumerate(blocks):
            part = g_ref[g, j]
            more = nt(part, low_up_ref[g, :, j * width : (j + 1) * width])
            glow = more if glow is None else glow + more
            own_ref[(g + gather.t) % 2, j] = tn(low, part).astype(BF)
        glow = glow.astype(BF)
        glow_ref[...] = glow
        y = tn(glow, norm_ref[...]).astype(BF)
        for side in range(2):
            for n in range(features // width):
                own_ref[side, 3 + n] = y[:, n * width : (n + 1) * width]
            own_ref[side, own_ref.shape[1] - 1] = tag_ref[...]
        gather.round(0)

    pl.when(s == 1)(lambda: load_w().wait())

    @pl.when(s > 0)
    def _():
        at = pl.ds(pl.multiple_of((s - 1) * chunk, chunk), chunk)
        total = nn(glow_ref[at, :], low_in_ref[...])
        for g, j in blocks:
            total = total + nt(g_ref[g, j, at, :], w_ref[:, g, j].reshape(features, width))
        grad = resid_ref[...] + norm_back(tok_ref[...].astype(F32), gain_ref[...], total)
        grad_ref[...] = grad
        send_ref[s - 1] = grad.astype(BF)

        @pl.when(moves)
        def _():
            swap(s - 1).start()

    for k in range(1, gather.rounds):
        pl.when(s == min(k, parts))(lambda k=k: gather.round(k))

    @pl.when(s == parts)
    def _():
        gather.finish()

        @pl.when(moves)
        def _():
            for n in range(parts):
                swap(n).wait()


def project_qkv_back(grad, w, low_up, low_in, normed, low, tok, gain, resid, tag, ident):
    rows, features = tok.shape
    shards, groups, _, part, width = w.shape
    rank = low_in.shape[0]
    planes = shards // 4
    parts = 4
    chunk = rows // parts
    late = (3 + features // width + 1, rank, width)
    anywhere = pl.BlockSpec(memory_space=pl.ANY)

    def keep(shape):
        return pl.BlockSpec(shape, lambda s: (0,) * len(shape), pipeline_mode=pl.Buffered(1))

    some = pl.BlockSpec((chunk, features), lambda s: (jnp.maximum(s - 1, 0), 0))
    return pl.pallas_call(
        functools.partial(qkv_back_kernel, planes),
        out_shape=(
            jax.ShapeDtypeStruct((rows, features), F32),
            jax.ShapeDtypeStruct((shards, 2) + late, BF),
            jax.ShapeDtypeStruct((rows, features), BF),
        ),
        grid=(1 + parts,),
        in_specs=[
            keep(grad.shape), anywhere, keep((groups, rank, 3 * width)), keep((rank, features)),
            keep((rows, features)), keep((rows, rank)), some, keep((1, features)), some,
            keep((rank, width)),
        ],
        out_specs=[some, anywhere, anywhere],
        scratch_shapes=[
            pltpu.VMEM(w.shape, BF),
            pltpu.VMEM((2,) + late, BF),
            pltpu.VMEM((rows, rank), BF),
            pltpu.VMEM((parts, chunk, features), BF),
            pltpu.SemaphoreType.DMA,
            pltpu.SemaphoreType.DMA((2, parts)),
            *gather_sems(1, planes),
        ],
        compiler_params=pltpu.CompilerParams(
            dimension_semantics=("arbitrary",), vmem_limit_bytes=VMEM,
            collective_id=ident, has_side_effects=True,
        ),
        cost_estimate=cost(5 * rows * features * groups * 3 * width, 4 * rows * groups * 3 * width),
        name="project_qkv_back",
    )(grad, w, low_up, low_in, normed, low, tok, gain, resid, tag)


GELU = math.sqrt(2.0 / math.pi)


def gelu_and_slope(v):
    v2 = v * v
    half = 0.5 + 0.5 * jnp.tanh(v * (GELU + (GELU * 0.044715) * v2))
    hidden = v * half
    return hidden, half + hidden * (1.0 - half) * (2.0 * GELU + (6.0 * 0.044715 * GELU) * v2)


def middle_kernel(
    groups, nf,
    w_ref, sh_ref, wo_ref, sho_ref, tok_ref, mix_ref, cot_any, far_any, gain_ref, bias_ref, rep_ref,
    out_ref, resid_ref, gr_ref, do_ref,
    acc_ref, norm_ref, hid_ref, slope_ref, lacc_ref, llow_ref, send_ref, sems, own_sem, cot_ref, cot_sem,
):
    rows, features = tok_ref.shape
    rank = sh_ref.shape[0]
    s = pl.program_id(0)
    b_out, a_up, b_down = rep_ref[0], rep_ref[1], rep_ref[2]
    co = wo_ref.shape[-1]
    up0, down0 = groups, groups + nf
    upb0, end0 = groups + 2 * nf, groups + 3 * nf
    b, sib = pair_core()
    pl.when(s == 0)(lambda: greet_core(sib))
    keeps = b == lax.axis_index("tensor")

    def load_cot(source):
        return pltpu.make_async_copy(source, cot_ref, cot_sem)

    pl.when((s == 0) & keeps)(lambda: load_cot(cot_any).start())
    pl.when((s == 0) & jnp.logical_not(keeps))(lambda: load_cot(far_any).start())

    for g in range(groups):

        @pl.when(s == g)
        def _():
            part = mix_ref[g]
            y = nt(part, wo_ref[...].reshape(features, co))
            low = nt(part, sho_ref[...])
            if g == 0:
                resid_ref[...] = tok_ref[...].astype(F32) + y
                lacc_ref[...] = low
            else:
                resid_ref[...] += y
                lacc_ref[...] += low

    @pl.when(s == up0 - 1)
    def _():
        def body(at):
            low = lacc_ref[at, :].astype(BF)
            llow_ref[0, at, :] = low
            resid = resid_ref[at, :] + nn(low, b_out)
            resid_ref[at, :] = resid
            center, r = stats(resid)
            normed = (center * r * gain_ref[...] + bias_ref[...]).astype(BF)
            norm_ref[at, :] = normed
            llow_ref[1, at, :] = nt(normed, a_up).astype(BF)

        row_loop(rows, 256, body)
        load_cot(cot_any).wait()
        llow_ref[3] = nt(cot_ref[...], b_down).astype(BF)
        acc_ref[...] = jnp.zeros_like(acc_ref)
        lacc_ref[...] = jnp.zeros_like(lacc_ref)

    @pl.when((s >= up0) & (s < down0))
    def _():
        f = s - up0
        w = w_ref[...].reshape(features, -1)

        chunks = [slice(n * 256, (n + 1) * 256) for n in range(rows // 256)]

        def scores(at):
            return nn(norm_ref[at, :], w) + nn(llow_ref[1, at, :], sh_ref[...])

        ahead = [scores(at) for at in chunks[:2]]
        for n, at in enumerate(chunks):
            if n + 2 < len(chunks):
                ahead.append(scores(chunks[n + 2]))
            hidden, slope = gelu_and_slope(ahead[n])
            hid_ref[f, at, :] = hidden.astype(BF)
            slope_ref[f, at, :] = slope.astype(BF)

    @pl.when((s >= down0) & (s < upb0))
    def _():
        f = s - down0
        w = w_ref[...].reshape(features, -1)
        sh = sh_ref[...]
        hidden = hid_ref[f]
        acc_ref[...] += nt(hidden, w)
        lacc_ref[...] += nt(hidden, sh)
        g_hidden = nn(cot_ref[...], w) + nn(llow_ref[3], sh)
        g_pre = (g_hidden * slope_ref[f].astype(F32)).astype(BF)
        slope_ref[f] = g_pre
        gr_ref[:rank, :] = tn(llow_ref[3], hidden).astype(BF)
        gr_ref[rank:, :] = tn(llow_ref[1], g_pre).astype(BF)

    @pl.when(s == upb0 - 1)
    def _():
        def body(at):
            low = lacc_ref[at, :].astype(BF)
            llow_ref[2, at, :] = low
            out_ref[at, :] = (resid_ref[at, :] + acc_ref[at, :] + nn(low, b_down)).astype(BF)

        row_loop(rows, 512, body)
        acc_ref[...] = jnp.zeros_like(acc_ref)
        lacc_ref[...] = jnp.zeros_like(lacc_ref)

    @pl.when((s >= upb0) & (s < end0))
    def _():
        f = s - upb0
        w = w_ref[...].reshape(features, -1)
        part = slope_ref[f]
        acc_ref[...] += nt(part, w)
        lacc_ref[...] += nt(part, sh_ref[...])

    @pl.when(s == end0 - 1)
    def _():
        gr_ref[:rank, :] = tn(llow_ref[2], cot_ref[...]).astype(BF)
        llow_ref[4] = lacc_ref[...].astype(BF)
        gr_ref[rank:, :] = tn(llow_ref[4], norm_ref[...]).astype(BF)

        def body(at):
            total = acc_ref[at, :] + nn(llow_ref[4, at, :], a_up)
            g = cot_ref[at, :].astype(F32) + norm_back(resid_ref[at, :], gain_ref[...], total)
            resid_ref[at, :] = g
            branch = g.astype(BF)
            norm_ref[at, :] = branch
            llow_ref[5, at, :] = nt(branch, b_out).astype(BF)

        row_loop(rows, 256, body)

    def far():
        return to_core(send_ref.at[0], do_ref.at[b], sems, 0, sib)

    def own():
        return pltpu.make_async_copy(send_ref.at[1], do_ref.at[b], own_sem)

    @pl.when(s >= end0)
    def _():
        turn = s - end0
        g = jnp.where(turn == 0, 1 - b, b)
        wo = wo_ref[...].reshape(features, co)
        y = nn(norm_ref[...], wo) + nn(llow_ref[5], sho_ref[...])
        send_ref[turn] = y.astype(BF)
        at = pl.ds(pl.multiple_of(g * co, co), co)
        gr_ref[:rank, at] = tn(llow_ref[5], mix_ref[g]).astype(BF)

    @pl.when(s == end0)
    def _():
        far().start()
        gr_ref[rank:, :] = tn(llow_ref[0], norm_ref[...]).astype(BF)

    @pl.when(s == end0 + 1)
    def _():
        own().start()
        own().wait()
        far().wait()


def middle(w, shared, tok, mix, cot, far_cot, gain, bias, rep, ident):
    rows, features = tok.shape
    shards, groups, part, total = w.shape
    rank = rep.shape[1]
    co = mix.shape[2]
    ffw = (total - co) // 2
    c = features
    halves = ffw // c
    nf = groups * halves
    first = (shared.shape[2] - 2 * ffw) // c
    out_at, out_shared = 2 * ffw // co, (shared.shape[2] - 2 * ffw) // co - 1
    blocks = [(f // halves, f % halves) for f in range(nf)]
    up = [(t, h, h) for t, h in blocks]
    down_step = [(t, halves + h, halves + h) for t, h in blocks]
    shared_group = [t for t, _ in blocks]
    order = [up[0]] * groups + up + down_step + up + [up[-1]] * groups
    shared_of = [0] * groups + shared_group * 3 + [shared_group[-1]] * groups
    of_grad = [0] * (groups + nf) + list(range(nf)) + [nf + 1] * nf + [nf] * groups
    last = len(order) - groups
    anywhere = pl.BlockSpec(memory_space=pl.ANY)

    def group(s):
        b = lax.axis_index("dp") % 2
        return jnp.where(s < last, jnp.minimum(s, groups - 1), jnp.where(s == last, 1 - b, b))

    once = pl.Buffered(1)

    def keep(shape):
        return pl.BlockSpec(shape, lambda s, *_: (0,) * len(shape), pipeline_mode=once)

    def at(table_row):
        def index(s):
            got = table_row[0]
            for n in range(1, len(table_row)):
                if table_row[n] != table_row[n - 1]:
                    got = got + jnp.where(s >= n, table_row[n] - table_row[n - 1], 0)
            return got
        return index

    w_t, w_c = at([x[0] for x in order]), at([x[1] for x in order])
    s_t, s_c, gi = at(shared_of), at([x[2] for x in order]), at(of_grad)
    return pl.pallas_call(
        functools.partial(middle_kernel, groups, nf),
        out_shape=(
            jax.ShapeDtypeStruct((rows, features), BF),
            jax.ShapeDtypeStruct((rows, features), F32),
            jax.ShapeDtypeStruct((nf + 2, 2 * rank, c), BF),
            jax.ShapeDtypeStruct(mix.shape, BF),
        ),
        grid=(len(order),),
        in_specs=[
            pl.BlockSpec((shards, None, part, c), lambda s: (0, w_t(s), 0, w_c(s))),
            pl.BlockSpec((None, rank, c), lambda s: (s_t(s), 0, s_c(s) + first)),
            pl.BlockSpec((shards, None, part, co), lambda s: (0, group(s), 0, out_at)),
            pl.BlockSpec((None, rank, co), lambda s: (group(s), 0, out_shared)),
            keep((rows, features)), keep(mix.shape), anywhere, anywhere,
            keep((1, features)), keep((1, features)), keep(rep.shape),
        ],
        out_specs=[
            keep((rows, features)), keep((rows, features)),
            pl.BlockSpec((None, 2 * rank, c), lambda s: (gi(s), 0, 0)), anywhere,
        ],
        scratch_shapes=[
            pltpu.VMEM((rows, features), F32),
            pltpu.VMEM((rows, features), BF),
            pltpu.VMEM((nf, rows, c), BF),
            pltpu.VMEM((nf, rows, c), BF),
            pltpu.VMEM((rows, rank), F32),
            pltpu.VMEM((6, rows, rank), BF),
            pltpu.VMEM(mix.shape, BF),
            pltpu.SemaphoreType.DMA((2, 1)),
            pltpu.SemaphoreType.DMA,
            pltpu.VMEM((rows, features), BF),
            pltpu.SemaphoreType.DMA,
        ],
        compiler_params=pltpu.CompilerParams(
            dimension_semantics=("arbitrary",), vmem_limit_bytes=VMEM,
            collective_id=ident, has_side_effects=True,
        ),
        cost_estimate=cost(6 * rows * features * groups * total, 4 * features * groups * total),
        name="middle",
    )(w, shared, w, shared, tok, mix, cot, far_cot, gain, bias, rep)


class Gather:
    def __init__(self, shard, full, out_sem, in_sem, own_sem, planes, shard_near=None):
        self.shard, self.full, self.planes = shard, full, planes
        self.shard_near = shard if shard_near is None else shard_near
        self.chunks = out_sem.shape[0]
        self.out_sem, self.in_sem, self.own_sem = out_sem, in_sem, own_sem
        self.rounds = planes + 2
        dp, t = lax.axis_index("dp"), lax.axis_index("tensor")
        z, x, c = dp // 4, (dp // 2) % 2, dp % 2
        self.dp, self.z, self.x, self.c, self.t = dp, z, x, c, t
        self.low, self.high = z > 0, z < planes - 1
        self.below = jnp.maximum(dp - 4, 0), t
        self.above = jnp.minimum(dp + 4, 4 * planes - 1), t
        self.near = dp, 1 - t
        self.across = self.place(z, 1 - x, c), t
        self.sib = self.place(z, x, 1 - c), t
        self.plan = [self.lay_out(k) for k in range(self.rounds)]

    def place(self, z, x, c):
        return z * 4 + x * 2 + c

    def greet(self, extra=()):
        barrier = pltpu.get_barrier_semaphore()

        def hello(who):
            pl.semaphore_signal(barrier, inc=1, device_id=who, device_id_type=MESH)

        for who in (self.near, self.across, self.sib):
            hello(who)
        count = 3
        for cond, who in ((self.low, self.below), (self.high, self.above)) + tuple(extra):
            pl.when(cond)(lambda who=who: hello(who))
            count = count + cond.astype(jnp.int32)
        pl.semaphore_wait(barrier, count)

    def piece(self, ref, n):
        if self.chunks == 1:
            return ref
        size = ref.shape[-2] // self.chunks
        every = (slice(None),) * (len(ref.shape) - 2)
        return ref.at[every + (pl.ds(n * size, size), slice(None))]

    def copy(self, n, at, who, sem, own=False):
        slot = self.piece(self.full.at[at[0], at[1]], n)
        mine = self.shard_near if who is self.near else self.shard
        return pltpu.make_async_remote_copy(
            src_ref=self.piece(mine, n) if own else slot, dst_ref=slot,
            send_sem=self.out_sem.at[n, sem],
            recv_sem=self.in_sem.at[n, at[0] * 2 + at[1]], device_id=who, device_id_type=MESH,
        )

    def arrive(self, n, at):
        self.copy(n, at, self.sib, 0).wait_recv()

    def own_copy(self, n):
        here = self.piece(self.full.at[self.dp, self.t], n)
        return pltpu.make_async_copy(self.piece(self.shard, n), here, self.own_sem.at[n])

    def lay_out(self, k):
        z, planes, t = self.z, self.planes, self.t
        events = []

        def ways(hops):
            if not 0 <= hops < planes:
                return []
            if hops == 0:
                return [(z, None, [(self.low, self.below, 0), (self.high, self.above, 1)])]
            up, down = z >= hops, z + hops < planes
            return [
                (z - hops, up, [(up & self.high, self.above, 1)]),
                (z + hops, down, [(down & self.low, self.below, 0)]),
            ]

        for n in range(self.chunks):
            for zz, cond, on in ways(k):
                sends = on + [(cond, self.across, 2), (cond, self.sib, 4)]
                if k == 0:
                    sends = [(None, self.near, 3)] + sends
                events.append((n, cond, (self.place(zz, self.x, self.c), t), k == 0, zz, sends))
            for zz, cond, on in ways(k - 1):
                sends = [(c, who, kind + 5) for c, who, kind in on]
                sends += [(cond, self.across, 7), (cond, self.sib, 8)]
                events.append((n, cond, (self.place(zz, self.x, self.c), 1 - t), False, zz, sends))
                far = self.place(zz, 1 - self.x, self.c), t
                events.append((n, cond, far, False, zz, [(cond, self.sib, 9)]))
            for zz, cond, _ in ways(k - 2):
                far = self.place(zz, 1 - self.x, self.c), 1 - t
                events.append((n, cond, far, False, zz, [(cond, self.sib, 10)]))
        return [
            (n, cond, where, own, [(c, who, kind * planes + zz) for c, who, kind in sends])
            for n, cond, where, own, zz, sends in events
        ]

    def when(self, cond, act):
        if cond is None:
            act()
        else:
            pl.when(cond)(act)

    def round(self, k):
        for n, cond, where, own, sends in self.plan[k]:
            if not own:
                self.when(cond, lambda n=n, where=where: self.arrive(n, where))
            for c, who, sem in sends:
                self.when(
                    c,
                    lambda n=n, where=where, who=who, sem=sem, own=own: self.copy(
                        n, where, who, sem, own
                    ).start(),
                )
            if own:
                self.own_copy(n).start()

    def finish(self):
        for n in range(self.chunks):
            for zz in range(self.planes):
                for x in (self.x, 1 - self.x):
                    for t in (self.t, 1 - self.t):
                        self.arrive(n, (self.place(zz, x, 1 - self.c), t))
            self.own_copy(n).wait()
        for events in self.plan:
            for n, _, where, own, sends in events:
                for c, who, sem in sends:
                    self.when(
                        c,
                        lambda n=n, where=where, who=who, sem=sem, own=own: self.copy(
                            n, where, who, sem, own
                        ).wait_send(),
                    )


def gather_sems(n, planes):
    return [
        pltpu.SemaphoreType.DMA((n, 11 * planes)),
        pltpu.SemaphoreType.DMA((n, 8 * planes)),
        pltpu.SemaphoreType.DMA((n,)),
    ]


def spread_kernel(n_all, kinds, planes, *refs):
    n_swap = len(kinds)
    shard = refs[:n_all]
    swap_in = refs[n_all : n_all + n_swap]
    full = refs[n_all + n_swap : 2 * n_all + n_swap]
    swap_out = refs[2 * n_all + n_swap : 2 * n_all + 2 * n_swap]
    *sems, swap_sem = refs[2 * n_all + 2 * n_swap :]
    g = Gather(shard[0], full[0], *sems, planes)
    moves = g.c != g.t
    keeps = jnp.logical_not(moves)
    partner = (g.place(g.z, g.x, g.t), g.c)
    g.greet([(moves, partner)])
    rules = {"partner": (moves, partner, moves), "near": (moves, g.near, keeps), "sibling": (keeps, g.sib, moves)}

    def swap_copy(n):
        return pltpu.make_async_remote_copy(
            src_ref=swap_in[n], dst_ref=swap_out[n], send_sem=swap_sem.at[n, 0],
            recv_sem=swap_sem.at[n, 1], device_id=rules[kinds[n]][1], device_id_type=MESH,
        )

    for n in range(n_swap):
        pl.when(rules[kinds[n]][0])(lambda n=n: swap_copy(n).start())
    for k in range(g.rounds):
        g.round(k)
    g.finish()
    for n in range(n_swap):
        pl.when(rules[kinds[n]][0])(lambda n=n: swap_copy(n).wait_send())
        pl.when(rules[kinds[n]][2])(lambda n=n: swap_copy(n).wait_recv())


def spread(gathered, handed, shards, ident):
    planes = shards // 4
    swapped = [a for a, _ in handed]
    n_all, n_swap = len(gathered), len(swapped)
    anywhere = pl.BlockSpec(memory_space=pl.ANY)
    return pl.pallas_call(
        functools.partial(spread_kernel, n_all, [k for _, k in handed], planes),
        out_shape=[jax.ShapeDtypeStruct((shards, 2) + a.shape, a.dtype) for a in gathered]
        + [jax.ShapeDtypeStruct(a.shape, a.dtype) for a in swapped],
        in_specs=[anywhere] * (n_all + n_swap),
        out_specs=[anywhere] * (n_all + n_swap),
        scratch_shapes=[
            *gather_sems(SPREAD_CHUNKS, planes),
            pltpu.SemaphoreType.DMA((max(n_swap, 1), 2)),
        ],
        compiler_params=pltpu.CompilerParams(collective_id=ident, has_side_effects=True),
        cost_estimate=cost(0, 60 * MIB),
        name="spread%d" % ident,
    )(*gathered, *swapped)


def sum_kernel(pieces, sel_ref, t_ref, *refs):
    ins, outs = refs[: len(refs) - len(pieces)], refs[len(refs) - len(pieces) :]
    step = pl.program_id(0)
    devices = ins[0].shape[0]

    @pl.when(step == 0)
    def _():
        for out in outs:
            out[...] = jnp.zeros_like(out)

    @pl.loop(0, devices)
    def _(d):
        for (at, which, blocks), out in zip(pieces, outs):
            slot = sel_ref[step * devices + d, which]
            rank = out.shape[-2]
            c = ins[at].shape[-1]
            for k, (block, row) in enumerate(blocks):
                new = ins[at][d, block, row : row + rank, :].astype(F32)
                if len(out.shape) == 4:
                    out[slot, k] += new
                else:
                    out[slot, :, k * c : (k + 1) * c] += new


def sum_picks(sel, t, arrays, pieces, slots, rank, name):
    steps = 4
    in_specs = []
    for a, shape, where in arrays:
        in_specs.append(
            pl.BlockSpec(
                (a.shape[0] // steps,) + shape, lambda s, sel, t, where=where: (s,) + where(t[0])
            )
        )
    shapes = []
    for at, _, blocks, flat in pieces:
        n, c = len(blocks), arrays[at][1][-1]
        shapes.append((slots, rank, n * c) if flat else (slots, n, rank, c))
    return pl.pallas_call(
        functools.partial(sum_kernel, [p[:3] for p in pieces]),
        out_shape=[jax.ShapeDtypeStruct(shape, F32) for shape in shapes],
        grid_spec=pltpu.PrefetchScalarGridSpec(
            num_scalar_prefetch=2, grid=(steps,), in_specs=in_specs,
            out_specs=[whole(shape) for shape in shapes],
        ),
        compiler_params=pltpu.CompilerParams(
            dimension_semantics=("arbitrary",), vmem_limit_bytes=VMEM
        ),
        cost_estimate=cost(0, 30 * MIB),
        name=name,
    )(sel, t, *[a for a, _, _ in arrays])


def pick_kernel(idx_ref, bq_ref, ao_ref, bu_ref, ad_ref, aq_ref, bo_ref, au_ref, bd_ref, marks_ref, half_ref, rest_ref, m_ref):
    at = 0
    for j in range(bq_ref.shape[0]):
        half_ref[:, at : at + bq_ref.shape[2]] = bq_ref[j]
        at += bq_ref.shape[2]
    for ref in (ao_ref, bu_ref, ad_ref):
        half_ref[:, at : at + ref.shape[1]] = ref[...]
        at += ref.shape[1]
    for n, ref in enumerate((aq_ref, bo_ref, au_ref, bd_ref)):
        rest_ref[n] = ref[...]
    m_ref[...] = jnp.broadcast_to(marks_ref[...], m_ref.shape)


def pick_adapters(idx, split, full, marks):
    rank = full[0].shape[1]
    width = split[0].shape[1] * split[0].shape[3] + sum(a.shape[2] for a in split[1:])

    def one(a, which):
        rest = a.shape[1:]
        return pl.BlockSpec((None,) + rest, lambda i, idx: (idx[which],) + (0,) * len(rest))

    in_specs = [one(a, n) for n, a in enumerate(split)] + [one(a, n) for n, a in enumerate(full)]
    return pl.pallas_call(
        pick_kernel,
        out_shape=(
            jax.ShapeDtypeStruct((rank, width), BF),
            jax.ShapeDtypeStruct((len(full),) + full[0].shape[1:], BF),
            jax.ShapeDtypeStruct((8, 128), jnp.int32),
        ),
        grid_spec=pltpu.PrefetchScalarGridSpec(
            num_scalar_prefetch=1, grid=(1,), in_specs=in_specs + [whole(marks.shape)],
            out_specs=[whole((rank, width)), whole((len(full),) + full[0].shape[1:]), whole((8, 128))],
        ),
        compiler_params=pltpu.CompilerParams(dimension_semantics=("arbitrary",)),
        cost_estimate=cost(0, MIB),
        name="pick_adapters",
    )(idx, *split, *full, marks)


def chip_device(
    tokens, w_qkv, w_out, w_up, w_down, ln1_gain, ln1_bias, ln2_gain, ln2_bias,
    a_qkv, b_qkv, a_out, b_out, a_up, b_up, a_down, b_down, adapter_idx, pic_start, cotangent,
):
    shards = lax.axis_size("dp")
    dp, t = lax.axis_index("dp"), lax.axis_index("tensor")
    keeps = dp % 2 == t
    both = ("dp", "tensor")
    swap = []
    for c in range(shards // 2):
        one, two = 2 * (2 * c + 1), 2 * (2 * c) + 1
        swap += [(one, two), (two, one)]

    def swapped(x):
        return lax.ppermute(x, both, swap)

    def row(v):
        return v.reshape(1, -1)

    rank, slots = a_qkv.shape[2], a_qkv.shape[0]
    features, width = tokens.shape[1], w_out.shape[0]
    chosen = adapter_idx[0]

    turned = lambda v: v.transpose(0, 2, 1)
    marks = jnp.concatenate([chosen, pic_start[0]])
    half, rest, marks = pick_adapters(
        chosen,
        [b_qkv.transpose(0, 2, 1, 3), turned(a_out), b_up, turned(a_down)],
        [turned(a_qkv), b_out, turned(a_up), b_down],
        jnp.pad(marks, (0, 128 - marks.shape[0]))[None],
    )

    qkv_shard = w_qkv.transpose(1, 0, 2)
    rest_shard = jnp.concatenate([w_up, w_down.T, w_out.T], axis=1)
    rest_full = lax.all_gather(rest_shard, both, axis=0)
    rest_full = rest_full.reshape(shards, 2, *rest_shard.shape)
    qkv_full, far_tokens, near_half, partner_half, core_half, core_rest, core_marks = spread(
        [qkv_shard],
        [
            (tokens, "partner"), (half, "near"), (half, "partner"),
            (half, "sibling"), (rest, "sibling"), (marks, "sibling"),
        ],
        shards,
        0,
    )
    later, far_tokens = lax.optimization_barrier((cotangent, far_tokens))
    far_cot = swapped(later)
    tok = jnp.where(keeps, tokens, far_tokens)
    own_half = jnp.where(keeps, half, core_half)
    far_half = jnp.where(keeps, near_half, partner_half)
    shared = jnp.where(t == 0, jnp.stack([own_half, far_half]), jnp.stack([far_half, own_half]))
    rep = jnp.where(keeps, rest, core_rest)
    marks = jnp.where(keeps, marks, core_marks)[0]
    starts = marks[4 : 4 + pic_start.shape[1]]
    tag = jnp.pad(marks[:4].astype(BF)[None], ((0, rank - 1), (0, width - 4)))

    normed, low, qkv = project_qkv(tok, row(ln1_gain), row(ln1_bias), rep[0], qkv_full, shared, 2)
    mixed, lse, mix = attend_rows(starts, qkv, 3)
    layer_out, g_resid, g_early, g_mix = middle(
        rest_full, shared, tok, mix, cotangent, far_cot, row(ln2_gain), row(ln2_bias), rep[1:], 4
    )
    early = lax.all_gather(g_early, both, axis=0)
    out = jnp.where(keeps, layer_out, swapped(layer_out))
    g_qkv = attend_rows_back(starts, qkv, mixed, g_mix, lse, 5)
    grad_tok, late, far_grad = project_qkv_back(
        g_qkv, qkv_full, shared, rep[0], normed, low, tok, row(ln1_gain), g_resid, tag, 1
    )
    grad_input = jnp.where(keeps, grad_tok, far_grad.astype(F32))

    late = late.reshape(2 * shards, *late.shape[2:])
    sel = late[:, -1, 0, :4].astype(jnp.int32)
    side = t.reshape(1).astype(jnp.int32)
    nf, c = g_early.shape[0] - 2, g_early.shape[2]
    near = range(nf // 2)
    rows2 = 2 * rank
    early = early.reshape(2 * shards, *g_early.shape)
    (
        grad_a_out, grad_b_out, grad_a_up, grad_b_up, grad_a_down, grad_b_down, grad_b_qkv, grad_a_qkv,
    ) = sum_picks(
        sel, side,
        [
            (early, (nf // 2, rows2, c), lambda u: (u, 0, 0)),
            (early, (1, rows2, width), lambda u: (nf, 0, u)),
            (early, (2, rows2, c), lambda u: (nf // 2, 0, 0)),
            (late, (3, rank, width), lambda u: (0, 0, 0)),
            (late, (3, rank, width), lambda u: (1, 0, 0)),
        ],
        [
            (1, 1, [(0, 0)], True),
            (2, 1, [(0, rank)], True),
            (2, 2, [(1, rank)], True),
            (0, 2, [(i, rank) for i in near], True),
            (0, 3, [(i, 0) for i in near], True),
            (2, 3, [(1, 0)], True),
            (3, 0, [(0, 0), (1, 0), (2, 0)], False),
            (4, 0, [(0, 0), (1, 0)], True),
        ],
        slots, rank, "sum_picks",
    )
    return (
        out, grad_input, turned(grad_a_qkv), grad_b_qkv.transpose(0, 2, 1, 3),
        turned(grad_a_out), grad_b_out, turned(grad_a_up), grad_b_up, turned(grad_a_down), grad_b_down,
    )


def solution(mesh):
    placed = (
        P(("dp", "tensor"), None),
        P("dp", None, "tensor"),
        P("tensor", "dp"),
        P("dp", "tensor"),
        P("tensor", "dp"),
        P(),
        P(),
        P(),
        P(),
        P(),
        P(None, None, None, "tensor"),
        P(None, "tensor", None),
        P(),
        P(),
        P(None, None, "tensor"),
        P(None, "tensor", None),
        P(),
        P("dp", None),
        P("dp", None),
        P(("dp", "tensor"), None),
    )
    paired = mesh.shape["tensor"] == 2 and mesh.shape["dp"] % 2 == 0
    return jax.shard_map(
        chip_device if paired else per_device,
        mesh=mesh,
        in_specs=placed,
        out_specs=(
            P(("dp", "tensor"), None),
            P(("dp", "tensor"), None),
            P(),
            P(None, None, None, "tensor"),
            P(None, "tensor", None),
            P(),
            P(),
            P(None, None, "tensor"),
            P(None, "tensor", None),
            P(),
        ),
        check_vma=False,
    )
```

```python
import functools
import math

import jax
import jax.numpy as jnp
from jax import lax
from jax.experimental import pallas as pl
from jax.experimental.pallas import tpu as pltpu
from jax.sharding import PartitionSpec as P

HD = 64
SPAN = 256
BLOCK = 512


def matmul(left, right):
    return jnp.dot(left, right, preferred_element_type=jnp.float32)


def contract_rows(left, right):
    return lax.dot_general(
        left, right, (((0,), (0,)), ((), ())), preferred_element_type=jnp.float32
    )


def against(left, right):
    return lax.dot_general(
        left, right, (((1,), (1,)), ((), ())), preferred_element_type=jnp.float32
    )


def layer_norm(values, multiplier, addend):
    center = values - jnp.mean(values, axis=-1, keepdims=True)
    spread = jnp.mean(center * center, axis=-1, keepdims=True)
    return center * lax.rsqrt(spread + 1e-05) * multiplier + addend


def span_labels(positions, starts):
    inside = (positions[:, None] >= starts[None, :]) & (positions[:, None] < starts[None, :] + SPAN)
    labels = jnp.arange(1, starts.shape[0] + 1, dtype=jnp.int32)
    return jnp.sum(jnp.where(inside, labels[None, :], 0), axis=1)


def allowed_mask(offset, row_count, length, starts):
    row_pos = offset + jnp.arange(row_count, dtype=jnp.int32)
    col_pos = jnp.arange(length, dtype=jnp.int32)
    row_span = span_labels(row_pos, starts)
    col_span = span_labels(col_pos, starts)
    causal = col_pos[None, :] <= row_pos[:, None]
    joined = (row_span[:, None] == col_span[None, :]) & (row_span[:, None] > 0)
    return causal | joined


def masked_scores(query_block, key_rows, offset, length, starts, factor):
    scores = (
        jnp.einsum("qhd,khd->hqk", query_block, key_rows, preferred_element_type=jnp.float32)
        * factor
    )
    allowed = allowed_mask(offset, BLOCK, length, starts)
    return jnp.where(allowed[None], scores, -1000000000.0)


def attend(queries, key_rows, value_rows, starts):
    length, heads, width = queries.shape
    factor = width ** (-0.5)

    def one_block(block_number):
        offset = block_number * BLOCK
        query_block = lax.dynamic_slice_in_dim(queries, offset, BLOCK, 0)
        scores = masked_scores(query_block, key_rows, offset, length, starts, factor)
        peak = jnp.max(scores, axis=-1, keepdims=True)
        raised = jnp.exp(scores - peak)
        totals = jnp.sum(raised, axis=-1, keepdims=True)
        weights_low = (raised / totals).astype(jnp.bfloat16)
        blended = jnp.einsum(
            "hqk,khd->qhd", weights_low, value_rows, preferred_element_type=jnp.float32
        )
        return (
            blended.astype(jnp.bfloat16).reshape(BLOCK, heads * width),
            (peak + jnp.log(totals))[..., 0],
        )

    blended, log_sums = lax.map(one_block, jnp.arange(length // BLOCK, dtype=jnp.int32))
    return (blended.reshape(length, heads * width), log_sums)


def attend_back(queries, key_rows, value_rows, grad_mix, log_sums, starts):
    length, heads, width = queries.shape
    factor = width ** (-0.5)

    def one_block(carry, inputs_pair):
        key_grad, value_grad = carry
        block_number, block_sums = inputs_pair
        offset = block_number * BLOCK
        query_block = lax.dynamic_slice_in_dim(queries, offset, BLOCK, 0)
        grad_block = lax.dynamic_slice_in_dim(grad_mix, offset, BLOCK, 0)
        scores = masked_scores(query_block, key_rows, offset, length, starts, factor)
        weights = jnp.exp(scores - block_sums[:, :, None])
        dots = jnp.einsum(
            "qhd,khd->hqk", grad_block, value_rows, preferred_element_type=jnp.float32
        )
        inner = jnp.sum(weights * dots, axis=-1, keepdims=True)
        slopes = (weights * (dots - inner) * factor).astype(jnp.bfloat16)
        query_grad = jnp.einsum(
            "hqk,khd->qhd", slopes, key_rows, preferred_element_type=jnp.float32
        )
        key_grad = key_grad + jnp.einsum(
            "hqk,qhd->khd", slopes, query_block, preferred_element_type=jnp.float32
        )
        value_grad = value_grad + jnp.einsum(
            "hqk,qhd->khd",
            weights.astype(jnp.bfloat16),
            grad_block,
            preferred_element_type=jnp.float32,
        )
        return ((key_grad, value_grad), query_grad)

    initial = jnp.zeros(key_rows.shape, jnp.float32)
    numbers = jnp.arange(length // BLOCK, dtype=jnp.int32)
    (key_grad, value_grad), query_grad = lax.scan(
        one_block, (initial, initial), (numbers, log_sums)
    )
    return (query_grad.reshape(length, heads, width), key_grad, value_grad)


def fetch_frozen(first, second):
    return (
        lax.all_gather(first, "dp", axis=0, tiled=True),
        lax.all_gather(second, "dp", axis=1, tiled=True),
    )


def enter_rows(normed, reduced):
    return (
        lax.all_gather(normed, "tensor", axis=0, tiled=True),
        lax.all_gather(reduced, "tensor", axis=0, tiled=True),
    )


def leave_rows(partial_value, reduced):
    return (
        lax.psum_scatter(partial_value, "tensor", scatter_dimension=0, tiled=True),
        lax.psum_scatter(reduced, "tensor", scatter_dimension=0, tiled=True),
    )


def enter_grads(branch, reduced):
    return (
        lax.all_gather(branch, "tensor", axis=0, tiled=True),
        lax.all_gather(reduced, "tensor", axis=0, tiled=True),
    )


def leave_grads(partial_value, reduced):
    return (
        lax.psum_scatter(partial_value, "tensor", scatter_dimension=0, tiled=True),
        lax.psum_scatter(reduced, "tensor", scatter_dimension=0, tiled=True),
    )


def per_device(
    tokens,
    w_qkv,
    w_out,
    w_up,
    w_down,
    ln1_gain,
    ln1_bias,
    ln2_gain,
    ln2_bias,
    a_qkv,
    b_qkv,
    a_out,
    b_out,
    a_up,
    b_up,
    a_down,
    b_down,
    adapter_idx,
    pic_start,
    cotangent,
):
    selection = adapter_idx[0]
    starts = pic_start[0]

    def chosen(stacked, which_one):
        return lax.dynamic_index_in_dim(stacked, selection[which_one], 0, keepdims=False)

    low_qkv_in = chosen(a_qkv, 0)
    rank = low_qkv_in.shape[1]
    low_qkv_out = chosen(b_qkv, 0).reshape(rank, -1)
    low_out_in = chosen(a_out, 1)
    low_out_out = chosen(b_out, 1)
    low_up_in = chosen(a_up, 2)
    low_up_out = chosen(b_up, 2)
    low_down_in = chosen(a_down, 3)
    low_down_out = chosen(b_down, 3)
    heads_here = low_out_in.shape[0] // HD

    def run_forward(own_tokens, frozen):
        qkv_rows, out_rows, up_rows, down_rows = frozen
        qkv_full, out_full = fetch_frozen(qkv_rows, out_rows)
        qkv_flat = qkv_full.reshape(qkv_full.shape[0], -1)
        own_float = own_tokens.astype(jnp.float32)
        normed = layer_norm(own_float, ln1_gain, ln1_bias).astype(jnp.bfloat16)
        reduced = matmul(normed, low_qkv_in).astype(jnp.bfloat16)
        normed_all, reduced_all = enter_rows(normed, reduced)
        length = normed_all.shape[0]
        project = (matmul(normed_all, qkv_flat) + matmul(reduced_all, low_qkv_out)).astype(
            jnp.bfloat16
        )
        split = project.reshape(length, 3, heads_here, HD)
        blended, log_sums = attend(split[:, 0], split[:, 1], split[:, 2], starts)
        main_part, low_part = leave_rows(matmul(blended, out_full), matmul(blended, low_out_in))
        low_out_val = low_part.astype(jnp.bfloat16)
        residual = own_float + main_part + matmul(low_out_val, low_out_out)
        up_full, down_full = fetch_frozen(up_rows, down_rows)
        normed_two = layer_norm(residual, ln2_gain, ln2_bias).astype(jnp.bfloat16)
        reduced_two = matmul(normed_two, low_up_in).astype(jnp.bfloat16)
        normed_two_all, reduced_two_all = enter_rows(normed_two, reduced_two)
        pre_act = matmul(normed_two_all, up_full) + matmul(reduced_two_all, low_up_out)
        hidden = jax.nn.gelu(pre_act, approximate=True).astype(jnp.bfloat16)
        main_two, low_two = leave_rows(matmul(hidden, down_full), matmul(hidden, low_down_in))
        low_down_val = low_two.astype(jnp.bfloat16)
        output = residual + main_two + matmul(low_down_val, low_down_out)
        kept_state = (
            qkv_flat,
            out_full,
            up_full,
            down_full,
            normed,
            reduced_all,
            split,
            blended,
            log_sums,
            low_out_val,
            residual,
            normed_two,
            reduced_two_all,
            pre_act,
            hidden,
            low_down_val,
        )
        return (output, kept_state)

    frozen = (w_qkv, w_out, w_up, w_down)
    output, kept_state = run_forward(tokens, frozen)
    (
        qkv_flat,
        out_full,
        up_full,
        down_full,
        normed,
        reduced_all,
        split,
        blended,
        log_sums,
        low_out_val,
        residual,
        normed_two,
        reduced_two_all,
        pre_act,
        hidden,
        low_down_val,
    ) = kept_state
    cot_float = cotangent.astype(jnp.float32)
    grad_low_down = against(cotangent, low_down_out).astype(jnp.bfloat16)
    grad_b_down_here = contract_rows(low_down_val, cotangent)
    cot_all, grad_low_down_all = enter_grads(cotangent, grad_low_down)
    grad_hidden = against(cot_all, down_full) + against(grad_low_down_all, low_down_in)
    grad_a_down_here = contract_rows(hidden, grad_low_down_all)
    gelu_pull = jax.vjp(lambda inner_val: jax.nn.gelu(inner_val, approximate=True), pre_act)[1]
    grad_pre = gelu_pull(grad_hidden)[0].astype(jnp.bfloat16)
    grad_b_up_here = contract_rows(reduced_two_all, grad_pre)
    grad_normed_two, grad_reduced_two = leave_grads(
        against(grad_pre, up_full), against(grad_pre, low_up_out)
    )
    grad_low_up = grad_reduced_two.astype(jnp.bfloat16)
    grad_a_up_here = contract_rows(normed_two, grad_low_up)
    grad_normed_two = grad_normed_two + against(grad_low_up, low_up_in)
    norm_pull_two = jax.vjp(lambda inner_val: layer_norm(inner_val, ln2_gain, ln2_bias), residual)[
        1
    ]
    grad_resid = cot_float + norm_pull_two(grad_normed_two)[0]
    branch_low = grad_resid.astype(jnp.bfloat16)
    grad_low_out = against(branch_low, low_out_out).astype(jnp.bfloat16)
    grad_b_out_here = contract_rows(low_out_val, branch_low)
    branch_all, grad_low_out_all = enter_grads(branch_low, grad_low_out)
    grad_mix = (against(branch_all, out_full) + against(grad_low_out_all, low_out_in)).astype(
        jnp.bfloat16
    )
    grad_a_out_here = contract_rows(blended, grad_low_out_all)
    length = grad_mix.shape[0]
    query_grad, key_grad, value_grad = attend_back(
        split[:, 0],
        split[:, 1],
        split[:, 2],
        grad_mix.reshape(length, heads_here, HD),
        log_sums,
        starts,
    )
    grad_qkv = (
        jnp.stack([query_grad, key_grad, value_grad], axis=1)
        .reshape(length, -1)
        .astype(jnp.bfloat16)
    )
    grad_b_qkv_here = contract_rows(reduced_all, grad_qkv)
    grad_normed_one, grad_reduced_one = leave_grads(
        against(grad_qkv, qkv_flat), against(grad_qkv, low_qkv_out)
    )
    grad_low_qkv = grad_reduced_one.astype(jnp.bfloat16)
    grad_a_qkv_here = contract_rows(normed, grad_low_qkv)
    grad_normed_one = grad_normed_one + against(grad_low_qkv, low_qkv_in)
    norm_pull_one = jax.vjp(
        lambda inner_val: layer_norm(inner_val, ln1_gain, ln1_bias), tokens.astype(jnp.float32)
    )[1]
    grad_input = grad_resid + norm_pull_one(grad_normed_one)[0]
    slots = a_qkv.shape[0]

    def spread(gradient, which_one):
        onehot = (jnp.arange(slots, dtype=jnp.int32) == selection[which_one]).astype(jnp.float32)
        return onehot.reshape((slots,) + (1,) * gradient.ndim) * gradient[None]

    sharded = (
        lax.psum(spread(grad_b_qkv_here.reshape(rank, 3, -1), 0).astype(jnp.bfloat16), "dp").astype(
            jnp.float32
        ),
        lax.psum(spread(grad_a_out_here, 1).astype(jnp.bfloat16), "dp").astype(jnp.float32),
        lax.psum(spread(grad_b_up_here, 2).astype(jnp.bfloat16), "dp").astype(jnp.float32),
        lax.psum(spread(grad_a_down_here, 3).astype(jnp.bfloat16), "dp").astype(jnp.float32),
    )
    shared = lax.psum(
        (
            spread(grad_a_qkv_here, 0),
            spread(grad_b_out_here, 1),
            spread(grad_a_up_here, 2),
            spread(grad_b_down_here, 3),
        ),
        ("dp", "tensor"),
    )
    return (
        output.astype(jnp.bfloat16),
        grad_input,
        shared[0],
        sharded[0],
        sharded[1],
        shared[1],
        shared[2],
        sharded[2],
        sharded[3],
        shared[3],
    )


SPREAD_CHUNKS = 1
LOG2E = math.log2(math.e)
MASKED = -1e30
MIB = 1 << 20
VMEM = 62 * MIB
BF = jnp.bfloat16
F32 = jnp.float32
MESH = pl.DeviceIdType.MESH


def nt(a, b):
    return lax.dot_general(a, b, (((1,), (1,)), ((), ())), preferred_element_type=F32)


def nn(a, b):
    return lax.dot_general(a, b, (((1,), (0,)), ((), ())), preferred_element_type=F32)


def tn(a, b):
    return lax.dot_general(a, b, (((0,), (0,)), ((), ())), preferred_element_type=F32)


def last_key(starts_ref, pos):
    lim = pos
    for n in range(starts_ref.shape[0]):
        first = starts_ref[n]
        lim = jnp.where((pos >= first) & (pos < first + SPAN), first + SPAN - 1, lim)
    return lim


def head_parts(x):
    lane = lax.broadcasted_iota(jnp.int32, x.shape, 1)
    zero = jnp.zeros_like(x)
    return jnp.where(lane < HD, x, zero), jnp.where(lane >= HD, x, zero)


def cost(flops, moved):
    return pl.CostEstimate(flops=int(flops), bytes_accessed=int(moved), transcendentals=0)


def pair_core():
    dp, t = lax.axis_index("dp"), lax.axis_index("tensor")
    b = dp % 2
    return b, (dp + 1 - 2 * b, t)


def greet_core(sib):
    barrier = pltpu.get_barrier_semaphore()
    pl.semaphore_signal(barrier, inc=1, device_id=sib, device_id_type=MESH)
    pl.semaphore_wait(barrier, 1)


def to_core(src, dst, sems, n, sib):
    return pltpu.make_async_remote_copy(
        src_ref=src, dst_ref=dst, send_sem=sems.at[0, n], recv_sem=sems.at[1, n],
        device_id=sib, device_id_type=MESH,
    )


def attend_kernel(
    starts_ref, q_ref, k_ref, v_ref, o_ref, lse_ref, mix_ref, vt_ref, send_ref, sems, own_sems
):
    p, qi = pl.program_id(0), pl.program_id(1)
    pairs = pl.num_programs(0)
    bq = bk = k_ref.shape[1]
    scale = LOG2E * HD ** -0.5
    b, sib = pair_core()
    pl.when((p == 0) & (qi == 0))(lambda: greet_core(sib))

    @pl.when(qi == 0)
    def _():
        for n in range(k_ref.shape[0]):
            vt_ref[:, n * bk : (n + 1) * bk] = jnp.transpose(v_ref[n])

    qs = head_parts(q_ref[...])
    base = qi * bq
    lim = last_key(starts_ref, base + lax.broadcasted_iota(jnp.int32, (1, bq), 1))

    sub = 256
    qt = [jnp.transpose(x) for x in qs]

    def step(masked, j, carry):
        off = pl.multiple_of(j * bk, bk)
        state = list(carry)
        turns = [(h, n) for n in range(bk // sub) for h in range(2)]

        def first(n):
            return max(0, n * sub - SPAN) // SPAN * SPAN if masked else 0

        def scores(h, n):
            at = first(n)
            s = nn(k_ref[j, n * sub : (n + 1) * sub, :], qt[h][:, at:])
            if masked:
                ok = off + n * sub + lax.broadcasted_iota(jnp.int32, s.shape, 0) <= lim[:, at:]
                s = jnp.where(ok, s, MASKED)
            return s

        def take(h, n, s):
            at = first(n)
            m, l, acc = (x[:, at:] for x in state[h])
            top = jnp.maximum(m, jnp.max(s, axis=0, keepdims=True))
            w = jnp.exp2((s - top) * scale)
            al = jnp.exp2((m - top) * scale)
            l = al * l + jnp.sum(w, axis=0, keepdims=True)
            keys = pl.ds(pl.multiple_of(off + n * sub, sub), sub)
            acc = acc * al + nn(vt_ref[h * HD : (h + 1) * HD, keys], w.astype(BF))
            new = top, l, acc
            if at:
                new = [jnp.concatenate([x[:, :at], y], axis=1) for x, y in zip(state[h], new)]
            state[h] = tuple(new)

        ahead = [scores(*turn) for turn in turns[:4]]
        for i, turn in enumerate(turns):
            if i + 4 < len(turns):
                ahead.append(scores(*turns[i + 4]))
            take(*turn, ahead[i])
        return tuple(state)

    init = (jnp.full((1, bq), MASKED, F32), jnp.zeros((1, bq), F32), jnp.zeros((HD, bq), F32))
    carry = lax.fori_loop(0, qi, functools.partial(step, False), (init, init))
    carry = step(True, qi, carry)
    mixed = jnp.transpose(jnp.concatenate([carry[h][2] / carry[h][1] for h in range(2)], axis=0)).astype(BF)
    o_ref[...] = mixed
    for h in range(2):
        lse_ref[0, h : h + 1, :] = carry[h][0] * scale + jnp.log2(carry[h][1])

    def place(n, core):
        return mix_ref.at[core, :, pl.ds(pl.multiple_of(n * 2 * HD, 2 * HD), 2 * HD)]

    def far(n):
        return to_core(send_ref.at[n, 1], place(n, b), sems, n, sib)

    def own(n):
        return pltpu.make_async_copy(send_ref.at[n, 0], place(n, b), own_sems.at[n])

    @pl.when(qi == b)
    def _():
        send_ref[p, 0] = mixed
        own(p).start()

    @pl.when(qi != b)
    def _():
        send_ref[p, 1] = mixed
        far(p).start()

    @pl.when((p == pairs - 1) & (qi == pl.num_programs(1) - 1))
    def _():
        for n in range(send_ref.shape[0]):
            own(n).wait()
            far(n).wait()


def attend_rows(starts, qkv, ident):
    parts, _, rows, width = qkv.shape
    pairs = width // (2 * HD)
    length = parts * rows

    def all_parts(which):
        return pl.BlockSpec((parts, None, rows, 2 * HD), lambda p, i, s: (0, which, 0, p))

    return pl.pallas_call(
        attend_kernel,
        out_shape=(
            jax.ShapeDtypeStruct((parts, rows, width), BF),
            jax.ShapeDtypeStruct((pairs, 2, length), F32),
            jax.ShapeDtypeStruct((parts, rows, width), BF),
        ),
        grid_spec=pltpu.PrefetchScalarGridSpec(
            num_scalar_prefetch=1,
            grid=(pairs, parts),
            in_specs=[
                pl.BlockSpec((None, None, rows, 2 * HD), lambda p, i, s: (i, 0, 0, p)),
                all_parts(1),
                all_parts(2),
            ],
            out_specs=[
                pl.BlockSpec((None, rows, 2 * HD), lambda p, i, s: (i, 0, p)),
                pl.BlockSpec((1, 2, rows), lambda p, i, s: (p, 0, i)),
                pl.BlockSpec(memory_space=pl.ANY),
            ],
            scratch_shapes=[
                pltpu.VMEM((2 * HD, length), BF),
                pltpu.VMEM((pairs, 2, rows, 2 * HD), BF),
                pltpu.SemaphoreType.DMA((2, pairs)),
                pltpu.SemaphoreType.DMA((pairs,)),
            ],
        ),
        compiler_params=pltpu.CompilerParams(
            dimension_semantics=("arbitrary", "arbitrary"), vmem_limit_bytes=VMEM,
            collective_id=ident, has_side_effects=True,
        ),
        cost_estimate=cost(24 * length * length * width, 16 * length * width),
        name="attend",
    )(starts, qkv, qkv, qkv)


def attend_back_kernel(
    bq, bk, starts_ref, q_ref, k_ref, v_ref, o_ref, do_ref, lse_ref, all_ref,
    kt_ref, dqt_ref, delta_ref, qm_ref, dom_ref, dk_ref, dv_ref, send_ref, sems, own_sems, qt_ref, dot_ref,
):
    p_now = pl.program_id(0)
    b, sib = pair_core()
    pl.when(p_now == 0)(lambda: greet_core(sib))
    g_ref = send_ref.at[p_now]
    parts, rows, _ = q_ref.shape
    length = parts * rows
    scale = LOG2E * HD ** -0.5
    nq = length // bq
    per = rows // bq
    dqt_ref[...] = jnp.zeros_like(dqt_ref)
    for i in range(nq):
        part, at = i // per, slice((i % per) * bq, (i % per + 1) * bq)
        flat = slice(i * bq, (i + 1) * bq)
        kt_ref[:, flat] = jnp.transpose(k_ref[part, at, :])
        do = do_ref[part, at, :]
        for h, (q_h, do_h) in enumerate(zip(head_parts(q_ref[part, at, :]), head_parts(do))):
            qm_ref[h, flat, :] = q_h
            dom_ref[h, flat, :] = do_h
            qt_ref[h, :, flat] = jnp.transpose(q_h)
            dot_ref[h, :, flat] = jnp.transpose(do_h)
        prod = jnp.transpose(do.astype(F32) * o_ref[part, at, :].astype(F32))
        for h in range(2):
            delta_ref[h : h + 1, flat] = jnp.sum(prod[h * HD : (h + 1) * HD], axis=0, keepdims=True)

    half = bk // 2

    def tile(masked, keys, vals, koff, nk, qoff, nq_):
        at = pl.ds(qoff, nq_)
        dk = dv = None
        if masked:
            lim = last_key(starts_ref, qoff + lax.broadcasted_iota(jnp.int32, (1, nq_), 1))
            ok = koff + lax.broadcasted_iota(jnp.int32, (nk, nq_), 0) <= lim
        heads = range(2)
        ss = [nn(keys, qt_ref[h, :, at]) for h in heads]
        dps = [nn(vals, dot_ref[h, :, at]) for h in heads]
        ps = [jnp.exp2(ss[h] * scale - lse_ref[0, h : h + 1, at]) for h in heads]
        if masked:
            ps = [jnp.where(ok, p, 0.0) for p in ps]
        dss = [(ps[h] * (dps[h] - delta_ref[h : h + 1, at])).astype(BF) for h in heads]
        pbs = [p.astype(BF) for p in ps]
        dv = nn(pbs[0], dom_ref[0, at, :]) + nn(pbs[1], dom_ref[1, at, :])
        dk = nn(dss[0], qm_ref[0, at, :]) + nn(dss[1], qm_ref[1, at, :])
        for h in heads:
            head = slice(h * HD, (h + 1) * HD)
            dqt_ref[head, at] += nn(kt_ref[head, pl.ds(koff, nk)], dss[h])
        return dk, dv

    @pl.loop(0, length // bk)
    def _(j):
        koff = pl.multiple_of(j * bk, bk)
        part = j // (rows // bk)
        inside = pl.multiple_of((j % (rows // bk)) * bk, bk)
        keys = k_ref[part, pl.ds(inside, bk), :]
        vals = v_ref[part, pl.ds(inside, bk), :]

        def step(i, carry):
            dk, dv = tile(False, keys, vals, koff, bk, pl.multiple_of(i * bq, bq), bq)
            return carry[0] + dk, carry[1] + dv

        zero = jnp.zeros((bk, 2 * HD), F32)
        dk, dv = lax.fori_loop(j + 1, nq, step, (zero, zero))
        own = tile(True, keys, vals, koff, bk, koff, bk)
        dk_ref[...] = dk + own[0]
        dv_ref[...] = dv + own[1]

        @pl.when(j % (rows // bk) > 0)
        def _():
            before = pl.multiple_of(jnp.maximum(koff - half, 0), half)
            got = tile(True, keys[:half], vals[:half], koff, half, before, half)
            dk_ref[:half, :] += got[0]
            dv_ref[:half, :] += got[1]

        g_ref[part, 1, pl.ds(inside, bk), :] = (dk_ref[...] * HD ** -0.5).astype(BF)
        g_ref[part, 2, pl.ds(inside, bk), :] = dv_ref[...].astype(BF)

    for i in range(nq):
        part, at = i // per, slice((i % per) * bq, (i % per + 1) * bq)
        dq = jnp.transpose(dqt_ref[:, i * bq : (i + 1) * bq])
        g_ref[part, 0, at, :] = (dq * HD ** -0.5).astype(BF)

    def place(n):
        return all_ref.at[b, :, :, pl.ds(pl.multiple_of(n * 2 * HD, 2 * HD), 2 * HD)]

    def far(n):
        return to_core(send_ref.at[n, 1 - b], place(n), sems, n, sib)

    def own(n):
        return pltpu.make_async_copy(send_ref.at[n, b], place(n), own_sems.at[n])

    far(p_now).start()
    own(p_now).start()

    @pl.when(p_now == pl.num_programs(0) - 1)
    def _():
        for n in range(send_ref.shape[0]):
            own(n).wait()
            far(n).wait()


def attend_rows_back(starts, qkv, mixed, grad_mix, lse, ident):
    parts, _, rows, width = qkv.shape
    pairs = width // (2 * HD)
    length = parts * rows
    bq = bk = max(min(512, rows), 2 * SPAN)

    def one(which):
        return pl.BlockSpec((parts, None, rows, 2 * HD), lambda p, s: (0, which, 0, p))

    flat = pl.BlockSpec((parts, rows, 2 * HD), lambda p, s: (0, 0, p))
    return pl.pallas_call(
        functools.partial(attend_back_kernel, bq, bk),
        out_shape=jax.ShapeDtypeStruct((parts, 3, rows, width), BF),
        grid_spec=pltpu.PrefetchScalarGridSpec(
            num_scalar_prefetch=1,
            grid=(pairs,),
            in_specs=[one(0), one(1), one(2), flat, flat,
                      pl.BlockSpec((1, 2, length), lambda p, s: (p, 0, 0))],
            out_specs=pl.BlockSpec(memory_space=pl.ANY),
            scratch_shapes=[
                pltpu.VMEM((2 * HD, length), BF),
                pltpu.VMEM((2 * HD, length), F32),
                pltpu.VMEM((2, length), F32),
                pltpu.VMEM((2, length, 2 * HD), BF),
                pltpu.VMEM((2, length, 2 * HD), BF),
                pltpu.VMEM((bk, 2 * HD), F32),
                pltpu.VMEM((bk, 2 * HD), F32),
                pltpu.VMEM((pairs, parts, 3, rows, 2 * HD), BF),
                pltpu.SemaphoreType.DMA((2, pairs)),
                pltpu.SemaphoreType.DMA((pairs,)),
                pltpu.VMEM((2, 2 * HD, length), BF),
                pltpu.VMEM((2, 2 * HD, length), BF),
            ],
        ),
        compiler_params=pltpu.CompilerParams(
            dimension_semantics=("arbitrary",), vmem_limit_bytes=VMEM,
            collective_id=ident, has_side_effects=True,
        ),
        cost_estimate=cost(40 * length * length * width, 24 * length * width),
        name="attend_back",
    )(starts, qkv, qkv, qkv, mixed, grad_mix, lse)


def stats(x):
    center = x - jnp.mean(x, axis=-1, keepdims=True)
    return center, lax.rsqrt(jnp.mean(center * center, axis=-1, keepdims=True) + 1e-05)


def norm_back(x, gain, grad):
    center, r = stats(x)
    n = center * r
    e = grad * gain
    return r * (e - jnp.mean(e, axis=-1, keepdims=True) - n * jnp.mean(e * n, axis=-1, keepdims=True))


def row_loop(rows, chunk, body):
    if chunk == rows:
        body(slice(None))
        return

    @pl.loop(0, rows // chunk)
    def _(i):
        body(pl.ds(pl.multiple_of(i * chunk, chunk), chunk))


def qkv_kernel(
    tok_ref, gain_ref, bias_ref, low_in_ref, w_ref, low_up_ref, norm_ref, low_ref, all_ref,
    send_ref, sems, own_sems,
):
    rows = tok_ref.shape[0]
    side, j = pl.program_id(0), pl.program_id(1)
    b, sib = pair_core()

    @pl.when((side == 0) & (j == 0))
    def _():
        def body(at):
            center, r = stats(tok_ref[at, :].astype(F32))
            normed = (center * r * gain_ref[...] + bias_ref[...]).astype(BF)
            norm_ref[at, :] = normed
            low_ref[at, :] = nt(normed, low_in_ref[...]).astype(BF)

        row_loop(rows, 256, body)
        greet_core(sib)

    w = w_ref[...].reshape(norm_ref.shape[1], -1)
    y = nn(norm_ref[...], w) + nn(low_ref[...], low_up_ref[...])
    send_ref[side, j] = y.astype(BF)

    def far(n):
        return to_core(send_ref.at[0, n], all_ref.at[b, n], sems, n, sib)

    def own(n):
        return pltpu.make_async_copy(send_ref.at[1, n], all_ref.at[b, n], own_sems.at[n])

    pl.when(side == 0)(lambda: far(j).start())
    pl.when(side == 1)(lambda: own(j).start())

    @pl.when((side == 1) & (j == 2))
    def _():
        for n in range(3):
            own(n).wait()
            far(n).wait()


def whole(shape):
    return pl.BlockSpec(shape, lambda *_: (0,) * len(shape))


def project_qkv(tok, gain, bias, low_in, w, low_up, ident):
    rows, features = tok.shape
    shards, groups, _, part, width = w.shape
    rank = low_in.shape[0]

    def heads(side):
        b = lax.axis_index("dp") % 2
        return jnp.where(side == 0, 1 - b, b)

    return pl.pallas_call(
        qkv_kernel,
        out_shape=(
            jax.ShapeDtypeStruct((rows, features), BF),
            jax.ShapeDtypeStruct((rows, rank), BF),
            jax.ShapeDtypeStruct((groups, 3, rows, width), BF),
        ),
        grid=(groups, 3),
        in_specs=[
            whole((rows, features)), whole((1, features)), whole((1, features)),
            whole((rank, features)),
            pl.BlockSpec((shards, None, None, part, width), lambda g, j: (0, heads(g), j, 0, 0)),
            pl.BlockSpec((None, rank, width), lambda g, j: (heads(g), 0, j)),
        ],
        out_specs=[
            whole((rows, features)), whole((rows, rank)), pl.BlockSpec(memory_space=pl.ANY),
        ],
        scratch_shapes=[
            pltpu.VMEM((groups, 3, rows, width), BF),
            pltpu.SemaphoreType.DMA((2, 3)),
            pltpu.SemaphoreType.DMA((3,)),
        ],
        compiler_params=pltpu.CompilerParams(
            dimension_semantics=("arbitrary", "arbitrary"), vmem_limit_bytes=VMEM,
            collective_id=ident, has_side_effects=True,
        ),
        cost_estimate=cost(4 * rows * features * groups * 3 * width, 4 * rows * groups * 3 * width),
        name="project_qkv",
    )(tok, gain, bias, low_in, w, low_up)


def qkv_back_kernel(
    planes, g_ref, w_any, low_up_ref, low_in_ref, norm_ref, low_ref, tok_ref, gain_ref, resid_ref, tag_ref,
    grad_ref, late_ref, far_ref,
    w_ref, own_ref, glow_ref, send_ref, w_sem, swap_sem, *sems,
):
    s = pl.program_id(0)
    groups, _, rows, width = g_ref.shape
    chunk, features = tok_ref.shape
    parts = rows // chunk
    gather = Gather(own_ref.at[0], late_ref, *sems, planes, own_ref.at[1])
    moves = gather.c != gather.t
    partner = (gather.place(gather.z, gather.x, gather.t), gather.c)
    blocks = [(g, j) for g in range(groups) for j in range(3)]

    def load_w():
        return pltpu.make_async_copy(w_any, w_ref, w_sem)

    def swap(n):
        return to_core(
            send_ref.at[n], far_ref.at[pl.ds(n * chunk, chunk)], swap_sem, n, partner
        )

    @pl.when(s == 0)
    def _():
        load_w().start()
        gather.greet([(moves, partner)])
        low = low_ref[...]
        glow = None
        for n, (g, j) in enumerate(blocks):
            part = g_ref[g, j]
            more = nt(part, low_up_ref[g, :, j * width : (j + 1) * width])
            glow = more if glow is None else glow + more
            own_ref[(g + gather.t) % 2, j] = tn(low, part).astype(BF)
        glow = glow.astype(BF)
        glow_ref[...] = glow
        y = tn(glow, norm_ref[...]).astype(BF)
        for side in range(2):
            for n in range(features // width):
                own_ref[side, 3 + n] = y[:, n * width : (n + 1) * width]
            own_ref[side, own_ref.shape[1] - 1] = tag_ref[...]
        gather.round(0)

    @pl.when(s == 1)
    def _():
        gather.round(1)
        load_w().wait()

    @pl.when(s > 0)
    def _():
        at = pl.ds(pl.multiple_of((s - 1) * chunk, chunk), chunk)
        total = nn(glow_ref[at, :], low_in_ref[...])
        for g, j in blocks:
            total = total + nt(g_ref[g, j, at, :], w_ref[:, g, j].reshape(features, width))
        grad = resid_ref[...] + norm_back(tok_ref[...].astype(F32), gain_ref[...], total)
        grad_ref[...] = grad
        send_ref[s - 1] = grad.astype(BF)

        @pl.when(moves)
        def _():
            swap(s - 1).start()

    for k in range(2, gather.rounds):
        pl.when(s == min(k - 1, parts))(lambda k=k: gather.round(k))

    @pl.when(s == parts)
    def _():
        gather.finish()

        @pl.when(moves)
        def _():
            for n in range(parts):
                swap(n).wait()


def project_qkv_back(grad, w, low_up, low_in, normed, low, tok, gain, resid, tag, ident):
    rows, features = tok.shape
    shards, groups, _, part, width = w.shape
    rank = low_in.shape[0]
    planes = shards // 4
    parts = 4
    chunk = rows // parts
    late = (3 + features // width + 1, rank, width)
    anywhere = pl.BlockSpec(memory_space=pl.ANY)

    def keep(shape):
        return pl.BlockSpec(shape, lambda s: (0,) * len(shape), pipeline_mode=pl.Buffered(1))

    some = pl.BlockSpec((chunk, features), lambda s: (jnp.maximum(s - 1, 0), 0))
    return pl.pallas_call(
        functools.partial(qkv_back_kernel, planes),
        out_shape=(
            jax.ShapeDtypeStruct((rows, features), F32),
            jax.ShapeDtypeStruct((shards, 2) + late, BF),
            jax.ShapeDtypeStruct((rows, features), BF),
        ),
        grid=(1 + parts,),
        in_specs=[
            keep(grad.shape), anywhere, keep((groups, rank, 3 * width)), keep((rank, features)),
            keep((rows, features)), keep((rows, rank)), some, keep((1, features)), some,
            keep((rank, width)),
        ],
        out_specs=[some, anywhere, anywhere],
        scratch_shapes=[
            pltpu.VMEM(w.shape, BF),
            pltpu.VMEM((2,) + late, BF),
            pltpu.VMEM((rows, rank), BF),
            pltpu.VMEM((parts, chunk, features), BF),
            pltpu.SemaphoreType.DMA,
            pltpu.SemaphoreType.DMA((2, parts)),
            *gather_sems(1, planes),
        ],
        compiler_params=pltpu.CompilerParams(
            dimension_semantics=("arbitrary",), vmem_limit_bytes=VMEM,
            collective_id=ident, has_side_effects=True,
        ),
        cost_estimate=cost(5 * rows * features * groups * 3 * width, 4 * rows * groups * 3 * width),
        name="project_qkv_back",
    )(grad, w, low_up, low_in, normed, low, tok, gain, resid, tag)


GELU = math.sqrt(2.0 / math.pi)


def gelu_and_slope(v):
    v2 = v * v
    half = 0.5 + 0.5 * jnp.tanh(v * (GELU + (GELU * 0.044715) * v2))
    hidden = v * half
    return hidden, half + hidden * (1.0 - half) * (2.0 * GELU + (6.0 * 0.044715 * GELU) * v2)


def middle_kernel(
    groups, nf,
    w_ref, sh_ref, wo_ref, sho_ref, tok_ref, mix_ref, cot_any, far_any, gain_ref, bias_ref, rep_ref,
    out_ref, resid_ref, gr_ref, do_ref,
    acc_ref, norm_ref, hid_ref, slope_ref, lacc_ref, llow_ref, send_ref, sems, own_sem, cot_ref, cot_sem,
):
    rows, features = tok_ref.shape
    rank = sh_ref.shape[0]
    s = pl.program_id(0)
    b_out, a_up, b_down = rep_ref[0], rep_ref[1], rep_ref[2]
    co = wo_ref.shape[-1]
    up0, down0 = groups, groups + nf
    upb0, end0 = groups + 2 * nf, groups + 3 * nf
    b, sib = pair_core()
    pl.when(s == 0)(lambda: greet_core(sib))
    keeps = b == lax.axis_index("tensor")

    def load_cot(source):
        return pltpu.make_async_copy(source, cot_ref, cot_sem)

    pl.when((s == 0) & keeps)(lambda: load_cot(cot_any).start())
    pl.when((s == 0) & jnp.logical_not(keeps))(lambda: load_cot(far_any).start())

    for g in range(groups):

        @pl.when(s == g)
        def _():
            part = mix_ref[g]
            y = nt(part, wo_ref[...].reshape(features, co))
            low = nt(part, sho_ref[...])
            if g == 0:
                resid_ref[...] = tok_ref[...].astype(F32) + y
                lacc_ref[...] = low
            else:
                resid_ref[...] += y
                lacc_ref[...] += low

    @pl.when(s == up0 - 1)
    def _():
        def body(at):
            low = lacc_ref[at, :].astype(BF)
            llow_ref[0, at, :] = low
            resid = resid_ref[at, :] + nn(low, b_out)
            resid_ref[at, :] = resid
            center, r = stats(resid)
            normed = (center * r * gain_ref[...] + bias_ref[...]).astype(BF)
            norm_ref[at, :] = normed
            llow_ref[1, at, :] = nt(normed, a_up).astype(BF)

        row_loop(rows, 256, body)
        load_cot(cot_any).wait()
        llow_ref[3] = nt(cot_ref[...], b_down).astype(BF)
        acc_ref[...] = jnp.zeros_like(acc_ref)
        lacc_ref[...] = jnp.zeros_like(lacc_ref)

    @pl.when((s >= up0) & (s < down0))
    def _():
        f = s - up0
        w = w_ref[...].reshape(features, -1)

        chunks = [slice(n * 256, (n + 1) * 256) for n in range(rows // 256)]

        def scores(at):
            return nn(norm_ref[at, :], w) + nn(llow_ref[1, at, :], sh_ref[...])

        ahead = [scores(at) for at in chunks[:2]]
        for n, at in enumerate(chunks):
            if n + 2 < len(chunks):
                ahead.append(scores(chunks[n + 2]))
            hidden, slope = gelu_and_slope(ahead[n])
            hid_ref[f, at, :] = hidden.astype(BF)
            slope_ref[f, at, :] = slope.astype(BF)

    @pl.when((s >= down0) & (s < upb0))
    def _():
        f = s - down0
        w = w_ref[...].reshape(features, -1)
        sh = sh_ref[...]
        hidden = hid_ref[f]
        acc_ref[...] += nt(hidden, w)
        lacc_ref[...] += nt(hidden, sh)
        g_hidden = nn(cot_ref[...], w) + nn(llow_ref[3], sh)
        g_pre = (g_hidden * slope_ref[f].astype(F32)).astype(BF)
        slope_ref[f] = g_pre
        gr_ref[:rank, :] = tn(llow_ref[3], hidden).astype(BF)
        gr_ref[rank:, :] = tn(llow_ref[1], g_pre).astype(BF)

    @pl.when(s == upb0 - 1)
    def _():
        def body(at):
            low = lacc_ref[at, :].astype(BF)
            llow_ref[2, at, :] = low
            out_ref[at, :] = (resid_ref[at, :] + acc_ref[at, :] + nn(low, b_down)).astype(BF)

        row_loop(rows, 512, body)
        acc_ref[...] = jnp.zeros_like(acc_ref)
        lacc_ref[...] = jnp.zeros_like(lacc_ref)

    @pl.when((s >= upb0) & (s < end0))
    def _():
        f = s - upb0
        w = w_ref[...].reshape(features, -1)
        part = slope_ref[f]
        acc_ref[...] += nt(part, w)
        lacc_ref[...] += nt(part, sh_ref[...])

    @pl.when(s == end0 - 1)
    def _():
        gr_ref[:rank, :] = tn(llow_ref[2], cot_ref[...]).astype(BF)
        llow_ref[4] = lacc_ref[...].astype(BF)
        gr_ref[rank:, :] = tn(llow_ref[4], norm_ref[...]).astype(BF)

        def body(at):
            total = acc_ref[at, :] + nn(llow_ref[4, at, :], a_up)
            g = cot_ref[at, :].astype(F32) + norm_back(resid_ref[at, :], gain_ref[...], total)
            resid_ref[at, :] = g
            branch = g.astype(BF)
            norm_ref[at, :] = branch
            llow_ref[5, at, :] = nt(branch, b_out).astype(BF)

        row_loop(rows, 256, body)

    def far():
        return to_core(send_ref.at[0], do_ref.at[b], sems, 0, sib)

    def own():
        return pltpu.make_async_copy(send_ref.at[1], do_ref.at[b], own_sem)

    @pl.when(s >= end0)
    def _():
        turn = s - end0
        g = jnp.where(turn == 0, 1 - b, b)
        wo = wo_ref[...].reshape(features, co)
        y = nn(norm_ref[...], wo) + nn(llow_ref[5], sho_ref[...])
        send_ref[turn] = y.astype(BF)
        at = pl.ds(pl.multiple_of(g * co, co), co)
        gr_ref[:rank, at] = tn(llow_ref[5], mix_ref[g]).astype(BF)

    @pl.when(s == end0)
    def _():
        far().start()
        gr_ref[rank:, :] = tn(llow_ref[0], norm_ref[...]).astype(BF)

    @pl.when(s == end0 + 1)
    def _():
        own().start()
        own().wait()
        far().wait()


def middle(w, shared, tok, mix, cot, far_cot, gain, bias, rep, ident):
    rows, features = tok.shape
    shards, groups, part, total = w.shape
    rank = rep.shape[1]
    co = mix.shape[2]
    ffw = (total - co) // 2
    c = features
    halves = ffw // c
    nf = groups * halves
    first = (shared.shape[2] - 2 * ffw) // c
    out_at, out_shared = 2 * ffw // co, (shared.shape[2] - 2 * ffw) // co - 1
    blocks = [(f // halves, f % halves) for f in range(nf)]
    up = [(t, h, h) for t, h in blocks]
    down_step = [(t, halves + h, halves + h) for t, h in blocks]
    shared_group = [t for t, _ in blocks]
    order = [up[0]] * groups + up + down_step + up + [up[-1]] * groups
    shared_of = [0] * groups + shared_group * 3 + [shared_group[-1]] * groups
    of_grad = [0] * (groups + nf) + list(range(nf)) + [nf + 1] * nf + [nf] * groups
    last = len(order) - groups
    anywhere = pl.BlockSpec(memory_space=pl.ANY)

    def group(s):
        b = lax.axis_index("dp") % 2
        return jnp.where(s < last, jnp.minimum(s, groups - 1), jnp.where(s == last, 1 - b, b))

    once = pl.Buffered(1)

    def keep(shape):
        return pl.BlockSpec(shape, lambda s, *_: (0,) * len(shape), pipeline_mode=once)

    def at(table_row):
        def index(s):
            got = table_row[0]
            for n in range(1, len(table_row)):
                if table_row[n] != table_row[n - 1]:
                    got = got + jnp.where(s >= n, table_row[n] - table_row[n - 1], 0)
            return got
        return index

    w_t, w_c = at([x[0] for x in order]), at([x[1] for x in order])
    s_t, s_c, gi = at(shared_of), at([x[2] for x in order]), at(of_grad)
    return pl.pallas_call(
        functools.partial(middle_kernel, groups, nf),
        out_shape=(
            jax.ShapeDtypeStruct((rows, features), BF),
            jax.ShapeDtypeStruct((rows, features), F32),
            jax.ShapeDtypeStruct((nf + 2, 2 * rank, c), BF),
            jax.ShapeDtypeStruct(mix.shape, BF),
        ),
        grid=(len(order),),
        in_specs=[
            pl.BlockSpec((shards, None, part, c), lambda s: (0, w_t(s), 0, w_c(s))),
            pl.BlockSpec((None, rank, c), lambda s: (s_t(s), 0, s_c(s) + first)),
            pl.BlockSpec((shards, None, part, co), lambda s: (0, group(s), 0, out_at)),
            pl.BlockSpec((None, rank, co), lambda s: (group(s), 0, out_shared)),
            keep((rows, features)), keep(mix.shape), anywhere, anywhere,
            keep((1, features)), keep((1, features)), keep(rep.shape),
        ],
        out_specs=[
            keep((rows, features)), keep((rows, features)),
            pl.BlockSpec((None, 2 * rank, c), lambda s: (gi(s), 0, 0)), anywhere,
        ],
        scratch_shapes=[
            pltpu.VMEM((rows, features), F32),
            pltpu.VMEM((rows, features), BF),
            pltpu.VMEM((nf, rows, c), BF),
            pltpu.VMEM((nf, rows, c), BF),
            pltpu.VMEM((rows, rank), F32),
            pltpu.VMEM((6, rows, rank), BF),
            pltpu.VMEM(mix.shape, BF),
            pltpu.SemaphoreType.DMA((2, 1)),
            pltpu.SemaphoreType.DMA,
            pltpu.VMEM((rows, features), BF),
            pltpu.SemaphoreType.DMA,
        ],
        compiler_params=pltpu.CompilerParams(
            dimension_semantics=("arbitrary",), vmem_limit_bytes=VMEM,
            collective_id=ident, has_side_effects=True,
        ),
        cost_estimate=cost(6 * rows * features * groups * total, 4 * features * groups * total),
        name="middle",
    )(w, shared, w, shared, tok, mix, cot, far_cot, gain, bias, rep)


class Gather:
    def __init__(self, shard, full, out_sem, in_sem, own_sem, planes, shard_near=None):
        self.shard, self.full, self.planes = shard, full, planes
        self.shard_near = shard if shard_near is None else shard_near
        self.chunks = out_sem.shape[0]
        self.out_sem, self.in_sem, self.own_sem = out_sem, in_sem, own_sem
        self.rounds = planes + 2
        dp, t = lax.axis_index("dp"), lax.axis_index("tensor")
        z, x, c = dp // 4, (dp // 2) % 2, dp % 2
        self.dp, self.z, self.x, self.c, self.t = dp, z, x, c, t
        self.low, self.high = z > 0, z < planes - 1
        self.below = jnp.maximum(dp - 4, 0), t
        self.above = jnp.minimum(dp + 4, 4 * planes - 1), t
        self.near = dp, 1 - t
        self.across = self.place(z, 1 - x, c), t
        self.sib = self.place(z, x, 1 - c), t
        self.plan = [self.lay_out(k) for k in range(self.rounds)]

    def place(self, z, x, c):
        return z * 4 + x * 2 + c

    def greet(self, extra=()):
        barrier = pltpu.get_barrier_semaphore()

        def hello(who):
            pl.semaphore_signal(barrier, inc=1, device_id=who, device_id_type=MESH)

        for who in (self.near, self.across, self.sib):
            hello(who)
        count = 3
        for cond, who in ((self.low, self.below), (self.high, self.above)) + tuple(extra):
            pl.when(cond)(lambda who=who: hello(who))
            count = count + cond.astype(jnp.int32)
        pl.semaphore_wait(barrier, count)

    def piece(self, ref, n):
        if self.chunks == 1:
            return ref
        size = ref.shape[-2] // self.chunks
        every = (slice(None),) * (len(ref.shape) - 2)
        return ref.at[every + (pl.ds(n * size, size), slice(None))]

    def copy(self, n, at, who, sem, own=False):
        slot = self.piece(self.full.at[at[0], at[1]], n)
        mine = self.shard_near if who is self.near else self.shard
        return pltpu.make_async_remote_copy(
            src_ref=self.piece(mine, n) if own else slot, dst_ref=slot,
            send_sem=self.out_sem.at[n, sem],
            recv_sem=self.in_sem.at[n, at[0] * 2 + at[1]], device_id=who, device_id_type=MESH,
        )

    def arrive(self, n, at):
        self.copy(n, at, self.sib, 0).wait_recv()

    def own_copy(self, n):
        here = self.piece(self.full.at[self.dp, self.t], n)
        return pltpu.make_async_copy(self.piece(self.shard, n), here, self.own_sem.at[n])

    def lay_out(self, k):
        z, planes, t = self.z, self.planes, self.t
        events = []

        def ways(hops):
            if not 0 <= hops < planes:
                return []
            if hops == 0:
                return [(z, None, [(self.low, self.below, 0), (self.high, self.above, 1)])]
            up, down = z >= hops, z + hops < planes
            return [
                (z - hops, up, [(up & self.high, self.above, 1)]),
                (z + hops, down, [(down & self.low, self.below, 0)]),
            ]

        for n in range(self.chunks):
            for zz, cond, on in ways(k):
                sends = on + [(cond, self.across, 2), (cond, self.sib, 4)]
                if k == 0:
                    sends = [(None, self.near, 3)] + sends
                events.append((n, cond, (self.place(zz, self.x, self.c), t), k == 0, zz, sends))
            for zz, cond, on in ways(k - 1):
                sends = [(c, who, kind + 5) for c, who, kind in on]
                sends += [(cond, self.across, 7), (cond, self.sib, 8)]
                events.append((n, cond, (self.place(zz, self.x, self.c), 1 - t), False, zz, sends))
                far = self.place(zz, 1 - self.x, self.c), t
                events.append((n, cond, far, False, zz, [(cond, self.sib, 9)]))
            for zz, cond, _ in ways(k - 2):
                far = self.place(zz, 1 - self.x, self.c), 1 - t
                events.append((n, cond, far, False, zz, [(cond, self.sib, 10)]))
        return [
            (n, cond, where, own, [(c, who, kind * planes + zz) for c, who, kind in sends])
            for n, cond, where, own, zz, sends in events
        ]

    def when(self, cond, act):
        if cond is None:
            act()
        else:
            pl.when(cond)(act)

    def round(self, k):
        for n, cond, where, own, sends in self.plan[k]:
            if not own:
                self.when(cond, lambda n=n, where=where: self.arrive(n, where))
            for c, who, sem in sends:
                self.when(
                    c,
                    lambda n=n, where=where, who=who, sem=sem, own=own: self.copy(
                        n, where, who, sem, own
                    ).start(),
                )
            if own:
                self.own_copy(n).start()

    def finish(self):
        for n in range(self.chunks):
            for zz in range(self.planes):
                for x in (self.x, 1 - self.x):
                    for t in (self.t, 1 - self.t):
                        self.arrive(n, (self.place(zz, x, 1 - self.c), t))
            self.own_copy(n).wait()
        for events in self.plan:
            for n, _, where, own, sends in events:
                for c, who, sem in sends:
                    self.when(
                        c,
                        lambda n=n, where=where, who=who, sem=sem, own=own: self.copy(
                            n, where, who, sem, own
                        ).wait_send(),
                    )


def gather_sems(n, planes):
    return [
        pltpu.SemaphoreType.DMA((n, 11 * planes)),
        pltpu.SemaphoreType.DMA((n, 8 * planes)),
        pltpu.SemaphoreType.DMA((n,)),
    ]


def spread_kernel(n_all, kinds, planes, *refs):
    n_swap = len(kinds)
    shard = refs[:n_all]
    swap_in = refs[n_all : n_all + n_swap]
    full = refs[n_all + n_swap : 2 * n_all + n_swap]
    swap_out = refs[2 * n_all + n_swap : 2 * n_all + 2 * n_swap]
    *sems, swap_sem = refs[2 * n_all + 2 * n_swap :]
    g = Gather(shard[0], full[0], *sems, planes)
    moves = g.c != g.t
    keeps = jnp.logical_not(moves)
    partner = (g.place(g.z, g.x, g.t), g.c)
    g.greet([(moves, partner)])
    rules = {"partner": (moves, partner, moves), "near": (moves, g.near, keeps), "sibling": (keeps, g.sib, moves)}

    def swap_copy(n):
        return pltpu.make_async_remote_copy(
            src_ref=swap_in[n], dst_ref=swap_out[n], send_sem=swap_sem.at[n, 0],
            recv_sem=swap_sem.at[n, 1], device_id=rules[kinds[n]][1], device_id_type=MESH,
        )

    for n in range(n_swap):
        pl.when(rules[kinds[n]][0])(lambda n=n: swap_copy(n).start())
    for k in range(g.rounds):
        g.round(k)
    g.finish()
    for n in range(n_swap):
        pl.when(rules[kinds[n]][0])(lambda n=n: swap_copy(n).wait_send())
        pl.when(rules[kinds[n]][2])(lambda n=n: swap_copy(n).wait_recv())


def spread(gathered, handed, shards, ident):
    planes = shards // 4
    swapped = [a for a, _ in handed]
    n_all, n_swap = len(gathered), len(swapped)
    anywhere = pl.BlockSpec(memory_space=pl.ANY)
    return pl.pallas_call(
        functools.partial(spread_kernel, n_all, [k for _, k in handed], planes),
        out_shape=[jax.ShapeDtypeStruct((shards, 2) + a.shape, a.dtype) for a in gathered]
        + [jax.ShapeDtypeStruct(a.shape, a.dtype) for a in swapped],
        in_specs=[anywhere] * (n_all + n_swap),
        out_specs=[anywhere] * (n_all + n_swap),
        scratch_shapes=[
            *gather_sems(SPREAD_CHUNKS, planes),
            pltpu.SemaphoreType.DMA((max(n_swap, 1), 2)),
        ],
        compiler_params=pltpu.CompilerParams(collective_id=ident, has_side_effects=True),
        cost_estimate=cost(0, 60 * MIB),
        name="spread%d" % ident,
    )(*gathered, *swapped)


def sum_kernel(pieces, sel_ref, t_ref, *refs):
    ins, outs = refs[: len(refs) - len(pieces)], refs[len(refs) - len(pieces) :]
    step = pl.program_id(0)
    devices = ins[0].shape[0]

    @pl.when(step == 0)
    def _():
        for out in outs:
            out[...] = jnp.zeros_like(out)

    @pl.loop(0, devices)
    def _(d):
        for (at, which, blocks), out in zip(pieces, outs):
            slot = sel_ref[step * devices + d, which]
            rank = out.shape[-2]
            c = ins[at].shape[-1]
            for k, (block, row) in enumerate(blocks):
                new = ins[at][d, block, row : row + rank, :].astype(F32)
                if len(out.shape) == 4:
                    out[slot, k] += new
                else:
                    out[slot, :, k * c : (k + 1) * c] += new


def sum_picks(sel, t, arrays, pieces, slots, rank, name):
    steps = 4
    in_specs = []
    for a, shape, where in arrays:
        in_specs.append(
            pl.BlockSpec(
                (a.shape[0] // steps,) + shape, lambda s, sel, t, where=where: (s,) + where(t[0])
            )
        )
    shapes = []
    for at, _, blocks, flat in pieces:
        n, c = len(blocks), arrays[at][1][-1]
        shapes.append((slots, rank, n * c) if flat else (slots, n, rank, c))
    return pl.pallas_call(
        functools.partial(sum_kernel, [p[:3] for p in pieces]),
        out_shape=[jax.ShapeDtypeStruct(shape, F32) for shape in shapes],
        grid_spec=pltpu.PrefetchScalarGridSpec(
            num_scalar_prefetch=2, grid=(steps,), in_specs=in_specs,
            out_specs=[whole(shape) for shape in shapes],
        ),
        compiler_params=pltpu.CompilerParams(
            dimension_semantics=("arbitrary",), vmem_limit_bytes=VMEM
        ),
        cost_estimate=cost(0, 30 * MIB),
        name=name,
    )(sel, t, *[a for a, _, _ in arrays])


def pick_kernel(idx_ref, bq_ref, ao_ref, bu_ref, ad_ref, aq_ref, bo_ref, au_ref, bd_ref, marks_ref, half_ref, rest_ref, m_ref):
    at = 0
    for j in range(bq_ref.shape[0]):
        half_ref[:, at : at + bq_ref.shape[2]] = bq_ref[j]
        at += bq_ref.shape[2]
    for ref in (ao_ref, bu_ref, ad_ref):
        half_ref[:, at : at + ref.shape[1]] = ref[...]
        at += ref.shape[1]
    for n, ref in enumerate((aq_ref, bo_ref, au_ref, bd_ref)):
        rest_ref[n] = ref[...]
    m_ref[...] = jnp.broadcast_to(marks_ref[...], m_ref.shape)


def pick_adapters(idx, split, full, marks):
    rank = full[0].shape[1]
    width = split[0].shape[1] * split[0].shape[3] + sum(a.shape[2] for a in split[1:])

    def one(a, which):
        rest = a.shape[1:]
        return pl.BlockSpec((None,) + rest, lambda i, idx: (idx[which],) + (0,) * len(rest))

    in_specs = [one(a, n) for n, a in enumerate(split)] + [one(a, n) for n, a in enumerate(full)]
    return pl.pallas_call(
        pick_kernel,
        out_shape=(
            jax.ShapeDtypeStruct((rank, width), BF),
            jax.ShapeDtypeStruct((len(full),) + full[0].shape[1:], BF),
            jax.ShapeDtypeStruct((8, 128), jnp.int32),
        ),
        grid_spec=pltpu.PrefetchScalarGridSpec(
            num_scalar_prefetch=1, grid=(1,), in_specs=in_specs + [whole(marks.shape)],
            out_specs=[whole((rank, width)), whole((len(full),) + full[0].shape[1:]), whole((8, 128))],
        ),
        compiler_params=pltpu.CompilerParams(dimension_semantics=("arbitrary",)),
        cost_estimate=cost(0, MIB),
        name="pick_adapters",
    )(idx, *split, *full, marks)


def chip_device(
    tokens, w_qkv, w_out, w_up, w_down, ln1_gain, ln1_bias, ln2_gain, ln2_bias,
    a_qkv, b_qkv, a_out, b_out, a_up, b_up, a_down, b_down, adapter_idx, pic_start, cotangent,
):
    shards = lax.axis_size("dp")
    dp, t = lax.axis_index("dp"), lax.axis_index("tensor")
    keeps = dp % 2 == t
    both = ("dp", "tensor")
    swap = []
    for c in range(shards // 2):
        one, two = 2 * (2 * c + 1), 2 * (2 * c) + 1
        swap += [(one, two), (two, one)]

    def swapped(x):
        return lax.ppermute(x, both, swap)

    def row(v):
        return v.reshape(1, -1)

    rank, slots = a_qkv.shape[2], a_qkv.shape[0]
    features, width = tokens.shape[1], w_out.shape[0]
    chosen = adapter_idx[0]

    turned = lambda v: v.transpose(0, 2, 1)
    marks = jnp.concatenate([chosen, pic_start[0]])
    half, rest, marks = pick_adapters(
        chosen,
        [b_qkv.transpose(0, 2, 1, 3), turned(a_out), b_up, turned(a_down)],
        [turned(a_qkv), b_out, turned(a_up), b_down],
        jnp.pad(marks, (0, 128 - marks.shape[0]))[None],
    )

    qkv_shard = w_qkv.transpose(1, 0, 2)
    rest_shard = jnp.concatenate([w_up, w_down.T, w_out.T], axis=1)
    rest_full = lax.all_gather(rest_shard, both, axis=0)
    rest_full = rest_full.reshape(shards, 2, *rest_shard.shape)
    qkv_full, far_tokens, near_half, partner_half, core_half, core_rest, core_marks = spread(
        [qkv_shard],
        [
            (tokens, "partner"), (half, "near"), (half, "partner"),
            (half, "sibling"), (rest, "sibling"), (marks, "sibling"),
        ],
        shards,
        0,
    )
    later, far_tokens = lax.optimization_barrier((cotangent, far_tokens))
    far_cot = swapped(later)
    tok = jnp.where(keeps, tokens, far_tokens)
    own_half = jnp.where(keeps, half, core_half)
    far_half = jnp.where(keeps, near_half, partner_half)
    shared = jnp.where(t == 0, jnp.stack([own_half, far_half]), jnp.stack([far_half, own_half]))
    rep = jnp.where(keeps, rest, core_rest)
    marks = jnp.where(keeps, marks, core_marks)[0]
    starts = marks[4 : 4 + pic_start.shape[1]]
    tag = jnp.pad(marks[:4].astype(BF)[None], ((0, rank - 1), (0, width - 4)))

    normed, low, qkv = project_qkv(tok, row(ln1_gain), row(ln1_bias), rep[0], qkv_full, shared, 2)
    mixed, lse, mix = attend_rows(starts, qkv, 3)
    layer_out, g_resid, g_early, g_mix = middle(
        rest_full, shared, tok, mix, cotangent, far_cot, row(ln2_gain), row(ln2_bias), rep[1:], 4
    )
    early = lax.all_gather(g_early, both, axis=0)
    out = jnp.where(keeps, layer_out, swapped(layer_out))
    g_qkv = attend_rows_back(starts, qkv, mixed, g_mix, lse, 5)
    grad_tok, late, far_grad = project_qkv_back(
        g_qkv, qkv_full, shared, rep[0], normed, low, tok, row(ln1_gain), g_resid, tag, 1
    )
    grad_input = jnp.where(keeps, grad_tok, far_grad.astype(F32))

    late = late.reshape(2 * shards, *late.shape[2:])
    sel = late[:, -1, 0, :4].astype(jnp.int32)
    side = t.reshape(1).astype(jnp.int32)
    nf, c = g_early.shape[0] - 2, g_early.shape[2]
    near = range(nf // 2)
    rows2 = 2 * rank
    early = early.reshape(2 * shards, *g_early.shape)
    (
        grad_a_out, grad_b_out, grad_a_up, grad_b_up, grad_a_down, grad_b_down, grad_b_qkv, grad_a_qkv,
    ) = sum_picks(
        sel, side,
        [
            (early, (nf // 2, rows2, c), lambda u: (u, 0, 0)),
            (early, (1, rows2, width), lambda u: (nf, 0, u)),
            (early, (2, rows2, c), lambda u: (nf // 2, 0, 0)),
            (late, (3, rank, width), lambda u: (0, 0, 0)),
            (late, (3, rank, width), lambda u: (1, 0, 0)),
        ],
        [
            (1, 1, [(0, 0)], True),
            (2, 1, [(0, rank)], True),
            (2, 2, [(1, rank)], True),
            (0, 2, [(i, rank) for i in near], True),
            (0, 3, [(i, 0) for i in near], True),
            (2, 3, [(1, 0)], True),
            (3, 0, [(0, 0), (1, 0), (2, 0)], False),
            (4, 0, [(0, 0), (1, 0)], True),
        ],
        slots, rank, "sum_picks",
    )
    return (
        out, grad_input, turned(grad_a_qkv), grad_b_qkv.transpose(0, 2, 1, 3),
        turned(grad_a_out), grad_b_out, turned(grad_a_up), grad_b_up, turned(grad_a_down), grad_b_down,
    )


def solution(mesh):
    placed = (
        P(("dp", "tensor"), None),
        P("dp", None, "tensor"),
        P("tensor", "dp"),
        P("dp", "tensor"),
        P("tensor", "dp"),
        P(),
        P(),
        P(),
        P(),
        P(),
        P(None, None, None, "tensor"),
        P(None, "tensor", None),
        P(),
        P(),
        P(None, None, "tensor"),
        P(None, "tensor", None),
        P(),
        P("dp", None),
        P("dp", None),
        P(("dp", "tensor"), None),
    )
    paired = mesh.shape["tensor"] == 2 and mesh.shape["dp"] % 2 == 0
    return jax.shard_map(
        chip_device if paired else per_device,
        mesh=mesh,
        in_specs=placed,
        out_specs=(
            P(("dp", "tensor"), None),
            P(("dp", "tensor"), None),
            P(),
            P(None, None, None, "tensor"),
            P(None, "tensor", None),
            P(),
            P(),
            P(None, None, "tensor"),
            P(None, "tensor", None),
            P(),
        ),
        check_vma=False,
    )
```
